32 devices in a mesh: dp: 8 (over z, x), segment: 4 (over y, core).
Axes of the slice: x: 2, y: 2, z: 4, core: 2. Of those that a mesh axis runs over, the one named last changes fastest.
Arguments:
- latents: float32 [24, 4, 4, 16, 16], P('dp'), may hold values from -6 to 6
- noise_draw: float32 [24, 4, 4, 16, 16], P('dp'), may hold values from -6 to 6
- timesteps: int32 [24], P('dp'), may hold values from 1 to 999
- captions: bfloat16 [24, 300, 4096], P('dp'), may hold values from -2 to 2
- caption_len: int32 [24], P('dp'), may hold values from 1 to 300, as said below
- attention_weights: float32 [12, 384, 384], P(None, None, 'dp'), may hold values from -0.3125 to 0.3125
- feed_weights: float32 [4, 384, 1536], P(None, None, 'dp')
- side_weights: float32 [7456, 384], P(None, 'dp')
- vector_weights: float32 [45, 384], P(None, 'dp'), may hold values from -3 to 3
- attention_momentum: float32 [12, 384, 384], P(None, None, 'dp'), may hold values from -2.670288e-05 to 2.670288e-05
- feed_momentum: float32 [4, 384, 1536], P(None, None, 'dp'), may hold values from -2.670288e-05 to 2.670288e-05
- side_first: float32 [7456, 384], P(None, 'dp'), may hold values from -3.33786e-06 to 3.33786e-06
- side_second: float32 [7456, 384], P(None, 'dp'), may hold values from 3.566765e-15 to 1.426706e-14
- vector_first: float32 [45, 384], P(None, 'dp'), may hold values from -3.0517578e-05 to 3.0517578e-05
- vector_second: float32 [45, 384], P(None, 'dp'), may hold values from 3.5667652e-13 to 1.4267061e-12
- step_count: int32 [1], replicated, may hold values from 2 to 20
Outputs:
- loss_value: float32 [], replicated
- grad_norm: float32 [], replicated
- attention_new: float32 [12, 384, 384], P(None, None, 'dp')
- attention_moment: float32 [12, 384, 384], P(None, None, 'dp')
- feed_new: float32 [4, 384, 1536], P(None, None, 'dp')
- feed_moment: float32 [4, 384, 1536], P(None, None, 'dp')
- side_new: float32 [7456, 384], P(None, 'dp')
- side_first_new: float32 [7456, 384], P(None, 'dp')
- side_second_new: float32 [7456, 384], P(None, 'dp')
- vector_new: float32 [45, 384], P(None, 'dp')
- vector_first_new: float32 [45, 384], P(None, 'dp')
- vector_second_new: float32 [45, 384], P(None, 'dp')
- attention_bf16: bfloat16 [12, 384, 384], P(None, None, 'dp')
- feed_bf16: bfloat16 [4, 384, 1536], P(None, None, 'dp')
- side_bf16: bfloat16 [7456, 384], P(None, 'dp')
- vector_bf16: bfloat16 [45, 384], P(None, 'dp')
The draws below stay inside these ranges and needn't reach their ends.
Inputs may be any that keep to these rules, and one draw needn't show every extreme that they name: `caption_len`: each clip has 1 to 300 valid caption tokens, the first clip exactly 300.
All inputs are finite; a program needn't handle non-finite values.
Results may differ from the reference program's by a relative error of at most 0.0015.
The reference program's roundings to bfloat16 on the way count: a program that leaves them out, or rounds other values in their place, can miss the bound.
Values may be sent and summed in bfloat16 or wider, within the bound.
A program may use at most 256 MiB of HBM per device.

```python
import math
import jax
import jax.numpy as jnp
from jax import lax

D = 384
HEADS = 6
FF = 1536
TXT = 4096
LTXT = 300
FR = 4
LAT = 16
CLIPS = 24
SIDE = 7456
NVEC = 45
PARAMS = 7009152


def draw_caption_len(key, part):
    first_key, second_key = jax.random.split(jax.random.fold_in(key, 11))
    uniform_one = jax.random.randint(first_key, (CLIPS,), 1, LTXT + 1)
    uniform_two = jax.random.randint(second_key, (CLIPS,), 1, LTXT + 1)
    lengths = jnp.maximum(uniform_one * uniform_two // LTXT, 1)
    return lengths.at[0].set(LTXT).astype(jnp.int32)


def draw_feed_weights(key, part):
    fans = jnp.array([D, FF, D, FF], dtype=jnp.float32)
    values = jax.random.normal(jax.random.fold_in(key, 12), (4, D, FF), jnp.float32)
    return values * lax.rsqrt(fans)[:, None, None]


def draw_side_weights(key, part):
    places = jnp.arange(SIDE)
    caption_rows = jnp.logical_and(places >= 272 + D, places < 272 + D + TXT)
    fans = jnp.where(places < 16, 16.0, jnp.where(places < 272, 256.0, jnp.where(caption_rows, 1.0 * TXT, 1.0 * D)))
    values = jax.random.normal(jax.random.fold_in(key, 13), (SIDE, D), jnp.float32)
    return values * lax.rsqrt(fans)[:, None]


def place_ends(entries, key, least, high):
    shape = entries.shape
    place = [jax.random.randint(jax.random.fold_in(key, axis), (), 0, shape[axis]) for axis in range(len(shape))]
    entries = entries.at[tuple(place)].set(least)
    longest = shape.index(max(shape))
    place[longest] = (place[longest] + 1) % shape[longest]
    return entries.at[tuple(place)].set(high)


def shard_levels(stream_key, extent, cuts, low, high):
    level, own = 1.0, jax.random.fold_in(stream_key, 6)
    for position, parts in cuts:
        heights = jnp.exp(jax.random.uniform(jax.random.fold_in(own, position), (parts,), jnp.float32, low / len(cuts), high / len(cuts)))
        level = level * jnp.repeat(heights, extent[position] // parts).reshape([-1 if axis == position else 1 for axis in range(len(extent))])
    return level


def gaussian(own_key, dims, deviation, reach, cuts=(), held_as=jnp.bfloat16):
    values = jax.random.normal(own_key, dims, jnp.float32) * deviation
    if len(cuts) > 0:
        values = shard_levels(own_key, dims, cuts, -0.22, 0.18) * values
    return jnp.clip(values, min=-reach, max=reach).astype(held_as)


def setup_inputs(seed: int = 0) -> dict:
    splits = jax.random.split(jax.random.key(seed), 17)
    latents = gaussian(splits[0], (CLIPS, FR, 4, LAT, LAT), 1.0, 6.0, ((0, 8),), jnp.float32)
    noise_draw = gaussian(splits[1], (CLIPS, FR, 4, LAT, LAT), 1.0, 6.0, ((0, 8),), jnp.float32)
    timesteps = place_ends(jax.random.randint(splits[2], (CLIPS,), 1, 1000), jax.random.fold_in(splits[2], 1), 1, 999).astype(jnp.int32)
    captions = gaussian(splits[3], (CLIPS, LTXT, TXT), 0.25, 2.0, ((0, 8),))
    caption_len = draw_caption_len(jax.random.fold_in(splits[16], 71), 0)
    attention_weights = gaussian(splits[5], (12, D, D), D ** -0.5, 0.3125, ((2, 8),), jnp.float32)
    feed_weights = draw_feed_weights(jax.random.fold_in(splits[16], 71), 0)
    side_weights = draw_side_weights(jax.random.fold_in(splits[16], 71), 0)
    vector_weights = gaussian(splits[8], (NVEC, D), 0.5, 3.0, ((1, 8),), jnp.float32)
    attention_momentum = gaussian(splits[9], (12, D, D), (0.005 / PARAMS ** 0.5), 2.6702880859375e-05, ((2, 8),), jnp.float32)
    feed_momentum = gaussian(splits[10], (4, D, FF), (0.005 / PARAMS ** 0.5), 2.6702880859375e-05, ((2, 8),), jnp.float32)
    side_first = gaussian(splits[11], (SIDE, D), (0.0006 / PARAMS ** 0.5), 3.337860107421875e-06, ((1, 8),), jnp.float32)
    side_second = jnp.clip(jnp.exp(math.log(1.426706043345001e-14) - 1.3862944 * jax.random.uniform(splits[12], (SIDE, D), jnp.float32) ** shard_levels(splits[12], (SIDE, D), ((1, 8),), -0.2, 0.2)), 3.5667651083625025e-15, 1.426706043345001e-14)
    vector_first = gaussian(splits[13], (NVEC, D), (0.006 / PARAMS ** 0.5), 3.0517578125e-05, ((1, 8),), jnp.float32)
    vector_second = jnp.clip(jnp.exp(math.log(1.4267060840025825e-12) - 1.3862944 * jax.random.uniform(splits[14], (NVEC, D), jnp.float32) ** shard_levels(splits[14], (NVEC, D), ((1, 8),), -0.2, 0.2)), 3.566765210006456e-13, 1.4267060840025825e-12)
    step_count = jax.random.randint(splits[15], (1,), 2, 21).astype(jnp.int32)
    return {"latents": latents, "noise_draw": noise_draw, "timesteps": timesteps, "captions": captions, "caption_len": caption_len, "attention_weights": attention_weights, "feed_weights": feed_weights, "side_weights": side_weights, "vector_weights": vector_weights, "attention_momentum": attention_momentum, "feed_momentum": feed_momentum, "side_first": side_first, "side_second": side_second, "vector_first": vector_first, "vector_second": vector_second, "step_count": step_count}


@jax.custom_vjp
def low(v):
    return lax.optimization_barrier(v.astype(jnp.bfloat16)).astype(jnp.float32)

@jax.custom_vjp
def low_back(v):
    return v

def low_keep(v):
    return (low(v), None)

def low_pass(kept, grad):
    return (grad,)

def back_keep(v):
    return (v, None)

def back_low(kept, grad):
    return (low(grad),)
low.defvjp(low_keep, low_pass)
low_back.defvjp(back_keep, back_low)
highest = lax.Precision.HIGHEST
snr_gamma = 5.0
max_norm = 0.005
momentum_decay = 0.95
muon_rate = 0.05
adam_rate = 0.02
beta_one = 0.9
beta_two = 0.999
weight_decay = 0.01
coef_a = 3.4445
coef_b = -4.775
coef_c = 2.0315

def matmul(left, right):
    return jnp.dot(left, right, precision=highest, preferred_element_type=jnp.float32)

def two_way(value):
    return low(low_back(value))

def layer_norm(value):
    centred = value - lax.optimization_barrier(jnp.mean(value, axis=-1, keepdims=True))
    return centred * lax.rsqrt(lax.optimization_barrier(jnp.mean(centred * centred, axis=-1, keepdims=True)) + 1e-06)

def sincos(places, model_width):
    half_width = model_width // 2
    freqs = jnp.exp(-math.log(10000.0) * jnp.arange(half_width, dtype=jnp.float32) / half_width)
    angles = places[:, None] * freqs[None, :]
    return jnp.concatenate([jnp.sin(angles), jnp.cos(angles)], axis=1)

def alpha_level(steps_t):
    return jnp.cos((steps_t.astype(jnp.float32) / 1000.0 + 0.008) / 1.008 * (math.pi / 2)) ** 2

def snr_weight(steps_t):
    level = alpha_level(steps_t)
    ratio = level / (1.0 - level)
    return jnp.minimum(ratio, snr_gamma) / ratio

def patchify(frames):
    count, channels, height, breadth = frames.shape
    grid = frames.reshape(count, channels, height // 2, 2, breadth // 2, 2)
    grid = grid.transpose(0, 2, 4, 3, 5, 1)
    return grid.reshape(count * (height // 2) * (breadth // 2), 4 * channels)

def attend(queries, key_rows, value_rows, allowed):
    score_scale = queries.shape[-1] ** (-0.5)
    scores = low_back(jnp.einsum('bqhd,bkhd->bhqk', queries, key_rows, precision=highest) * score_scale)
    if allowed is not None:
        scores = jnp.where(allowed, scores, -1e+30)
    softmax_out = low(jax.nn.softmax(scores, axis=-1))
    return two_way(jnp.einsum('bhqk,bkhd->bqhd', softmax_out, value_rows, precision=highest))

def time_embed(params, steps_t):
    side_rows, vectors = (params[2], params[3])
    model_width = side_rows.shape[1]
    freqs = jnp.exp(-math.log(10000.0) * jnp.arange(128, dtype=jnp.float32) / 128)
    angles = steps_t.astype(jnp.float32) * freqs
    feature = jnp.concatenate([jnp.cos(angles), jnp.sin(angles)])[None, :]
    hidden = matmul(low(feature), side_rows[16:272]) + vectors[1]
    embedded = matmul(low(jax.nn.silu(hidden)), side_rows[272:272 + model_width]) + vectors[2]
    offset = side_rows.shape[0] - 6 * model_width
    modulate = matmul(low(jax.nn.silu(embedded)), side_rows[offset:].T) + vectors[3:9].reshape(-1)
    return (embedded[0], modulate[0].reshape(6, model_width))

def self_attention(resident, modulate, matrices, biases, temporal, frames):
    token_count, model_width = resident.shape

    def split_heads(value):
        value = value.reshape(frames, token_count // frames, HEADS, model_width // HEADS)
        return jnp.swapaxes(value, 0, 1) if temporal else value
    normed = low(layer_norm(resident) * (1.0 + modulate[1]) + modulate[0])
    queries = two_way(matmul(normed, matrices[0]) + biases[0])
    key_rows = two_way(matmul(normed, matrices[1]))
    value_rows = two_way(matmul(normed, matrices[2]) + biases[1])
    mixture = attend(split_heads(queries), split_heads(key_rows), split_heads(value_rows), None)
    if temporal:
        mixture = jnp.swapaxes(mixture, 0, 1)
    branch = low_back(matmul(mixture.reshape(token_count, model_width), matrices[3]) + biases[2])
    return resident + modulate[2] * branch

def cross_attend(resident, matrices, biases, caption_keys, allowed):
    token_count, model_width = resident.shape
    queries = two_way(matmul(low(resident), matrices[0]) + biases[0])
    key_rows = two_way(matmul(caption_keys, matrices[1]))
    value_rows = two_way(matmul(caption_keys, matrices[2]) + biases[1])

    def split_heads(value):
        return value.reshape(1, value.shape[0], HEADS, model_width // HEADS)
    mixture = attend(split_heads(queries), split_heads(key_rows), split_heads(value_rows), allowed)
    return resident + low_back(matmul(mixture.reshape(token_count, model_width), matrices[3]) + biases[2])

def feed_forward(resident, modulate, up_proj, down_proj, biases):
    normed = low(layer_norm(resident) * (1.0 + modulate[4]) + modulate[3])
    inner = low_back(matmul(normed, up_proj) + biases[3:7].reshape(-1))
    branch = low_back(matmul(low(jax.nn.gelu(inner, approximate=True)), down_proj.T) + biases[7])
    return resident + modulate[5] * branch

def caption_features(params, caption):
    side_rows, vectors = (params[2], params[3])
    model_width = side_rows.shape[1]
    offset = 272 + model_width
    text_width = caption.shape[1]
    hidden = matmul(low(caption), side_rows[offset:offset + text_width]) + vectors[9]
    second = side_rows[offset + text_width:offset + text_width + model_width]
    return two_way(matmul(low(jax.nn.gelu(hidden, approximate=True)), second) + vectors[10])

def segment_embed(params, resident, sample):
    side_rows, vectors = (params[2], params[3])
    latent, noise_part, steps_t = (sample[0], sample[1], sample[2])
    level = alpha_level(steps_t)
    tokens = jnp.sqrt(level) * patchify(latent) + jnp.sqrt(1.0 - level) * patchify(noise_part)
    count, height = (latent.shape[0], latent.shape[2] // 2)
    model_width = side_rows.shape[1]
    places = jnp.arange(height * height)
    grid_rows = (places // height).astype(jnp.float32)
    grid_cols = (places % height).astype(jnp.float32)
    spatial = jnp.concatenate([sincos(grid_rows, model_width // 2), sincos(grid_cols, model_width // 2)], axis=1)
    embedded = matmul(low(tokens), side_rows[0:16]) + vectors[0] + jnp.tile(spatial, (count, 1))
    return (embedded, jnp.zeros((), jnp.float32))

def segment_spatial(params, resident, sample):
    matrices, feeds, vectors = (params[0], params[1], params[3])
    embedded, modulate = time_embed(params, sample[2])
    modulate = vectors[19:25] + modulate
    resident = self_attention(resident, modulate, matrices[0:4], vectors[11:14], False, sample[0].shape[0])
    resident = feed_forward(resident, modulate, feeds[0], feeds[1], vectors[11:19])
    return (resident, jnp.zeros((), jnp.float32))

def segment_temporal(params, resident, sample):
    matrices, feeds, vectors = (params[0], params[1], params[3])
    frames = sample[0].shape[0]
    token_count, model_width = resident.shape
    timing = sincos(jnp.arange(frames).astype(jnp.float32), model_width)
    resident = resident + jnp.repeat(timing, token_count // frames, axis=0)
    embedded, modulate = time_embed(params, sample[2])
    modulate = vectors[33:39] + modulate
    resident = self_attention(resident, modulate, matrices[4:8], vectors[25:28], True, frames)
    caption_keys = caption_features(params, sample[3])
    allowed = (jnp.arange(sample[3].shape[0]) < sample[4])[None, None, None, :]
    resident = cross_attend(resident, matrices[8:12], vectors[39:42], caption_keys, allowed)
    resident = feed_forward(resident, modulate, feeds[2], feeds[3], vectors[25:33])
    return (resident, jnp.zeros((), jnp.float32))

def segment_final(params, resident, sample):
    side_rows, vectors = (params[2], params[3])
    model_width = side_rows.shape[1]
    embedded, modulate = time_embed(params, sample[2])
    table = vectors[42:44] + embedded
    normed = low(layer_norm(resident) * (1.0 + table[1]) + table[0])
    offset = side_rows.shape[0] - 6 * model_width - 16
    predicted = low_back(matmul(normed, side_rows[offset:offset + 16].T) + vectors[44, :16])
    target = patchify(sample[1])
    squared = jnp.mean((predicted - target) ** 2)
    return (jnp.zeros_like(resident), snr_weight(sample[2]) * squared)

def clip_error(params, sample):
    resident = two_way(segment_embed(params, None, sample)[0])
    resident = two_way(segment_spatial(params, resident, sample)[0])
    resident = two_way(segment_temporal(params, resident, sample)[0])
    return segment_final(params, resident, sample)[1]

def gram_of(matrix):
    return jnp.einsum('mik,mjk->mij', matrix, matrix, precision=highest)

def newton_step(matrix, gram):
    poly = coef_b * gram + coef_c * jnp.einsum('mij,mjk->mik', gram, gram, precision=highest)
    return coef_a * matrix + jnp.einsum('mij,mjk->mik', poly, matrix, precision=highest)

def muon_update(weight, momentum, grad):
    moment = momentum_decay * momentum + grad
    update = grad + momentum_decay * moment
    matrix = update / (jnp.sqrt(lax.optimization_barrier(jnp.sum(update * update, axis=(1, 2), keepdims=True))) + 1e-07)
    for sweep in range(5):
        matrix = newton_step(matrix, gram_of(matrix))
    rate = muon_rate * 0.2 * math.sqrt(weight.shape[2])
    return (weight * (1.0 - muon_rate * weight_decay) - rate * matrix, moment)

def adamw_update(weight, first, second, grad, count):
    first = beta_one * first + (1.0 - beta_one) * grad
    second = beta_two * second + (1.0 - beta_two) * grad * grad
    first_hat = first / (1.0 - jnp.power(beta_one, count))
    second_hat = second / (1.0 - jnp.power(beta_two, count))
    weight = weight - adam_rate * (first_hat / (jnp.sqrt(second_hat) + 1e-08) + weight_decay * weight)
    return (weight, first, second)

def reference(latents, noise_draw, timesteps, captions, caption_len, attention_weights, feed_weights, side_weights, vector_weights, attention_momentum, feed_momentum, side_first, side_second, vector_first, vector_second, step_count):
    weights = tuple((item.astype(jnp.bfloat16).astype(jnp.float32) for item in (attention_weights, feed_weights, side_weights, vector_weights)))
    total_weight = jnp.sum(snr_weight(timesteps))

    def loss_of(params):

        def accumulate(running, sample):
            sample = (sample[0], sample[1], sample[2], sample[3].astype(jnp.float32), sample[4])
            return (running + jax.checkpoint(clip_error)(params, sample), None)
        summed, _ = lax.scan(accumulate, jnp.zeros((), jnp.float32), (latents, noise_draw, timesteps, captions, caption_len))
        return summed / total_weight
    loss_value, pullback = jax.vjp(loss_of, weights)
    grads = pullback(jnp.ones((), jnp.float32))[0]
    squares = sum((jnp.sum(item * item) for item in grads))
    grad_norm = jnp.sqrt(squares)
    factor = jnp.minimum(1.0, max_norm / (grad_norm + 1e-06))
    attention_grad, feed_grad, side_grad, vector_grad = (item * factor for item in grads)
    attention_new, attention_moment = muon_update(attention_weights, attention_momentum, attention_grad)
    feed_new, feed_moment = muon_update(feed_weights, feed_momentum, feed_grad)
    count = step_count[0].astype(jnp.float32)
    side_new, side_first_new, side_second_new = adamw_update(side_weights, side_first, side_second, side_grad, count)
    vector_new, vector_first_new, vector_second_new = adamw_update(vector_weights, vector_first, vector_second, vector_grad, count)
    return (loss_value, grad_norm, attention_new, attention_moment, feed_new, feed_moment, side_new, side_first_new, side_second_new, vector_new, vector_first_new, vector_second_new, attention_new.astype(jnp.bfloat16), feed_new.astype(jnp.bfloat16), side_new.astype(jnp.bfloat16), vector_new.astype(jnp.bfloat16))
```

```python
import functools
import math

import jax
import jax.numpy as jnp
import numpy as np
from jax import lax
from jax.experimental import pallas as pl
from jax.experimental.pallas import tpu as pltpu
from jax.sharding import PartitionSpec as P

HEADS = 6
HEAD = 64
LP = 304
KP = 384

highest = lax.Precision.HIGHEST
snr_gamma = 5.0
max_norm = 0.005
momentum_decay = 0.95
muon_rate = 0.05
adam_rate = 0.02
beta_one = 0.9
beta_two = 0.999
weight_decay = 0.01
coef_a = 3.4445
coef_b = -4.775
coef_c = 2.0315

f32, bf16 = jnp.float32, jnp.bfloat16
MESH = pl.DeviceIdType.MESH
ANY = pl.BlockSpec(memory_space=pl.ANY)
VM = pl.BlockSpec(memory_space=pltpu.VMEM)
SM = pl.BlockSpec(memory_space=pltpu.SMEM)
VMEM_LIMIT = 60000 * 1024


def low(value):
    return value.astype(bf16)


def nt(left, right):
    return lax.dot_general(left, right, (((1,), (1,)), ((), ())), preferred_element_type=f32)


def nn(left, right):
    return lax.dot_general(left, right, (((1,), (0,)), ((), ())), preferred_element_type=f32)


def tn(left, right):
    return lax.dot_general(left, right, (((0,), (0,)), ((), ())), preferred_element_type=f32)


def snr_weight(steps_t):
    level = jnp.cos((steps_t / 1000.0 + 0.008) / 1.008 * (math.pi / 2)) ** 2
    ratio = level / (1.0 - level)
    return level, jnp.minimum(ratio, snr_gamma) / ratio


def patchify(frames):
    clips, count, channels, height, breadth = frames.shape
    grid = frames.reshape(clips, count, channels, height // 2, 2, breadth // 2, 2)
    grid = grid.transpose(0, 1, 3, 5, 4, 6, 2)
    return grid.reshape(clips, count, (height // 2) * (breadth // 2), 4 * channels)


def sincos(places, model_width):
    half_width = model_width // 2
    freqs = np.exp(-math.log(10000.0) * np.arange(half_width) / half_width)
    angles = places[:, None] * freqs[None, :]
    return np.concatenate([np.sin(angles), np.cos(angles)], axis=1).astype(np.float32)


def col_sum(value):
    return jnp.sum(value.astype(f32), axis=0, keepdims=True)


def norm(value):
    centred = value - jnp.mean(value, axis=-1, keepdims=True)
    inv = lax.rsqrt(jnp.mean(centred * centred, axis=-1, keepdims=True) + 1e-06)
    return centred * inv, inv


def norm_back(grad, normed, inv):
    return inv * (
        grad
        - jnp.mean(grad, axis=-1, keepdims=True)
        - normed * jnp.mean(grad * normed, axis=-1, keepdims=True)
    )


GELU_C = math.sqrt(2.0 / math.pi)


def gelu(value):
    inner = GELU_C * (value + 0.044715 * (value * value * value))
    return value * (0.5 * (1.0 + jnp.tanh(inner)))


def gelu_both(value):
    square = value * value
    tanh = jnp.tanh(GELU_C * (value + 0.044715 * (square * value)))
    cdf = 0.5 * (1.0 + tanh)
    slope = 0.5 * (1.0 - tanh * tanh) * (GELU_C * (1.0 + 3 * 0.044715 * square))
    return value * cdf, cdf + value * slope


def lanes_low():
    lane = lax.broadcasted_iota(jnp.int32, (1, 128), 1)
    first = jnp.where(lane < HEAD, 1.0, 0.0)
    return low(first), low(1.0 - first), lane < HEAD


def stack_heads(pair, first, second):
    return jnp.concatenate([pair * first, pair * second], axis=0)


def attend(queries, keys, values, allowed):
    first, second, lower = lanes_low()
    rows = queries.shape[0]
    mixed, probs = [], []
    for pair in range(HEADS // 2):
        cut = slice(pair * 128, pair * 128 + 128)
        scores = nt(stack_heads(queries[:, cut], first, second), keys[:, cut]) * 0.125
        scores = jnp.where(allowed, scores, -1e30)
        weight = jnp.exp(scores - jnp.max(scores, axis=-1, keepdims=True))
        prob = weight / jnp.sum(weight, axis=-1, keepdims=True)
        probs.append(prob)
        out = nn(low(prob), values[:, cut])
        mixed.append(jnp.where(lower, out[:rows], out[rows:]))
    return low(jnp.concatenate(mixed, axis=1)), probs


def attend_back(grad, queries, keys, values, probs):
    first, second, lower = lanes_low()
    rows = queries.shape[0]
    dq, dk, dv = [], [], []
    for pair in range(HEADS // 2):
        cut = slice(pair * 128, pair * 128 + 128)
        stacked = stack_heads(grad[:, cut], first, second)
        prob = probs[pair]
        dv.append(tn(low(prob), stacked))
        dprob = nt(stacked, values[:, cut])
        dscore = low(prob * (dprob - jnp.sum(prob * dprob, axis=-1, keepdims=True)))
        part = nn(dscore, keys[:, cut])
        dq.append(jnp.where(lower, part[:rows], part[rows:]) * 0.125)
        dk.append(tn(dscore, stack_heads(queries[:, cut], first, second)) * 0.125)
    return tuple(jnp.concatenate(piece, axis=1) for piece in (dq, dk, dv))


def self_forward(x, mods, weights, bias, allowed):
    normed, inv = norm(x)
    a = low(normed * (1.0 + mods[1]) + mods[0])
    q = low(nt(a, weights[0]) + bias[0])
    k = low(nt(a, weights[1]))
    v = low(nt(a, weights[2]) + bias[1])
    o, probs = attend(q, k, v, allowed)
    branch = nt(o, weights[3]) + bias[2]
    return x + mods[2] * branch, (normed, inv, a, q, k, v, o, probs, branch)


def self_backward(dx, kept, mods, weights):
    normed, inv, a, q, k, v, o, probs, branch = kept
    dm2 = col_sum(dx * branch)
    dbr = low(dx * mods[2])
    do = low(nn(dbr, weights[3]))
    dq, dk, dv = (low(piece) for piece in attend_back(do, q, k, v, probs))
    da = nn(dq, weights[0]) + nn(dk, weights[1]) + nn(dv, weights[2])
    dm1, dm0 = col_sum(da * normed), col_sum(da)
    dx = dx + norm_back(da * (1.0 + mods[1]), normed, inv)
    return dx, (dm0, dm1, dm2), (col_sum(dq), col_sum(dv), col_sum(dbr)), (a, dq, dk, dv, o, dbr)


def feed_forward(x, mods, feed, bias_up, bias_down):
    normed, inv = norm(x)
    c = low(normed * (1.0 + mods[4]) + mods[3])
    u = nt(c, feed[0]) + bias_up
    g = low(gelu(u))
    branch = nn(g, feed[1]) + bias_down
    return x + mods[5] * branch, (normed, inv, c, u, g, branch)


def feed_backward(dx, kept, mods, feed):
    normed, inv, c, u, g, branch = kept
    dm5 = col_sum(dx * branch)
    dbr = low(dx * mods[5])
    du = low(nt(dbr, feed[1]) * gelu_both(u)[1])
    dc = nn(du, feed[0])
    dm4, dm3 = col_sum(dc * normed), col_sum(dc)
    dx = dx + norm_back(dc * (1.0 + mods[4]), normed, inv)
    return dx, (dm3, dm4, dm5), (col_sum(du), col_sum(dbr)), (c, dbr, du, g)


def pair_mask(kind):
    row = lax.broadcasted_iota(jnp.int32, (256, 128), 0) % 128
    col = lax.broadcasted_iota(jnp.int32, (256, 128), 1)
    if kind == 0:
        return row // 64 == col // 64
    return row % 32 == col % 32


VEC0, EMB0, HEAD0 = 0, 45, 61


def mod_rows(mq, vec, table, clip):
    rows = []
    for r in range(6):
        at = (r % 2) * 384
        rows.append(
            mq[r // 2, pl.ds(clip, 1), at : at + 384]
            + vec[3 + r : 4 + r]
            + vec[table + r : table + r + 1]
        )
    return rows


def up_bias(vec, start):
    return jnp.concatenate([vec[start + i : start + i + 1] for i in range(4)], axis=1)


def condition_kernel(rank, wt, ww, wm, perm, vec, hid, temb, mq, y2p):
    turned = jnp.transpose(ww[:, 1024:1152].astype(f32))
    vec[...] = turned
    feature = low(wt[:, 0:256])
    first = nt(feature, ww[:, 0:256]) + turned[1:2]
    hid[...] = first
    second = nt(low(first * jax.nn.sigmoid(first)), ww[:, 256:640]) + turned[2:3]
    temb[...] = second
    own = temb[pl.ds(pl.multiple_of(rank[0] * 8, 8), 8), :]
    mq[...] = nn(low(own * jax.nn.sigmoid(own)), wm[...])
    for h in range(2):
        y2p[h] = low(nt(ww[:, 640:1024], perm[h]))


def embed_chunk(tok_ref, vec, pos_ref, chunk):
    tokens = tok_ref[pl.ds(pl.multiple_of(chunk * 128, 128), 128), :]
    return low(nn(tokens, low(vec[...])) + (pos_ref[...] + vec[0:1])), tokens


def spatial_bias(vec):
    return (vec[11:12], vec[12:13], vec[13:14])


def first_kernel(role, half, tok, pos, mq, vec, wa, wf, wy, perm, captions, h1, hq, gq, cap, sems):
    @pl.when(role[0] == 1)
    def _():
        clips = captions.shape[0]
        for c in range(clips):
            pltpu.make_async_copy(captions.at[c], cap.at[c], sems.at[c]).start()
        bias = nt(low(vec[9:10]), perm[half[0]])
        for c in range(clips):
            pltpu.make_async_copy(captions.at[c], cap.at[c], sems.at[c]).wait()
            value = nt(cap[c], wy[...]) + bias
            rows = value.shape[0]
            pad = jnp.zeros((LP - rows, value.shape[1]), f32)
            hq[c] = jnp.concatenate([value, pad], axis=0)
            gq[c] = low(jnp.concatenate([gelu(value), pad], axis=0))

    @pl.when(role[0] == 0)
    def _():
        allowed = pair_mask(0)
        count = h1.shape[0]
        bu = up_bias(vec, 14)

        def step(chunk, carry):
            m = mod_rows(mq, vec, 19, (half[0] * count + chunk) // 2)
            h0, _ = embed_chunk(tok, vec, pos, chunk)
            x, _ = self_forward(h0.astype(f32), m, wa, spatial_bias(vec), allowed)
            x, _ = feed_forward(x, m, wf, bu, vec[18:19])
            out = low(x)
            for frame in range(2):
                for part in range(2):
                    start = frame * 64 + part * 32
                    h1[chunk, part, frame * 32 : frame * 32 + 32, :] = out[start : start + 32]
            return carry

        lax.fori_loop(0, count, step, 0)


def last_kernel(
    role, half, tok, pos, mq, vec, wa, wb, wf, dh, dkv, extra, grads_t, dmod_t,
    acts, actf, actw, dkvb, dy, vect, dmod, grads,
):
    @pl.when(role[0] == 0)
    def _():
        grads[...] = jnp.zeros_like(grads)
        dmod[...] = jnp.zeros_like(dmod)
        allowed = pair_mask(0)
        count = dh.shape[0]
        bu = up_bias(vec, 14)

        def step(chunk, carry):
            m = mod_rows(mq, vec, 19, (half[0] * count + chunk) // 2)
            h0, tokens = embed_chunk(tok, vec, pos, chunk)
            x, kept = self_forward(h0.astype(f32), m, wa, spatial_bias(vec), allowed)
            _, kept_f = feed_forward(x, m, wf, bu, vec[18:19])
            parts = []
            for frame in range(2):
                for part in range(2):
                    parts.append(dh[chunk, part, frame * 32 : frame * 32 + 32, :])
            dx = jnp.concatenate(parts, axis=0).astype(f32)
            dx, dm_f, db_f, act_f = feed_backward(dx, kept_f, m, wf)
            dx, dm_a, db_a, act_a = self_backward(dx, kept, m, wa)
            dh0 = low(dx)
            where = pl.ds(pl.multiple_of(chunk * 128, 128), 128)
            for i, value in enumerate(act_a):
                acts[i, where, :] = value
            for i in range(2):
                actf[i, where, :] = act_f[i]
                actw[i, where, :] = act_f[2 + i]
            mods = dm_a + dm_f
            dmod[chunk, 0:6, :] = jnp.concatenate(mods, axis=0)
            grads[...] += tn(tokens, dh0)
            grads[0:1] += col_sum(dh0)
            for i in range(3):
                grads[11 + i : 12 + i] += db_a[i]
            for i in range(4):
                grads[14 + i : 15 + i] += db_f[0][:, i * 384 : i * 384 + 384]
            grads[18:19] += db_f[1]
            for i in range(6):
                grads[19 + i : 20 + i] += mods[i]
            return carry

        lax.fori_loop(0, count, step, 0)

    @pl.when(role[0] == 1)
    def _():
        grads[...] = grads_t[...]
        dmod[...] = dmod_t[...]
        dy[...] = jnp.zeros_like(dy)
        dkvb[...] = jnp.zeros_like(dkvb)
        ncl = dy.shape[0]
        for c in range(ncl):

            @pl.when(jnp.logical_or(half[0] == 0, c > 0))
            def _():
                pieces = []
                for i in range(2):
                    value = dkv[i, c]
                    if c == ncl - 1:
                        value = value + jnp.where(half[0] == 0, extra[i], 0.0)
                    pieces.append(low(value))
                dkvb[0, c], dkvb[1, c] = pieces
                back = low(nn(pieces[0], wb[1]) + nn(pieces[1], wb[2]))
                dy[c] = back
                grads[40:41] += col_sum(pieces[1])
                grads[10:11] += col_sum(back)

    vect[...] = jnp.transpose(grads[...])


def temporal_kernel(
    role, half, rank, lens, errw, h1, timing, mq, vec, temb, wa, wb, wf, gq, y2p, target,
    dh1, acts, actf, actw, ybuf, dkv, grads, dmod, loss, kx, vx,
):
    @pl.when(role[0] == 0)
    def _():
        loss[...] = jnp.zeros_like(loss)

    @pl.when(role[0] == 1)
    def _():
        allowed = pair_mask(1)
        count = h1.shape[0]
        ncl = ybuf.shape[0]
        for ref in (kx, vx, dkv, grads, loss):
            ref[...] = jnp.zeros_like(ref)
        first_clip = (half[0] * count) // 2
        for c in range(ncl):
            clip = jnp.minimum(first_clip + c, gq.shape[1] - 1)
            y = low(nt(gq[0, clip], y2p[0]) + nt(gq[1, clip], y2p[1]) + vec[10:11])
            ybuf[c] = y
            kx[c, 0:LP, :] = low(nt(y, wb[1]))
            vx[c, 0:LP, :] = low(nt(y, wb[2]) + vec[40:41])
        bu = up_bias(vec, 28)
        lane = lax.broadcasted_iota(jnp.int32, (1, 128), 1)
        real = jnp.logical_and(lane >= HEAD0, lane < HEAD0 + 16)
        bias_h = pltpu.roll(jnp.broadcast_to(vec[44:45, 0:128], (8, 128)), HEAD0, 1)[0:1]
        head = low(vec[...])

        def step(chunk, carry):
            clip = (half[0] * count + chunk) // 2
            here = clip - first_clip
            m = mod_rows(mq, vec, 33, clip)
            emb = temb[pl.ds(rank[0] * 8 + clip, 1), :]
            m6, m7 = vec[42:43] + emb, vec[43:44] + emb
            h = jnp.concatenate([h1[chunk, 0], h1[chunk, 1]], axis=0)
            x = h.astype(f32) + timing[...]
            x, kept = self_forward(x, m, wa, (vec[25:26], vec[26:27], vec[27:28]), allowed)
            xb = low(x)
            cq = low(nt(xb, wb[0]) + vec[39:40])
            keys, values = kx[here], vx[here]
            seen = lax.broadcasted_iota(jnp.int32, (1, KP), 1) < lens[clip]
            co, probs = attend(cq, keys, values, seen)
            x = x + (nt(co, wb[3]) + vec[41:42])
            x, kept_f = feed_forward(x, m, wf, bu, vec[32:33])
            h2 = low(x).astype(f32)
            normed, inv = norm(h2)
            cf = low(normed * (1.0 + m7) + m6)
            where = pl.ds(pl.multiple_of(chunk * 128, 128), 128)
            diff = jnp.where(real, nt(cf, head) + bias_h - target[where, :], 0.0)
            scale = errw[clip]
            loss[...] += col_sum(diff * diff) * scale
            dpred = low(diff * (2.0 * scale))
            dcf = nn(dpred, head)
            grads[...] += tn(dpred, cf)
            dbh = pltpu.roll(jnp.broadcast_to(col_sum(dpred), (8, 128)), 128 - HEAD0, 1)[0:1]
            grads[44:45, 0:128] += dbh
            dm7, dm6 = col_sum(dcf * normed), col_sum(dcf)
            dx = low(norm_back(dcf * (1.0 + m7), normed, inv)).astype(f32)
            dx, dm_f, db_f, act_f = feed_backward(dx, kept_f, m, wf)
            dcbr = low(dx)
            dco = low(nn(dcbr, wb[3]))
            dcq, dck, dcv = attend_back(dco, cq, keys, values, probs)
            dcq = low(dcq)
            dkv[0, here] += dck[0:LP]
            dkv[1, here] += dcv[0:LP]
            dx = dx + nn(dcq, wb[0])
            dx, dm_a, db_a, act_a = self_backward(dx, kept, m, wa)
            out = low(dx)
            dh1[chunk, 0] = out[0:64]
            dh1[chunk, 1] = out[64:128]
            for i, value in enumerate(act_a + (xb, dcq, co, dcbr)):
                acts[i, where, :] = value
            for i in range(2):
                actf[i, where, :] = act_f[i]
                actw[i, where, :] = act_f[2 + i]
            mods = dm_a + dm_f + (dm6, dm7)
            dmod[chunk] = jnp.concatenate(mods, axis=0)
            for i in range(3):
                grads[25 + i : 26 + i] += db_a[i]
            for i in range(4):
                grads[28 + i : 29 + i] += db_f[0][:, i * 384 : i * 384 + 384]
            grads[32:33] += db_f[1]
            for i in range(6):
                grads[33 + i : 34 + i] += mods[i]
            grads[39:40] += col_sum(dcq)
            grads[41:42] += col_sum(dcbr)
            grads[42:43] += dm6
            grads[43:44] += dm7
            return carry

        lax.fori_loop(0, count, step, 0)


def weight_grad_kernel(
    role, half, acts_s, acts_t, racts, actf_s, actf_t, ractf, actw_s, actw_t, ractw,
    ybuf, rybuf, dkvb, rdkvb, dy, rdy, gq, hq, y2p, perm, captions,
    ga, gf, gy2, gy1, la, ra, lf, rf, lw, rw, cap, sems,
):
    side = ga.shape[1]
    six = acts_s.shape[0]

    def copies(r, h):
        if h == 0:
            local = acts_s if r == 0 else acts_t
            size = local.shape[0]
            return [
                (local, la.at[pl.ds(0, size)], 0),
                (racts.at[pl.ds(0, size)], ra.at[pl.ds(0, size)], 1),
            ]
        pick = ((actf_s, actw_s), (actf_t, actw_t))[r]
        return [(pick[0], lf, 0), (ractf, rf, 1), (pick[1], lw, 2), (ractw, rw, 3)]

    def text():
        return [(captions.at[c], cap.at[c], 4 + c) for c in range(captions.shape[0])]

    def run(group, finish):
        for src, dst, i in group:
            copy = pltpu.make_async_copy(src, dst, sems.at[i])
            copy.wait() if finish else copy.start()

    for r in range(2):
        for h in range(2):

            @pl.when(jnp.logical_and(role[0] == r, half[0] == h))
            def _():
                run(copies(r, h), False)
                if r == 1:
                    run(text(), False)
                run(copies(r, h), True)

    def both(i, j):
        return tn(la[i], la[j]) + tn(ra[i], ra[j])

    @pl.when(half[0] == 0)
    def _():
        for i in range(3):
            ga[i] = low(both(1 + i, 0))
        ga[3] = low(both(5, 4))

        @pl.when(role[0] == 1)
        def _():
            ga[4] = low(both(7, 6))
            for i in range(2):
                total = jnp.zeros((side, side), f32)
                for c in range(ybuf.shape[0]):
                    total = total + tn(dkvb[i, c], ybuf[c]) + tn(rdkvb[i, c], rybuf[c])
                ga[5 + i] = low(total)
            ga[7] = low(both(9, 8))

    @pl.when(half[0] == 1)
    def _():
        for pair in range(2):
            for tile in range(4):
                cut = slice(tile * 384, tile * 384 + 384)
                gf[pair, cut, :] = low(
                    tn(lw[pair, :, cut], lf[pair]) + tn(rw[pair, :, cut], rf[pair])
                )

    @pl.when(role[0] == 1)
    def _():
        clips = captions.shape[0]
        rows = captions.shape[1]
        owners = [((2 * c) // clips, c - (((2 * c) // clips) * clips) // 2) for c in range(clips)]

        def dy_of(c):
            h, at = owners[c]
            return jnp.where(half[0] == h, dy[at].astype(f32), rdy[at].astype(f32)).astype(bf16)

        @pl.when(half[0] == 1)
        def _():
            total = jnp.zeros((side, side), f32)
            for c in range(clips):
                plain = nn(gq[0, c], perm[0]) + nn(gq[1, c], perm[1])
                total = total + tn(dy_of(c), low(plain))
            gy2[...] = total

        turned = []
        sums = jnp.zeros((gy1.shape[0], 128), f32)
        ones = jnp.ones((rows, 128), bf16)
        for c in range(clips):
            back = nn(dy_of(c), y2p[half[0]]) * gelu_both(hq[c])[1]
            turned.append(low(jnp.transpose(back))[:, 0:rows])
            sums = sums + nn(turned[c], ones)
        run(text(), True)
        for tile in range(captions.shape[2] // 512):
            cut = slice(tile * 512, tile * 512 + 512)
            total = nn(turned[0], cap[0, :, cut])
            for c in range(1, clips):
                total = total + nn(turned[c], cap[c, :, cut])
            gy1[:, cut] = low(total)
        gy1[:, captions.shape[2] :] = low(sums)


def exact(left, right, dims):
    lh, rh = low(left), low(right)
    ll, rl = low(left - lh.astype(f32)), low(right - rh.astype(f32))

    def dot(a, b):
        return lax.dot_general(a, b, dims, preferred_element_type=f32)

    return dot(lh, rh) + (dot(lh, rl) + dot(ll, rh))


D_NN, D_NT, D_TN = ((((1,), (0,)), ((), ())), (((1,), (1,)), ((), ())), (((0,), (0,)), ((), ())))


def muon_kernel(half, ua, uf, xa, xf):
    @pl.when(half[0] == 0)
    def _():
        u = ua[...]
        x = u / (jnp.sqrt(jnp.sum(u * u)) + 1e-07)
        for sweep in range(5):
            gram = exact(x, x, D_NT)
            poly = coef_b * gram + coef_c * exact(gram, gram, D_NN)
            x = coef_a * x + exact(poly, x, D_NN)
        xa[...] = low(x)

    @pl.when(half[0] == 1)
    def _():
        width = uf.shape[1]
        tiles = uf.shape[0] // width
        gram = jnp.zeros((width, width), f32)
        for t in range(tiles):
            piece = uf[t * width : t * width + width, :]
            gram = gram + exact(piece, piece, D_TN)
        row = lax.broadcasted_iota(jnp.int32, (width, width), 0)
        col = lax.broadcasted_iota(jnp.int32, (width, width), 1)
        eye = jnp.where(row == col, 1.0, 0.0)
        inv = 1.0 / (jnp.sqrt(jnp.sum(gram * eye)) + 1e-07)
        gram = gram * (inv * inv)
        whole = None
        for sweep in range(5):
            poly = coef_a * eye + coef_b * gram + coef_c * exact(gram, gram, D_NN)
            whole = poly if whole is None else exact(poly, whole, D_NN)
            if sweep < 4:
                gram = exact(exact(poly, gram, D_NN), poly, D_NN)
        whole = whole * inv
        for t in range(tiles):
            cut = slice(t * width, t * width + width)
            xf[cut, :] = low(exact(uf[cut, :], whole, D_NN))


def local_call(kernel, out_shape, in_specs, args, scratch=()):
    return pl.pallas_call(
        kernel,
        out_shape=out_shape,
        in_specs=in_specs,
        out_specs=jax.tree.map(lambda _: VM, out_shape),
        scratch_shapes=scratch,
        compiler_params=pltpu.CompilerParams(vmem_limit_bytes=VMEM_LIMIT),
    )(*args)


def here():
    return lax.axis_index("dp"), lax.axis_index("segment")


def dev(d, s):
    return {"dp": d, "segment": s}


def remote(src, dst, send, recv, target):
    return pltpu.make_async_remote_copy(
        src_ref=src, dst_ref=dst, send_sem=send, recv_sem=recv, device_id=target,
        device_id_type=MESH,
    )


def greet(targets):
    barrier = pltpu.get_barrier_semaphore()
    for target in targets:
        pl.semaphore_signal(barrier, inc=1, device_id=target, device_id_type=MESH)
    pl.semaphore_wait(barrier, len(targets))


def greet_dp(n, extra=()):
    d, s = here()
    barrier = pltpu.get_barrier_semaphore()

    def step(k, carry):
        pl.semaphore_signal(
            barrier, inc=1, device_id=dev(lax.rem(d + k, n), s), device_id_type=MESH
        )
        return carry

    lax.fori_loop(1, n, step, 0)
    for target in extra:
        pl.semaphore_signal(barrier, inc=1, device_id=target, device_id_type=MESH)
    pl.semaphore_wait(barrier, n - 1 + len(extra))


def comm_call(kernel, cid, args, out_shape, sems):
    return pl.pallas_call(
        kernel,
        out_shape=out_shape,
        in_specs=[ANY] * len(args),
        out_specs=jax.tree.map(lambda _: ANY, out_shape),
        scratch_shapes=[pltpu.SemaphoreType.DMA(shape) for shape in sems],
        compiler_params=pltpu.CompilerParams(collective_id=cid, has_side_effects=True),
    )(*args)


def gather_kernel(n, pa, pb, pf, pw, py, pm, pt, wa, wb, wf, ww, wy, wm, wt,
                  send, recv, crecv, own):
    pair = 2 if n % 2 == 0 else 1
    line = n // pair
    d, s = here()
    role, half = s // 2, lax.rem(s, 2)
    a, x = d // pair, lax.rem(d, pair)
    mate = dev(d, role * 2 + 1 - half)
    above, below = dev(d + pair, s), dev(d - pair, s)
    across = dev(a * pair + (pair - 1 - x), s)
    barrier = pltpu.get_barrier_semaphore()

    def signal(target):
        pl.semaphore_signal(barrier, inc=1, device_id=target, device_id_type=MESH)

    signal(mate)
    if pair == 2:
        signal(across)

    @pl.when(a < line - 1)
    def _():
        signal(above)

    @pl.when(a > 0)
    def _():
        signal(below)

    pl.semaphore_wait(barrier, pair + jnp.minimum(a, 1) + jnp.minimum(line - 1 - a, 1))

    first = {
        0: {0: [(0, pa, wa, 4), (2, pw, ww, 0)], 1: [(0, pf, wf, 2)]},
        1: {0: [(0, pa, wa, 4), (1, pb, wb, 4), (2, pw, ww, 0)], 1: [(0, pf, wf, 2)]},
    }

    def slot(ref, lead, o):
        return ref.at[:, o] if lead else ref.at[o]

    for r in range(2):
        for h in range(2):

            @pl.when(jnp.logical_and(role == r, half == h))
            def _():
                parts = [(i, src, dst, lead, True) for i, src, dst, lead in first[r][h]]
                parts.append((3, pt, wt, 0, False))
                if (r, h) != (1, 1):
                    parts.append((4, pm, wm, 0, False))
                if r == 1:
                    parts.append((5, py, wy, 0, False))

                def move(part, way, o, target, is_own=False):
                    i, src, dst, lead, common = part
                    there = slot(dst, lead, o)
                    sem = crecv if way == 3 else recv
                    return remote(
                        src if is_own else there, there, send.at[way, i, o], sem.at[i, o], target
                    )

                def forward(o, up, down, side, is_own, finish):
                    def go(way, target):
                        for part in parts:
                            if way == 3 and not part[4]:
                                continue
                            copy = move(part, way, o, target, is_own)
                            copy.wait_send() if finish else copy.start()

                    if up is not None:
                        pl.when(up)(lambda: go(0, above))
                    if down is not None:
                        pl.when(down)(lambda: go(1, below))
                    if side and pair == 2:
                        go(2, across)
                    go(3, mate)

                def arrive(o):
                    for part in parts:
                        move(part, 0, o, across).wait_recv()

                for part in parts:
                    i, src, dst, lead, common = part
                    pltpu.make_async_copy(src, slot(dst, lead, d), own.at[i]).start()
                forward(d, a < line - 1, a > 0, True, True, False)
                other = pair - 1 - x

                def sweep(finish):
                    def step(k, carry):
                        @pl.when(a - k >= 0)
                        def _():
                            o = (a - k) * pair + x
                            if not finish:
                                arrive(o)
                            forward(o, a < line - 1, None, True, False, finish)

                        @pl.when(a + k < line)
                        def _():
                            o = (a + k) * pair + x
                            if not finish:
                                arrive(o)
                            forward(o, None, a > 0, True, False, finish)

                        if pair == 2:

                            @pl.when(a - (k - 1) >= 0)
                            def _():
                                o = (a - (k - 1)) * pair + other
                                if not finish:
                                    arrive(o)
                                forward(o, None, None, False, False, finish)

                            @pl.when(jnp.logical_and(k > 1, a + (k - 1) < line))
                            def _():
                                o = (a + (k - 1)) * pair + other
                                if not finish:
                                    arrive(o)
                                forward(o, None, None, False, False, finish)

                        return carry

                    lax.fori_loop(1, line + 1, step, 0)

                sweep(False)
                forward(d, a < line - 1, a > 0, True, True, True)
                sweep(True)
                for part in parts:
                    i, src, dst, lead, common = part
                    pltpu.make_async_copy(src, slot(dst, lead, d), own.at[i]).wait()

                def collect(o, carry):
                    for i, src, dst, lead in first[r][1 - h]:
                        there = slot(dst, lead, o)
                        remote(there, there, send.at[3, i, o], crecv.at[i, o], mate).wait_recv()
                    return carry

                lax.fori_loop(0, n, collect, 0)


def segment_kernel(count, *refs):
    ins, outs = refs[:count], refs[count : 2 * count]
    send, recv, own = refs[2 * count :]
    d, s = here()
    peers = [dev(d, lax.rem(s + k, 4)) for k in range(1, 4)]
    greet(peers)
    for i in range(count):
        pltpu.make_async_copy(ins[i], outs[i].at[s], own.at[i]).start()
        for k in range(1, 4):
            remote(ins[i], outs[i].at[s], send.at[i, k], recv.at[i, k], peers[k - 1]).start()
    for i in range(count):
        pltpu.make_async_copy(ins[i], outs[i].at[s], own.at[i]).wait()
        for k in range(1, 4):
            o = lax.rem(s + 4 - k, 4)
            remote(ins[i], outs[i].at[o], send.at[i, k], recv.at[i, k], dev(d, o)).wait()


def segment_exchange(cid, arrays):
    shapes = [jax.ShapeDtypeStruct((4,) + a.shape, a.dtype) for a in arrays]
    k = len(arrays)
    return comm_call(
        functools.partial(segment_kernel, k), cid, arrays, shapes, [(k, 4), (k, 4), (k,)]
    )


def dp_gather_kernel(n, src, dst, send, recv, own):
    d, s = here()
    greet_dp(n)
    pltpu.make_async_copy(src, dst.at[d], own.at[0]).start()

    def start(k, carry):
        remote(src, dst.at[d], send.at[k], recv.at[k], dev(lax.rem(d + k, n), s)).start()
        return carry

    def finish(k, carry):
        o = lax.rem(d + n - k, n)
        remote(src, dst.at[o], send.at[k], recv.at[k], dev(o, s)).wait()
        return carry

    lax.fori_loop(1, n, start, 0)
    lax.fori_loop(1, n, finish, 0)
    pltpu.make_async_copy(src, dst.at[d], own.at[0]).wait()


def forward_kernel(count, h1s, gq, h1t, gqs, send, recv, msend, mrecv):
    relay_half_clips(count, 0, h1s, h1t, send, recv, None, (gq, gqs, msend, mrecv))


def relay_half_clips(count, from_role, src, dst, send, recv, extra, swap=None):
    d, s = here()
    role, half = s // 2, lax.rem(s, 2)
    peers = [dev(d, (1 - role) * 2), dev(d, (1 - role) * 2 + 1)]
    mate = dev(d, role * 2 + 1 - half)
    peers.append(mate)
    greet(peers)

    def unit(i, part):
        there = half * count + i
        clip, own = there // 2, lax.rem(there, 2)
        other = 2 * clip + part
        return own, other // count, lax.rem(other, count)

    def copy(i, part):
        own, to, slot = unit(i, part)
        return remote(
            src.at[i, part], dst.at[slot, own], send.at[i, part], recv.at[slot, own],
            dev(d, (1 - from_role) * 2 + to),
        )

    if swap is not None:
        mine, both, msend, mrecv = swap

        @pl.when(role == 1)
        def _():
            pltpu.make_async_copy(mine, both.at[half], msend.at[1]).start()
            remote(mine, both.at[half], msend.at[0], mrecv.at[0], mate).start()

    if extra is not None:
        own_src, own_dst, esend, erecv = extra

        @pl.when(jnp.logical_and(role == 1, half == 1))
        def _():
            remote(own_src, own_dst, esend.at[0], erecv.at[0], dev(d, 2)).start()

    @pl.when(role == from_role)
    def _():
        for i in range(count):
            for part in range(2):
                copy(i, part).start()
        for i in range(count):
            for part in range(2):
                copy(i, part).wait_send()

    @pl.when(role == 1 - from_role)
    def _():
        for i in range(count):
            for part in range(2):
                remote(
                    src.at[i, part], dst.at[i, part], send.at[i, part], recv.at[i, part],
                    dev(d, from_role * 2),
                ).wait_recv()

    if swap is not None:

        @pl.when(role == 1)
        def _():
            pltpu.make_async_copy(mine, both.at[half], msend.at[1]).wait()
            remote(mine, both.at[1 - half], msend.at[0], mrecv.at[0], mate).wait()

    if extra is not None:

        @pl.when(jnp.logical_and(role == 1, half == 1))
        def _():
            remote(own_src, own_dst, esend.at[0], erecv.at[0], dev(d, 2)).wait_send()

        @pl.when(jnp.logical_and(role == 1, half == 0))
        def _():
            remote(own_src, own_dst, esend.at[0], erecv.at[0], dev(d, 2)).wait_recv()


def backward_kernel(count, dh1, dkv, dhs, extra, send, recv, esend, erecv):
    relay_half_clips(
        count, 1, dh1, dhs, send, recv, (dkv.at[:, 0], extra, esend, erecv)
    )


def swap_kernel(acts_s, acts_t, actf_s, actf_t, actw_s, actw_t, ybuf, dkvb, dy, dmod,
                racts, ractf, ractw, rybuf, rdkvb, rdy, dmods,
                send, recv, send_all, recv_all, own):
    d, s = here()
    role, half = s // 2, lax.rem(s, 2)
    peers = [dev(d, lax.rem(s + k, 4)) for k in range(1, 4)]
    greet(peers)
    mate = dev(d, role * 2 + 1 - half)
    six = acts_s.shape[0]
    pltpu.make_async_copy(dmod, dmods.at[s], own.at[0]).start()
    for k in range(1, 4):
        remote(dmod, dmods.at[s], send_all.at[k], recv_all.at[k], peers[k - 1]).start()
    gives = {
        (0, 0): [(0, actf_s, ractf), (1, actw_s, ractw)],
        (0, 1): [(0, acts_s, racts.at[pl.ds(0, six)])],
        (1, 0): [(0, actf_t, ractf), (1, actw_t, ractw), (2, dy, rdy)],
        (1, 1): [(0, acts_t, racts), (1, ybuf, rybuf), (3, dkvb, rdkvb), (2, dy, rdy)],
    }
    for (r, h), mine in gives.items():

        @pl.when(jnp.logical_and(role == r, half == h))
        def _():
            for i, src, dst in mine:
                remote(src, dst, send.at[i], recv.at[i], mate).start()
            for i, src, dst in mine:
                remote(src, dst, send.at[i], recv.at[i], mate).wait_send()
            for i, src, dst in gives[(r, 1 - h)]:
                remote(src, dst, send.at[i], recv.at[i], mate).wait_recv()

    pltpu.make_async_copy(dmod, dmods.at[s], own.at[0]).wait()
    for k in range(1, 4):
        o = lax.rem(s + 4 - k, 4)
        remote(dmod, dmods.at[o], send_all.at[k], recv_all.at[k], dev(d, o)).wait()


def scatter_kernel(n, ga, gf, gy2, gy1, dm, vec, ra, rf, ry2, ry1, rm, rv, send, recv, own):
    d, s = here()
    role, half = s // 2, lax.rem(s, 2)
    greet_dp(n)

    def parts(r, h):
        if h == 0:
            if r == 0:
                first = [(0, lambda p: ga.at[pl.ds(0, 4), p], lambda o: ra.at[o, pl.ds(0, 4)])]
            else:
                first = [(0, lambda p: ga.at[:, p], lambda o: ra.at[o])]
        else:
            first = [(0, lambda p: gf.at[:, p], lambda o: rf.at[o])]
            if r == 1:
                first.append((1, lambda p: gy2.at[p], lambda o: ry2.at[o]))
        if r == 1:
            first.append((2, lambda p: gy1.at[p], lambda o: ry1.at[o]))
        return first + [
            (3, lambda p: dm, lambda o: rm.at[o]),
            (4, lambda p: vec.at[p], lambda o: rv.at[o]),
        ]

    for r in range(2):
        for h in range(2):

            @pl.when(jnp.logical_and(role == r, half == h))
            def _():
                group = parts(r, h)
                for i, src, dst in group:
                    pltpu.make_async_copy(src(d), dst(d), own.at[i]).start()

                def start(k, carry):
                    to = lax.rem(d + k, n)
                    for i, src, dst in group:
                        remote(src(to), dst(d), send.at[i, k], recv.at[i, k], dev(to, s)).start()
                    return carry

                def finish(k, carry):
                    o = lax.rem(d + n - k, n)
                    for i, src, dst in group:
                        remote(src(o), dst(o), send.at[i, k], recv.at[i, k], dev(o, s)).wait()
                    return carry

                lax.fori_loop(1, n, start, 0)
                lax.fori_loop(1, n, finish, 0)
                for i, src, dst in group:
                    pltpu.make_async_copy(src(d), dst(d), own.at[i]).wait()


def middle_kernel(n, dtemb, vec, tile, dtembs, vecs, tiles, send, recv, send_all, recv_all, own):
    d, s = here()
    peers = [dev(d, lax.rem(s + k, 4)) for k in range(1, 4)]
    greet_dp(n, peers)
    pltpu.make_async_copy(dtemb, dtembs.at[d], own.at[0]).start()

    def start(k, carry):
        remote(dtemb, dtembs.at[d], send.at[k], recv.at[k], dev(lax.rem(d + k, n), s)).start()
        return carry

    def finish(k, carry):
        o = lax.rem(d + n - k, n)
        remote(dtemb, dtembs.at[o], send.at[k], recv.at[k], dev(o, s)).wait()
        return carry

    lax.fori_loop(1, n, start, 0)
    pairs = [(0, vec, vecs), (1, tile, tiles)]
    for i, src, dst in pairs:
        pltpu.make_async_copy(src, dst.at[s], own.at[1 + i]).start()
        for k in range(1, 4):
            remote(src, dst.at[s], send_all.at[i, k], recv_all.at[i, k], peers[k - 1]).start()
    for i, src, dst in pairs:
        pltpu.make_async_copy(src, dst.at[s], own.at[1 + i]).wait()
        for k in range(1, 4):
            o = lax.rem(s + 4 - k, 4)
            remote(src, dst.at[o], send_all.at[i, k], recv_all.at[i, k], dev(d, o)).wait()
    lax.fori_loop(1, n, finish, 0)
    pltpu.make_async_copy(dtemb, dtembs.at[d], own.at[0]).wait()


class Relay:
    def __init__(self, send, recv):
        self.d, self.s = here()
        self.role, self.half = self.s // 2, lax.rem(self.s, 2)
        self.other = dev(self.d, (1 - self.role) * 2 + self.half)
        self.mate = dev(self.d, self.role * 2 + 1 - self.half)
        self.send, self.recv = send, recv

    def at(self, r, h):
        return jnp.logical_and(self.role == r, self.half == h)

    def copy(self, i, leg, src, dst):
        target = self.other if leg == 0 else self.mate
        return remote(src, dst, self.send.at[i, leg], self.recv.at[i, leg], target)

    def start(self, i, src, dst):
        self.copy(i, 0, src, dst).start()
        self.copy(i, 1, src, dst).start()

    def middle(self, i, dst):
        self.copy(i, 0, dst, dst).wait_recv()
        self.copy(i, 2, dst, dst).start()

    def finish(self, r, h, items):
        @pl.when(self.at(r, h))
        def _():
            for i, src, dst in items:
                self.copy(i, 0, src, dst).wait_send()
                self.copy(i, 1, src, dst).wait_send()

        @pl.when(self.at(1 - r, h))
        def _():
            for i, src, dst in items:
                self.copy(i, 2, dst, dst).wait_send()

        @pl.when(self.at(r, 1 - h))
        def _():
            for i, src, dst in items:
                self.copy(i, 1, dst, dst).wait_recv()

        @pl.when(self.at(1 - r, 1 - h))
        def _():
            for i, src, dst in items:
                self.copy(i, 2, dst, dst).wait_recv()


def owner_first(role, mat):
    return 2 * mat + mat % 2 if role == 0 else mat


def owner_second(mat):
    return 2 + 3 * mat


def collect_kernel(n, ua, uf, ga, gf, gy1, gy2, oa, of, xa, xf, xy1, xy2,
                   send, recv, own, gsend, grecv, gown):
    relay = Relay(gsend, grecv)
    d, s, role, half = relay.d, relay.s, relay.role, relay.half
    greet_dp(n, [relay.other, relay.mate])
    four = pl.ds(0, 4)
    shared = {
        (0, 0): [(0, ga.at[four], xa.at[0, four])],
        (0, 1): [(1, gf, xf.at[0])],
        (1, 0): [(2, ga, xa.at[1]), (3, gy1, xy1.at[0])],
        (1, 1): [(4, gf, xf.at[1]), (5, gy1, xy1.at[1]), (6, gy2, xy2)],
    }
    groups = []
    for r in range(2):
        mats = 4 if r == 0 else 8
        groups.append((r, 0, [(m, owner_first(r, m), ua.at[m], oa) for m in range(mats)]))
        groups.append((r, 1, [(m, owner_second(m), uf.at[m], of) for m in range(2)]))
    for r, h, mats in groups:

        @pl.when(relay.at(r, h))
        def _():
            for m, o, src, dst in mats:

                @pl.when(d == o)
                def _():
                    pltpu.make_async_copy(src, dst.at[d], own.at[0]).start()

                @pl.when(d != o)
                def _():
                    remote(src, dst.at[d], send.at[m], recv.at[d], dev(o, s)).start()

            for i, src, dst in shared[(r, h)]:
                pltpu.make_async_copy(src, dst, gown.at[i]).start()
                relay.start(i, src, dst)

    for (r, h), items in shared.items():

        @pl.when(relay.at(1 - r, h))
        def _():
            for i, src, dst in items:
                relay.middle(i, dst)

    for r, h, mats in groups:

        @pl.when(relay.at(r, h))
        def _():
            for i, src, dst in shared[(r, h)]:
                pltpu.make_async_copy(src, dst, gown.at[i]).wait()
            for m, o, src, dst in mats:

                @pl.when(d == o)
                def _():
                    pltpu.make_async_copy(src, dst.at[d], own.at[0]).wait()

                    def finish(k, carry):
                        p = lax.rem(d + n - k, n)
                        remote(src, dst.at[p], send.at[m], recv.at[p], dev(p, s)).wait_recv()
                        return carry

                    lax.fori_loop(1, n, finish, 0)

                @pl.when(d != o)
                def _():
                    remote(src, dst.at[d], send.at[m], recv.at[d], dev(o, s)).wait_send()

    for (r, h), items in shared.items():
        relay.finish(r, h, items)


def spread_kernel(n, xa, xf, oa, of, send, recv, rsend, rrecv, own):
    relay = Relay(rsend, rrecv)
    d, s, role, half = relay.d, relay.s, relay.role, relay.half
    greet_dp(n, [relay.other, relay.mate])
    groups = []
    for r in range(2):
        mats = 4 if r == 0 else 8
        groups.append((r, 0, mats, functools.partial(owner_first, r), xa, oa, 10 * r))
        groups.append((r, 1, 2, owner_second, xf, of, 10 * r + 8))
    for r, h, mats, owner, src, dst, base in groups:

        @pl.when(relay.at(r, h))
        def _():
            for m in range(mats):

                @pl.when(d == owner(m))
                def _():
                    pltpu.make_async_copy(src.at[d], dst.at[r, m], own.at[m]).start()

                    def start(k, carry):
                        to = lax.rem(d + k, n)
                        remote(
                            src.at[to], dst.at[r, m], send.at[k], recv.at[m], dev(to, s)
                        ).start()
                        return carry

                    lax.fori_loop(1, n, start, 0)

            for m in range(mats):

                @pl.when(d == owner(m))
                def _():
                    pltpu.make_async_copy(src.at[d], dst.at[r, m], own.at[m]).wait()

                @pl.when(d != owner(m))
                def _():
                    remote(
                        src.at[d], dst.at[r, m], send.at[1], recv.at[m], dev(owner(m), s)
                    ).wait_recv()

                relay.start(base + m, dst.at[r, m], dst.at[r, m])

    for r, h, mats, owner, src, dst, base in groups:

        @pl.when(relay.at(1 - r, h))
        def _():
            for m in range(mats):
                relay.middle(base + m, dst.at[r, m])

    for r, h, mats, owner, src, dst, base in groups:

        @pl.when(relay.at(r, h))
        def _():
            for m in range(mats):

                @pl.when(d == owner(m))
                def _():
                    def finish(k, carry):
                        to = lax.rem(d + k, n)
                        remote(
                            src.at[to], dst.at[r, m], send.at[k], recv.at[m], dev(to, s)
                        ).wait_send()
                        return carry

                    lax.fori_loop(1, n, finish, 0)

        relay.finish(r, h, [(base + m, dst.at[r, m], dst.at[r, m]) for m in range(mats)])


def adamw_update(weight, first, second, grad, count):
    first = beta_one * first + (1.0 - beta_one) * grad
    second = beta_two * second + (1.0 - beta_two) * grad * grad
    first_hat = first / (1.0 - jnp.power(beta_one, count))
    second_hat = second / (1.0 - jnp.power(beta_two, count))
    weight = weight - adam_rate * (
        first_hat / (jnp.sqrt(second_hat) + 1e-08) + weight_decay * weight
    )
    return (weight, first, second)


def silu_slope(value):
    gate = jax.nn.sigmoid(value)
    return gate * (1.0 + value * (1.0 - gate))


def dot32(left, right, dims):
    return lax.dot_general(left, right, (dims, ((), ())), precision=highest)


def body(
    latents,
    noise_draw,
    timesteps,
    captions,
    caption_len,
    attention_weights,
    feed_weights,
    side_weights,
    vector_weights,
    attention_momentum,
    feed_momentum,
    side_first,
    side_second,
    vector_first,
    vector_second,
    step_count,
):
    n = lax.axis_size("dp")
    d, s = here()
    role, half = s // 2, lax.rem(s, 2)
    count = latents.shape[0]
    frames = latents.shape[1]
    width = attention_weights.shape[1]
    cols, feed_cols = attention_weights.shape[2], feed_weights.shape[2]
    hidden = n * feed_cols
    text = captions.shape[2]
    sds = jax.ShapeDtypeStruct
    role_s, half_s = role.reshape(1).astype(jnp.int32), half.reshape(1).astype(jnp.int32)

    o_time = 16
    o_text = o_time + 256 + width
    o_text2 = o_text + text
    o_head = o_text2 + width
    o_mod = o_head + 16
    six = 6 * width
    own_rows = -(-cols // 2)
    lanes = n * own_rows

    perm_np = np.zeros((2, lanes, width), np.float32)
    for h in range(width):
        origin, col = divmod(h, cols)
        perm_np[col // own_rows, origin * own_rows + col % own_rows, h] = 1.0
    perm = jnp.asarray(perm_np, bf16)

    att_t = jnp.swapaxes(attention_weights, 1, 2)
    feed_t = jnp.swapaxes(feed_weights, 1, 2)
    side_t = side_weights.T
    side_b = low(side_t)
    pa = low(lax.dynamic_slice_in_dim(att_t, 4 * role, 4, 0))
    pb = low(att_t[8:12])
    pf = low(lax.dynamic_slice_in_dim(feed_t, 2 * role, 2, 0))
    pw = jnp.concatenate(
        [
            side_b[:, o_time:o_text],
            side_b[:, o_text2:o_head],
            low(vector_weights.T),
            side_b[:, 0:16],
            side_b[:, o_head:o_mod],
            jnp.zeros((cols, 128 - 77), bf16),
        ],
        axis=1,
    )
    text_rows = jnp.pad(side_b[:, o_text:o_text2], ((0, 2 * own_rows - cols), (0, 0)))
    py = lax.dynamic_slice_in_dim(text_rows, half * own_rows, own_rows, 0)
    pm = lax.dynamic_slice_in_dim(side_b[:, o_mod:], jnp.minimum(s, 2) * 2 * width, 2 * width, 1)
    freqs = jnp.exp(-math.log(10000.0) * jnp.arange(128, dtype=f32) / 128)
    angles = timesteps.astype(f32)[:, None] * freqs[None, :]
    level, snr = snr_weight(timesteps.astype(f32))
    pt = jnp.concatenate([jnp.cos(angles), jnp.sin(angles), snr[:, None]], axis=1)
    pt = jnp.pad(pt, ((0, 8 - count), (0, width - 257)))

    wa, wb, wf, ww, wy, wm, wt = comm_call(
        functools.partial(gather_kernel, n),
        1,
        (pa, pb, pf, pw, py, pm, pt),
        [
            sds((4, n, cols, width), bf16),
            sds((4, n, cols, width), bf16),
            sds((2, n, feed_cols, width), bf16),
            sds((n, cols, 1152), bf16),
            sds((n, own_rows, text), bf16),
            sds((n, cols, 2 * width), bf16),
            sds((n, 8, width), f32),
        ],
        [(4, 6, n), (6, n), (6, n), (6,)],
    )
    wa = wa.reshape(4, width, width)
    wb = wb.reshape(4, width, width)
    wf = wf.reshape(2, hidden, width)
    ww = ww.reshape(width, 1152)
    wy = wy.reshape(lanes, text)
    wm = wm.reshape(width, 2 * width)
    total_weight = jnp.sum(wt[:, :, 256])

    rank_s = d.reshape(1).astype(jnp.int32)
    vec, hid, temb, mq_own, y2p = local_call(
        condition_kernel,
        [
            sds((128, width), f32),
            sds((n * 8, width), f32),
            sds((n * 8, width), f32),
            sds((8, 2 * width), f32),
            sds((2, width, lanes), bf16),
        ],
        [SM] + [VM] * 4,
        (rank_s, wt.reshape(n * 8, width), ww, wm, perm),
    )
    (mq,) = segment_exchange(2, (mq_own,))

    level = level[:, None, None, None, None]
    noisy = low(jnp.sqrt(level) * latents + jnp.sqrt(1.0 - level) * noise_draw).astype(f32)
    patches = patchify(jnp.where(role == 0, noisy, noise_draw))
    per_clip = frames * patches.shape[2]
    half_tokens = count * per_clip // 2
    regrouped = patches.reshape(count, frames, 2, 32, 16).transpose(0, 2, 1, 3, 4)
    regrouped = regrouped.reshape(count * per_clip, 16)
    rows = jnp.where(role == 0, patches.reshape(count * per_clip, 16), regrouped)
    rows = lax.dynamic_slice_in_dim(rows, half * half_tokens, half_tokens, 0)
    tok = low(jnp.pad(rows, ((0, 0), (EMB0, 112 - EMB0))))
    target = jnp.pad(rows, ((0, 0), (HEAD0, 112 - HEAD0)))
    places = np.arange(patches.shape[2])
    edge = latents.shape[3] // 2
    pos = np.concatenate(
        [sincos(places // edge, width // 2), sincos(places % edge, width // 2)], axis=1
    )
    pos = jnp.asarray(np.tile(pos, (2, 1)))
    timing = jnp.asarray(np.repeat(sincos(np.arange(frames), width), 32, axis=0))

    clip_rows = captions.shape[1]
    h1s, hq, gq_own = local_call(
        first_kernel,
        [
            sds((count, 2, 64, width), bf16),
            sds((count, LP, lanes), f32),
            sds((count, LP, lanes), bf16),
        ],
        [SM] * 2 + [VM] * 8 + [ANY],
        (role_s, half_s, tok, pos, mq, vec, wa, wf, wy, perm, captions),
        [pltpu.VMEM((count, clip_rows, text), bf16), pltpu.SemaphoreType.DMA((count,))],
    )
    h1t, gq = comm_call(
        functools.partial(forward_kernel, count),
        3,
        (h1s, gq_own),
        [sds((count, 2, 64, width), bf16), sds((2, count, LP, lanes), bf16)],
        [(count, 2), (count, 2), (2,), (1,)],
    )

    ncl = (count + 1) // 2
    errw = snr / (total_weight * (per_clip * 16.0))
    wide = sds((2, half_tokens, hidden), bf16)
    thin = sds((2, half_tokens, width), bf16)
    cap_like = sds((ncl, LP, width), bf16)
    dh1, acts_t, actf_t, actw_t, ybuf, dkv, grads_t, dmod_t, loss_t = local_call(
        temporal_kernel,
        [
            sds((count, 2, 64, width), bf16),
            sds((10, half_tokens, width), bf16),
            thin,
            wide,
            cap_like,
            sds((2, ncl, LP, width), f32),
            sds((128, width), f32),
            sds((count, 8, width), f32),
            sds((1, 128), f32),
        ],
        [SM] * 5 + [VM] * 11,
        (
            role_s, half_s, rank_s, caption_len, errw, h1t, timing, mq, vec, temb, wa, wb, wf, gq,
            y2p, target,
        ),
        [pltpu.VMEM((ncl, KP, width), bf16), pltpu.VMEM((ncl, KP, width), bf16)],
    )
    dhs, extra = comm_call(
        functools.partial(backward_kernel, count),
        4,
        (dh1, dkv),
        [sds((count, 2, 64, width), bf16), sds((2, LP, width), f32)],
        [(count, 2), (count, 2), (1,), (1,)],
    )
    acts_s, actf_s, actw_s, dkvb, dy, vect, dmod = local_call(
        last_kernel,
        [
            sds((6, half_tokens, width), bf16),
            thin,
            wide,
            sds((2, ncl, LP, width), bf16),
            cap_like,
            sds((width, 128), f32),
            sds((count, 8, width), f32),
        ],
        [SM] * 2 + [VM] * 12,
        (role_s, half_s, tok, pos, mq, vec, wa, wb, wf, dhs, dkv, extra, grads_t, dmod_t),
        [pltpu.VMEM((128, width), f32)],
    )
    racts, ractf, ractw, rybuf, rdkvb, rdy, dmods = comm_call(
        swap_kernel,
        5,
        (acts_s, acts_t, actf_s, actf_t, actw_s, actw_t, ybuf, dkvb, dy, dmod),
        [
            sds((10, half_tokens, width), bf16),
            thin,
            wide,
            cap_like,
            sds((2, ncl, LP, width), bf16),
            cap_like,
            sds((4, count, 8, width), f32),
        ],
        [(4,), (4,), (4,), (4,), (1,)],
    )
    ga, gf, gy2, gy1 = local_call(
        weight_grad_kernel,
        [
            sds((8, width, width), bf16),
            sds((2, hidden, width), bf16),
            sds((width, width), f32),
            sds((lanes, text + 128), bf16),
        ],
        [SM] * 2 + [ANY] * 9 + [VM] * 10 + [ANY],
        (
            role_s, half_s, acts_s, acts_t, racts, actf_s, actf_t, ractf, actw_s, actw_t, ractw,
            ybuf, rybuf, dkvb, rdkvb, dy, rdy, gq, hq, y2p, perm, captions,
        ),
        [
            pltpu.VMEM((10, half_tokens, width), bf16),
            pltpu.VMEM((10, half_tokens, width), bf16),
            pltpu.VMEM(thin.shape, bf16),
            pltpu.VMEM(thin.shape, bf16),
            pltpu.VMEM(wide.shape, bf16),
            pltpu.VMEM(wide.shape, bf16),
            pltpu.VMEM((count, clip_rows, text), bf16),
            pltpu.SemaphoreType.DMA((4 + count,)),
        ],
    )

    dm_clip = []
    for clip in range(count):
        total = 0.0
        for seg in range(4):
            for i in range(count):
                if ((seg % 2) * count + i) // 2 == clip:
                    total = total + dmods[seg, i]
        dm_clip.append(total)
    dm = jnp.concatenate(dm_clip, axis=0)

    ra, rf, ry2, ry1, rm, rv = comm_call(
        functools.partial(scatter_kernel, n),
        6,
        (
            ga.reshape(8, n, cols, width),
            gf.reshape(2, n, feed_cols, width),
            gy2.reshape(n, cols, width),
            gy1.reshape(n, own_rows, text + 128),
            dm,
            vect.reshape(n, cols, 128),
        ),
        [
            sds((n, 8, cols, width), bf16),
            sds((n, 2, feed_cols, width), bf16),
            sds((n, cols, width), f32),
            sds((n, own_rows, text + 128), bf16),
            sds((n, 8 * count, width), f32),
            sds((n, cols, 128), f32),
        ],
        [(5, n), (5, n), (5,)],
    )
    mats = jnp.arange(8)[:, None, None]
    real = jnp.logical_and(half == 0, jnp.logical_or(role == 1, mats < 4))
    grad_a = jnp.where(real, jnp.sum(ra.astype(f32), axis=0), 0.0)
    grad_f = jnp.where(half == 1, jnp.sum(rf.astype(f32), axis=0), 0.0)
    grad_y2 = jnp.where(s == 3, jnp.sum(ry2, axis=0), 0.0)
    valid = half * own_rows + jnp.arange(own_rows)[:, None] < cols
    grad_y1 = jnp.where(jnp.logical_and(role == 1, valid), jnp.sum(ry1.astype(f32), axis=0), 0.0)
    grad_v = jnp.sum(rv, axis=0)

    per = rm.reshape(n * count, 8, width)
    dmod_all = per[:, :6].reshape(n * count, six)
    wm_own = side_b[:, o_mod:]

    def own_cols(value):
        return lax.dynamic_slice_in_dim(value, d * cols, cols, value.ndim - 1)

    def clips_of(value):
        return value.reshape(n, 8, -1)[:, :count].reshape(n * count, -1)

    hid_all, temb_all = clips_of(hid), clips_of(temb)
    feature = low(clips_of(wt.reshape(n * 8, width))[:, :256])
    sh_all = low(jax.nn.silu(hid_all))
    temb_own = own_cols(temb_all)
    dsil = dot32(dmod_all, wm_own.astype(f32), ((1,), (1,)))
    dtemb = dsil * silu_slope(temb_own) + own_cols(per[:, 6] + per[:, 7])
    grad_mod = dot32(low(jax.nn.silu(temb_own)).astype(f32), dmod_all, ((0,), (0,)))
    grad_time2 = dot32(dtemb, sh_all.astype(f32), ((0,), (0,)))
    once = jnp.sum(grad_mod * grad_mod) + jnp.sum(grad_time2 * grad_time2)

    def squares(value):
        return jnp.sum(value * value)

    partial = (
        squares(grad_a)
        + squares(grad_f)
        + squares(grad_y2)
        + squares(grad_y1[:, : text + 1])
    )
    tile = jnp.concatenate(
        [jnp.full((4, 128), partial, f32), jnp.full((4, 128), jnp.sum(loss_t), f32)]
    )
    pad_rows = -(-(n * count) // 8) * 8
    dtembs, vecs, tiles = comm_call(
        functools.partial(middle_kernel, n),
        7,
        (jnp.pad(dtemb, ((0, pad_rows - n * count), (0, 128 - cols))), grad_v, tile),
        [sds((n, pad_rows, 128), f32), sds((4, cols, 128), f32), sds((4, 8, 128), f32)],
        [(n,), (n,), (2, 4), (2, 4), (3,)],
    )
    dtemb_all = dtembs[:, : n * count, :cols].transpose(1, 0, 2).reshape(n * count, width)
    w2_own = lax.dynamic_slice_in_dim(ww[:, 256 : 256 + width], d * cols, cols, 1)
    dsh = dot32(dtemb_all, w2_own.astype(f32), ((1,), (0,)))
    dhid = dsh * silu_slope(own_cols(hid_all))
    grad_time1 = dot32(dhid, feature.astype(f32), ((0,), (0,)))
    extra_rows = jnp.concatenate(
        [
            jnp.sum(dhid, axis=0)[:, None],
            jnp.sum(dtemb, axis=0)[:, None],
            own_cols(jnp.sum(dmod_all, axis=0).reshape(6, width)).T,
        ],
        axis=1,
    )
    grad_v = jnp.sum(vecs, axis=0)
    grad_v = jnp.concatenate([grad_v[:, 0:1], extra_rows, grad_v[:, 9:77]], axis=1)
    partial = jnp.sum(tiles[:, 0, 0]) + once + squares(grad_v) + squares(grad_time1)
    tile = jnp.concatenate(
        [jnp.full((4, 128), partial, f32), jnp.full((4, 128), jnp.sum(tiles[:, 4, 0]), f32)]
    )
    tiles = comm_call(
        functools.partial(dp_gather_kernel, n),
        8,
        (tile,),
        sds((n, 8, 128), f32),
        [(n,), (n,), (1,)],
    )
    grad_norm = jnp.sqrt(jnp.sum(tiles[:, 0, 0]))
    loss_value = jnp.sum(tiles[:, 4, 0])
    factor = jnp.minimum(1.0, max_norm / (grad_norm + 1e-06))

    att_m = jnp.swapaxes(attention_momentum, 1, 2)
    feed_m = jnp.swapaxes(feed_momentum, 1, 2)
    role_m = jnp.where(role == 0, jnp.pad(att_m[0:4], ((0, 4), (0, 0), (0, 0))), att_m[4:12])
    role_f = lax.dynamic_slice_in_dim(feed_m, 2 * role, 2, 0)
    fast = momentum_decay
    look_a = factor * grad_a * (1.0 + fast) + fast * fast * role_m
    look_f = factor * grad_f * (1.0 + fast) + fast * fast * role_f
    ua, uf, ga2, gf2, gy12, gy22 = comm_call(
        functools.partial(collect_kernel, n),
        9,
        (look_a, look_f, grad_a, grad_f, low(grad_y1), grad_y2),
        [
            sds((n, cols, width), f32),
            sds((n, feed_cols, width), f32),
            sds((2, 8, cols, width), f32),
            sds((2, 2, feed_cols, width), f32),
            sds((2, own_rows, text + 128), bf16),
            sds((cols, width), f32),
        ],
        [(8,), (n,), (1,), (7, 3), (7, 3), (7,)],
    )
    xa, xf = local_call(
        muon_kernel,
        [sds((width, width), bf16), sds((hidden, width), bf16)],
        [SM] + [VM] * 2,
        (half_s, ua.reshape(width, width), uf.reshape(hidden, width)),
    )
    xa_all, xf_all = comm_call(
        functools.partial(spread_kernel, n),
        10,
        (xa.reshape(n, cols, width), xf.reshape(n, feed_cols, width)),
        [sds((2, 8, cols, width), bf16), sds((2, 2, feed_cols, width), bf16)],
        [(n,), (8,), (20, 3), (20, 3), (8,)],
    )

    grad_att = jnp.concatenate([ga2[0, 0:4], ga2[1]], axis=0) * factor
    grad_feed = gf2.reshape(4, feed_cols, width) * factor
    full_att = jnp.concatenate([xa_all[0, 0:4], xa_all[1]], axis=0).astype(f32)
    full_feed = xf_all.reshape(4, feed_cols, width).astype(f32)
    att_moment = fast * att_m + grad_att
    feed_moment = fast * feed_m + grad_feed
    shrink = 1.0 - muon_rate * weight_decay
    att_new = att_t * shrink - (muon_rate * 0.2 * math.sqrt(n * cols)) * full_att
    feed_new = feed_t * shrink - (muon_rate * 0.2 * math.sqrt(hidden)) * full_feed

    text_grad = gy12.astype(f32).reshape(2 * own_rows, text + 128)[:cols]
    grad_v = jnp.concatenate(
        [grad_v[:, 0:9], text_grad[:, text : text + 1], grad_v[:, 10:77]], axis=1
    )
    side_grad = jnp.concatenate(
        [
            grad_v[:, 45:61],
            grad_time1,
            grad_time2,
            text_grad[:, :text],
            gy22,
            grad_v[:, 61:77],
            grad_mod,
        ],
        axis=1,
    )
    clock = step_count[0].astype(f32)
    side_new, side_first_new, side_second_new = adamw_update(
        side_t, side_first.T, side_second.T, side_grad * factor, clock
    )
    vector_new, vector_first_new, vector_second_new = adamw_update(
        vector_weights, vector_first, vector_second, grad_v[:, 0:45].T * factor, clock
    )

    def back(value):
        return jnp.swapaxes(value, -1, -2)

    return (
        loss_value,
        grad_norm,
        back(att_new),
        back(att_moment),
        back(feed_new),
        back(feed_moment),
        back(side_new),
        back(side_first_new),
        back(side_second_new),
        vector_new,
        vector_first_new,
        vector_second_new,
        back(low(att_new)),
        back(low(feed_new)),
        back(low(side_new)),
        low(vector_new),
    )


def solution(mesh):
    column = P(None, "dp")
    matrix = P(None, None, "dp")
    return jax.shard_map(
        body,
        mesh=mesh,
        in_specs=(
            P("dp", None, None, None, None),
            P("dp", None, None, None, None),
            P("dp"),
            P("dp", None, None),
            P("dp"),
            matrix,
            matrix,
            column,
            column,
            matrix,
            matrix,
            column,
            column,
            column,
            column,
            P(),
        ),
        out_specs=(
            P(),
            P(),
            matrix,
            matrix,
            matrix,
            matrix,
            column,
            column,
            column,
            column,
            column,
            column,
            matrix,
            matrix,
            column,
            column,
        ),
        check_vma=False,
    )
```

```python
import functools
import math

import jax
import jax.numpy as jnp
import numpy as np
from jax import lax
from jax.experimental import pallas as pl
from jax.experimental.pallas import tpu as pltpu
from jax.sharding import PartitionSpec as P

HEADS = 6
HEAD = 64
LP = 304
KP = 384

highest = lax.Precision.HIGHEST
snr_gamma = 5.0
max_norm = 0.005
momentum_decay = 0.95
muon_rate = 0.05
adam_rate = 0.02
beta_one = 0.9
beta_two = 0.999
weight_decay = 0.01
coef_a = 3.4445
coef_b = -4.775
coef_c = 2.0315

f32, bf16 = jnp.float32, jnp.bfloat16
MESH = pl.DeviceIdType.MESH
ANY = pl.BlockSpec(memory_space=pl.ANY)
VM = pl.BlockSpec(memory_space=pltpu.VMEM)
SM = pl.BlockSpec(memory_space=pltpu.SMEM)
VMEM_LIMIT = 60000 * 1024


def low(value):
    return value.astype(bf16)


def nt(left, right):
    return lax.dot_general(left, right, (((1,), (1,)), ((), ())), preferred_element_type=f32)


def nn(left, right):
    return lax.dot_general(left, right, (((1,), (0,)), ((), ())), preferred_element_type=f32)


def tn(left, right):
    return lax.dot_general(left, right, (((0,), (0,)), ((), ())), preferred_element_type=f32)


def snr_weight(steps_t):
    level = jnp.cos((steps_t / 1000.0 + 0.008) / 1.008 * (math.pi / 2)) ** 2
    ratio = level / (1.0 - level)
    return level, jnp.minimum(ratio, snr_gamma) / ratio


def patchify(frames):
    clips, count, channels, height, breadth = frames.shape
    grid = frames.reshape(clips, count, channels, height // 2, 2, breadth // 2, 2)
    grid = grid.transpose(0, 1, 3, 5, 4, 6, 2)
    return grid.reshape(clips, count, (height // 2) * (breadth // 2), 4 * channels)


def sincos(places, model_width):
    half_width = model_width // 2
    freqs = np.exp(-math.log(10000.0) * np.arange(half_width) / half_width)
    angles = places[:, None] * freqs[None, :]
    return np.concatenate([np.sin(angles), np.cos(angles)], axis=1).astype(np.float32)


def col_sum(value):
    return jnp.sum(value.astype(f32), axis=0, keepdims=True)


def norm(value):
    centred = value - jnp.mean(value, axis=-1, keepdims=True)
    inv = lax.rsqrt(jnp.mean(centred * centred, axis=-1, keepdims=True) + 1e-06)
    return centred * inv, inv


def norm_back(grad, normed, inv):
    return inv * (
        grad
        - jnp.mean(grad, axis=-1, keepdims=True)
        - normed * jnp.mean(grad * normed, axis=-1, keepdims=True)
    )


GELU_C = math.sqrt(2.0 / math.pi)


def gelu(value):
    inner = GELU_C * (value + 0.044715 * (value * value * value))
    return value * (0.5 * (1.0 + jnp.tanh(inner)))


def gelu_both(value):
    square = value * value
    tanh = jnp.tanh(GELU_C * (value + 0.044715 * (square * value)))
    cdf = 0.5 * (1.0 + tanh)
    slope = 0.5 * (1.0 - tanh * tanh) * (GELU_C * (1.0 + 3 * 0.044715 * square))
    return value * cdf, cdf + value * slope


def lanes_low():
    lane = lax.broadcasted_iota(jnp.int32, (1, 128), 1)
    first = jnp.where(lane < HEAD, 1.0, 0.0)
    return low(first), low(1.0 - first), lane < HEAD


def stack_heads(pair, first, second):
    return jnp.concatenate([pair * first, pair * second], axis=0)


def attend(queries, keys, values, allowed):
    first, second, lower = lanes_low()
    rows = queries.shape[0]
    mixed, probs = [], []
    for pair in range(HEADS // 2):
        cut = slice(pair * 128, pair * 128 + 128)
        scores = nt(stack_heads(queries[:, cut], first, second), keys[:, cut]) * 0.125
        scores = jnp.where(allowed, scores, -1e30)
        weight = jnp.exp(scores - jnp.max(scores, axis=-1, keepdims=True))
        prob = weight / jnp.sum(weight, axis=-1, keepdims=True)
        probs.append(prob)
        out = nn(low(prob), values[:, cut])
        mixed.append(jnp.where(lower, out[:rows], out[rows:]))
    return low(jnp.concatenate(mixed, axis=1)), probs


def attend_back(grad, queries, keys, values, probs):
    first, second, lower = lanes_low()
    rows = queries.shape[0]
    dq, dk, dv = [], [], []
    for pair in range(HEADS // 2):
        cut = slice(pair * 128, pair * 128 + 128)
        stacked = stack_heads(grad[:, cut], first, second)
        prob = probs[pair]
        dv.append(tn(low(prob), stacked))
        dprob = nt(stacked, values[:, cut])
        dscore = low(prob * (dprob - jnp.sum(prob * dprob, axis=-1, keepdims=True)))
        part = nn(dscore, keys[:, cut])
        dq.append(jnp.where(lower, part[:rows], part[rows:]) * 0.125)
        dk.append(tn(dscore, stack_heads(queries[:, cut], first, second)) * 0.125)
    return tuple(jnp.concatenate(piece, axis=1) for piece in (dq, dk, dv))


def self_forward(x, mods, weights, bias, allowed):
    normed, inv = norm(x)
    a = low(normed * (1.0 + mods[1]) + mods[0])
    q = low(nt(a, weights[0]) + bias[0])
    k = low(nt(a, weights[1]))
    v = low(nt(a, weights[2]) + bias[1])
    o, probs = attend(q, k, v, allowed)
    branch = nt(o, weights[3]) + bias[2]
    return x + mods[2] * branch, (normed, inv, a, q, k, v, o, probs, branch)


def self_backward(dx, kept, mods, weights):
    normed, inv, a, q, k, v, o, probs, branch = kept
    dm2 = col_sum(dx * branch)
    dbr = low(dx * mods[2])
    do = low(nn(dbr, weights[3]))
    dq, dk, dv = (low(piece) for piece in attend_back(do, q, k, v, probs))
    da = nn(dq, weights[0]) + nn(dk, weights[1]) + nn(dv, weights[2])
    dm1, dm0 = col_sum(da * normed), col_sum(da)
    dx = dx + norm_back(da * (1.0 + mods[1]), normed, inv)
    return dx, (dm0, dm1, dm2), (col_sum(dq), col_sum(dv), col_sum(dbr)), (a, dq, dk, dv, o, dbr)


def feed_forward(x, mods, feed, bias_up, bias_down):
    normed, inv = norm(x)
    c = low(normed * (1.0 + mods[4]) + mods[3])
    u = nt(c, feed[0]) + bias_up
    g = low(gelu(u))
    branch = nn(g, feed[1]) + bias_down
    return x + mods[5] * branch, (normed, inv, c, u, g, branch)


def feed_backward(dx, kept, mods, feed):
    normed, inv, c, u, g, branch = kept
    dm5 = col_sum(dx * branch)
    dbr = low(dx * mods[5])
    du = low(nt(dbr, feed[1]) * gelu_both(u)[1])
    dc = nn(du, feed[0])
    dm4, dm3 = col_sum(dc * normed), col_sum(dc)
    dx = dx + norm_back(dc * (1.0 + mods[4]), normed, inv)
    return dx, (dm3, dm4, dm5), (col_sum(du), col_sum(dbr)), (c, dbr, du, g)


def pair_mask(kind):
    row = lax.broadcasted_iota(jnp.int32, (256, 128), 0) % 128
    col = lax.broadcasted_iota(jnp.int32, (256, 128), 1)
    if kind == 0:
        return row // 64 == col // 64
    return row % 32 == col % 32


VEC0, EMB0, HEAD0 = 0, 45, 61


def mod_rows(mq, vec, table, clip):
    rows = []
    for r in range(6):
        at = (r % 3) * 384
        rows.append(
            mq[r // 3, pl.ds(clip, 1), at : at + 384]
            + vec[3 + r : 4 + r]
            + vec[table + r : table + r + 1]
        )
    return rows


def up_bias(vec, start):
    return jnp.concatenate([vec[start + i : start + i + 1] for i in range(4)], axis=1)


def condition_kernel(rank, wt, ww, wm, perm, vec, hid, temb, mq, y2p):
    turned = jnp.transpose(ww[:, 1024:1152].astype(f32))
    vec[...] = turned
    feature = low(wt[:, 0:256])
    first = nt(feature, ww[:, 0:256]) + turned[1:2]
    hid[...] = first
    second = nt(low(first * jax.nn.sigmoid(first)), ww[:, 256:640]) + turned[2:3]
    temb[...] = second
    own = temb[pl.ds(pl.multiple_of(rank[0] * 8, 8), 8), :]
    mq[...] = nn(low(own * jax.nn.sigmoid(own)), wm[...])
    for h in range(2):
        y2p[h] = low(nt(ww[:, 640:1024], perm[h]))


def embed_chunk(tok_ref, vec, pos_ref, chunk):
    tokens = tok_ref[pl.ds(pl.multiple_of(chunk * 128, 128), 128), :]
    return low(nn(tokens, low(vec[...])) + (pos_ref[...] + vec[0:1])), tokens


def spatial_bias(vec):
    return (vec[11:12], vec[12:13], vec[13:14])


def first_kernel(role, half, tok, pos, mq, vec, wa, wf, wy, perm, captions, h1, hq, gq, cap, sems):
    @pl.when(role[0] == 1)
    def _():
        clips = captions.shape[0]
        for c in range(clips):
            pltpu.make_async_copy(captions.at[c], cap.at[c], sems.at[c]).start()
        bias = nt(low(vec[9:10]), perm[half[0]])
        for c in range(clips):
            pltpu.make_async_copy(captions.at[c], cap.at[c], sems.at[c]).wait()
            value = nt(cap[c], wy[...]) + bias
            rows = value.shape[0]
            pad = jnp.zeros((LP - rows, value.shape[1]), f32)
            hq[c] = jnp.concatenate([value, pad], axis=0)
            gq[c] = low(jnp.concatenate([gelu(value), pad], axis=0))

    @pl.when(role[0] == 0)
    def _():
        allowed = pair_mask(0)
        count = h1.shape[0]
        bu = up_bias(vec, 14)

        def step(chunk, carry):
            m = mod_rows(mq, vec, 19, (half[0] * count + chunk) // 2)
            h0, _ = embed_chunk(tok, vec, pos, chunk)
            x, _ = self_forward(h0.astype(f32), m, wa, spatial_bias(vec), allowed)
            x, _ = feed_forward(x, m, wf, bu, vec[18:19])
            out = low(x)
            for frame in range(2):
                for part in range(2):
                    start = frame * 64 + part * 32
                    h1[chunk, part, frame * 32 : frame * 32 + 32, :] = out[start : start + 32]
            return carry

        lax.fori_loop(0, count, step, 0)


def last_kernel(
    role, half, tok, pos, mq, vec, wa, wb, wf, dh, dkv, extra, grads_t, dmod_t,
    acts, actf, actw, dkvb, dy, vect, dmod, grads,
):
    @pl.when(role[0] == 0)
    def _():
        grads[...] = jnp.zeros_like(grads)
        dmod[...] = jnp.zeros_like(dmod)
        allowed = pair_mask(0)
        count = dh.shape[0]
        bu = up_bias(vec, 14)

        def step(chunk, carry):
            m = mod_rows(mq, vec, 19, (half[0] * count + chunk) // 2)
            h0, tokens = embed_chunk(tok, vec, pos, chunk)
            x, kept = self_forward(h0.astype(f32), m, wa, spatial_bias(vec), allowed)
            _, kept_f = feed_forward(x, m, wf, bu, vec[18:19])
            parts = []
            for frame in range(2):
                for part in range(2):
                    parts.append(dh[chunk, part, frame * 32 : frame * 32 + 32, :])
            dx = jnp.concatenate(parts, axis=0).astype(f32)
            dx, dm_f, db_f, act_f = feed_backward(dx, kept_f, m, wf)
            dx, dm_a, db_a, act_a = self_backward(dx, kept, m, wa)
            dh0 = low(dx)
            where = pl.ds(pl.multiple_of(chunk * 128, 128), 128)
            for i, value in enumerate(act_a):
                acts[i, where, :] = value
            for i in range(2):
                actf[i, where, :] = act_f[i]
                actw[i, where, :] = act_f[2 + i]
            mods = dm_a + dm_f
            dmod[chunk, 0:6, :] = jnp.concatenate(mods, axis=0)
            grads[...] += tn(tokens, dh0)
            grads[0:1] += col_sum(dh0)
            for i in range(3):
                grads[11 + i : 12 + i] += db_a[i]
            for i in range(4):
                grads[14 + i : 15 + i] += db_f[0][:, i * 384 : i * 384 + 384]
            grads[18:19] += db_f[1]
            for i in range(6):
                grads[19 + i : 20 + i] += mods[i]
            return carry

        lax.fori_loop(0, count, step, 0)

    @pl.when(role[0] == 1)
    def _():
        grads[...] = grads_t[...]
        dmod[...] = dmod_t[...]
        dy[...] = jnp.zeros_like(dy)
        dkvb[...] = jnp.zeros_like(dkvb)
        ncl = dy.shape[0]
        for c in range(ncl):

            @pl.when(jnp.logical_or(half[0] == 0, c > 0))
            def _():
                pieces = []
                for i in range(2):
                    value = dkv[i, c]
                    if c == ncl - 1:
                        value = value + jnp.where(half[0] == 0, extra[i], 0.0)
                    pieces.append(low(value))
                dkvb[0, c], dkvb[1, c] = pieces
                back = low(nn(pieces[0], wb[1]) + nn(pieces[1], wb[2]))
                dy[c] = back
                grads[40:41] += col_sum(pieces[1])
                grads[10:11] += col_sum(back)

    vect[...] = jnp.transpose(grads[...])


def temporal_kernel(
    role, half, rank, lens, errw, h1, timing, mq, vec, temb, wa, wb, wf, gq, rgq, y2p, target,
    dh1, acts, actf, actw, ybuf, dkv, grads, dmod, loss, kx, vx,
):
    @pl.when(role[0] == 0)
    def _():
        loss[...] = jnp.zeros_like(loss)

    @pl.when(role[0] == 1)
    def _():
        allowed = pair_mask(1)
        count = h1.shape[0]
        ncl = ybuf.shape[0]
        for ref in (kx, vx, dkv, grads, loss):
            ref[...] = jnp.zeros_like(ref)
        first_clip = (half[0] * count) // 2
        for c in range(ncl):
            clip = jnp.minimum(first_clip + c, gq.shape[0] - 1)
            y = nt(gq[clip], y2p[half[0]]) + nt(rgq[clip], y2p[1 - half[0]])
            y = low(y + vec[10:11])
            ybuf[c] = y
            kx[c, 0:LP, :] = low(nt(y, wb[1]))
            vx[c, 0:LP, :] = low(nt(y, wb[2]) + vec[40:41])
        bu = up_bias(vec, 28)
        lane = lax.broadcasted_iota(jnp.int32, (1, 128), 1)
        real = jnp.logical_and(lane >= HEAD0, lane < HEAD0 + 16)
        bias_h = pltpu.roll(jnp.broadcast_to(vec[44:45, 0:128], (8, 128)), HEAD0, 1)[0:1]
        head = low(vec[...])

        def step(chunk, carry):
            clip = (half[0] * count + chunk) // 2
            here = clip - first_clip
            m = mod_rows(mq, vec, 33, clip)
            emb = temb[pl.ds(rank[0] * 8 + clip, 1), :]
            m6, m7 = vec[42:43] + emb, vec[43:44] + emb
            h = jnp.concatenate([h1[chunk, 0], h1[chunk, 1]], axis=0)
            x = h.astype(f32) + timing[...]
            x, kept = self_forward(x, m, wa, (vec[25:26], vec[26:27], vec[27:28]), allowed)
            xb = low(x)
            cq = low(nt(xb, wb[0]) + vec[39:40])
            keys, values = kx[here], vx[here]
            seen = lax.broadcasted_iota(jnp.int32, (1, KP), 1) < lens[clip]
            co, probs = attend(cq, keys, values, seen)
            x = x + (nt(co, wb[3]) + vec[41:42])
            x, kept_f = feed_forward(x, m, wf, bu, vec[32:33])
            h2 = low(x).astype(f32)
            normed, inv = norm(h2)
            cf = low(normed * (1.0 + m7) + m6)
            where = pl.ds(pl.multiple_of(chunk * 128, 128), 128)
            diff = jnp.where(real, nt(cf, head) + bias_h - target[where, :], 0.0)
            scale = errw[clip]
            loss[...] += col_sum(diff * diff) * scale
            dpred = low(diff * (2.0 * scale))
            dcf = nn(dpred, head)
            grads[...] += tn(dpred, cf)
            dbh = pltpu.roll(jnp.broadcast_to(col_sum(dpred), (8, 128)), 128 - HEAD0, 1)[0:1]
            grads[44:45, 0:128] += dbh
            dm7, dm6 = col_sum(dcf * normed), col_sum(dcf)
            dx = low(norm_back(dcf * (1.0 + m7), normed, inv)).astype(f32)
            dx, dm_f, db_f, act_f = feed_backward(dx, kept_f, m, wf)
            dcbr = low(dx)
            dco = low(nn(dcbr, wb[3]))
            dcq, dck, dcv = attend_back(dco, cq, keys, values, probs)
            dcq = low(dcq)
            dkv[0, here] += dck[0:LP]
            dkv[1, here] += dcv[0:LP]
            dx = dx + nn(dcq, wb[0])
            dx, dm_a, db_a, act_a = self_backward(dx, kept, m, wa)
            out = low(dx)
            dh1[chunk, 0] = out[0:64]
            dh1[chunk, 1] = out[64:128]
            for i, value in enumerate(act_a + (xb, dcq, co, dcbr)):
                acts[i, where, :] = value
            for i in range(2):
                actf[i, where, :] = act_f[i]
                actw[i, where, :] = act_f[2 + i]
            mods = dm_a + dm_f + (dm6, dm7)
            dmod[chunk] = jnp.concatenate(mods, axis=0)
            for i in range(3):
                grads[25 + i : 26 + i] += db_a[i]
            for i in range(4):
                grads[28 + i : 29 + i] += db_f[0][:, i * 384 : i * 384 + 384]
            grads[32:33] += db_f[1]
            for i in range(6):
                grads[33 + i : 34 + i] += mods[i]
            grads[39:40] += col_sum(dcq)
            grads[41:42] += col_sum(dcbr)
            grads[42:43] += dm6
            grads[43:44] += dm7
            return carry

        lax.fori_loop(0, count, step, 0)


def weight_grad_kernel(
    role, half, rank, acts_s, acts_t, racts, actf_s, actf_t, ractf, actw_s, actw_t, ractw,
    ybuf, rybuf, dkvb, rdkvb, dy, rdy, gq, rgq, hq, y2p, perm, captions,
    own, snd, own_text, snd_text, la, lf, lw, cap, sems,
):
    tokens = acts_s.shape[1]
    line, cols = own.shape[1], own.shape[2]
    odd = lax.rem(rank[0], 2) == 1
    near, far = pl.ds(0, tokens), pl.ds(tokens, tokens)

    def copies(r, h):
        if h == 0:
            local = acts_s if r == 0 else acts_t
            size = pl.ds(0, local.shape[0])
            return [(local, la.at[size, near], 0), (racts.at[size], la.at[size, far], 1)]
        thin, wide = ((actf_s, actw_s), (actf_t, actw_t))[r]
        return [
            (thin, lf.at[:, near], 0), (ractf, lf.at[:, far], 1),
            (wide, lw.at[:, near], 2), (ractw, lw.at[:, far], 3),
        ]

    def text():
        return [(captions.at[c], cap.at[c], 4 + c) for c in range(captions.shape[0])]

    def run(group, finish):
        for src, dst, i in group:
            copy = pltpu.make_async_copy(src, dst, sems.at[i])
            copy.wait() if finish else copy.start()

    for r in range(2):
        for h in range(2):

            @pl.when(jnp.logical_and(role[0] == r, half[0] == h))
            def _():
                run(copies(r, h), False)
                if r == 1:
                    run(text(), False)
                run(copies(r, h), True)

    def keep(unit, at, first, second):
        own[unit, at] = jnp.where(odd, second, first)
        snd[unit, at] = low(jnp.where(odd, first, second))

    def keep_square(unit, value):
        for p in range(line):
            cut = 2 * p * cols
            keep(unit, p, value[cut : cut + cols], value[cut + cols : cut + 2 * cols])

    def matrix(unit, left, right):
        keep_square(unit, tn(la[left], la[right]))

    @pl.when(half[0] == 0)
    def _():
        def inputs(i, carry):
            matrix(i, 1 + i, 0)
            return carry

        lax.fori_loop(0, 3, inputs, 0)

        def outputs(i, carry):
            matrix(3 + i, 5 + 2 * i, 4 + 2 * i)
            return carry

        lax.fori_loop(0, 1 + role[0], outputs, 0)

        @pl.when(role[0] == 1)
        def _():
            def cross(i, carry):
                total = tn(dkvb[i, 0], ybuf[0]) + tn(rdkvb[i, 0], rybuf[0])
                for c in range(1, ybuf.shape[0]):
                    total = total + tn(dkvb[i, c], ybuf[c]) + tn(rdkvb[i, c], rybuf[c])
                keep_square(5 + i, total)
                return carry

            lax.fori_loop(0, 2, cross, 0)
            matrix(7, 9, 8)

    @pl.when(half[0] == 1)
    def _():
        side = la.shape[2]
        tiles = lw.shape[2] // side
        block = 4 * cols
        per = side // (2 * block)

        def feed(i, carry):
            pair, tile = i // tiles, lax.rem(i, tiles)
            lanes = pl.ds(pl.multiple_of(tile * side, 128), side)
            value = tn(lw[pair, :, lanes], lf[pair])
            for p in range(per):
                for j in range(4):
                    at = 2 * p * block + j * cols
                    keep(
                        4 * pair + j, tile * per + p, value[at : at + cols],
                        value[at + block : at + block + cols],
                    )
            return carry

        lax.fori_loop(0, 2 * tiles, feed, 0)

    @pl.when(role[0] == 1)
    def _():
        clips = captions.shape[0]
        rows = captions.shape[1]
        owners = [((2 * c) // clips, c - (((2 * c) // clips) * clips) // 2) for c in range(clips)]

        def dy_of(c):
            h, at = owners[c]
            return jnp.where(half[0] == h, dy[at].astype(f32), rdy[at].astype(f32)).astype(bf16)

        @pl.when(half[0] == 1)
        def _():
            total = None
            for c in range(clips):
                plain = low(nn(gq[c], perm[1]) + nn(rgq[c], perm[0]))
                part = tn(dy_of(c), plain)
                total = part if total is None else total + part
            keep_square(8, total)

        units = own_text.shape[1]

        def keep_text(lanes, value):
            for p in range(line):
                cut = 2 * p * units
                first, second = value[cut : cut + units], value[cut + units : cut + 2 * units]
                own_text[p, :, lanes] = low(jnp.where(odd, second, first))
                snd_text[p, :, lanes] = low(jnp.where(odd, first, second))

        turned = []
        sums = None
        ones = jnp.ones((rows, 128), bf16)
        for c in range(clips):
            back = nn(dy_of(c), y2p[half[0]]) * gelu_both(hq[c])[1]
            turned.append(low(jnp.transpose(back))[:, 0:rows])
            part = nn(turned[c], ones)
            sums = part if sums is None else sums + part
        run(text(), True)

        def text_tile(t, carry):
            lanes = pl.ds(pl.multiple_of(t * 512, 512), 512)
            total = nn(turned[0], cap[0, :, lanes])
            for c in range(1, clips):
                total = total + nn(turned[c], cap[c, :, lanes])
            keep_text(lanes, total)
            return carry

        lax.fori_loop(0, captions.shape[2] // 512, text_tile, 0)
        keep_text(pl.ds(captions.shape[2], 128), sums)


def halves(value):
    first = low(value)
    return first, low(value - first.astype(f32))


def lefts(value, axis=1):
    first, second = halves(value)
    return jnp.concatenate([first, first, second], axis=axis)


def rights(value, axis=0):
    first, second = halves(value)
    return jnp.concatenate([first, second, first], axis=axis)


def muon_kernel(half, ua, uf, xa, xf, gram, whole):
    @pl.when(half[0] == 0)
    def _():
        u = ua[...]
        whole[...] = u / (jnp.sqrt(jnp.sum(u * u)) + 1e-07)

        def sweep(i, carry):
            x = whole[...]
            square = nt(lefts(x), rights(x, 1))
            poly = coef_b * square + coef_c * nn(lefts(square), rights(square))
            whole[...] = coef_a * x + nn(lefts(poly), rights(x))
            return carry

        lax.fori_loop(0, 5, sweep, 0)
        xa[...] = low(whole[...])

    @pl.when(half[0] == 1)
    def _():
        width = uf.shape[1]
        tiles = uf.shape[0] // width
        gram[...] = jnp.zeros_like(gram)

        def rows(t):
            return pl.ds(pl.multiple_of(t * width, 128), width)

        def first(t, carry):
            piece = uf[rows(t), :]
            gram[...] += tn(lefts(piece, 0), rights(piece, 0))
            return carry

        lax.fori_loop(0, tiles, first, 0)
        row = lax.broadcasted_iota(jnp.int32, (width, width), 0)
        col = lax.broadcasted_iota(jnp.int32, (width, width), 1)
        eye = jnp.where(row == col, 1.0, 0.0)
        start = gram[...]
        inv = 1.0 / (jnp.sqrt(jnp.sum(start * eye)) + 1e-07)
        gram[...] = start * (inv * inv)
        whole[...] = eye * inv

        def poly_of(a):
            return coef_a * eye + coef_b * a + coef_c * nn(lefts(a), rights(a))

        def sweep(i, carry):
            a = gram[...]
            left = lefts(poly_of(a))
            both = nn(left, rights(jnp.concatenate([a, whole[...]], axis=1)))
            whole[...] = both[:, width:]
            gram[...] = nn(left, rights(both[:, :width]))
            return carry

        lax.fori_loop(0, 4, sweep, 0)
        last = rights(nn(lefts(poly_of(gram[...])), rights(whole[...])))

        def apply(t, carry):
            xf[rows(t), :] = low(nn(lefts(uf[rows(t), :]), last))
            return carry

        lax.fori_loop(0, tiles, apply, 0)


def local_call(kernel, out_shape, in_specs, args, scratch=()):
    return pl.pallas_call(
        kernel,
        out_shape=out_shape,
        in_specs=in_specs,
        out_specs=jax.tree.map(lambda _: VM, out_shape),
        scratch_shapes=scratch,
        compiler_params=pltpu.CompilerParams(vmem_limit_bytes=VMEM_LIMIT),
    )(*args)


def here():
    return lax.axis_index("dp"), lax.axis_index("segment")


def dev(d, s):
    return {"dp": d, "segment": s}


def remote(src, dst, send, recv, target):
    return pltpu.make_async_remote_copy(
        src_ref=src, dst_ref=dst, send_sem=send, recv_sem=recv, device_id=target,
        device_id_type=MESH,
    )


def greet(targets):
    barrier = pltpu.get_barrier_semaphore()
    for target in targets:
        pl.semaphore_signal(barrier, inc=1, device_id=target, device_id_type=MESH)
    pl.semaphore_wait(barrier, len(targets))


def greet_dp(n, extra=()):
    d, s = here()
    barrier = pltpu.get_barrier_semaphore()

    def step(k, carry):
        pl.semaphore_signal(
            barrier, inc=1, device_id=dev(lax.rem(d + k, n), s), device_id_type=MESH
        )
        return carry

    lax.fori_loop(1, n, step, 0)
    for target in extra:
        pl.semaphore_signal(barrier, inc=1, device_id=target, device_id_type=MESH)
    pl.semaphore_wait(barrier, n - 1 + len(extra))


def comm_call(kernel, cid, args, out_shape, sems, out_specs=None, scratch=(), in_specs=None):
    if out_specs is None:
        out_specs = jax.tree.map(lambda _: ANY, out_shape)
    return pl.pallas_call(
        kernel,
        out_shape=out_shape,
        in_specs=[ANY] * len(args) if in_specs is None else in_specs,
        out_specs=out_specs,
        scratch_shapes=list(scratch) + [pltpu.SemaphoreType.DMA(shape) for shape in sems],
        compiler_params=pltpu.CompilerParams(
            collective_id=cid, has_side_effects=True, vmem_limit_bytes=VMEM_LIMIT
        ),
    )(*args)


def gather_kernel(n, pa, pb, pf, pw, py, pm, pt, wa, wb, wf, ww, wy, wm, wt,
                  send, recv, crecv, own):
    pair = 2 if n % 2 == 0 else 1
    line = n // pair
    d, s = here()
    role, half = s // 2, lax.rem(s, 2)
    a, x = d // pair, lax.rem(d, pair)
    mate = dev(d, role * 2 + 1 - half)
    above, below = dev(d + pair, s), dev(d - pair, s)
    across = dev(a * pair + (pair - 1 - x), s)
    barrier = pltpu.get_barrier_semaphore()

    def signal(target):
        pl.semaphore_signal(barrier, inc=1, device_id=target, device_id_type=MESH)

    signal(mate)
    if pair == 2:
        signal(across)

    @pl.when(a < line - 1)
    def _():
        signal(above)

    @pl.when(a > 0)
    def _():
        signal(below)

    pl.semaphore_wait(barrier, pair + jnp.minimum(a, 1) + jnp.minimum(line - 1 - a, 1))

    def two(i, ref, out):
        return [
            (i, ref.at[pl.ds(0, 2)], out.at[pl.ds(0, 2)], 2),
            (i + 1, ref.at[pl.ds(2, 2)], out.at[pl.ds(2, 2)], 2),
        ]

    feeds = [(m, pf.at[pl.ds(m, 1)], wf.at[pl.ds(m, 1)], 1) for m in range(2)]
    words = [(2, pw, ww, 0)]
    first = {
        0: {0: words + two(0, pa, wa), 1: feeds},
        1: {0: words + two(0, pa, wa) + two(6, pb, wb), 1: feeds},
    }

    def slot(ref, lead, o):
        return ref.at[:, o] if lead else ref.at[o]

    for r in range(2):
        for h in range(2):

            @pl.when(jnp.logical_and(role == r, half == h))
            def _():
                parts = [(i, src, dst, lead, True) for i, src, dst, lead in first[r][h]]
                parts.append((3, pt, wt, 0, False))
                if r == 0:
                    parts.append((4, pm, wm, 0, False))
                else:
                    parts.append((5, py, wy, 0, False))

                def move(part, way, o, target, is_own=False):
                    i, src, dst, lead, common = part
                    there = slot(dst, lead, o)
                    sem = crecv if way == 3 else recv
                    return remote(
                        src if is_own else there, there, send.at[way, i, o], sem.at[i, o], target
                    )

                def forward(o, up, down, side, is_own, finish, wait=False):
                    for part in parts:
                        if wait:
                            move(part, 0, o, across).wait_recv()

                        def go(way, target):
                            copy = move(part, way, o, target, is_own)
                            copy.wait_send() if finish else copy.start()

                        if side and pair == 2:
                            go(2, across)
                        if up is not None:
                            pl.when(up)(functools.partial(go, 0, above))
                        if down is not None:
                            pl.when(down)(functools.partial(go, 1, below))
                        if part[4]:
                            go(3, mate)

                for part in parts:
                    i, src, dst, lead, common = part
                    pltpu.make_async_copy(src, slot(dst, lead, d), own.at[i]).start()
                forward(d, a < line - 1, a > 0, True, True, False)
                other = pair - 1 - x

                def sweep(finish):
                    def step(k, carry):
                        @pl.when(a - k >= 0)
                        def _():
                            o = (a - k) * pair + x
                            forward(o, a < line - 1, None, True, False, finish, not finish)

                        @pl.when(a + k < line)
                        def _():
                            o = (a + k) * pair + x
                            forward(o, None, a > 0, True, False, finish, not finish)

                        if pair == 2:

                            @pl.when(a - (k - 1) >= 0)
                            def _():
                                o = (a - (k - 1)) * pair + other
                                forward(o, None, None, False, False, finish, not finish)

                            @pl.when(jnp.logical_and(k > 1, a + (k - 1) < line))
                            def _():
                                o = (a + (k - 1)) * pair + other
                                forward(o, None, None, False, False, finish, not finish)

                        return carry

                    lax.fori_loop(1, line + 1, step, 0)

                sweep(False)
                forward(d, a < line - 1, a > 0, True, True, True)
                sweep(True)
                for part in parts:
                    i, src, dst, lead, common = part
                    pltpu.make_async_copy(src, slot(dst, lead, d), own.at[i]).wait()

                def collect(o, carry):
                    for i, src, dst, lead in first[r][1 - h]:
                        there = slot(dst, lead, o)
                        remote(there, there, send.at[3, i, o], crecv.at[i, o], mate).wait_recv()
                    return carry

                lax.fori_loop(0, n, collect, 0)


def mate_kernel(src, dst, send, recv, own):
    d, s = here()
    role, half = s // 2, lax.rem(s, 2)
    mate = dev(d, role * 2 + 1 - half)

    @pl.when(role == 0)
    def _():
        greet([mate])
        pltpu.make_async_copy(src, dst.at[half], own.at[0]).start()
        remote(src, dst.at[half], send.at[0], recv.at[0], mate).start()
        pltpu.make_async_copy(src, dst.at[half], own.at[0]).wait()
        remote(src, dst.at[1 - half], send.at[0], recv.at[0], mate).wait()


def dp_gather_kernel(n, src, dst, send, recv, own):
    d, s = here()

    @pl.when(s // 2 == 0)
    def _():
        greet_dp(n)
        pltpu.make_async_copy(src, dst.at[d], own.at[0]).start()

        def start(k, carry):
            remote(src, dst.at[d], send.at[k], recv.at[k], dev(lax.rem(d + k, n), s)).start()
            return carry

        def finish(k, carry):
            o = lax.rem(d + n - k, n)
            remote(src, dst.at[o], send.at[k], recv.at[k], dev(o, s)).wait()
            return carry

        lax.fori_loop(1, n, start, 0)
        lax.fori_loop(1, n, finish, 0)
        pltpu.make_async_copy(src, dst.at[d], own.at[0]).wait()


def forward_kernel(count, h1s, gq, mq, h1t, gqs, mqt, send, recv, msend, mrecv, qsend, qrecv):
    relay_half_clips(
        count, 0, h1s, h1t, send, recv, swap=(gq, gqs, msend, mrecv), rows=(mq, mqt, qsend, qrecv)
    )


def relay_half_clips(count, from_role, src, dst, send, recv, extra=None, swap=None, rows=None):
    d, s = here()
    role, half = s // 2, lax.rem(s, 2)
    peers = [dev(d, (1 - role) * 2), dev(d, (1 - role) * 2 + 1)]
    mate = dev(d, role * 2 + 1 - half)
    peers.append(mate)
    greet(peers)

    def unit(i, part):
        there = half * count + i
        clip, own = there // 2, lax.rem(there, 2)
        other = 2 * clip + part
        return own, other // count, lax.rem(other, count)

    def copy(i, part):
        own, to, slot = unit(i, part)
        return remote(
            src.at[i, part], dst.at[slot, own], send.at[i, part], recv.at[slot, own],
            dev(d, (1 - from_role) * 2 + to),
        )

    def row_copy(to, finish):
        value, there, qsend, qrecv = rows
        slot = there.at[half] if from_role == 1 else there
        copy = remote(value, slot, qsend.at[to], qrecv.at[half], dev(d, (1 - from_role) * 2 + to))
        copy.wait_send() if finish else copy.start()

    def row_sends(finish):
        if rows is None:
            return

        @pl.when(role == from_role)
        def _():
            if from_role == 0:
                for to in range(2):
                    pl.when(half == to)(functools.partial(row_copy, to, finish))
            else:
                for to in range(2):
                    row_copy(to, finish)

    row_sends(False)
    if swap is not None:
        mine, both, msend, mrecv = swap

        @pl.when(role == 1)
        def _():
            remote(mine, both, msend.at[0], mrecv.at[0], mate).start()

    if extra is not None:
        own_src, own_dst, esend, erecv = extra

        @pl.when(jnp.logical_and(role == 1, half == 1))
        def _():
            remote(own_src, own_dst, esend.at[0], erecv.at[0], dev(d, 2)).start()

    @pl.when(role == from_role)
    def _():
        for i in range(count):
            for part in range(2):
                copy(i, part).start()
        for i in range(count):
            for part in range(2):
                copy(i, part).wait_send()

    @pl.when(role == 1 - from_role)
    def _():
        for i in range(count):
            for part in range(2):
                remote(
                    src.at[i, part], dst.at[i, part], send.at[i, part], recv.at[i, part],
                    dev(d, from_role * 2),
                ).wait_recv()

    row_sends(True)
    if rows is not None:
        value, there, qsend, qrecv = rows

        @pl.when(role == 1 - from_role)
        def _():
            if from_role == 0:
                remote(value, there, qsend.at[0], qrecv.at[half], mate).wait_recv()
            else:
                for o in range(2):
                    remote(value, there.at[o], qsend.at[0], qrecv.at[o], mate).wait_recv()

    if swap is not None:

        @pl.when(role == 1)
        def _():
            remote(mine, both, msend.at[0], mrecv.at[0], mate).wait()

    if extra is not None:

        @pl.when(jnp.logical_and(role == 1, half == 1))
        def _():
            remote(own_src, own_dst, esend.at[0], erecv.at[0], dev(d, 2)).wait_send()

        @pl.when(jnp.logical_and(role == 1, half == 0))
        def _():
            remote(own_src, own_dst, esend.at[0], erecv.at[0], dev(d, 2)).wait_recv()


def backward_kernel(count, dh1, dkv, dmod, dhs, extra, dmods, send, recv, esend, erecv, qsend,
                    qrecv):
    relay_half_clips(
        count, 1, dh1, dhs, send, recv, extra=(dkv.at[:, 0], extra, esend, erecv),
        rows=(dmod, dmods, qsend, qrecv),
    )


def swap_kernel(acts_s, acts_t, actf_s, actf_t, actw_s, actw_t, ybuf, dkvb, dy, dmod,
                racts, ractf, ractw, rybuf, rdkvb, rdy, rdmod, send, recv):
    d, s = here()
    role, half = s // 2, lax.rem(s, 2)
    mate = dev(d, role * 2 + 1 - half)
    greet([mate])
    six = acts_s.shape[0]
    gives = {
        (0, 0): [(0, actf_s, ractf), (1, actw_s, ractw), (4, dmod, rdmod)],
        (0, 1): [(0, acts_s, racts.at[pl.ds(0, six)]), (4, dmod, rdmod)],
        (1, 0): [(0, actf_t, ractf), (1, actw_t, ractw), (2, dy, rdy)],
        (1, 1): [(0, acts_t, racts), (1, ybuf, rybuf), (3, dkvb, rdkvb), (2, dy, rdy)],
    }
    for (r, h), mine in gives.items():

        @pl.when(jnp.logical_and(role == r, half == h))
        def _():
            for i, src, dst in mine:
                remote(src, dst, send.at[i], recv.at[i], mate).start()
            for i, src, dst in mine:
                remote(src, dst, send.at[i], recv.at[i], mate).wait_send()
            for i, src, dst in gives[(r, 1 - h)]:
                remote(src, dst, send.at[i], recv.at[i], mate).wait_recv()


TEXT_CUTS = 3


def scatter_kernel(n, own_in, snd, own_text, snd_text, dm, vec, loss, summed, text, rm, vsum, squares,
                   own, rx, up, down, sx, rz, town, trx, tsx, trz, rv,
                   osem, send1, recv1, send2, recv2, usend, urecv, dsend, drecv,
                   ssend, srecv, sown):
    line = n // 2
    d, s = here()
    role, half = s // 2, lax.rem(s, 2)
    a, x = d // 2, lax.rem(d, 2)
    across = dev(a * 2 + 1 - x, s)
    count = 8 - 4 * (1 - role) * (1 - half)
    greet_dp(n)
    squares[...] = jnp.zeros_like(squares)
    squares[1:2, 0:128] = loss[...]
    step = text.shape[1] // TEXT_CUTS
    is_text, is_last = role == 1, s == 3

    def first_copies(u):
        return (
            remote(snd.at[u], rx.at[u], send1.at[u], recv1.at[u], across),
            pltpu.make_async_copy(own_in.at[u], own.at[u], osem.at[u]),
        )

    def text_copies(k):
        lanes = pl.ds(pl.multiple_of(k * step, 128), step)
        return (
            remote(
                snd_text.at[:, :, lanes], trx.at[k], send1.at[9 + k], recv1.at[9 + k], across
            ),
            pltpu.make_async_copy(own_text.at[:, :, lanes], town.at[k], osem.at[9 + k]),
        )

    def begin(u, carry):
        for copy in first_copies(u):
            copy.start()
        return carry

    def small(finish):
        items = [(1, lambda p: vec.at[p], lambda o: rv.at[o], None),
                 (0, lambda p: dm, lambda o: rm.at[o], role == 0)]
        for i, src, dst, when in items:

            def go():
                def each(k, carry):
                    to, o = lax.rem(d + k, n), lax.rem(d + n - k, n)
                    if finish:
                        remote(src(o), dst(o), ssend.at[i, k], srecv.at[i, k], dev(o, s)).wait()
                    else:
                        remote(
                            src(to), dst(d), ssend.at[i, k], srecv.at[i, k], dev(to, s)
                        ).start()
                    return carry

                lax.fori_loop(1, n, each, 0)
                copy = pltpu.make_async_copy(src(d), dst(d), sown.at[i])
                copy.wait() if finish else copy.start()

            if when is None:
                go()
            else:
                pl.when(when)(go)

    lax.fori_loop(0, 1, begin, 0)
    small(False)
    lax.fori_loop(1, count, begin, 0)

    @pl.when(is_last)
    def _():
        begin(8, 0)

    @pl.when(is_text)
    def _():
        for k in range(TEXT_CUTS):
            for copy in text_copies(k):
                copy.start()

    def upward(u, p):
        return remote(up.at[u, p], up.at[u, p], usend.at[u, p], urecv.at[u, p], dev(d + 2, s))

    def downward(u, p):
        return remote(
            down.at[u, p], down.at[u, p], dsend.at[u, p], drecv.at[u, p], dev(d - 2, s)
        )

    def along_up(u):
        def add(i, carry):
            p = line - 1 - i

            @pl.when(a == 0)
            def _():
                up[u, p] = own[u, p]

            @pl.when(a > 0)
            def _():
                upward(u, p).wait_recv()
                up[u, p] = up[u, p] + own[u, p]

            return carry

        def send(i, carry):
            upward(u, line - 1 - i).start()
            return carry

        lax.fori_loop(0, line - 1 - a, add, 0)
        lax.fori_loop(0, line - 1 - a, send, 0)

    def along_down(u):
        def add(p, carry):
            @pl.when(a == line - 1)
            def _():
                down[u, p] = own[u, p]

            @pl.when(a < line - 1)
            def _():
                downward(u, p).wait_recv()
                down[u, p] = down[u, p] + own[u, p]

            return carry

        def send(p, carry):
            downward(u, p).start()
            return carry

        lax.fori_loop(0, a, add, 0)
        lax.fori_loop(0, a, send, 0)

    def pairs(u):
        for copy in first_copies(u):
            copy.wait()
        own[u] = own[u] + rx[u].astype(f32)

    def direct(i, total, line_in, finish):
        def each(k, carry):
            to, o = lax.rem(a + k, line), lax.rem(a + line - k, line)
            if finish:
                remote(
                    total.at[o], line_in.at[o], send2.at[i, k], recv2.at[i, k], dev(o * 2 + x, s)
                ).wait()
            else:
                remote(
                    total.at[to], line_in.at[a], send2.at[i, k], recv2.at[i, k],
                    dev(to * 2 + x, s),
                ).start()
            return carry

        lax.fori_loop(1, line, each, 0)

    def text_pairs(k):
        for copy in text_copies(k):
            copy.wait()
        tsx[k] = low(town[k].astype(f32) + trx[k].astype(f32))

    def round_trip(i, carry):
        @pl.when(i < count)
        def _():
            pairs(i)

        k = i - count

        @pl.when(jnp.logical_and(is_text, jnp.logical_and(k >= 0, k < TEXT_CUTS)))
        def _():
            text_pairs(k)

        @pl.when(jnp.logical_and(is_text, jnp.logical_and(k >= 1, k <= TEXT_CUTS)))
        def _():
            direct(k - 1, tsx.at[k - 1], trz.at[k - 1], False)

        @pl.when(jnp.logical_and(is_last, k == 0))
        def _():
            pairs(8)
            sx[...] = low(own[8])

        @pl.when(jnp.logical_and(is_last, k == 1))
        def _():
            direct(TEXT_CUTS, sx, rz, False)

        later = i - 1 - a

        @pl.when(jnp.logical_and(later >= 0, later < count))
        def _():
            along_up(later)

        other = i - line + a

        @pl.when(jnp.logical_and(other >= 0, other < count))
        def _():
            along_down(other)

        return carry

    lax.fori_loop(0, count + jnp.maximum(line, TEXT_CUTS + 1), round_trip, 0)
    small(True)
    vsum[...] = lax.fori_loop(0, n, lambda o, total: total + rv[o], jnp.zeros(vsum.shape, f32))

    def collect(u, carry):
        @pl.when(a > 0)
        def _():
            upward(u, a).wait_recv()
            own[u, a] = own[u, a] + up[u, a]

        @pl.when(a < line - 1)
        def _():
            downward(u, a).wait_recv()
            own[u, a] = own[u, a] + down[u, a]

        whole = own[u, a]
        summed[u] = whole
        squares[0:1, :] += col_sum(whole * whole)
        return carry

    lax.fori_loop(0, count, collect, 0)

    def drain(u, carry):
        def one(i, c):
            upward(u, line - 1 - i).wait_send()
            return c

        def two(p, c):
            downward(u, p).wait_send()
            return c

        lax.fori_loop(0, line - 1 - a, one, 0)
        lax.fori_loop(0, a, two, 0)
        return carry

    lax.fori_loop(0, count, drain, 0)

    def others(line_in, whole):
        return lax.fori_loop(
            1, line, lambda k, acc: acc + line_in[lax.rem(a + k, line)].astype(f32), whole
        )

    @pl.when(is_last)
    def _():
        direct(TEXT_CUTS, sx, rz, True)
        whole = others(rz, own[8, a])
        summed[8] = whole
        squares[0:1, :] += col_sum(whole * whole)

    @pl.when(is_text)
    def _():
        for k in range(TEXT_CUTS):
            direct(k, tsx.at[k], trz.at[k], True)
            whole = others(trz.at[k], town[k, a].astype(f32) + trx[k, a].astype(f32))
            text[:, k * step : k * step + step] = low(whole)
            counted = whole
            if k == TEXT_CUTS - 1:
                lane = lax.broadcasted_iota(jnp.int32, (1, step), 1)
                counted = jnp.where(lane <= step - 128, whole, 0.0)
            both = counted * counted
            for t in range(0, step, 128):
                squares[0:1, 0:128] += col_sum(both[:, t : t + 128])


def three(value):
    first = low(value)
    rest = value - first.astype(f32)
    second = low(rest)
    return first, second, low(rest - second.astype(f32))


def nn3(left, right):
    return sum(nn(piece, right) for piece in three(left))


def nt3(left, right):
    return sum(nt(piece, right) for piece in three(left))


def tn3(left, right):
    return sum(tn(left, piece) for piece in three(right))


def own_columns(rank, width, cols):
    row = lax.broadcasted_iota(jnp.int32, (width, 128), 0)
    col = lax.broadcasted_iota(jnp.int32, (width, 128), 1)
    return low(jnp.where(jnp.logical_and(row == rank * cols + col, col < cols), 1.0, 0.0))


def clip_groups(clips, rows):
    per = 8 * (rows // (clips // 8) // 8)
    left = lax.broadcasted_iota(jnp.int32, (clips, rows), 0)
    right = lax.broadcasted_iota(jnp.int32, (clips, rows), 1)
    match = (right // per) * 8 + (right % per) // 8 == left
    return low(jnp.where(match, 1.0, 0.0))


def silu_back(value):
    gate = jax.nn.sigmoid(value)
    return gate * (1.0 + value * (1.0 - gate))


def time_back_kernel(role, rank, rm, wm, temb, dtemb):
    pl.when(role[0] == 0)(lambda: time_back(rank, rm, wm, temb, dtemb))


def time_back(rank, rm, wm, temb, dtemb):
    cols, width = wm.shape[0], rm.shape[1]
    rows, clips = rm.shape[0], temb.shape[0]
    pick = own_columns(rank[0], width, cols)
    kind = lax.broadcasted_iota(jnp.int32, (rows, 1), 0) % 8
    value = rm[...]
    pieces = three(value)
    total = jnp.where(kind >= 6, nn3(value, pick), 0.0)
    zeros = jnp.zeros((128 - cols, width), bf16)
    for r in range(6):
        weight = jnp.concatenate([wm[:, r * width : r * width + width], zeros], axis=0)
        back = nt(pieces[0], weight) + nt(pieces[1], weight) + nt(pieces[2], weight)
        total = total + jnp.where(kind == r, back, 0.0)
    slope = silu_back(nn3(temb[...], pick))
    group = clip_groups(clips, rows)

    def collapse(part):
        first, second, third = three(part)
        return nn(group, first) + nn(group, second) + nn(group, third)

    dtemb[...] = collapse(jnp.where(kind < 6, total, 0.0)) * slope + collapse(
        jnp.where(kind >= 6, total, 0.0)
    )


def time_grad_kernel(
    role, half, rank, rm, dtembs, ww, temb, hid, wt, vsum, tile, gm, g2, g1, vout, tout
):
    vout[...] = vsum[...]
    tout[...] = tile[...]
    pl.when(role[0] == 0)(
        lambda: time_grad(half, rank, rm, dtembs, ww, temb, hid, wt, gm, g2, g1, vout, tout)
    )


def time_grad(half, rank, rm, dtembs, ww, temb, hid, wt, gm, g2, g1, vout, tout):
    width, cols = rm.shape[1], vout.shape[0]
    rows, clips = rm.shape[0], temb.shape[0]
    n = dtembs.shape[0]
    pick = own_columns(rank[0], width, cols)
    kind = lax.broadcasted_iota(jnp.int32, (rows, 1), 0) % 8
    value = rm[...]
    hidden = hid[...]
    own_hid, own_temb = nn3(hidden, pick), nn3(temb[...], pick)
    gates = low(own_temb * jax.nn.sigmoid(own_temb))
    spread = low(tn(clip_groups(clips, rows), gates))
    pieces = three(value)
    count = jnp.zeros((1, 1), f32)

    def squared(block):
        return jnp.sum(jnp.sum(block * block, axis=1, keepdims=True), axis=0, keepdims=True)

    for r in range(6):
        masked = jnp.where(kind == r, spread.astype(f32), 0.0).astype(bf16)
        block = sum(tn(masked, piece) for piece in pieces)[0:cols]
        gm[:, r * width : r * width + width] = block
        count = count + squared(block)
    mine = dtembs[rank[0]]
    mine_pieces = three(mine)
    act = low(hidden * jax.nn.sigmoid(hidden))
    block = sum(tn(piece, act) for piece in mine_pieces)[0:cols]
    g2[...] = block
    count = count + squared(block)
    back = jnp.zeros((clips, 128), f32)
    zeros = jnp.zeros((128 - cols, 128), bf16)
    for o in range(n):
        weight = low(nn(ww[o * cols : o * cols + cols, 256 : 256 + width], pick))
        back = back + nn3(dtembs[o], jnp.concatenate([weight, zeros], axis=0))
    dhid = back * silu_back(own_hid)
    dhid_pieces = three(dhid)
    feature = low(wt[:, 0:256])
    block = sum(tn(piece, feature) for piece in dhid_pieces)[0:cols]
    g1[...] = block
    count = count + squared(block)
    at = lax.broadcasted_iota(jnp.int32, (clips, 128), 1)
    first = low(jnp.where(at == 1, 1.0, 0.0))
    second = low(jnp.where(at == 2, 1.0, 0.0))
    total = sum(tn(piece, first) for piece in dhid_pieces)
    total = total + sum(tn(piece, second) for piece in mine_pieces)
    row_kind = lax.broadcasted_iota(jnp.int32, (rows, 128), 0) % 8
    row_lane = lax.broadcasted_iota(jnp.int32, (rows, 128), 1)
    put = jnp.logical_and(row_lane == row_kind + 3, row_kind < 6)
    put = low(jnp.where(put, 1.0, 0.0))
    total = total + sum(tn(piece, put) for piece in three(nn3(value, pick)))

    @pl.when(half[0] == 0)
    def _():
        vout[...] += total[0:cols]
        lane = lax.broadcasted_iota(jnp.int32, (1, 128), 1)
        tout[0:1, 0:128] += jnp.where(lane == 0, count, 0.0)


class Relay:
    def __init__(self, send, recv):
        self.d, self.s = here()
        self.role, self.half = self.s // 2, lax.rem(self.s, 2)
        self.other = dev(self.d, (1 - self.role) * 2 + self.half)
        self.mate = dev(self.d, self.role * 2 + 1 - self.half)
        self.send, self.recv = send, recv

    def at(self, r, h):
        return jnp.logical_and(self.role == r, self.half == h)

    def copy(self, i, leg, src, dst):
        target = self.other if leg == 0 else self.mate
        return remote(src, dst, self.send.at[i, leg], self.recv.at[i, leg], target)

    def start(self, i, src, dst):
        self.copy(i, 0, src, dst).start()
        self.copy(i, 1, src, dst).start()

    def middle(self, i, dst):
        self.copy(i, 0, dst, dst).wait_recv()
        self.copy(i, 2, dst, dst).start()

    def finish(self, r, h, items):
        @pl.when(self.at(r, h))
        def _():
            for i, src, dst in items:
                self.copy(i, 0, src, dst).wait_send()
                self.copy(i, 1, src, dst).wait_send()

        @pl.when(self.at(1 - r, h))
        def _():
            for i, src, dst in items:
                self.copy(i, 2, dst, dst).wait_send()

        @pl.when(self.at(r, 1 - h))
        def _():
            for i, src, dst in items:
                self.copy(i, 1, dst, dst).wait_recv()

        @pl.when(self.at(1 - r, 1 - h))
        def _():
            for i, src, dst in items:
                self.copy(i, 2, dst, dst).wait_recv()


def owner_first(role, mat):
    return 2 * mat + mat % 2 if role == 0 else mat


def owner_second(mat):
    return 2 + 3 * mat


def settle_kernel(n, vsum, tile, summed, mom, gm, g2, g1,
                  oa, of, xa, xf, xm, x2, x1, gv, stat,
                  vecs, tiles, mine, totals, look,
                  send, recv, own, gsend, grecv, gown, ssend, srecv, tsend, trecv):
    relay = Relay(gsend, grecv)
    d, s, role, half = relay.d, relay.s, relay.role, relay.half
    peers = [dev(d, lax.rem(s + k, 4)) for k in range(1, 4)]
    greet_dp(n, peers)
    four, eight = pl.ds(0, 4), pl.ds(0, 8)
    shared = {
        (0, 0): [(0, summed.at[four], xa.at[four]), (4, gm, xm)],
        (0, 1): [(1, summed.at[eight], xf.at[eight]), (5, g2, x2), (6, g1, x1)],
        (1, 0): [(2, summed.at[eight], xa.at[pl.ds(4, 8)])],
        (1, 1): [(3, summed.at[eight], xf.at[pl.ds(8, 8)])],
    }
    small = [(0, vsum, vecs), (1, tile, tiles)]
    for i, src, dst in small:
        for k in range(1, 4):
            remote(src, dst.at[s], ssend.at[i, k], srecv.at[i, k], peers[k - 1]).start()
    for (r, h), items in shared.items():

        @pl.when(relay.at(r, h))
        def _():
            for i, src, dst in items:
                pltpu.make_async_copy(src, dst, gown.at[i]).start()
                relay.start(i, src, dst)

    total, squares, losses = vsum[...], tile[0:1, :], tile[1:2, :]
    for k in range(1, 4):
        o = lax.rem(s + 4 - k, 4)
        for i, src, dst in small:
            remote(src, dst.at[o], ssend.at[i, k], srecv.at[i, k], dev(d, o)).wait()
        total = total + vecs[o]
        squares = squares + tiles[o, 0:1, :]
        losses = losses + tiles[o, 1:2, :]
    lane = lax.broadcasted_iota(jnp.int32, (1, 128), 1)
    total = jnp.where(jnp.logical_or(lane == 9, lane >= 77), 0.0, total)
    gv[...] = total

    def whole(block):
        return jnp.sum(jnp.sum(block, axis=1, keepdims=True), axis=0, keepdims=True)

    row = lax.broadcasted_iota(jnp.int32, (8, 128), 0)
    mine[...] = jnp.where(row < 4, whole(squares) + whole(total * total), whole(losses[:, 0:128]))
    so_far = mine[...]

    def start(k, carry):
        remote(mine, totals.at[d], tsend.at[k], trecv.at[k], dev(lax.rem(d + k, n), s)).start()
        return carry

    lax.fori_loop(1, n, start, 0)

    def finish(k, carry):
        o = lax.rem(d + n - k, n)
        remote(mine, totals.at[o], tsend.at[k], trecv.at[k], dev(o, s)).wait()
        return carry + totals[o]

    lax.fori_loop(1, n, lambda k, c: (finish(k, so_far), c)[1], 0)
    totals[d] = so_far
    so_far = lax.fori_loop(0, n, lambda o, c: c + totals[o], jnp.zeros((8, 128), f32))
    stat[...] = so_far
    factor = jnp.minimum(1.0, max_norm / (jnp.sqrt(so_far[0:1, 0:1]) + 1e-06))
    scale = factor * (1.0 + momentum_decay)

    def update(m, carry):
        look[m] = summed[m] * scale + mom[m] * (momentum_decay * momentum_decay)
        return carry

    lax.fori_loop(0, 8, update, 0)
    groups = []
    for r in range(2):
        mats = 4 if r == 0 else 8
        groups.append((r, 0, [(m, owner_first(r, m), look.at[m], oa) for m in range(mats)]))
        groups.append((
            r, 1, [(m, owner_second(m), look.at[pl.ds(4 * m, 4)], of) for m in range(2)]
        ))
    for r, h, mats in groups:

        @pl.when(relay.at(r, h))
        def _():
            for m, o, src, dst in mats:

                @pl.when(d == o)
                def _():
                    pltpu.make_async_copy(src, dst.at[d], own.at[0]).start()

                @pl.when(d != o)
                def _():
                    remote(src, dst.at[d], send.at[m], recv.at[d], dev(o, s)).start()

    for (r, h), items in shared.items():

        @pl.when(relay.at(1 - r, h))
        def _():
            for i, src, dst in items:
                relay.middle(i, dst)

    for r, h, mats in groups:

        @pl.when(relay.at(r, h))
        def _():
            for i, src, dst in shared[(r, h)]:
                pltpu.make_async_copy(src, dst, gown.at[i]).wait()
            for m, o, src, dst in mats:

                @pl.when(d == o)
                def _():
                    pltpu.make_async_copy(src, dst.at[d], own.at[0]).wait()

                    def arrived(k, carry):
                        p = lax.rem(d + n - k, n)
                        remote(src, dst.at[p], send.at[m], recv.at[p], dev(p, s)).wait_recv()
                        return carry

                    lax.fori_loop(1, n, arrived, 0)

                @pl.when(d != o)
                def _():
                    remote(src, dst.at[d], send.at[m], recv.at[d], dev(o, s)).wait_send()

    for (r, h), items in shared.items():
        relay.finish(r, h, items)


def spread_kernel(n, xa, xf, gy1, summed, oa, of, xy1, xy2, send, recv, rsend, rrecv, own, gown):
    relay = Relay(rsend, rrecv)
    d, s, role, half = relay.d, relay.s, relay.role, relay.half
    greet_dp(n, [relay.other, relay.mate])
    groups = []
    for r in range(2):
        mats = 4 if r == 0 else 8
        groups.append((r, 0, mats, functools.partial(owner_first, r), xa, oa, 10 * r, 4))
        groups.append((r, 1, 2, owner_second, xf, of, 10 * r + 8, 2))
    text = {
        (1, 0): [(20, gy1, xy1.at[0])],
        (1, 1): [(21, gy1, xy1.at[1]), (22, summed.at[8], xy2)],
    }
    for (r, h), items in text.items():

        @pl.when(relay.at(r, h))
        def _():
            for i, src, dst in items:
                pltpu.make_async_copy(src, dst, gown.at[i - 20]).start()
                relay.start(i, src, dst)

    for r, h, mats, owner, src, dst, base, per in groups:

        @pl.when(relay.at(r, h))
        def _():
            for m in range(mats):

                @pl.when(d == owner(m))
                def _():
                    pltpu.make_async_copy(src.at[d], dst.at[per * r + m], own.at[m]).start()

                    def start(k, carry):
                        to = lax.rem(d + k, n)
                        remote(
                            src.at[to], dst.at[per * r + m], send.at[k], recv.at[m], dev(to, s)
                        ).start()
                        return carry

                    lax.fori_loop(1, n, start, 0)

            for m in range(mats):

                @pl.when(d == owner(m))
                def _():
                    pltpu.make_async_copy(src.at[d], dst.at[per * r + m], own.at[m]).wait()

                @pl.when(d != owner(m))
                def _():
                    remote(
                        src.at[d], dst.at[per * r + m], send.at[1], recv.at[m], dev(owner(m), s)
                    ).wait_recv()

                relay.start(base + m, dst.at[per * r + m], dst.at[per * r + m])

    for (r, h), items in text.items():

        @pl.when(relay.at(1 - r, h))
        def _():
            for i, src, dst in items:
                relay.middle(i, dst)

    for r, h, mats, owner, src, dst, base, per in groups:

        @pl.when(relay.at(1 - r, h))
        def _():
            for m in range(mats):
                relay.middle(base + m, dst.at[per * r + m])

    for r, h, mats, owner, src, dst, base, per in groups:

        @pl.when(relay.at(r, h))
        def _():
            for m in range(mats):

                @pl.when(d == owner(m))
                def _():
                    def finish(k, carry):
                        to = lax.rem(d + k, n)
                        remote(
                            src.at[to], dst.at[per * r + m], send.at[k], recv.at[m], dev(to, s)
                        ).wait_send()
                        return carry

                    lax.fori_loop(1, n, finish, 0)

        relay.finish(r, h, [(base + m, dst.at[per * r + m], dst.at[per * r + m]) for m in range(mats)])

    for (r, h), items in text.items():

        @pl.when(relay.at(r, h))
        def _():
            for i, src, dst in items:
                pltpu.make_async_copy(src, dst, gown.at[i - 20]).wait()

        relay.finish(r, h, items)


def adamw_update(weight, first, second, grad, count):
    first = beta_one * first + (1.0 - beta_one) * grad
    second = beta_two * second + (1.0 - beta_two) * grad * grad
    first_hat = first / (1.0 - jnp.power(beta_one, count))
    second_hat = second / (1.0 - jnp.power(beta_two, count))
    weight = weight - adam_rate * (
        first_hat / (jnp.sqrt(second_hat) + 1e-08) + weight_decay * weight
    )
    return (weight, first, second)


def body(
    latents,
    noise_draw,
    timesteps,
    captions,
    caption_len,
    attention_weights,
    feed_weights,
    side_weights,
    vector_weights,
    attention_momentum,
    feed_momentum,
    side_first,
    side_second,
    vector_first,
    vector_second,
    step_count,
):
    n = lax.axis_size("dp")
    d, s = here()
    role, half = s // 2, lax.rem(s, 2)
    count = latents.shape[0]
    frames = latents.shape[1]
    width = attention_weights.shape[1]
    cols, feed_cols = attention_weights.shape[2], feed_weights.shape[2]
    hidden = n * feed_cols
    text = captions.shape[2]
    sds = jax.ShapeDtypeStruct
    role_s, half_s = role.reshape(1).astype(jnp.int32), half.reshape(1).astype(jnp.int32)

    o_time = 16
    o_text = o_time + 256 + width
    o_text2 = o_text + text
    o_head = o_text2 + width
    o_mod = o_head + 16
    six = 6 * width
    own_rows = -(-cols // 2)
    lanes = n * own_rows

    perm_np = np.zeros((2, lanes, width), np.float32)
    for h in range(width):
        origin, col = divmod(h, cols)
        perm_np[col // own_rows, origin * own_rows + col % own_rows, h] = 1.0
    perm = jnp.asarray(perm_np, bf16)

    att_t = jnp.swapaxes(attention_weights, 1, 2)
    feed_t = jnp.swapaxes(feed_weights, 1, 2)
    side_t = side_weights.T
    side_b = low(side_t)
    pa = low(lax.dynamic_slice_in_dim(att_t, 4 * role, 4, 0))
    pb = low(att_t[8:12])
    pf = low(lax.dynamic_slice_in_dim(feed_t, 2 * role, 2, 0))
    pw = jnp.concatenate(
        [
            side_b[:, o_time:o_text],
            side_b[:, o_text2:o_head],
            low(vector_weights.T),
            side_b[:, 0:16],
            side_b[:, o_head:o_mod],
            jnp.zeros((cols, 128 - 77), bf16),
        ],
        axis=1,
    )
    text_rows = jnp.pad(side_b[:, o_text:o_text2], ((0, 2 * own_rows - cols), (0, 0)))
    py = lax.dynamic_slice_in_dim(text_rows, half * own_rows, own_rows, 0)
    pm = lax.dynamic_slice_in_dim(side_b[:, o_mod:], half * 3 * width, 3 * width, 1)
    freqs = jnp.exp(-math.log(10000.0) * jnp.arange(128, dtype=f32) / 128)
    angles = timesteps.astype(f32)[:, None] * freqs[None, :]
    level, snr = snr_weight(timesteps.astype(f32))
    pt = jnp.concatenate([jnp.cos(angles), jnp.sin(angles), snr[:, None]], axis=1)
    pt = jnp.pad(pt, ((0, 8 - count), (0, width - 257)))

    wa, wb, wf, ww, wy, wm, wt = comm_call(
        functools.partial(gather_kernel, n),
        1,
        (pa, pb, pf, pw, py, pm, pt),
        [
            sds((4, n, cols, width), bf16),
            sds((4, n, cols, width), bf16),
            sds((2, n, feed_cols, width), bf16),
            sds((n, cols, 1152), bf16),
            sds((n, own_rows, text), bf16),
            sds((n, cols, 3 * width), bf16),
            sds((n, 8, width), f32),
        ],
        [(4, 8, n), (8, n), (8, n), (8,)],
    )
    wa = wa.reshape(4, width, width)
    wb = wb.reshape(4, width, width)
    wf = wf.reshape(2, hidden, width)
    ww = ww.reshape(width, 1152)
    wy = wy.reshape(lanes, text)
    wm = wm.reshape(width, 3 * width)
    total_weight = jnp.sum(wt[:, :, 256])

    rank_s = d.reshape(1).astype(jnp.int32)
    vec, hid, temb, mq_own, y2p = local_call(
        condition_kernel,
        [
            sds((128, width), f32),
            sds((n * 8, width), f32),
            sds((n * 8, width), f32),
            sds((8, 3 * width), f32),
            sds((2, width, lanes), bf16),
        ],
        [SM] + [VM] * 4,
        (rank_s, wt.reshape(n * 8, width), ww, wm, perm),
    )
    mq = comm_call(
        mate_kernel, 2, (mq_own,), sds((2, 8, 3 * width), f32), [(1,), (1,), (1,)]
    )

    level = level[:, None, None, None, None]
    noisy = low(jnp.sqrt(level) * latents + jnp.sqrt(1.0 - level) * noise_draw).astype(f32)
    patches = patchify(jnp.where(role == 0, noisy, noise_draw))
    per_clip = frames * patches.shape[2]
    half_tokens = count * per_clip // 2
    regrouped = patches.reshape(count, frames, 2, 32, 16).transpose(0, 2, 1, 3, 4)
    regrouped = regrouped.reshape(count * per_clip, 16)
    rows = jnp.where(role == 0, patches.reshape(count * per_clip, 16), regrouped)
    rows = lax.dynamic_slice_in_dim(rows, half * half_tokens, half_tokens, 0)
    tok = low(jnp.pad(rows, ((0, 0), (EMB0, 112 - EMB0))))
    target = jnp.pad(rows, ((0, 0), (HEAD0, 112 - HEAD0)))
    places = np.arange(patches.shape[2])
    edge = latents.shape[3] // 2
    pos = np.concatenate(
        [sincos(places // edge, width // 2), sincos(places % edge, width // 2)], axis=1
    )
    pos = jnp.asarray(np.tile(pos, (2, 1)))
    timing = jnp.asarray(np.repeat(sincos(np.arange(frames), width), 32, axis=0))

    clip_rows = captions.shape[1]
    h1s, hq, gq_own = local_call(
        first_kernel,
        [
            sds((count, 2, 64, width), bf16),
            sds((count, LP, lanes), f32),
            sds((count, LP, lanes), bf16),
        ],
        [SM] * 2 + [VM] * 8 + [ANY],
        (role_s, half_s, tok, pos, mq, vec, wa, wf, wy, perm, captions),
        [pltpu.VMEM((count, clip_rows, text), bf16), pltpu.SemaphoreType.DMA((count,))],
    )
    h1t, rgq, mqt = comm_call(
        functools.partial(forward_kernel, count),
        3,
        (h1s, gq_own, mq),
        [
            sds((count, 2, 64, width), bf16),
            sds((count, LP, lanes), bf16),
            sds((2, 8, 3 * width), f32),
        ],
        [(count, 2), (count, 2), (1,), (1,), (2,), (2,)],
    )

    ncl = (count + 1) // 2
    errw = snr / (total_weight * (per_clip * 16.0))
    wide = sds((2, half_tokens, hidden), bf16)
    thin = sds((2, half_tokens, width), bf16)
    cap_like = sds((ncl, LP, width), bf16)
    dh1, acts_t, actf_t, actw_t, ybuf, dkv, grads_t, dmod_t, loss_t = local_call(
        temporal_kernel,
        [
            sds((count, 2, 64, width), bf16),
            sds((10, half_tokens, width), bf16),
            thin,
            wide,
            cap_like,
            sds((2, ncl, LP, width), f32),
            sds((128, width), f32),
            sds((count, 8, width), f32),
            sds((1, 128), f32),
        ],
        [SM] * 5 + [VM] * 12,
        (
            role_s, half_s, rank_s, caption_len, errw, h1t, timing, mqt, vec, temb, wa, wb, wf,
            gq_own, rgq, y2p, target,
        ),
        [pltpu.VMEM((ncl, KP, width), bf16), pltpu.VMEM((ncl, KP, width), bf16)],
    )
    dhs, extra, dmods_t = comm_call(
        functools.partial(backward_kernel, count),
        4,
        (dh1, dkv, dmod_t),
        [
            sds((count, 2, 64, width), bf16),
            sds((2, LP, width), f32),
            sds((2, count, 8, width), f32),
        ],
        [(count, 2), (count, 2), (1,), (1,), (2,), (2,)],
    )
    acts_s, actf_s, actw_s, dkvb, dy, vect, dmod = local_call(
        last_kernel,
        [
            sds((6, half_tokens, width), bf16),
            thin,
            wide,
            sds((2, ncl, LP, width), bf16),
            cap_like,
            sds((width, 128), f32),
            sds((count, 8, width), f32),
        ],
        [SM] * 2 + [VM] * 12,
        (role_s, half_s, tok, pos, mq, vec, wa, wb, wf, dhs, dkv, extra, grads_t, dmod_t),
        [pltpu.VMEM((128, width), f32)],
    )
    racts, ractf, ractw, rybuf, rdkvb, rdy, rdmod = comm_call(
        swap_kernel,
        5,
        (acts_s, acts_t, actf_s, actf_t, actw_s, actw_t, ybuf, dkvb, dy, dmod),
        [
            sds((10, half_tokens, width), bf16),
            thin,
            wide,
            cap_like,
            sds((2, ncl, LP, width), bf16),
            cap_like,
            sds((count, 8, width), f32),
        ],
        [(5,), (5,)],
    )
    line = n // 2
    wide_text = text + 128
    cut_text = wide_text // TEXT_CUTS
    block = (9, line, cols, width)
    text_block = (TEXT_CUTS, line, own_rows, cut_text)
    tokens2 = 2 * half_tokens
    grad_own, grad_snd, text_own, text_snd = local_call(
        weight_grad_kernel,
        [
            sds(block, f32),
            sds(block, bf16),
            sds((line, own_rows, wide_text), bf16),
            sds((line, own_rows, wide_text), bf16),
        ],
        [SM] * 3 + [ANY] * 9 + [VM] * 11 + [ANY],
        (
            role_s, half_s, rank_s, acts_s, acts_t, racts, actf_s, actf_t, ractf, actw_s, actw_t,
            ractw, ybuf, rybuf, dkvb, rdkvb, dy, rdy, gq_own, rgq, hq, y2p, perm, captions,
        ),
        [
            pltpu.VMEM((10, tokens2, width), bf16),
            pltpu.VMEM((2, tokens2, width), bf16),
            pltpu.VMEM((2, tokens2, hidden), bf16),
            pltpu.VMEM((count, clip_rows, text), bf16),
            pltpu.SemaphoreType.DMA((4 + count,)),
        ],
    )

    mine0 = jnp.where(half == 0, dmod, rdmod)
    mine1 = jnp.where(half == 0, rdmod, dmod)
    sources = (mine0, mine1, dmods_t[0], dmods_t[1])
    dm_clip = []
    for clip in range(count):
        total = 0.0
        for seg in range(4):
            for i in range(count):
                if ((seg % 2) * count + i) // 2 == clip:
                    total = total + sources[seg][i]
        dm_clip.append(total)
    dm = jnp.concatenate(dm_clip, axis=0)

    summed, text_sum, rm, vsum, squares = comm_call(
        functools.partial(scatter_kernel, n),
        6,
        (grad_own, grad_snd, text_own, text_snd, dm, vect.reshape(n, cols, 128), loss_t),
        [
            sds((9, cols, width), f32),
            sds((own_rows, wide_text), bf16),
            sds((n, 8 * count, width), f32),
            sds((cols, 128), f32),
            sds((8, width), f32),
        ],
        [(12,), (12,), (12,)]
        + [(TEXT_CUTS + 1, line)] * 2
        + [(8, line)] * 4
        + [(2, n), (2, n), (2,)],
        [VM, VM, ANY, VM, VM],
        in_specs=[ANY] * 6 + [VM],
        scratch=[
            pltpu.VMEM(block, f32),
            pltpu.VMEM(block, bf16),
            pltpu.VMEM((8,) + block[1:], f32),
            pltpu.VMEM((8,) + block[1:], f32),
            pltpu.VMEM(block[1:], bf16),
            pltpu.VMEM(block[1:], bf16),
        ]
        + [pltpu.VMEM(text_block, bf16)] * 4
        + [pltpu.VMEM((n, cols, 128), f32)],
    )

    rm = rm.reshape(n * 8 * count, width)
    dtemb = local_call(
        time_back_kernel,
        sds((n * 8, 128), f32),
        [SM] * 2 + [VM] * 3,
        (role_s, rank_s, rm, side_b[:, o_mod:], temb),
    )
    dtembs = comm_call(
        functools.partial(dp_gather_kernel, n),
        7,
        (dtemb,),
        sds((n, n * 8, 128), f32),
        [(n,), (n,), (1,)],
    )
    grad_mod, grad_time2, grad_time1, vsum, tile = local_call(
        time_grad_kernel,
        [
            sds((cols, six), f32),
            sds((cols, width), f32),
            sds((cols, 256), f32),
            sds((cols, 128), f32),
            sds((8, width), f32),
        ],
        [SM] * 3 + [VM] * 8,
        (
            role_s, half_s, rank_s, rm, dtembs, ww, temb, hid, wt.reshape(n * 8, width), vsum,
            squares,
        ),
    )

    att_m = jnp.swapaxes(attention_momentum, 1, 2)
    feed_m = jnp.swapaxes(feed_momentum, 1, 2)
    role_a = jnp.where(role == 0, jnp.pad(att_m[0:4], ((0, 4), (0, 0), (0, 0))), att_m[4:12])
    role_f = lax.dynamic_slice_in_dim(feed_m, 2 * role, 2, 0).reshape(8, cols, width)
    own_m = jnp.where(half == 0, role_a, role_f)
    ua, uf, ga2, gf2, grad_mod, grad_time2, grad_time1, grad_v, stat = comm_call(
        functools.partial(settle_kernel, n),
        8,
        (vsum, tile, summed, own_m, grad_mod, grad_time2, grad_time1),
        [
            sds((n, cols, width), f32),
            sds((n, 4, cols, width), f32),
            sds((12, cols, width), f32),
            sds((16, cols, width), f32),
            sds((cols, six), f32),
            sds((cols, width), f32),
            sds((cols, 256), f32),
            sds((cols, 128), f32),
            sds((8, 128), f32),
        ],
        [(8,), (n,), (1,), (7, 3), (7, 3), (7,), (2, 4), (2, 4), (n,), (n,)],
        [ANY] * 7 + [VM] * 2,
        in_specs=[VM] * 4 + [ANY] * 3,
        scratch=[
            pltpu.VMEM((4, cols, 128), f32),
            pltpu.VMEM((4, 8, width), f32),
            pltpu.VMEM((8, 128), f32),
            pltpu.VMEM((n, 8, 128), f32),
            pltpu.VMEM((8, cols, width), f32),
        ],
    )
    grad_norm = jnp.sqrt(stat[0, 0])
    loss_value = stat[4, 0]
    factor = jnp.minimum(1.0, max_norm / (grad_norm + 1e-06))
    fast = momentum_decay
    xa, xf = local_call(
        muon_kernel,
        [sds((width, width), bf16), sds((hidden, width), bf16)],
        [SM] + [VM] * 2,
        (half_s, ua.reshape(width, width), uf.reshape(hidden, width)),
        [pltpu.VMEM((width, width), f32), pltpu.VMEM((width, width), f32)],
    )
    xa_all, xf_all, gy12, gy22 = comm_call(
        functools.partial(spread_kernel, n),
        10,
        (xa.reshape(n, cols, width), xf.reshape(n, feed_cols, width), text_sum, summed),
        [
            sds((12, cols, width), bf16),
            sds((4, feed_cols, width), bf16),
            sds((2, own_rows, wide_text), bf16),
            sds((cols, width), f32),
        ],
        [(n,), (8,), (23, 3), (23, 3), (8,), (3,)],
    )

    grad_att = ga2 * factor
    grad_feed = gf2.reshape(4, feed_cols, width) * factor
    full_att = xa_all.astype(f32)
    full_feed = xf_all.astype(f32)
    att_moment = fast * att_m + grad_att
    feed_moment = fast * feed_m + grad_feed
    shrink = 1.0 - muon_rate * weight_decay
    att_new = att_t * shrink - (muon_rate * 0.2 * math.sqrt(n * cols)) * full_att
    feed_new = feed_t * shrink - (muon_rate * 0.2 * math.sqrt(hidden)) * full_feed

    text_grad = gy12.astype(f32).reshape(2 * own_rows, wide_text)[:cols]
    grad_v = jnp.concatenate(
        [grad_v[:, 0:9], text_grad[:, text : text + 1], grad_v[:, 10:77]], axis=1
    )
    side_grad = jnp.concatenate(
        [
            grad_v[:, 45:61],
            grad_time1,
            grad_time2,
            text_grad[:, :text],
            gy22,
            grad_v[:, 61:77],
            grad_mod,
        ],
        axis=1,
    )
    clock = step_count[0].astype(f32)
    side_new, side_first_new, side_second_new = adamw_update(
        side_t, side_first.T, side_second.T, side_grad * factor, clock
    )
    vector_new, vector_first_new, vector_second_new = adamw_update(
        vector_weights, vector_first, vector_second, grad_v[:, 0:45].T * factor, clock
    )

    def back(value):
        return jnp.swapaxes(value, -1, -2)

    return (
        loss_value,
        grad_norm,
        back(att_new),
        back(att_moment),
        back(feed_new),
        back(feed_moment),
        back(side_new),
        back(side_first_new),
        back(side_second_new),
        vector_new,
        vector_first_new,
        vector_second_new,
        back(low(att_new)),
        back(low(feed_new)),
        back(low(side_new)),
        low(vector_new),
    )


def solution(mesh):
    column = P(None, "dp")
    matrix = P(None, None, "dp")
    return jax.shard_map(
        body,
        mesh=mesh,
        in_specs=(
            P("dp", None, None, None, None),
            P("dp", None, None, None, None),
            P("dp"),
            P("dp", None, None),
            P("dp"),
            matrix,
            matrix,
            column,
            column,
            matrix,
            matrix,
            column,
            column,
            column,
            column,
            P(),
        ),
        out_specs=(
            P(),
            P(),
            matrix,
            matrix,
            matrix,
            matrix,
            column,
            column,
            column,
            column,
            column,
            column,
            matrix,
            matrix,
            column,
            column,
        ),
        check_vma=False,
    )
```

```python
import functools
import math

import jax
import jax.numpy as jnp
import numpy as np
from jax import lax
from jax.experimental import pallas as pl
from jax.experimental.pallas import tpu as pltpu
from jax.sharding import PartitionSpec as P

HEADS = 6
HEAD = 64
LP = 304
KP = 384

highest = lax.Precision.HIGHEST
snr_gamma = 5.0
max_norm = 0.005
momentum_decay = 0.95
muon_rate = 0.05
adam_rate = 0.02
beta_one = 0.9
beta_two = 0.999
weight_decay = 0.01
coef_a = 3.4445
coef_b = -4.775
coef_c = 2.0315

f32, bf16 = jnp.float32, jnp.bfloat16
MESH = pl.DeviceIdType.MESH
ANY = pl.BlockSpec(memory_space=pl.ANY)
VM = pl.BlockSpec(memory_space=pltpu.VMEM)
SM = pl.BlockSpec(memory_space=pltpu.SMEM)
VMEM_LIMIT = 60000 * 1024


def low(value):
    return value.astype(bf16)


def nt(left, right):
    return lax.dot_general(left, right, (((1,), (1,)), ((), ())), preferred_element_type=f32)


def nn(left, right):
    return lax.dot_general(left, right, (((1,), (0,)), ((), ())), preferred_element_type=f32)


def tn(left, right):
    return lax.dot_general(left, right, (((0,), (0,)), ((), ())), preferred_element_type=f32)


def snr_weight(steps_t):
    level = jnp.cos((steps_t / 1000.0 + 0.008) / 1.008 * (math.pi / 2)) ** 2
    ratio = level / (1.0 - level)
    return level, jnp.minimum(ratio, snr_gamma) / ratio


def patchify(frames):
    clips, count, channels, height, breadth = frames.shape
    grid = frames.reshape(clips, count, channels, height // 2, 2, breadth // 2, 2)
    grid = grid.transpose(0, 1, 3, 5, 4, 6, 2)
    return grid.reshape(clips, count, (height // 2) * (breadth // 2), 4 * channels)


def sincos(places, model_width):
    half_width = model_width // 2
    freqs = np.exp(-math.log(10000.0) * np.arange(half_width) / half_width)
    angles = places[:, None] * freqs[None, :]
    return np.concatenate([np.sin(angles), np.cos(angles)], axis=1).astype(np.float32)


def col_sum(value):
    return jnp.sum(value.astype(f32), axis=0, keepdims=True)


def norm(value):
    centred = value - jnp.mean(value, axis=-1, keepdims=True)
    inv = lax.rsqrt(jnp.mean(centred * centred, axis=-1, keepdims=True) + 1e-06)
    return centred * inv, inv


def norm_back(grad, normed, inv):
    return inv * (
        grad
        - jnp.mean(grad, axis=-1, keepdims=True)
        - normed * jnp.mean(grad * normed, axis=-1, keepdims=True)
    )


GELU_C = math.sqrt(2.0 / math.pi)


def gelu(value):
    inner = GELU_C * (value + 0.044715 * (value * value * value))
    return value * (0.5 * (1.0 + jnp.tanh(inner)))


def gelu_both(value):
    square = value * value
    tanh = jnp.tanh(GELU_C * (value + 0.044715 * (square * value)))
    cdf = 0.5 * (1.0 + tanh)
    slope = 0.5 * (1.0 - tanh * tanh) * (GELU_C * (1.0 + 3 * 0.044715 * square))
    return value * cdf, cdf + value * slope


def lanes_low():
    lane = lax.broadcasted_iota(jnp.int32, (1, 128), 1)
    first = jnp.where(lane < HEAD, 1.0, 0.0)
    return low(first), low(1.0 - first), lane < HEAD


def stack_heads(pair, first, second):
    return jnp.concatenate([pair * first, pair * second], axis=0)


def attend(queries, keys, values, allowed):
    first, second, lower = lanes_low()
    rows = queries.shape[0]
    mixed, probs = [], []
    for pair in range(HEADS // 2):
        cut = slice(pair * 128, pair * 128 + 128)
        scores = nt(stack_heads(queries[:, cut], first, second), keys[:, cut]) * 0.125
        scores = jnp.where(allowed, scores, -1e30)
        weight = jnp.exp(scores - jnp.max(scores, axis=-1, keepdims=True))
        prob = weight / jnp.sum(weight, axis=-1, keepdims=True)
        probs.append(prob)
        out = nn(low(prob), values[:, cut])
        mixed.append(jnp.where(lower, out[:rows], out[rows:]))
    return low(jnp.concatenate(mixed, axis=1)), probs


def attend_back(grad, queries, keys, values, probs):
    first, second, lower = lanes_low()
    rows = queries.shape[0]
    dq, dk, dv = [], [], []
    for pair in range(HEADS // 2):
        cut = slice(pair * 128, pair * 128 + 128)
        stacked = stack_heads(grad[:, cut], first, second)
        prob = probs[pair]
        dv.append(tn(low(prob), stacked))
        dprob = nt(stacked, values[:, cut])
        dscore = low(prob * (dprob - jnp.sum(prob * dprob, axis=-1, keepdims=True)))
        part = nn(dscore, keys[:, cut])
        dq.append(jnp.where(lower, part[:rows], part[rows:]) * 0.125)
        dk.append(tn(dscore, stack_heads(queries[:, cut], first, second)) * 0.125)
    return tuple(jnp.concatenate(piece, axis=1) for piece in (dq, dk, dv))


def self_forward(x, mods, weights, bias, allowed):
    normed, inv = norm(x)
    a = low(normed * (1.0 + mods[1]) + mods[0])
    q = low(nt(a, weights[0]) + bias[0])
    k = low(nt(a, weights[1]))
    v = low(nt(a, weights[2]) + bias[1])
    o, probs = attend(q, k, v, allowed)
    branch = nt(o, weights[3]) + bias[2]
    return x + mods[2] * branch, (normed, inv, a, q, k, v, o, probs, branch)


def self_backward(dx, kept, mods, weights):
    normed, inv, a, q, k, v, o, probs, branch = kept
    dm2 = col_sum(dx * branch)
    dbr = low(dx * mods[2])
    do = low(nn(dbr, weights[3]))
    dq, dk, dv = (low(piece) for piece in attend_back(do, q, k, v, probs))
    da = nn(dq, weights[0]) + nn(dk, weights[1]) + nn(dv, weights[2])
    dm1, dm0 = col_sum(da * normed), col_sum(da)
    dx = dx + norm_back(da * (1.0 + mods[1]), normed, inv)
    return dx, (dm0, dm1, dm2), (col_sum(dq), col_sum(dv), col_sum(dbr)), (a, dq, dk, dv, o, dbr)


def feed_forward(x, mods, feed, bias_up, bias_down):
    normed, inv = norm(x)
    c = low(normed * (1.0 + mods[4]) + mods[3])
    u = nt(c, feed[0]) + bias_up
    g = low(gelu(u))
    branch = nn(g, feed[1]) + bias_down
    return x + mods[5] * branch, (normed, inv, c, u, g, branch)


def feed_backward(dx, kept, mods, feed):
    normed, inv, c, u, g, branch = kept
    dm5 = col_sum(dx * branch)
    dbr = low(dx * mods[5])
    value, slope = gelu_both(u)
    g = low(value)
    du = low(nt(dbr, feed[1]) * slope)
    dc = nn(du, feed[0])
    dm4, dm3 = col_sum(dc * normed), col_sum(dc)
    dx = dx + norm_back(dc * (1.0 + mods[4]), normed, inv)
    return dx, (dm3, dm4, dm5), (col_sum(du), col_sum(dbr)), (c, dbr, du, g)


def pair_mask(kind):
    row = lax.broadcasted_iota(jnp.int32, (256, 128), 0) % 128
    col = lax.broadcasted_iota(jnp.int32, (256, 128), 1)
    if kind == 0:
        return row // 64 == col // 64
    return row % 32 == col % 32


VEC0, EMB0, HEAD0 = 0, 45, 61


def mod_rows(mq, vec, table, clip):
    rows = []
    for r in range(6):
        at = (r % 3) * 384
        rows.append(
            mq[r // 3, pl.ds(clip, 1), at : at + 384]
            + vec[3 + r : 4 + r]
            + vec[table + r : table + r + 1]
        )
    return rows


def up_bias(vec, start):
    return jnp.concatenate([vec[start + i : start + i + 1] for i in range(4)], axis=1)


def units_of(hand, lanes, width, cols):
    per = -(-cols // 2)
    unit = lax.broadcasted_iota(jnp.int32, (lanes, width), 0)
    column = lax.broadcasted_iota(jnp.int32, (lanes, width), 1)
    inside = hand * per + unit % per
    match = jnp.logical_and((unit // per) * cols + inside == column, inside < cols)
    return low(jnp.where(match, 1.0, 0.0))


def condition_kernel(rank, wt, ww, wm, vec, hid, temb, mq, y2p, errs, *, per_clip, cols):
    turned = jnp.transpose(ww[:, 1024:1152].astype(f32))
    vec[...] = turned
    feature = low(wt[:, 0:256])
    first = nt(feature, ww[:, 0:256]) + turned[1:2]
    hid[...] = first
    second = nt(low(first * jax.nn.sigmoid(first)), ww[:, 256:640]) + turned[2:3]
    temb[...] = second
    own = temb[pl.ds(pl.multiple_of(rank[0] * 8, 8), 8), :]
    mq[...] = nn(low(own * jax.nn.sigmoid(own)), wm[...])
    for h in range(2):
        y2p[h] = low(nt(ww[:, 640:1024], units_of(h, y2p.shape[2], y2p.shape[1], cols)))
    total = jnp.sum(wt[:, 256:257], axis=0, keepdims=True)
    weight = wt[pl.ds(pl.multiple_of(rank[0] * 8, 8), 8), 256:257] / (total * (per_clip * 16.0))
    errs[...] = jnp.broadcast_to(weight, errs.shape)


def embed_chunk(tok_ref, vec, pos_ref, chunk):
    tokens = tok_ref[pl.ds(pl.multiple_of(chunk * 128, 128), 128), :]
    places = pos_ref[...] + vec[0:1]
    return low(nn(tokens, low(vec[...])) + jnp.concatenate([places, places], axis=0)), tokens


def spatial_bias(vec):
    return (vec[11:12], vec[12:13], vec[13:14])


def residual_copies(sources, targets, sems):
    def of(chunk):
        rows = pl.ds(pl.multiple_of(chunk * 128, 128), 128)
        cuts = [lambda r: r.at[:, rows], lambda r: r.at[:, rows], lambda r: r.at[rows],
                lambda r: r.at[chunk]]
        return [
            pltpu.make_async_copy(cut(src), cut(dst), sems.at[chunk, i])
            for i, (cut, src, dst) in enumerate(zip(cuts, sources, targets))
        ]

    return of


def first_kernel(
    cols, role, half, tok, pos, mq, vec, wa, wf, wy, captions,
    h1, hq, gq, out_b, out_f, out_u, out_p, kept_b, kept_f, kept_u, kept_p, cap, sems, ksem,
):
    @pl.when(role[0] == 1)
    def _():
        clips = captions.shape[0]
        for c in range(clips):
            pltpu.make_async_copy(captions.at[c], cap.at[c], sems.at[c]).start()
        bias = nt(low(vec[9:10]), units_of(half[0], wy.shape[0], vec.shape[1], cols))
        for c in range(clips):
            pltpu.make_async_copy(captions.at[c], cap.at[c], sems.at[c]).wait()
            value = nt(cap[c], wy[...]) + bias
            rows = value.shape[0]
            pad = jnp.zeros((LP - rows, value.shape[1]), f32)
            hq[c] = jnp.concatenate([value, pad], axis=0)
            gq[c] = low(jnp.concatenate([gelu(value), pad], axis=0))

    @pl.when(role[0] == 0)
    def _():
        allowed = pair_mask(0)
        count = h1.shape[0]
        bu = up_bias(vec, 14)
        residuals = residual_copies((kept_b, kept_f, kept_u, kept_p), (out_b, out_f, out_u, out_p), ksem)

        def step(chunk, carry):
            @pl.when(chunk > 0)
            def _():
                for copy in residuals(chunk - 1):
                    copy.start()

            m = mod_rows(mq, vec, 19, (half[0] * count + chunk) // 2)
            h0, _ = embed_chunk(tok, vec, pos, chunk)
            x1, kept = self_forward(h0.astype(f32), m, wa, spatial_bias(vec), allowed)
            x, kept_feed = feed_forward(x1, m, wf, bu, vec[18:19])
            out = low(x)
            where = pl.ds(pl.multiple_of(chunk * 128, 128), 128)
            for i, value in enumerate((h0,) + kept[3:7]):
                kept_b[i, where, :] = value
            for i, value in enumerate((x1, kept[8], kept_feed[5])):
                kept_f[i, where, :] = value
            kept_u[where, :] = kept_feed[3]
            for pair in range(3):
                kept_p[chunk, pair] = kept[7][pair]
            for frame in range(2):
                for part in range(2):
                    start = frame * 64 + part * 32
                    h1[chunk, part, frame * 32 : frame * 32 + 32, :] = out[start : start + 32]
            return carry

        lax.fori_loop(0, count, step, 0)
        for copy in residuals(count - 1):
            copy.start()
        for chunk in range(count):
            for copy in residuals(chunk):
                copy.wait()


def last_kernel(
    role, half, tok, mq, vec, wa, wb, wf, in_b, in_f, in_u, in_p, dh, dkv, extra, grads_t, dmod_t,
    acts, actf, actw, dkvb, dy, vect, dmod, grads, kept_b, kept_f, kept_u, kept_p, ksem,
):
    @pl.when(role[0] == 0)
    def _():
        grads[...] = jnp.zeros_like(grads)
        dmod[...] = jnp.zeros_like(dmod)
        count = dh.shape[0]
        residuals = residual_copies((in_b, in_f, in_u, in_p), (kept_b, kept_f, kept_u, kept_p), ksem)
        for chunk in range(count):
            for copy in residuals(chunk):
                copy.start()

        def step(chunk, carry):
            for copy in residuals(chunk):
                copy.wait()
            m = mod_rows(mq, vec, 19, (half[0] * count + chunk) // 2)
            where = pl.ds(pl.multiple_of(chunk * 128, 128), 128)
            tokens = tok[where, :]
            h0, q, k, v, o = (kept_b[i, where, :] for i in range(5))
            x1, branch, branch_f = (kept_f[i, where, :] for i in range(3))
            normed, inv = norm(h0.astype(f32))
            a = low(normed * (1.0 + m[1]) + m[0])
            probs = [kept_p[chunk, pair] for pair in range(3)]
            kept = (normed, inv, a, q, k, v, o, probs, branch)
            normed_f, inv_f = norm(x1)
            c = low(normed_f * (1.0 + m[4]) + m[3])
            kept_feed = (normed_f, inv_f, c, kept_u[where, :], None, branch_f)
            parts = []
            for frame in range(2):
                for part in range(2):
                    parts.append(dh[chunk, part, frame * 32 : frame * 32 + 32, :])
            dx = jnp.concatenate(parts, axis=0).astype(f32)
            dx, dm_f, db_f, act_f = feed_backward(dx, kept_feed, m, wf)
            dx, dm_a, db_a, act_a = self_backward(dx, kept, m, wa)
            dh0 = low(dx)
            for i, value in enumerate(act_a):
                acts[i, where, :] = value
            for i in range(2):
                actf[i, where, :] = act_f[i]
                actw[i, where, :] = act_f[2 + i]
            mods = dm_a + dm_f
            dmod[chunk, 0:6, :] = jnp.concatenate(mods, axis=0)
            grads[...] += tn(tokens, dh0)
            grads[0:1] += col_sum(dh0)
            for i in range(3):
                grads[11 + i : 12 + i] += db_a[i]
            for i in range(4):
                grads[14 + i : 15 + i] += db_f[0][:, i * 384 : i * 384 + 384]
            grads[18:19] += db_f[1]
            for i in range(6):
                grads[19 + i : 20 + i] += mods[i]
            return carry

        lax.fori_loop(0, count, step, 0)

    @pl.when(role[0] == 1)
    def _():
        grads[...] = grads_t[...]
        dmod[...] = dmod_t[...]
        dy[...] = jnp.zeros_like(dy)
        dkvb[...] = jnp.zeros_like(dkvb)
        ncl = dy.shape[0]
        for c in range(ncl):

            @pl.when(jnp.logical_or(half[0] == 0, c > 0))
            def _():
                pieces = []
                for i in range(2):
                    value = dkv[i, c]
                    if c == ncl - 1:
                        value = value + jnp.where(half[0] == 0, extra[i], 0.0)
                    pieces.append(low(value))
                dkvb[0, c], dkvb[1, c] = pieces
                back = low(nn(pieces[0], wb[1]) + nn(pieces[1], wb[2]))
                dy[c] = back
                grads[40:41] += col_sum(pieces[1])
                grads[10:11] += col_sum(back)

    vect[...] = jnp.transpose(grads[...])


def temporal_kernel(
    role, half, rank, lens, errw, h1, timing, mq, vec, temb, wa, wb, wf, gq, rgq, y2p, target,
    dh1, acts, actf, actw, ybuf, dkv, grads, dmod, loss, kx, vx,
):
    @pl.when(role[0] == 0)
    def _():
        loss[...] = jnp.zeros_like(loss)

    @pl.when(role[0] == 1)
    def _():
        allowed = pair_mask(1)
        count = h1.shape[0]
        ncl = ybuf.shape[0]
        for ref in (kx, vx, dkv, grads, loss):
            ref[...] = jnp.zeros_like(ref)
        first_clip = (half[0] * count) // 2
        for c in range(ncl):
            clip = jnp.minimum(first_clip + c, gq.shape[0] - 1)
            y = nt(gq[clip], y2p[half[0]]) + nt(rgq[clip], y2p[1 - half[0]])
            y = low(y + vec[10:11])
            ybuf[c] = y
            kx[c, 0:LP, :] = low(nt(y, wb[1]))
            vx[c, 0:LP, :] = low(nt(y, wb[2]) + vec[40:41])
        bu = up_bias(vec, 28)
        lane = lax.broadcasted_iota(jnp.int32, (1, 128), 1)
        real = jnp.logical_and(lane >= HEAD0, lane < HEAD0 + 16)
        bias_h = pltpu.roll(jnp.broadcast_to(vec[44:45, 0:128], (8, 128)), HEAD0, 1)[0:1]
        head = low(vec[...])

        def step(chunk, carry):
            clip = (half[0] * count + chunk) // 2
            here = clip - first_clip
            m = mod_rows(mq, vec, 33, clip)
            emb = temb[pl.ds(rank[0] * 8 + clip, 1), :]
            m6, m7 = vec[42:43] + emb, vec[43:44] + emb
            h = jnp.concatenate([h1[chunk, 0], h1[chunk, 1]], axis=0)
            x = h.astype(f32) + jnp.concatenate(
                [jnp.broadcast_to(timing[i : i + 1], (32, h.shape[1])) for i in range(4)], axis=0
            )
            x, kept = self_forward(x, m, wa, (vec[25:26], vec[26:27], vec[27:28]), allowed)
            xb = low(x)
            cq = low(nt(xb, wb[0]) + vec[39:40])
            keys, values = kx[here], vx[here]
            seen = lax.broadcasted_iota(jnp.int32, (1, KP), 1) < lens[clip]
            co, probs = attend(cq, keys, values, seen)
            x = x + (nt(co, wb[3]) + vec[41:42])
            x, kept_f = feed_forward(x, m, wf, bu, vec[32:33])
            h2 = low(x).astype(f32)
            normed, inv = norm(h2)
            cf = low(normed * (1.0 + m7) + m6)
            where = pl.ds(pl.multiple_of(chunk * 128, 128), 128)
            diff = jnp.where(real, nt(cf, head) + bias_h - target[where, :], 0.0)
            scale = errw[pl.ds(clip, 1), 0:1]
            loss[...] += col_sum(diff * diff) * scale
            dpred = low(diff * (2.0 * scale))
            dcf = nn(dpred, head)
            grads[...] += tn(dpred, cf)
            dbh = pltpu.roll(jnp.broadcast_to(col_sum(dpred), (8, 128)), 128 - HEAD0, 1)[0:1]
            grads[44:45, 0:128] += dbh
            dm7, dm6 = col_sum(dcf * normed), col_sum(dcf)
            dx = low(norm_back(dcf * (1.0 + m7), normed, inv)).astype(f32)
            dx, dm_f, db_f, act_f = feed_backward(dx, kept_f, m, wf)
            dcbr = low(dx)
            dco = low(nn(dcbr, wb[3]))
            dcq, dck, dcv = attend_back(dco, cq, keys, values, probs)
            dcq = low(dcq)
            dkv[0, here] += dck[0:LP]
            dkv[1, here] += dcv[0:LP]
            dx = dx + nn(dcq, wb[0])
            dx, dm_a, db_a, act_a = self_backward(dx, kept, m, wa)
            out = low(dx)
            dh1[chunk, 0] = out[0:64]
            dh1[chunk, 1] = out[64:128]
            for i, value in enumerate(act_a + (xb, dcq, co, dcbr)):
                acts[i, where, :] = value
            for i in range(2):
                actf[i, where, :] = act_f[i]
                actw[i, where, :] = act_f[2 + i]
            mods = dm_a + dm_f + (dm6, dm7)
            dmod[chunk] = jnp.concatenate(mods, axis=0)
            for i in range(3):
                grads[25 + i : 26 + i] += db_a[i]
            for i in range(4):
                grads[28 + i : 29 + i] += db_f[0][:, i * 384 : i * 384 + 384]
            grads[32:33] += db_f[1]
            for i in range(6):
                grads[33 + i : 34 + i] += mods[i]
            grads[39:40] += col_sum(dcq)
            grads[41:42] += col_sum(dcbr)
            grads[42:43] += dm6
            grads[43:44] += dm7
            return carry

        lax.fori_loop(0, count, step, 0)


def weight_grad_kernel(
    role, half, rank, acts_s, acts_t, racts, actf_s, actf_t, ractf, actw_s, actw_t, ractw,
    ybuf, rybuf, dkvb, rdkvb, dy, rdy, gq, rgq, hq, y2p, captions,
    own, snd, text_out, la, lf, lw, cap, sems,
):
    tokens = acts_s.shape[1]
    line, cols = own.shape[1], own.shape[2]
    odd = lax.rem(rank[0], 2) == 1
    near, far = pl.ds(0, tokens), pl.ds(tokens, tokens)

    def copies(r, h):
        if h == 0:
            local = acts_s if r == 0 else acts_t
            size = pl.ds(0, local.shape[0])
            return [(local, la.at[size, near], 0), (racts.at[size], la.at[size, far], 1)]
        thin, wide = ((actf_s, actw_s), (actf_t, actw_t))[r]
        return [
            (thin, lf.at[:, near], 0), (ractf, lf.at[:, far], 1),
            (wide, lw.at[:, near], 2), (ractw, lw.at[:, far], 3),
        ]

    def text():
        return [(captions.at[c], cap.at[c], 4 + c) for c in range(captions.shape[0])]

    def run(group, finish):
        for src, dst, i in group:
            copy = pltpu.make_async_copy(src, dst, sems.at[i])
            copy.wait() if finish else copy.start()

    for r in range(2):
        for h in range(2):

            @pl.when(jnp.logical_and(role[0] == r, half[0] == h))
            def _():
                run(copies(r, h), False)
                if r == 1:
                    run(text(), False)
                run(copies(r, h), True)

    def keep(unit, at, first, second):
        own[unit, at] = jnp.where(odd, second, first)
        snd[unit, at] = low(jnp.where(odd, first, second))

    def keep_square(unit, value):
        for p in range(line):
            cut = 2 * p * cols
            keep(unit, p, value[cut : cut + cols], value[cut + cols : cut + 2 * cols])

    def matrix(unit, left, right):
        keep_square(unit, tn(la[left], la[right]))

    @pl.when(half[0] == 0)
    def _():
        def inputs(i, carry):
            matrix(i, 1 + i, 0)
            return carry

        lax.fori_loop(0, 3, inputs, 0)

        def outputs(i, carry):
            matrix(3 + i, 5 + 2 * i, 4 + 2 * i)
            return carry

        lax.fori_loop(0, 1 + role[0], outputs, 0)

        @pl.when(role[0] == 1)
        def _():
            def cross(i, carry):
                total = tn(dkvb[i, 0], ybuf[0]) + tn(rdkvb[i, 0], rybuf[0])
                for c in range(1, ybuf.shape[0]):
                    total = total + tn(dkvb[i, c], ybuf[c]) + tn(rdkvb[i, c], rybuf[c])
                keep_square(5 + i, total)
                return carry

            lax.fori_loop(0, 2, cross, 0)
            matrix(7, 9, 8)

    @pl.when(half[0] == 1)
    def _():
        side = la.shape[2]
        tiles = lw.shape[2] // side
        block = 4 * cols
        per = side // (2 * block)

        def feed(i, carry):
            pair, tile = i // tiles, lax.rem(i, tiles)
            lanes = pl.ds(pl.multiple_of(tile * side, 128), side)
            value = tn(lw[pair, :, lanes], lf[pair])
            for p in range(per):
                for j in range(4):
                    at = 2 * p * block + j * cols
                    keep(
                        4 * pair + j, tile * per + p, value[at : at + cols],
                        value[at + block : at + block + cols],
                    )
            return carry

        lax.fori_loop(0, 2 * tiles, feed, 0)

    @pl.when(role[0] == 1)
    def _():
        clips = captions.shape[0]
        rows = captions.shape[1]
        owners = [((2 * c) // clips, c - (((2 * c) // clips) * clips) // 2) for c in range(clips)]

        def dy_of(c):
            h, at = owners[c]
            return jnp.where(half[0] == h, dy[at].astype(f32), rdy[at].astype(f32)).astype(bf16)

        @pl.when(half[0] == 1)
        def _():
            total = None
            shape = (y2p.shape[2], y2p.shape[1], cols)
            mine, theirs = units_of(1, *shape), units_of(0, *shape)
            for c in range(clips):
                plain = low(nn(gq[c], mine) + nn(rgq[c], theirs))
                part = tn(dy_of(c), plain)
                total = part if total is None else total + part
            keep_square(8, total)

        units = text_out.shape[2]

        def keep_text(lanes, value):
            for p in range(line):
                for q in range(2):
                    cut = (2 * p + q) * units
                    text_out[p, q, :, lanes] = low(value[cut : cut + units])

        turned = []
        sums = None
        ones = jnp.ones((rows, 128), bf16)
        for c in range(clips):
            back = nn(dy_of(c), y2p[half[0]]) * gelu_both(hq[c])[1]
            turned.append(low(jnp.transpose(back))[:, 0:rows])
            part = nn(turned[c], ones)
            sums = part if sums is None else sums + part
        run(text(), True)

        def text_tile(t, carry):
            lanes = pl.ds(pl.multiple_of(t * 512, 512), 512)
            total = nn(turned[0], cap[0, :, lanes])
            for c in range(1, clips):
                total = total + nn(turned[c], cap[c, :, lanes])
            keep_text(lanes, total)
            return carry

        lax.fori_loop(0, captions.shape[2] // 512, text_tile, 0)
        keep_text(pl.ds(captions.shape[2], 128), sums)


def halves(value):
    first = low(value)
    return first, low(value - first.astype(f32))


def lefts(value, axis=1):
    first, second = halves(value)
    return jnp.concatenate([first, first, second], axis=axis)


def rights(value, axis=0):
    first, second = halves(value)
    return jnp.concatenate([first, second, first], axis=axis)


def gram_of(value, dot):
    first, second = halves(value)
    both = dot(first, first), dot(first, second)
    return both[0] + (both[1] + jnp.transpose(both[1]))


def muon_kernel(half, ua, uf, xa, xf, gram, whole):
    @pl.when(half[0] == 0)
    def _():
        u = ua[...]
        whole[...] = u / (jnp.sqrt(jnp.sum(u * u)) + 1e-07)

        def sweep(i, carry):
            x = whole[...]
            square = gram_of(x, nt)
            poly = coef_b * square + coef_c * gram_of(square, nt)
            whole[...] = coef_a * x + nn(lefts(poly), rights(x))
            return carry

        lax.fori_loop(0, 5, sweep, 0)
        xa[...] = low(whole[...])

    @pl.when(half[0] == 1)
    def _():
        width = uf.shape[1]
        tiles = uf.shape[0] // width
        gram[...] = jnp.zeros_like(gram)

        def rows(t):
            return pl.ds(pl.multiple_of(t * width, 128), width)

        def first(t, carry):
            piece = uf[rows(t), :]
            gram[...] += gram_of(piece, tn)
            return carry

        lax.fori_loop(0, tiles, first, 0)
        row = lax.broadcasted_iota(jnp.int32, (width, width), 0)
        col = lax.broadcasted_iota(jnp.int32, (width, width), 1)
        eye = jnp.where(row == col, 1.0, 0.0)
        start = gram[...]
        inv = 1.0 / (jnp.sqrt(jnp.sum(start * eye)) + 1e-07)
        gram[...] = start * (inv * inv)
        whole[...] = eye * inv

        def poly_of(a):
            return coef_a * eye + coef_b * a + coef_c * nn(lefts(a), rights(a))

        def sweep(i, carry):
            a = gram[...]
            left = lefts(poly_of(a))
            both = nn(left, rights(jnp.concatenate([a, whole[...]], axis=1)))
            whole[...] = both[:, width:]
            gram[...] = nn(left, rights(both[:, :width]))
            return carry

        lax.fori_loop(0, 4, sweep, 0)
        last = rights(nn(lefts(poly_of(gram[...])), rights(whole[...])))

        def apply(t, carry):
            xf[rows(t), :] = low(nn(lefts(uf[rows(t), :]), last))
            return carry

        lax.fori_loop(0, tiles, apply, 0)


def local_call(kernel, out_shape, in_specs, args, scratch=(), out_specs=None):
    return pl.pallas_call(
        kernel,
        out_shape=out_shape,
        in_specs=in_specs,
        out_specs=jax.tree.map(lambda _: VM, out_shape) if out_specs is None else out_specs,
        scratch_shapes=scratch,
        compiler_params=pltpu.CompilerParams(vmem_limit_bytes=VMEM_LIMIT),
    )(*args)


def here():
    return lax.axis_index("dp"), lax.axis_index("segment")


def dev(d, s):
    return {"dp": d, "segment": s}


def remote(src, dst, send, recv, target):
    return pltpu.make_async_remote_copy(
        src_ref=src, dst_ref=dst, send_sem=send, recv_sem=recv, device_id=target,
        device_id_type=MESH,
    )


def greet(targets):
    barrier = pltpu.get_barrier_semaphore()
    for target in targets:
        pl.semaphore_signal(barrier, inc=1, device_id=target, device_id_type=MESH)
    pl.semaphore_wait(barrier, len(targets))


def greet_dp(n, extra=()):
    d, s = here()
    barrier = pltpu.get_barrier_semaphore()

    def step(k, carry):
        pl.semaphore_signal(
            barrier, inc=1, device_id=dev(lax.rem(d + k, n), s), device_id_type=MESH
        )
        return carry

    lax.fori_loop(1, n, step, 0)
    for target in extra:
        pl.semaphore_signal(barrier, inc=1, device_id=target, device_id_type=MESH)
    pl.semaphore_wait(barrier, n - 1 + len(extra))


def comm_call(kernel, cid, args, out_shape, sems, out_specs=None, scratch=(), in_specs=None):
    if out_specs is None:
        out_specs = jax.tree.map(lambda _: ANY, out_shape)
    return pl.pallas_call(
        kernel,
        out_shape=out_shape,
        in_specs=[ANY] * len(args) if in_specs is None else in_specs,
        out_specs=out_specs,
        scratch_shapes=list(scratch) + [pltpu.SemaphoreType.DMA(shape) for shape in sems],
        compiler_params=pltpu.CompilerParams(
            collective_id=cid, has_side_effects=True, vmem_limit_bytes=VMEM_LIMIT
        ),
    )(*args)


def gather_kernel(n, pa, pb, pf, pw, py, pm, pt, wa, wb, wf, ww, wy, wm, wt,
                  send, recv, crecv, own):
    pair = 2 if n % 2 == 0 else 1
    line = n // pair
    d, s = here()
    role, half = s // 2, lax.rem(s, 2)
    a, x = d // pair, lax.rem(d, pair)
    mate = dev(d, role * 2 + 1 - half)
    above, below = dev(d + pair, s), dev(d - pair, s)
    across = dev(a * pair + (pair - 1 - x), s)
    barrier = pltpu.get_barrier_semaphore()

    def signal(target):
        pl.semaphore_signal(barrier, inc=1, device_id=target, device_id_type=MESH)

    signal(mate)
    if pair == 2:
        signal(across)

    @pl.when(a < line - 1)
    def _():
        signal(above)

    @pl.when(a > 0)
    def _():
        signal(below)

    pl.semaphore_wait(barrier, pair + jnp.minimum(a, 1) + jnp.minimum(line - 1 - a, 1))

    def two(i, ref, out):
        return [
            (i, ref.at[pl.ds(0, 2)], out.at[pl.ds(0, 2)], 2),
            (i + 1, ref.at[pl.ds(2, 2)], out.at[pl.ds(2, 2)], 2),
        ]

    first, last = half == 0, role == 1
    both = jnp.logical_and(first, last)
    shared = [((2, pw, ww, 0), first, True)]
    shared += [(item, first, True) for item in two(0, pa, wa)]
    shared += [(item, both, last) for item in two(5, pb, wb)]
    for m in range(2):
        item = (m, pf.at[pl.ds(m, 1)], wf.at[pl.ds(m, 1)], 1)
        shared.append((item, jnp.logical_not(first), True))
    alone = [((3, pt, wt, 0), True), ((4, pm, wm, 0), role == 0), ((4, py, wy, 0), role == 1)]
    parts = [(item, when, True) for item, when, _ in shared]
    parts += [(item, when, False) for item, when in alone]

    def slot(ref, lead, o):
        return ref.at[:, o] if lead else ref.at[o]

    def given(when, act):
        if when is True:
            act()
        else:
            pl.when(when)(act)

    def move(item, way, o, target, is_own=False):
        i, src, dst, lead = item
        there = slot(dst, lead, o)
        sem = crecv if way == 3 else recv
        return remote(src if is_own else there, there, send.at[way, i, o], sem.at[i, o], target)

    def forward(o, up, down, side, is_own, finish, wait=False):
        for item, when, common in parts:

            def act(item=item, common=common):
                if wait:
                    move(item, 0, o, across).wait_recv()

                def go(way, target):
                    copy = move(item, way, o, target, is_own)
                    copy.wait_send() if finish else copy.start()

                if side and pair == 2:
                    go(2, across)
                if up is not None:
                    pl.when(up)(functools.partial(go, 0, above))
                if down is not None:
                    pl.when(down)(functools.partial(go, 1, below))
                if common:
                    go(3, mate)

            given(when, act)

    def keep(finish):
        for item, when, common in parts:

            def act(item=item):
                i, src, dst, lead = item
                copy = pltpu.make_async_copy(src, slot(dst, lead, d), own.at[i])
                copy.wait() if finish else copy.start()

            given(when, act)

    forward(d, a < line - 1, a > 0, True, True, False)
    keep(False)
    other = pair - 1 - x

    def sweep(finish):
        def step(k, carry):
            @pl.when(a - k >= 0)
            def _():
                forward((a - k) * pair + x, a < line - 1, None, True, False, finish, not finish)

            @pl.when(a + k < line)
            def _():
                forward((a + k) * pair + x, None, a > 0, True, False, finish, not finish)

            if pair == 2:

                def from_side(o, carry):
                    forward(o * pair + other, None, None, False, False, finish, not finish)
                    return carry

                @pl.when(a - (k - 1) >= 0)
                def _():
                    from_side(a - (k - 1), 0)

                @pl.when(jnp.logical_and(k > 1, a + (k - 1) < line))
                def _():
                    from_side(a + (k - 1), 0)

            return carry

        lax.fori_loop(1, line + 1, step, 0)

    sweep(False)
    forward(d, a < line - 1, a > 0, True, True, True)
    sweep(True)
    keep(True)

    def collect(o, carry):
        for item, when, arrives in shared:
            mine = when if when is not both else first

            def act(item=item):
                i, src, dst, lead = item
                there = slot(dst, lead, o)
                remote(there, there, send.at[3, i, o], crecv.at[i, o], mate).wait_recv()

            given(jnp.logical_and(jnp.logical_not(mine), arrives), act)
        return carry

    lax.fori_loop(0, n, collect, 0)


def mate_kernel(src, dst, send, recv, own):
    d, s = here()
    role, half = s // 2, lax.rem(s, 2)
    mate = dev(d, role * 2 + 1 - half)

    @pl.when(role == 0)
    def _():
        greet([mate])
        pltpu.make_async_copy(src, dst.at[half], own.at[0]).start()
        remote(src, dst.at[half], send.at[0], recv.at[0], mate).start()
        pltpu.make_async_copy(src, dst.at[half], own.at[0]).wait()
        remote(src, dst.at[1 - half], send.at[0], recv.at[0], mate).wait()


def forward_kernel(count, h1s, gq, mq, h1t, gqs, mqt, send, recv, msend, mrecv, qsend, qrecv):
    relay_half_clips(
        count, 0, h1s, h1t, send, recv, swap=(gq, gqs, msend, mrecv), rows=(mq, mqt, qsend, qrecv)
    )


def relay_half_clips(count, from_role, src, dst, send, recv, extra=None, swap=None, rows=None):
    d, s = here()
    role, half = s // 2, lax.rem(s, 2)
    peers = [dev(d, (1 - role) * 2), dev(d, (1 - role) * 2 + 1)]
    mate = dev(d, role * 2 + 1 - half)
    peers.append(mate)
    greet(peers)

    def unit(i, part):
        there = half * count + i
        clip, own = there // 2, lax.rem(there, 2)
        other = 2 * clip + part
        return own, other // count, lax.rem(other, count)

    def copy(i, part):
        own, to, slot = unit(i, part)
        return remote(
            src.at[i, part], dst.at[slot, own], send.at[i, part], recv.at[slot, own],
            dev(d, (1 - from_role) * 2 + to),
        )

    def row_copy(to, finish):
        value, there, qsend, qrecv = rows
        slot = there.at[half] if from_role == 1 else there
        copy = remote(value, slot, qsend.at[to], qrecv.at[half], dev(d, (1 - from_role) * 2 + to))
        copy.wait_send() if finish else copy.start()

    def row_sends(finish):
        if rows is None:
            return

        @pl.when(role == from_role)
        def _():
            if from_role == 0:
                for to in range(2):
                    pl.when(half == to)(functools.partial(row_copy, to, finish))
            else:
                for to in range(2):
                    row_copy(to, finish)

    row_sends(False)
    if swap is not None:
        mine, both, msend, mrecv = swap

        @pl.when(role == 1)
        def _():
            remote(mine, both, msend.at[0], mrecv.at[0], mate).start()

    if extra is not None:
        own_src, own_dst, esend, erecv = extra

        @pl.when(jnp.logical_and(role == 1, half == 1))
        def _():
            remote(own_src, own_dst, esend.at[0], erecv.at[0], dev(d, 2)).start()

    @pl.when(role == from_role)
    def _():
        for i in range(count):
            for part in range(2):
                copy(i, part).start()
        for i in range(count):
            for part in range(2):
                copy(i, part).wait_send()

    @pl.when(role == 1 - from_role)
    def _():
        for i in range(count):
            for part in range(2):
                remote(
                    src.at[i, part], dst.at[i, part], send.at[i, part], recv.at[i, part],
                    dev(d, from_role * 2),
                ).wait_recv()

    row_sends(True)
    if rows is not None:
        value, there, qsend, qrecv = rows

        @pl.when(role == 1 - from_role)
        def _():
            if from_role == 0:
                remote(value, there, qsend.at[0], qrecv.at[half], mate).wait_recv()
            else:
                for o in range(2):
                    remote(value, there.at[o], qsend.at[0], qrecv.at[o], mate).wait_recv()

    if swap is not None:

        @pl.when(role == 1)
        def _():
            remote(mine, both, msend.at[0], mrecv.at[0], mate).wait()

    if extra is not None:

        @pl.when(jnp.logical_and(role == 1, half == 1))
        def _():
            remote(own_src, own_dst, esend.at[0], erecv.at[0], dev(d, 2)).wait_send()

        @pl.when(jnp.logical_and(role == 1, half == 0))
        def _():
            remote(own_src, own_dst, esend.at[0], erecv.at[0], dev(d, 2)).wait_recv()


def backward_kernel(count, dh1, dkv, dmod, dhs, extra, dmods, send, recv, esend, erecv, qsend,
                    qrecv):
    relay_half_clips(
        count, 1, dh1, dhs, send, recv, extra=(dkv.at[:, 0], extra, esend, erecv),
        rows=(dmod, dmods, qsend, qrecv),
    )


def swap_kernel(acts_s, acts_t, actf_s, actf_t, actw_s, actw_t, ybuf, dkvb, dy, dmod,
                racts, ractf, ractw, rybuf, rdkvb, rdy, rdmod, send, recv):
    d, s = here()
    role, half = s // 2, lax.rem(s, 2)
    mate = dev(d, role * 2 + 1 - half)
    greet([mate])
    six = acts_s.shape[0]
    gives = {
        (0, 0): [(0, actf_s, ractf), (1, actw_s, ractw), (4, dmod, rdmod)],
        (0, 1): [(0, acts_s, racts.at[pl.ds(0, six)]), (4, dmod, rdmod)],
        (1, 0): [(0, actf_t, ractf), (1, actw_t, ractw), (2, dy, rdy)],
        (1, 1): [(0, acts_t, racts), (1, ybuf, rybuf), (3, dkvb, rdkvb), (2, dy, rdy)],
    }
    for (r, h), mine in gives.items():

        @pl.when(jnp.logical_and(role == r, half == h))
        def _():
            for i, src, dst in mine:
                remote(src, dst, send.at[i], recv.at[i], mate).start()
            for i, src, dst in mine:
                remote(src, dst, send.at[i], recv.at[i], mate).wait_send()
            for i, src, dst in gives[(r, 1 - h)]:
                remote(src, dst, send.at[i], recv.at[i], mate).wait_recv()


TEXT_CUTS = 11


def scatter_kernel(n, own_in, snd, text_in, dm, vec, loss, wm, temb, ww, hid, wt,
                   summed, text, vsum, squares, gm, g2, g1,
                   own, rx, up, down, sx, rz, tin, trx, tsx, trz, rv, rm, dtembs,
                   osem, send1, recv1, send2, recv2, usend, urecv, dsend, drecv,
                   ssend, srecv, sown, tsend, trecv, esend, erecv):
    line = n // 2
    d, s = here()
    role, half = s // 2, lax.rem(s, 2)
    a, x = d // 2, lax.rem(d, 2)
    across = dev(a * 2 + 1 - x, s)
    other = dev(d, (1 - role) * 2 + half)
    count = 8 - 4 * (1 - role) * (1 - half)
    greet_dp(n, [other])
    squares[...] = jnp.zeros_like(squares)
    squares[1:2, 0:128] = loss[...]
    step = text.shape[1] // TEXT_CUTS
    is_text, is_last, is_time = role == 0, s == 3, s == 0
    clip_rows = dm.shape[0]

    def first_copies(u):
        return (
            remote(snd.at[u], rx.at[u], send1.at[u], recv1.at[u], across),
            pltpu.make_async_copy(own_in.at[u], own.at[u], osem.at[u]),
        )

    def text_hop(k):
        lanes = pl.ds(pl.multiple_of(k * step, 128), step)
        return remote(text_in.at[:, :, :, lanes], tin.at[k], tsend.at[k], trecv.at[k], other)

    def text_across(k):
        return remote(tin.at[k, :, 1 - x], trx.at[k], send1.at[9 + k], recv1.at[9 + k], across)

    def begin(u, carry):
        for copy in first_copies(u):
            copy.start()
        return carry

    def rows_at(o):
        return rm.at[pl.ds(pl.multiple_of(o * clip_rows, 8), clip_rows)]

    def small(i, finish):
        src, dst = (
            (lambda p: vec.at[p], lambda o: rv.at[o]) if i else (lambda p: dm, rows_at)
        )

        def each(k, carry):
            to, o = lax.rem(d + k, n), lax.rem(d + n - k, n)
            if finish:
                remote(src(o), dst(o), ssend.at[i, k], srecv.at[i, k], dev(o, s)).wait()
            else:
                remote(src(to), dst(d), ssend.at[i, k], srecv.at[i, k], dev(to, s)).start()
            return carry

        lax.fori_loop(1, n, each, 0)
        copy = pltpu.make_async_copy(src(d), dst(d), sown.at[i])
        copy.wait() if finish else copy.start()

    pl.when(is_time)(lambda: small(0, False))
    lax.fori_loop(0, 1, begin, 0)
    small(1, False)
    lax.fori_loop(1, count, begin, 0)

    @pl.when(is_last)
    def _():
        begin(8, 0)

    @pl.when(role == 1)
    def _():
        lax.fori_loop(0, TEXT_CUTS, lambda k, c: (text_hop(k).start(), c)[1], 0)

    def embeds(finish):
        def each(k, carry):
            to, o = lax.rem(d + k, n), lax.rem(d + n - k, n)
            if finish:
                remote(dtembs.at[o], dtembs.at[o], esend.at[k], erecv.at[k], dev(o, s)).wait()
            else:
                remote(dtembs.at[d], dtembs.at[d], esend.at[k], erecv.at[k], dev(to, s)).start()
            return carry

        lax.fori_loop(1, n, each, 0)

    def upward(u, p):
        return remote(up.at[u, p], up.at[u, p], usend.at[u, p], urecv.at[u, p], dev(d + 2, s))

    def downward(u, p):
        return remote(
            down.at[u, p], down.at[u, p], dsend.at[u, p], drecv.at[u, p], dev(d - 2, s)
        )

    def along_up(u):
        def add(i, carry):
            p = line - 1 - i

            @pl.when(a == 0)
            def _():
                up[u, p] = own[u, p]

            @pl.when(a > 0)
            def _():
                upward(u, p).wait_recv()
                up[u, p] = up[u, p] + own[u, p]

            return carry

        def send(i, carry):
            upward(u, line - 1 - i).start()
            return carry

        lax.fori_loop(0, line - 1 - a, add, 0)
        lax.fori_loop(0, line - 1 - a, send, 0)

    def along_down(u):
        def add(p, carry):
            @pl.when(a == line - 1)
            def _():
                down[u, p] = own[u, p]

            @pl.when(a < line - 1)
            def _():
                downward(u, p).wait_recv()
                down[u, p] = down[u, p] + own[u, p]

            return carry

        def send(p, carry):
            downward(u, p).start()
            return carry

        lax.fori_loop(0, a, add, 0)
        lax.fori_loop(0, a, send, 0)

    def pairs(u):
        for copy in first_copies(u):
            copy.wait()
        own[u] = own[u] + rx[u].astype(f32)

    def direct(i, total, line_in, finish):
        def each(k, carry):
            to, o = lax.rem(a + k, line), lax.rem(a + line - k, line)
            if finish:
                remote(
                    total.at[o], line_in.at[o], send2.at[i, k], recv2.at[i, k], dev(o * 2 + x, s)
                ).wait()
            else:
                remote(
                    total.at[to], line_in.at[a], send2.at[i, k], recv2.at[i, k],
                    dev(to * 2 + x, s),
                ).start()
            return carry

        lax.fori_loop(1, line, each, 0)

    def round_trip(i, carry):
        @pl.when(i < count)
        def _():
            pairs(i)

        @pl.when(jnp.logical_and(is_time, i == 1))
        def _():
            small(0, True)
            time_back([d], rm, wm, temb, dtembs.at[d])

        pl.when(jnp.logical_and(is_time, i == 2))(lambda: embeds(False))

        @pl.when(is_text)
        def _():
            def cut_at(delay, act):
                k = i - delay
                pl.when(jnp.logical_and(k >= 0, k < TEXT_CUTS))(lambda: act(k))

            def arrive(k):
                text_hop(k).wait_recv()
                text_across(k).start()

            def add(k):
                text_across(k).wait()
                tsx[k] = low(tin[k, :, x].astype(f32) + trx[k].astype(f32))

            cut_at(4, lambda k: direct(k, tsx.at[k], trz.at[k], False))
            cut_at(1, arrive)
            cut_at(3, add)

        k = i - count

        @pl.when(jnp.logical_and(is_last, k == 0))
        def _():
            pairs(8)
            sx[...] = low(own[8])

        @pl.when(jnp.logical_and(is_last, k == 1))
        def _():
            direct(TEXT_CUTS, sx, rz, False)

        later = i - 1 - a

        @pl.when(jnp.logical_and(later >= 0, later < count))
        def _():
            along_up(later)

        other = i - line + a

        @pl.when(jnp.logical_and(other >= 0, other < count))
        def _():
            along_down(other)

        return carry

    lax.fori_loop(0, jnp.maximum(count + line, TEXT_CUTS + 4), round_trip, 0)
    small(1, True)
    vsum[...] = lax.fori_loop(0, n, lambda o, total: total + rv[o], jnp.zeros(vsum.shape, f32))

    @pl.when(is_time)
    def _():
        embeds(True)
        time_grad([d], rm, dtembs, ww, temb, hid, wt, gm, g2, g1, vsum, squares)

    @pl.when(role == 1)
    def _():
        lax.fori_loop(0, TEXT_CUTS, lambda k, c: (text_hop(k).wait_send(), c)[1], 0)

    def collect(u, carry):
        @pl.when(a > 0)
        def _():
            upward(u, a).wait_recv()
            own[u, a] = own[u, a] + up[u, a]

        @pl.when(a < line - 1)
        def _():
            downward(u, a).wait_recv()
            own[u, a] = own[u, a] + down[u, a]

        whole = own[u, a]
        summed[u] = whole
        squares[0:1, :] += col_sum(whole * whole)
        return carry

    lax.fori_loop(0, count, collect, 0)

    def drain(u, carry):
        def one(i, c):
            upward(u, line - 1 - i).wait_send()
            return c

        def two(p, c):
            downward(u, p).wait_send()
            return c

        lax.fori_loop(0, line - 1 - a, one, 0)
        lax.fori_loop(0, a, two, 0)
        return carry

    lax.fori_loop(0, count, drain, 0)

    def others(line_in, whole):
        return lax.fori_loop(
            1, line, lambda k, acc: acc + line_in[lax.rem(a + k, line)].astype(f32), whole
        )

    @pl.when(is_last)
    def _():
        direct(TEXT_CUTS, sx, rz, True)
        whole = others(rz, own[8, a])
        summed[8] = whole
        squares[0:1, :] += col_sum(whole * whole)

    @pl.when(is_text)
    def _():
        def whole_cut(k, carry):
            direct(k, tsx.at[k], trz.at[k], True)
            whole = others(trz.at[k], tin[k, a, x].astype(f32) + trx[k, a].astype(f32))
            text[:, pl.ds(pl.multiple_of(k * step, 128), step)] = low(whole)
            lane = lax.broadcasted_iota(jnp.int32, (1, step), 1)
            spare = jnp.logical_and(k == TEXT_CUTS - 1, lane > step - 128)
            counted = jnp.where(spare, 0.0, whole)
            squares[0:1, :] += col_sum(counted * counted)
            return carry

        lax.fori_loop(0, TEXT_CUTS, whole_cut, 0)


def three(value):
    first = low(value)
    rest = value - first.astype(f32)
    second = low(rest)
    return first, second, low(rest - second.astype(f32))


def nn3(left, right):
    return sum(nn(piece, right) for piece in three(left))


def nt3(left, right):
    return sum(nt(piece, right) for piece in three(left))


def tn3(left, right):
    return sum(tn(left, piece) for piece in three(right))


def own_columns(rank, width, cols):
    row = lax.broadcasted_iota(jnp.int32, (width, 128), 0)
    col = lax.broadcasted_iota(jnp.int32, (width, 128), 1)
    return low(jnp.where(jnp.logical_and(row == rank * cols + col, col < cols), 1.0, 0.0))


def clip_groups(clips, rows):
    per = 8 * (rows // (clips // 8) // 8)
    left = lax.broadcasted_iota(jnp.int32, (clips, rows), 0)
    right = lax.broadcasted_iota(jnp.int32, (clips, rows), 1)
    match = (right // per) * 8 + (right % per) // 8 == left
    return low(jnp.where(match, 1.0, 0.0))


def silu_back(value):
    gate = jax.nn.sigmoid(value)
    return gate * (1.0 + value * (1.0 - gate))


def time_back(rank, rm, wm, temb, dtemb):
    cols, width = wm.shape[0], rm.shape[1]
    rows, clips = rm.shape[0], temb.shape[0]
    pick = own_columns(rank[0], width, cols)
    kind = lax.broadcasted_iota(jnp.int32, (rows, 1), 0) % 8
    value = rm[...]
    pieces = three(value)
    total = jnp.where(kind >= 6, nn3(value, pick), 0.0)
    zeros = jnp.zeros((128 - cols, width), bf16)

    def one(r, total):
        lanes = pl.ds(pl.multiple_of(r * width, 128), width)
        weight = jnp.concatenate([wm[:, lanes], zeros], axis=0)
        back = nt(pieces[0], weight) + nt(pieces[1], weight) + nt(pieces[2], weight)
        return total + jnp.where(kind == r, back, 0.0)

    total = lax.fori_loop(0, 6, one, total)
    slope = silu_back(nn3(temb[...], pick))
    group = clip_groups(clips, rows)

    def collapse(part):
        first, second, third = three(part)
        return nn(group, first) + nn(group, second) + nn(group, third)

    dtemb[...] = collapse(jnp.where(kind < 6, total, 0.0)) * slope + collapse(
        jnp.where(kind >= 6, total, 0.0)
    )


def time_grad(rank, rm, dtembs, ww, temb, hid, wt, gm, g2, g1, vout, tout):
    width, cols = rm.shape[1], vout.shape[0]
    rows, clips = rm.shape[0], temb.shape[0]
    n = dtembs.shape[0]
    pick = own_columns(rank[0], width, cols)
    kind = lax.broadcasted_iota(jnp.int32, (rows, 1), 0) % 8
    value = rm[...]
    hidden = hid[...]
    own_hid, own_temb = nn3(hidden, pick), nn3(temb[...], pick)
    gates = low(own_temb * jax.nn.sigmoid(own_temb))
    spread = low(tn(clip_groups(clips, rows), gates))
    pieces = three(value)
    count = jnp.zeros((1, 1), f32)

    def squared(block):
        return jnp.sum(jnp.sum(block * block, axis=1, keepdims=True), axis=0, keepdims=True)

    def one(r, count):
        masked = jnp.where(kind == r, spread.astype(f32), 0.0).astype(bf16)
        block = sum(tn(masked, piece) for piece in pieces)[0:cols]
        gm[:, pl.ds(pl.multiple_of(r * width, 128), width)] = block
        return count + squared(block)

    count = lax.fori_loop(0, 6, one, count)
    mine = dtembs[rank[0]]
    mine_pieces = three(mine)
    act = low(hidden * jax.nn.sigmoid(hidden))
    block = sum(tn(piece, act) for piece in mine_pieces)[0:cols]
    g2[...] = block
    count = count + squared(block)
    back = jnp.zeros((clips, 128), f32)
    zeros = jnp.zeros((128 - cols, 128), bf16)
    picked = low(nn(ww[:, 256 : 256 + width], pick))
    for o in range(n):
        weight = picked[o * cols : o * cols + cols]
        back = back + nn3(dtembs[o], jnp.concatenate([weight, zeros], axis=0))
    dhid = back * silu_back(own_hid)
    dhid_pieces = three(dhid)
    feature = low(wt[:, 0:256])
    block = sum(tn(piece, feature) for piece in dhid_pieces)[0:cols]
    g1[...] = block
    count = count + squared(block)
    at = lax.broadcasted_iota(jnp.int32, (clips, 128), 1)
    first = low(jnp.where(at == 1, 1.0, 0.0))
    second = low(jnp.where(at == 2, 1.0, 0.0))
    total = sum(tn(piece, first) for piece in dhid_pieces)
    total = total + sum(tn(piece, second) for piece in mine_pieces)
    row_kind = lax.broadcasted_iota(jnp.int32, (rows, 128), 0) % 8
    row_lane = lax.broadcasted_iota(jnp.int32, (rows, 128), 1)
    put = jnp.logical_and(row_lane == row_kind + 3, row_kind < 6)
    put = low(jnp.where(put, 1.0, 0.0))
    total = total + sum(tn(piece, put) for piece in three(nn3(value, pick)))

    vout[...] += total[0:cols]
    lane = lax.broadcasted_iota(jnp.int32, (1, 128), 1)
    tout[0:1, 0:128] += jnp.where(lane == 0, count, 0.0)


class Relay:
    def __init__(self, send, recv):
        self.d, self.s = here()
        self.role, self.half = self.s // 2, lax.rem(self.s, 2)
        self.other = dev(self.d, (1 - self.role) * 2 + self.half)
        self.mate = dev(self.d, self.role * 2 + 1 - self.half)
        self.send, self.recv = send, recv

    def at(self, r, h):
        return jnp.logical_and(self.role == r, self.half == h)

    def copy(self, i, leg, src, dst):
        target = self.other if leg == 0 else self.mate
        return remote(src, dst, self.send.at[i, leg], self.recv.at[i, leg], target)

    def start(self, i, src, dst):
        self.copy(i, 0, src, dst).start()
        self.copy(i, 1, src, dst).start()

    def middle(self, i, dst):
        self.copy(i, 0, dst, dst).wait_recv()
        self.copy(i, 2, dst, dst).start()

    def finish(self, r, h, items):
        @pl.when(self.at(r, h))
        def _():
            for i, src, dst in items:
                self.copy(i, 0, src, dst).wait_send()
                self.copy(i, 1, src, dst).wait_send()

        @pl.when(self.at(1 - r, h))
        def _():
            for i, src, dst in items:
                self.copy(i, 2, dst, dst).wait_send()

        @pl.when(self.at(r, 1 - h))
        def _():
            for i, src, dst in items:
                self.copy(i, 1, dst, dst).wait_recv()

        @pl.when(self.at(1 - r, 1 - h))
        def _():
            for i, src, dst in items:
                self.copy(i, 2, dst, dst).wait_recv()


def owner_first(role, mat):
    return 2 * mat + mat % 2 if role == 0 else mat


def owner_second(mat):
    return 2 + 3 * mat


def settle_kernel(n, vsum, tile, summed, att_m, feed_m, gm, g2, g1,
                  oa, of, xa, xf, xm, x2, x1, gv, stat,
                  vecs, tiles, mine, totals, look, mom,
                  msem, send, recv, own, gsend, grecv, gown, ssend, srecv, tsend, trecv):
    relay = Relay(gsend, grecv)
    d, s, role, half = relay.d, relay.s, relay.role, relay.half
    peers = [dev(d, lax.rem(s + k, 4)) for k in range(1, 4)]
    greet_dp(n, peers)
    four, eight = pl.ds(0, 4), pl.ds(0, 8)
    shared = {
        (0, 0): [(0, summed.at[four], xa.at[four]), (4, gm, xm), (5, g2, x2), (6, g1, x1)],
        (0, 1): [(1, summed.at[eight], xf.at[eight])],
        (1, 0): [(2, summed.at[eight], xa.at[pl.ds(4, 8)])],
        (1, 1): [(3, summed.at[eight], xf.at[pl.ds(8, 8)])],
    }
    def momentum(finish):
        sources = {
            (0, 0): (att_m.at[four], mom.at[four]),
            (0, 1): (feed_m.at[eight], mom),
            (1, 0): (att_m.at[pl.ds(4, 8)], mom),
            (1, 1): (feed_m.at[pl.ds(8, 8)], mom),
        }
        for (r, h), (src, dst) in sources.items():

            @pl.when(relay.at(r, h))
            def _():
                copy = pltpu.make_async_copy(src, dst, msem.at[0])
                copy.wait() if finish else copy.start()

    momentum(False)
    small = [(0, vsum, vecs), (1, tile, tiles)]
    for i, src, dst in small:
        for k in range(1, 4):
            remote(src, dst.at[s], ssend.at[i, k], srecv.at[i, k], peers[k - 1]).start()
    for (r, h), items in shared.items():

        @pl.when(relay.at(r, h))
        def _():
            for i, src, dst in items:
                pltpu.make_async_copy(src, dst, gown.at[i]).start()
                relay.start(i, src, dst)

    total, squares, losses = vsum[...], tile[0:1, :], tile[1:2, :]
    for k in range(1, 4):
        o = lax.rem(s + 4 - k, 4)
        for i, src, dst in small:
            remote(src, dst.at[o], ssend.at[i, k], srecv.at[i, k], dev(d, o)).wait()
        total = total + vecs[o]
        squares = squares + tiles[o, 0:1, :]
        losses = losses + tiles[o, 1:2, :]
    lane = lax.broadcasted_iota(jnp.int32, (1, 128), 1)
    total = jnp.where(jnp.logical_or(lane == 9, lane >= 77), 0.0, total)
    gv[...] = total

    def whole(block):
        return jnp.sum(jnp.sum(block, axis=1, keepdims=True), axis=0, keepdims=True)

    row = lax.broadcasted_iota(jnp.int32, (8, 128), 0)
    mine[...] = jnp.where(row < 4, whole(squares) + whole(total * total), whole(losses[:, 0:128]))
    so_far = mine[...]

    def start(k, carry):
        remote(mine, totals.at[d], tsend.at[k], trecv.at[k], dev(lax.rem(d + k, n), s)).start()
        return carry

    lax.fori_loop(1, n, start, 0)

    def finish(k, carry):
        o = lax.rem(d + n - k, n)
        remote(mine, totals.at[o], tsend.at[k], trecv.at[k], dev(o, s)).wait()
        return carry + totals[o]

    lax.fori_loop(1, n, lambda k, c: (finish(k, so_far), c)[1], 0)
    totals[d] = so_far
    so_far = lax.fori_loop(0, n, lambda o, c: c + totals[o], jnp.zeros((8, 128), f32))
    stat[...] = so_far
    factor = jnp.minimum(1.0, max_norm / (jnp.sqrt(so_far[0:1, 0:1]) + 1e-06))
    scale = factor * (1.0 + momentum_decay)

    momentum(True)

    def update(m, carry):
        look[m] = summed[m] * scale + mom[m] * (momentum_decay * momentum_decay)
        return carry

    lax.fori_loop(0, 8, update, 0)
    groups = []
    for r in range(2):
        mats = 4 if r == 0 else 8
        groups.append((r, 0, [(m, owner_first(r, m), look.at[m], oa) for m in range(mats)]))
        groups.append((
            r, 1, [(m, owner_second(m), look.at[pl.ds(4 * m, 4)], of) for m in range(2)]
        ))
    for r, h, mats in groups:

        @pl.when(relay.at(r, h))
        def _():
            for m, o, src, dst in mats:

                @pl.when(d == o)
                def _():
                    pltpu.make_async_copy(src, dst.at[d], own.at[0]).start()

                @pl.when(d != o)
                def _():
                    remote(src, dst.at[d], send.at[m], recv.at[d], dev(o, s)).start()

    for (r, h), items in shared.items():

        @pl.when(relay.at(1 - r, h))
        def _():
            for i, src, dst in items:
                relay.middle(i, dst)

    for r, h, mats in groups:

        @pl.when(relay.at(r, h))
        def _():
            for i, src, dst in shared[(r, h)]:
                pltpu.make_async_copy(src, dst, gown.at[i]).wait()
            for m, o, src, dst in mats:

                @pl.when(d == o)
                def _():
                    pltpu.make_async_copy(src, dst.at[d], own.at[0]).wait()

                    def arrived(k, carry):
                        p = lax.rem(d + n - k, n)
                        remote(src, dst.at[p], send.at[m], recv.at[p], dev(p, s)).wait_recv()
                        return carry

                    lax.fori_loop(1, n, arrived, 0)

                @pl.when(d != o)
                def _():
                    remote(src, dst.at[d], send.at[m], recv.at[d], dev(o, s)).wait_send()

    for (r, h), items in shared.items():
        relay.finish(r, h, items)


def spread_kernel(n, xa, xf, gy1, summed, oa, of, xy1, xy2, send, recv, rsend, rrecv, own, gown):
    relay = Relay(rsend, rrecv)
    d, s, role, half = relay.d, relay.s, relay.role, relay.half
    greet_dp(n, [relay.other, relay.mate])
    groups = []
    for r in range(2):
        mats = 4 if r == 0 else 8
        groups.append((r, 0, mats, functools.partial(owner_first, r), xa, oa, 10 * r, 4))
        groups.append((r, 1, 2, owner_second, xf, of, 10 * r + 8, 2))
    text = {
        (0, 0): [(20, gy1, xy1.at[0])],
        (0, 1): [(21, gy1, xy1.at[1])],
        (1, 1): [(22, summed.at[8], xy2)],
    }
    for (r, h), items in text.items():

        @pl.when(relay.at(r, h))
        def _():
            for i, src, dst in items:
                pltpu.make_async_copy(src, dst, gown.at[i - 20]).start()
                relay.start(i, src, dst)

    for r, h, mats, owner, src, dst, base, per in groups:

        @pl.when(relay.at(r, h))
        def _():
            for m in range(mats):

                @pl.when(d == owner(m))
                def _():
                    pltpu.make_async_copy(src.at[d], dst.at[per * r + m], own.at[m]).start()

                    def start(k, carry):
                        to = lax.rem(d + k, n)
                        remote(
                            src.at[to], dst.at[per * r + m], send.at[k], recv.at[m], dev(to, s)
                        ).start()
                        return carry

                    lax.fori_loop(1, n, start, 0)

            for m in range(mats):

                @pl.when(d == owner(m))
                def _():
                    pltpu.make_async_copy(src.at[d], dst.at[per * r + m], own.at[m]).wait()

                @pl.when(d != owner(m))
                def _():
                    remote(
                        src.at[d], dst.at[per * r + m], send.at[1], recv.at[m], dev(owner(m), s)
                    ).wait_recv()

                relay.start(base + m, dst.at[per * r + m], dst.at[per * r + m])

    for (r, h), items in text.items():

        @pl.when(relay.at(1 - r, h))
        def _():
            for i, src, dst in items:
                relay.middle(i, dst)

    for r, h, mats, owner, src, dst, base, per in groups:

        @pl.when(relay.at(1 - r, h))
        def _():
            for m in range(mats):
                relay.middle(base + m, dst.at[per * r + m])

    for r, h, mats, owner, src, dst, base, per in groups:

        @pl.when(relay.at(r, h))
        def _():
            for m in range(mats):

                @pl.when(d == owner(m))
                def _():
                    def finish(k, carry):
                        to = lax.rem(d + k, n)
                        remote(
                            src.at[to], dst.at[per * r + m], send.at[k], recv.at[m], dev(to, s)
                        ).wait_send()
                        return carry

                    lax.fori_loop(1, n, finish, 0)

        relay.finish(r, h, [(base + m, dst.at[per * r + m], dst.at[per * r + m]) for m in range(mats)])

    for (r, h), items in text.items():

        @pl.when(relay.at(r, h))
        def _():
            for i, src, dst in items:
                pltpu.make_async_copy(src, dst, gown.at[i - 20]).wait()

        relay.finish(r, h, items)


def adamw_update(weight, first, second, grad, fix_one, fix_two):
    first = beta_one * first + (1.0 - beta_one) * grad
    second = beta_two * second + (1.0 - beta_two) * grad * grad
    first_hat = first / fix_one
    second_hat = second / fix_two
    weight = weight - adam_rate * (
        first_hat / (jnp.sqrt(second_hat) + 1e-08) + weight_decay * weight
    )
    return (weight, first, second)


def update_kernel(
    rates, pieces, scal, stat,
    aw, am, ag, ax, fw, fm, fg, fx, sw, s1, s2, gv, g1, g2, gt, gy2, gm, vw, v1, v2, gvall, gtall,
    aw_, am_, ab_, fw_, fm_, fb_, sw_, s1_, s2_, sb_, vw_, v1_, v2_, vb_, loss_, norm_,
):
    grad_norm = jnp.sqrt(stat[0:1, 0:1])
    factor = jnp.minimum(1.0, max_norm / (grad_norm + 1e-06))
    fix_one, fix_two = scal[0], scal[1]
    loss_[...] = stat[4:5, 0:1]
    norm_[...] = grad_norm
    shrink = 1.0 - muon_rate * weight_decay
    for rate, (w, m, g, x, w_, m_, b_) in zip(
        rates, ((aw, am, ag, ax, aw_, am_, ab_), (fw, fm, fg, fx, fw_, fm_, fb_))
    ):
        m_[...] = momentum_decay * m[...] + g[...] * factor
        fresh = w[...] * shrink - rate * x[...].astype(f32)
        w_[...] = fresh
        b_[...] = low(fresh)
    text = gt.shape[1] - 128
    shards = {
        "embed": gv[:, EMB0 : EMB0 + 16],
        "time": g1[...],
        "time2": g2[...],
        "text": None,
        "text2": gy2[...],
        "head": gv[:, HEAD0 : HEAD0 + 16],
        "mod": gm[...],
    }
    for name, at, size in pieces:
        stride = size if name != "text" else 512
        for start in range(0, size, stride):
            cut = slice(at + start, at + start + stride)
            grad = gt[:, start : start + stride].astype(f32) if name == "text" else shards[name]
            fresh, one, two = adamw_update(
                sw[:, cut], s1[:, cut], s2[:, cut], grad * factor, fix_one, fix_two
            )
            sw_[:, cut], s1_[:, cut], s2_[:, cut] = fresh, one, two
            sb_[:, cut] = low(fresh)

    @pl.when(pl.program_id(0) == 0)
    def _():
        lane = lax.broadcasted_iota(jnp.int32, (1, 128), 1)
        column = gtall[:, text : text + 128].astype(f32)
        whole = jnp.where(lane == 9, column, gvall[...])
        rows = vw.shape[0]
        grad = jnp.transpose(whole)[0:rows, :] * factor
        fresh, one, two = adamw_update(vw[...], v1[...], v2[...], grad, fix_one, fix_two)
        vw_[...], v1_[...], v2_[...] = fresh, one, two
        vb_[...] = low(fresh)


def body(
    latents,
    noise_draw,
    timesteps,
    captions,
    caption_len,
    attention_weights,
    feed_weights,
    side_weights,
    vector_weights,
    attention_momentum,
    feed_momentum,
    side_first,
    side_second,
    vector_first,
    vector_second,
    step_count,
):
    n = lax.axis_size("dp")
    d, s = here()
    role, half = s // 2, lax.rem(s, 2)
    count = latents.shape[0]
    frames = latents.shape[1]
    width = attention_weights.shape[1]
    cols, feed_cols = attention_weights.shape[2], feed_weights.shape[2]
    hidden = n * feed_cols
    text = captions.shape[2]
    sds = jax.ShapeDtypeStruct
    role_s, half_s = role.reshape(1).astype(jnp.int32), half.reshape(1).astype(jnp.int32)

    o_time = 16
    o_text = o_time + 256 + width
    o_text2 = o_text + text
    o_head = o_text2 + width
    o_mod = o_head + 16
    six = 6 * width
    own_rows = -(-cols // 2)
    lanes = n * own_rows

    att_t = jnp.swapaxes(attention_weights, 1, 2)
    feed_t = jnp.swapaxes(feed_weights, 1, 2)
    side_t = side_weights.T
    side_b = low(side_t)
    pa = low(lax.dynamic_slice_in_dim(att_t, 4 * role, 4, 0))
    pb = low(att_t[8:12])
    pf = low(lax.dynamic_slice_in_dim(feed_t, 2 * role, 2, 0))
    pw = jnp.concatenate(
        [
            side_b[:, o_time:o_text],
            side_b[:, o_text2:o_head],
            low(vector_weights.T),
            side_b[:, 0:16],
            side_b[:, o_head:o_mod],
            jnp.zeros((cols, 128 - 77), bf16),
        ],
        axis=1,
    )
    text_rows = jnp.pad(side_b[:, o_text:o_text2], ((0, 2 * own_rows - cols), (0, 0)))
    py = lax.dynamic_slice_in_dim(text_rows, half * own_rows, own_rows, 0)
    pm = lax.dynamic_slice_in_dim(side_b[:, o_mod:], half * 3 * width, 3 * width, 1)
    freqs = jnp.exp(-math.log(10000.0) * jnp.arange(128, dtype=f32) / 128)
    angles = timesteps.astype(f32)[:, None] * freqs[None, :]
    level, snr = snr_weight(timesteps.astype(f32))
    pt = jnp.concatenate([jnp.cos(angles), jnp.sin(angles), snr[:, None]], axis=1)
    pt = jnp.pad(pt, ((0, 8 - count), (0, width - 257)))

    wa, wb, wf, ww, wy, wm, wt = comm_call(
        functools.partial(gather_kernel, n),
        1,
        (pa, pb, pf, pw, py, pm, pt),
        [
            sds((4, n, cols, width), bf16),
            sds((4, n, cols, width), bf16),
            sds((2, n, feed_cols, width), bf16),
            sds((n, cols, 1152), bf16),
            sds((n, own_rows, text), bf16),
            sds((n, cols, 3 * width), bf16),
            sds((n, 8, width), f32),
        ],
        [(4, 7, n), (7, n), (7, n), (7,)],
    )
    wa = wa.reshape(4, width, width)
    wb = wb.reshape(4, width, width)
    wf = wf.reshape(2, hidden, width)
    ww = ww.reshape(width, 1152)
    wy = wy.reshape(lanes, text)
    wm = wm.reshape(width, 3 * width)
    rank_s = d.reshape(1).astype(jnp.int32)
    per_clip = frames * (latents.shape[3] // 2) * (latents.shape[4] // 2)
    vec, hid, temb, mq_own, y2p, errs = local_call(
        functools.partial(condition_kernel, per_clip=per_clip, cols=cols),
        [
            sds((128, width), f32),
            sds((n * 8, width), f32),
            sds((n * 8, width), f32),
            sds((8, 3 * width), f32),
            sds((2, width, lanes), bf16),
            sds((8, 128), f32),
        ],
        [SM] + [VM] * 3,
        (rank_s, wt.reshape(n * 8, width), ww, wm),
    )
    mq = comm_call(
        mate_kernel, 2, (mq_own,), sds((2, 8, 3 * width), f32), [(1,), (1,), (1,)]
    )

    half_tokens = count * per_clip // 2

    def own_rows_of(value):
        return lax.dynamic_slice_in_dim(
            value.reshape(count * per_clip, 16), half * half_tokens, half_tokens, 0
        )

    def tokens(clean, noise):
        mix = level[:, None, None, None, None]
        noisy = low(jnp.sqrt(mix) * clean + jnp.sqrt(1.0 - mix) * noise)
        return jnp.pad(own_rows_of(patchify(noisy)), ((0, 0), (EMB0, 112 - EMB0)))

    def targets(noise):
        value = patchify(noise).reshape(count, frames, 2, 32, 16).transpose(0, 2, 1, 3, 4)
        return jnp.pad(own_rows_of(value), ((0, 0), (HEAD0, 112 - HEAD0)))

    tok = lax.cond(
        role == 0,
        tokens,
        lambda clean, noise: jnp.zeros((half_tokens, 128), bf16),
        latents,
        noise_draw,
    )
    places = np.arange(per_clip // frames)
    edge = latents.shape[3] // 2
    pos = np.concatenate(
        [sincos(places // edge, width // 2), sincos(places % edge, width // 2)], axis=1
    )
    pos = jnp.asarray(pos)
    timing = jnp.asarray(sincos(np.arange(frames), width))

    clip_rows = captions.shape[1]
    residuals = [
        sds((5, half_tokens, width), bf16),
        sds((3, half_tokens, width), f32),
        sds((half_tokens, hidden), f32),
        sds((count, 3, 256, 128), f32),
    ]
    residual_scratch = [pltpu.VMEM(v.shape, v.dtype) for v in residuals]
    h1s, hq, gq_own, kept_b, kept_f, kept_u, kept_p = local_call(
        functools.partial(first_kernel, cols),
        [
            sds((count, 2, 64, width), bf16),
            sds((count, LP, lanes), f32),
            sds((count, LP, lanes), bf16),
        ]
        + residuals,
        [SM] * 2 + [VM] * 7 + [ANY],
        (role_s, half_s, tok, pos, mq, vec, wa, wf, wy, captions),
        residual_scratch
        + [
            pltpu.VMEM((count, clip_rows, text), bf16),
            pltpu.SemaphoreType.DMA((count,)),
            pltpu.SemaphoreType.DMA((count, 4)),
        ],
        [VM] * 3 + [ANY] * 4,
    )
    later_noise, gq_own = lax.optimization_barrier((noise_draw, gq_own))
    target = lax.cond(
        role == 1,
        targets,
        lambda noise: jnp.zeros((half_tokens, 128), f32),
        later_noise,
    )
    target, h1s = lax.optimization_barrier((target, h1s))
    h1t, rgq, mqt = comm_call(
        functools.partial(forward_kernel, count),
        3,
        (h1s, gq_own, mq),
        [
            sds((count, 2, 64, width), bf16),
            sds((count, LP, lanes), bf16),
            sds((2, 8, 3 * width), f32),
        ],
        [(count, 2), (count, 2), (1,), (1,), (2,), (2,)],
    )

    ncl = (count + 1) // 2
    wide = sds((2, half_tokens, hidden), bf16)
    thin = sds((2, half_tokens, width), bf16)
    cap_like = sds((ncl, LP, width), bf16)
    dh1, acts_t, actf_t, actw_t, ybuf, dkv, grads_t, dmod_t, loss_t = local_call(
        temporal_kernel,
        [
            sds((count, 2, 64, width), bf16),
            sds((10, half_tokens, width), bf16),
            thin,
            wide,
            cap_like,
            sds((2, ncl, LP, width), f32),
            sds((128, width), f32),
            sds((count, 8, width), f32),
            sds((1, 128), f32),
        ],
        [SM] * 4 + [VM] * 13,
        (
            role_s, half_s, rank_s, caption_len, errs, h1t, timing, mqt, vec, temb, wa, wb, wf,
            gq_own, rgq, y2p, target,
        ),
        [pltpu.VMEM((ncl, KP, width), bf16), pltpu.VMEM((ncl, KP, width), bf16)],
    )
    dhs, extra, dmods_t = comm_call(
        functools.partial(backward_kernel, count),
        4,
        (dh1, dkv, dmod_t),
        [
            sds((count, 2, 64, width), bf16),
            sds((2, LP, width), f32),
            sds((2, count, 8, width), f32),
        ],
        [(count, 2), (count, 2), (1,), (1,), (2,), (2,)],
    )
    acts_s, actf_s, actw_s, dkvb, dy, vect, dmod = local_call(
        last_kernel,
        [
            sds((6, half_tokens, width), bf16),
            thin,
            wide,
            sds((2, ncl, LP, width), bf16),
            cap_like,
            sds((width, 128), f32),
            sds((count, 8, width), f32),
        ],
        [SM] * 2 + [VM] * 6 + [ANY] * 4 + [VM] * 5,
        (
            role_s, half_s, tok, mq, vec, wa, wb, wf, kept_b, kept_f, kept_u, kept_p, dhs, dkv,
            extra, grads_t, dmod_t,
        ),
        [pltpu.VMEM((128, width), f32)]
        + residual_scratch
        + [pltpu.SemaphoreType.DMA((count, 4))],
    )
    racts, ractf, ractw, rybuf, rdkvb, rdy, rdmod = comm_call(
        swap_kernel,
        5,
        (acts_s, acts_t, actf_s, actf_t, actw_s, actw_t, ybuf, dkvb, dy, dmod),
        [
            sds((10, half_tokens, width), bf16),
            thin,
            wide,
            cap_like,
            sds((2, ncl, LP, width), bf16),
            cap_like,
            sds((count, 8, width), f32),
        ],
        [(5,), (5,)],
    )
    line = n // 2
    wide_text = text + 128
    cut_text = wide_text // TEXT_CUTS
    block = (9, line, cols, width)
    tokens2 = 2 * half_tokens
    grad_own, grad_snd, text_part = local_call(
        weight_grad_kernel,
        [
            sds(block, f32),
            sds(block, bf16),
            sds((line, 2, own_rows, wide_text), bf16),
        ],
        [SM] * 3 + [ANY] * 9 + [VM] * 10 + [ANY],
        (
            role_s, half_s, rank_s, acts_s, acts_t, racts, actf_s, actf_t, ractf, actw_s, actw_t,
            ractw, ybuf, rybuf, dkvb, rdkvb, dy, rdy, gq_own, rgq, hq, y2p, captions,
        ),
        [
            pltpu.VMEM((10, tokens2, width), bf16),
            pltpu.VMEM((2, tokens2, width), bf16),
            pltpu.VMEM((2, tokens2, hidden), bf16),
            pltpu.VMEM((count, clip_rows, text), bf16),
            pltpu.SemaphoreType.DMA((4 + count,)),
        ],
    )

    mine0 = jnp.where(half == 0, dmod, rdmod)
    mine1 = jnp.where(half == 0, rdmod, dmod)
    sources = (mine0, mine1, dmods_t[0], dmods_t[1])
    dm_clip = []
    for clip in range(count):
        total = 0.0
        for seg in range(4):
            for i in range(count):
                if ((seg % 2) * count + i) // 2 == clip:
                    total = total + sources[seg][i]
        dm_clip.append(total)
    dm = jnp.concatenate(dm_clip, axis=0)

    whole_clips = n * 8
    text_block = (TEXT_CUTS, line, own_rows, cut_text)
    summed, text_sum, vsum, tile, grad_mod, grad_time2, grad_time1 = comm_call(
        functools.partial(scatter_kernel, n),
        6,
        (
            grad_own, grad_snd, text_part, dm, vect.reshape(n, cols, 128), loss_t,
            side_b[:, o_mod:], temb, ww, hid, wt.reshape(whole_clips, width),
        ),
        [
            sds((9, cols, width), f32),
            sds((own_rows, wide_text), bf16),
            sds((cols, 128), f32),
            sds((8, width), f32),
            sds((cols, six), f32),
            sds((cols, width), f32),
            sds((cols, 256), f32),
        ],
        [(9,), (9 + TEXT_CUTS,), (9 + TEXT_CUTS,)]
        + [(TEXT_CUTS + 1, line)] * 2
        + [(8, line)] * 4
        + [(2, n), (2, n), (2,), (TEXT_CUTS,), (TEXT_CUTS,), (n,), (n,)],
        [VM] * 7,
        in_specs=[ANY] * 5 + [VM] * 6,
        scratch=[
            pltpu.VMEM(block, f32),
            pltpu.VMEM(block, bf16),
            pltpu.VMEM((8,) + block[1:], f32),
            pltpu.VMEM((8,) + block[1:], f32),
            pltpu.VMEM(block[1:], bf16),
            pltpu.VMEM(block[1:], bf16),
            pltpu.VMEM((TEXT_CUTS, line, 2, own_rows, cut_text), bf16),
        ]
        + [pltpu.VMEM(text_block, bf16)] * 3
        + [
            pltpu.VMEM((n, cols, 128), f32),
            pltpu.VMEM((n * 8 * count, width), f32),
            pltpu.VMEM((n, whole_clips, 128), f32),
        ],
    )

    att_m = jnp.swapaxes(attention_momentum, 1, 2)
    feed_m = jnp.swapaxes(feed_momentum, 1, 2)
    ua, uf, ga2, gf2, grad_mod, grad_time2, grad_time1, grad_v, stat = comm_call(
        functools.partial(settle_kernel, n),
        8,
        (
            vsum, tile, summed, att_m, feed_m.reshape(16, cols, width), grad_mod, grad_time2,
            grad_time1,
        ),
        [
            sds((n, cols, width), f32),
            sds((n, 4, cols, width), f32),
            sds((12, cols, width), f32),
            sds((16, cols, width), f32),
            sds((cols, six), f32),
            sds((cols, width), f32),
            sds((cols, 256), f32),
            sds((cols, 128), f32),
            sds((8, 128), f32),
        ],
        [(1,), (8,), (n,), (1,), (7, 3), (7, 3), (7,), (2, 4), (2, 4), (n,), (n,)],
        [ANY] * 7 + [VM] * 2,
        in_specs=[VM] * 3 + [ANY] * 5,
        scratch=[
            pltpu.VMEM((4, cols, 128), f32),
            pltpu.VMEM((4, 8, width), f32),
            pltpu.VMEM((8, 128), f32),
            pltpu.VMEM((n, 8, 128), f32),
            pltpu.VMEM((8, cols, width), f32),
            pltpu.VMEM((8, cols, width), f32),
        ],
    )
    xa, xf = local_call(
        muon_kernel,
        [sds((width, width), bf16), sds((hidden, width), bf16)],
        [SM] + [VM] * 2,
        (half_s, ua.reshape(width, width), uf.reshape(hidden, width)),
        [pltpu.VMEM((width, width), f32), pltpu.VMEM((width, width), f32)],
    )
    xa_all, xf_all, gy12, gy22 = comm_call(
        functools.partial(spread_kernel, n),
        10,
        (xa.reshape(n, cols, width), xf.reshape(n, feed_cols, width), text_sum, summed),
        [
            sds((12, cols, width), bf16),
            sds((4, feed_cols, width), bf16),
            sds((2, own_rows, wide_text), bf16),
            sds((cols, width), f32),
        ],
        [(n,), (8,), (23, 3), (23, 3), (8,), (3,)],
    )

    clock = step_count[0].astype(f32)
    scal = jnp.stack([1.0 - jnp.power(beta_one, clock), 1.0 - jnp.power(beta_two, clock)])
    text_grad = gy12.reshape(2 * own_rows, wide_text)[:cols]
    side_m, side_v = side_first.T, side_second.T
    side_rows = side_t.shape[1]
    pieces = (
        ("embed", 0, 16),
        ("time", o_time, 256),
        ("time2", o_time + 256, width),
        ("text", o_text, text),
        ("text2", o_text2, width),
        ("head", o_head, 16),
        ("mod", o_mod, six),
    )
    rates = tuple(
        muon_rate * 0.2 * math.sqrt(columns) for columns in (n * cols, n * feed_cols)
    )
    grid = cols // 8 if cols % 8 == 0 else 1

    def by_rows(value):
        return value.reshape(-1, value.shape[-1])

    def rows_spec(value):
        return pl.BlockSpec((value.shape[0] // grid, value.shape[1]), lambda i: (i, 0))

    def whole_spec(value):
        return pl.BlockSpec(value.shape, lambda i: (0, 0))

    cutup = [by_rows(v) for v in (att_t, att_m, ga2, xa_all, feed_t, feed_m, gf2, xf_all)] + [
        side_t, side_m, side_v, grad_v, grad_time1, grad_time2, text_grad, gy22, grad_mod,
    ]
    fixed = [vector_weights, vector_first, vector_second, grad_v, text_grad]
    a_like, f_like, s_like = (sds(v.shape, f32) for v in (cutup[0], cutup[4], side_t))
    v_like = sds(vector_weights.shape, f32)

    def low_of(like):
        return sds(like.shape, bf16)

    row_outs = [
        a_like, a_like, low_of(a_like), f_like, f_like, low_of(f_like), s_like, s_like, s_like,
        low_of(s_like),
    ]
    whole_outs = [v_like, v_like, v_like, low_of(v_like), sds((1, 1), f32), sds((1, 1), f32)]
    (
        att_new, att_moment, att_low, feed_new, feed_moment, feed_low, side_new, side_first_new,
        side_second_new, side_low, vector_new, vector_first_new, vector_second_new, vector_low,
        loss_value, grad_norm,
    ) = pl.pallas_call(
        functools.partial(update_kernel, rates, pieces),
        grid=(grid,),
        out_shape=row_outs + whole_outs,
        in_specs=[SM, whole_spec(stat)] + [rows_spec(v) for v in cutup] + [whole_spec(v) for v in fixed],
        out_specs=[rows_spec(v) for v in row_outs] + [whole_spec(v) for v in whole_outs],
        compiler_params=pltpu.CompilerParams(vmem_limit_bytes=VMEM_LIMIT),
    )(scal, stat, *cutup, *fixed)

    def att(value):
        return value.reshape(att_t.shape)

    def feed(value):
        return value.reshape(feed_t.shape)

    def back(value):
        return jnp.swapaxes(value, -1, -2)

    return (
        loss_value[0, 0],
        grad_norm[0, 0],
        back(att(att_new)),
        back(att(att_moment)),
        back(feed(feed_new)),
        back(feed(feed_moment)),
        back(side_new),
        back(side_first_new),
        back(side_second_new),
        vector_new,
        vector_first_new,
        vector_second_new,
        back(att(att_low)),
        back(feed(feed_low)),
        back(side_low),
        vector_low,
    )


def solution(mesh):
    column = P(None, "dp")
    matrix = P(None, None, "dp")
    return jax.shard_map(
        body,
        mesh=mesh,
        in_specs=(
            P("dp", None, None, None, None),
            P("dp", None, None, None, None),
            P("dp"),
            P("dp", None, None),
            P("dp"),
            matrix,
            matrix,
            column,
            column,
            matrix,
            matrix,
            column,
            column,
            column,
            column,
            P(),
        ),
        out_specs=(
            P(),
            P(),
            matrix,
            matrix,
            matrix,
            matrix,
            column,
            column,
            column,
            column,
            column,
            column,
            matrix,
            matrix,
            column,
            column,
        ),
        check_vma=False,
    )
```

```python
import functools
import math

import jax
import jax.numpy as jnp
import numpy as np
from jax import lax
from jax.experimental import pallas as pl
from jax.experimental.pallas import tpu as pltpu
from jax.sharding import PartitionSpec as P

HEADS = 6
HEAD = 64
LP = 304
KP = 384

highest = lax.Precision.HIGHEST
snr_gamma = 5.0
max_norm = 0.005
momentum_decay = 0.95
muon_rate = 0.05
adam_rate = 0.02
beta_one = 0.9
beta_two = 0.999
weight_decay = 0.01
coef_a = 3.4445
coef_b = -4.775
coef_c = 2.0315

f32, bf16 = jnp.float32, jnp.bfloat16
MESH = pl.DeviceIdType.MESH
ANY = pl.BlockSpec(memory_space=pl.ANY)
VM = pl.BlockSpec(memory_space=pltpu.VMEM)
SM = pl.BlockSpec(memory_space=pltpu.SMEM)
VMEM_LIMIT = 60000 * 1024


def low(value):
    return value.astype(bf16)


def nt(left, right):
    return lax.dot_general(left, right, (((1,), (1,)), ((), ())), preferred_element_type=f32)


def nn(left, right):
    return lax.dot_general(left, right, (((1,), (0,)), ((), ())), preferred_element_type=f32)


def tn(left, right):
    return lax.dot_general(left, right, (((0,), (0,)), ((), ())), preferred_element_type=f32)


def snr_weight(steps_t):
    level = jnp.cos((steps_t / 1000.0 + 0.008) / 1.008 * (math.pi / 2)) ** 2
    ratio = level / (1.0 - level)
    return level, jnp.minimum(ratio, snr_gamma) / ratio


def patchify(frames):
    clips, count, channels, height, breadth = frames.shape
    grid = frames.reshape(clips, count, channels, height // 2, 2, breadth // 2, 2)
    grid = grid.transpose(0, 1, 3, 5, 4, 6, 2)
    return grid.reshape(clips, count, (height // 2) * (breadth // 2), 4 * channels)


def sincos(places, model_width):
    half_width = model_width // 2
    freqs = np.exp(-math.log(10000.0) * np.arange(half_width) / half_width)
    angles = places[:, None] * freqs[None, :]
    return np.concatenate([np.sin(angles), np.cos(angles)], axis=1).astype(np.float32)


def col_sum(value):
    return jnp.sum(value.astype(f32), axis=0, keepdims=True)


def norm(value):
    centred = value - jnp.mean(value, axis=-1, keepdims=True)
    inv = lax.rsqrt(jnp.mean(centred * centred, axis=-1, keepdims=True) + 1e-06)
    return centred * inv, inv


def norm_back(grad, normed, inv):
    return inv * (
        grad
        - jnp.mean(grad, axis=-1, keepdims=True)
        - normed * jnp.mean(grad * normed, axis=-1, keepdims=True)
    )


GELU_C = math.sqrt(2.0 / math.pi)


def gelu(value):
    inner = GELU_C * (value + 0.044715 * (value * value * value))
    return value * (0.5 * (1.0 + jnp.tanh(inner)))


def gelu_both(value):
    square = value * value
    tanh = jnp.tanh(GELU_C * (value + 0.044715 * (square * value)))
    cdf = 0.5 * (1.0 + tanh)
    slope = 0.5 * (1.0 - tanh * tanh) * (GELU_C * (1.0 + 3 * 0.044715 * square))
    return value * cdf, cdf + value * slope


def lanes_low():
    lane = lax.broadcasted_iota(jnp.int32, (1, 128), 1)
    first = jnp.where(lane < HEAD, 1.0, 0.0)
    return low(first), low(1.0 - first), lane < HEAD


def stack_heads(pair, first, second):
    return jnp.concatenate([pair * first, pair * second], axis=0)


def attend(queries, keys, values, allowed):
    first, second, lower = lanes_low()
    rows = queries.shape[0]
    mixed, probs = [], []
    for pair in range(HEADS // 2):
        cut = slice(pair * 128, pair * 128 + 128)
        scores = nt(stack_heads(queries[:, cut], first, second), keys[:, cut]) * 0.125
        scores = jnp.where(allowed, scores, -1e30)
        weight = jnp.exp(scores - jnp.max(scores, axis=-1, keepdims=True))
        prob = weight / jnp.sum(weight, axis=-1, keepdims=True)
        probs.append(prob)
        out = nn(low(prob), values[:, cut])
        mixed.append(jnp.where(lower, out[:rows], out[rows:]))
    return low(jnp.concatenate(mixed, axis=1)), probs


def attend_back(grad, queries, keys, values, probs):
    first, second, lower = lanes_low()
    rows = queries.shape[0]
    dq, dk, dv = [], [], []
    for pair in range(HEADS // 2):
        cut = slice(pair * 128, pair * 128 + 128)
        stacked = stack_heads(grad[:, cut], first, second)
        prob = probs[pair]
        dv.append(tn(low(prob), stacked))
        dprob = nt(stacked, values[:, cut])
        dscore = low(prob * (dprob - jnp.sum(prob * dprob, axis=-1, keepdims=True)))
        part = nn(dscore, keys[:, cut])
        dq.append(jnp.where(lower, part[:rows], part[rows:]) * 0.125)
        dk.append(tn(dscore, stack_heads(queries[:, cut], first, second)) * 0.125)
    return tuple(jnp.concatenate(piece, axis=1) for piece in (dq, dk, dv))


def self_forward(x, mods, weights, bias, allowed):
    normed, inv = norm(x)
    a = low(normed * (1.0 + mods[1]) + mods[0])
    q = low(nt(a, weights[0]) + bias[0])
    k = low(nt(a, weights[1]))
    v = low(nt(a, weights[2]) + bias[1])
    o, probs = attend(q, k, v, allowed)
    branch = nt(o, weights[3]) + bias[2]
    return x + mods[2] * branch, (normed, inv, a, q, k, v, o, probs, branch)


def self_backward(dx, kept, mods, weights):
    normed, inv, a, q, k, v, o, probs, branch = kept
    dm2 = col_sum(dx * branch)
    dbr = low(dx * mods[2])
    do = low(nn(dbr, weights[3]))
    dq, dk, dv = (low(piece) for piece in attend_back(do, q, k, v, probs))
    da = nn(dq, weights[0]) + nn(dk, weights[1]) + nn(dv, weights[2])
    dm1, dm0 = col_sum(da * normed), col_sum(da)
    dx = dx + norm_back(da * (1.0 + mods[1]), normed, inv)
    return dx, (dm0, dm1, dm2), (col_sum(dq), col_sum(dv), col_sum(dbr)), (a, dq, dk, dv, o, dbr)


def feed_forward(x, mods, feed, bias_up, bias_down):
    normed, inv = norm(x)
    c = low(normed * (1.0 + mods[4]) + mods[3])
    u = nt(c, feed[0]) + bias_up
    g = low(gelu(u))
    branch = nn(g, feed[1]) + bias_down
    return x + mods[5] * branch, (normed, inv, c, u, g, branch)


def feed_backward(dx, kept, mods, feed):
    normed, inv, c, u, g, branch = kept
    dm5 = col_sum(dx * branch)
    dbr = low(dx * mods[5])
    value, slope = gelu_both(u)
    g = low(value)
    du = low(nt(dbr, feed[1]) * slope)
    dc = nn(du, feed[0])
    dm4, dm3 = col_sum(dc * normed), col_sum(dc)
    dx = dx + norm_back(dc * (1.0 + mods[4]), normed, inv)
    return dx, (dm3, dm4, dm5), (col_sum(du), col_sum(dbr)), (c, dbr, du, g)


def pair_mask(kind):
    row = lax.broadcasted_iota(jnp.int32, (256, 128), 0) % 128
    col = lax.broadcasted_iota(jnp.int32, (256, 128), 1)
    if kind == 0:
        return row // 64 == col // 64
    return row % 32 == col % 32


VEC0, EMB0, HEAD0 = 0, 45, 61


def mod_rows(mq, vec, table, clip):
    rows = []
    for r in range(6):
        at = (r % 3) * 384
        rows.append(
            mq[r // 3, pl.ds(clip, 1), at : at + 384]
            + vec[3 + r : 4 + r]
            + vec[table + r : table + r + 1]
        )
    return rows


def up_bias(vec, start):
    return jnp.concatenate([vec[start + i : start + i + 1] for i in range(4)], axis=1)


def pack_kernel(role, half, offsets, att, feed, side, vec, pa, pb, pf, pw, py, pm, wm):
    time, text, text2, head, mod = offsets
    width, per, rows = att.shape[2], pf.shape[0], py.shape[0]

    def rounded(at, size):
        return low(side[:, at : at + size])

    first = text - time
    pw[:, 0:first] = rounded(time, first)
    pw[:, first : first + width] = rounded(text2, width)
    cols = pw.shape[0]
    pw[:, first + width :] = low(jnp.concatenate(
        [vec[...], side[:, 0:16], side[:, head : head + 16], jnp.zeros((cols, 51), f32)], axis=1
    ))
    wm[...] = rounded(mod, 6 * width)
    for r in range(2):

        @pl.when(role[0] == r)
        def _():
            pa[...] = low(att[4 * r : 4 * r + 4])
            pf[...] = low(feed[per * r : per * r + per])
            if r == 1:
                pb[...] = low(att[8:12])

    for h in range(2):

        @pl.when(half[0] == h)
        def _():
            pm[...] = rounded(mod + h * 3 * width, 3 * width)
            top = min((h + 1) * rows, cols)
            py[0 : top - h * rows, :] = low(side[h * rows : top, text : text + py.shape[1]])


def units_of(hand, lanes, width, cols):
    per = -(-cols // 2)
    unit = lax.broadcasted_iota(jnp.int32, (lanes, width), 0)
    column = lax.broadcasted_iota(jnp.int32, (lanes, width), 1)
    inside = hand * per + unit % per
    match = jnp.logical_and((unit // per) * cols + inside == column, inside < cols)
    return low(jnp.where(match, 1.0, 0.0))


def condition_kernel(rank, wt, ww, wm, vec, hid, temb, mq, y2p, errs, *, per_clip, cols):
    turned = jnp.transpose(ww[:, 1024:1152].astype(f32))
    vec[...] = turned
    feature = low(wt[:, 0:256])
    first = nt(feature, ww[:, 0:256]) + turned[1:2]
    hid[...] = first
    second = nt(low(first * jax.nn.sigmoid(first)), ww[:, 256:640]) + turned[2:3]
    temb[...] = second
    own = temb[pl.ds(pl.multiple_of(rank[0] * 8, 8), 8), :]
    mq[...] = nn(low(own * jax.nn.sigmoid(own)), wm[...])
    for h in range(2):
        y2p[h] = low(nt(ww[:, 640:1024], units_of(h, y2p.shape[2], y2p.shape[1], cols)))
    total = jnp.sum(wt[:, 256:257], axis=0, keepdims=True)
    weight = wt[pl.ds(pl.multiple_of(rank[0] * 8, 8), 8), 256:257] / (total * (per_clip * 16.0))
    errs[...] = jnp.broadcast_to(weight, errs.shape)


def embed_chunk(tok_ref, vec, pos_ref, chunk):
    tokens = tok_ref[pl.ds(pl.multiple_of(chunk * 128, 128), 128), :]
    places = pos_ref[...] + vec[0:1]
    return low(nn(tokens, low(vec[...])) + jnp.concatenate([places, places], axis=0)), tokens


def spatial_bias(vec):
    return (vec[11:12], vec[12:13], vec[13:14])


def residual_copies(sources, targets, sems):
    def of(chunk):
        rows = pl.ds(pl.multiple_of(chunk * 128, 128), 128)
        cuts = [lambda r: r.at[:, rows], lambda r: r.at[:, rows], lambda r: r.at[rows],
                lambda r: r.at[chunk]]
        return [
            pltpu.make_async_copy(cut(src), cut(dst), sems.at[chunk, i])
            for i, (cut, src, dst) in enumerate(zip(cuts, sources, targets))
        ]

    return of


def first_kernel(
    cols, role, half, tok, pos, mq, vec, wa, wf, wy, captions,
    h1, hq, gq, out_b, out_f, out_u, out_p, kept_b, kept_f, kept_u, kept_p, cap, sems, ksem,
):
    @pl.when(role[0] == 1)
    def _():
        clips = captions.shape[0]
        for c in range(clips):
            pltpu.make_async_copy(captions.at[c], cap.at[c], sems.at[c]).start()
        bias = nt(low(vec[9:10]), units_of(half[0], wy.shape[0], vec.shape[1], cols))
        def layer(c, carry):
            pltpu.make_async_copy(captions.at[c], cap.at[c], sems.at[c]).wait()
            value = nt(cap[c], wy[...]) + bias
            rows = value.shape[0]
            pad = jnp.zeros((LP - rows, value.shape[1]), f32)
            hq[c] = jnp.concatenate([value, pad], axis=0)
            gq[c] = low(jnp.concatenate([gelu(value), pad], axis=0))
            return carry

        lax.fori_loop(0, clips, layer, 0)

    @pl.when(role[0] == 0)
    def _():
        allowed = pair_mask(0)
        count = h1.shape[0]
        bu = up_bias(vec, 14)
        residuals = residual_copies((kept_b, kept_f, kept_u, kept_p), (out_b, out_f, out_u, out_p), ksem)

        def step(chunk, carry):
            @pl.when(chunk > 0)
            def _():
                for copy in residuals(chunk - 1):
                    copy.start()

            m = mod_rows(mq, vec, 19, (half[0] * count + chunk) // 2)
            h0, _ = embed_chunk(tok, vec, pos, chunk)
            x1, kept = self_forward(h0.astype(f32), m, wa, spatial_bias(vec), allowed)
            x, kept_feed = feed_forward(x1, m, wf, bu, vec[18:19])
            out = low(x)
            where = pl.ds(pl.multiple_of(chunk * 128, 128), 128)
            for i, value in enumerate((h0,) + kept[3:7]):
                kept_b[i, where, :] = value
            for i, value in enumerate((x1, kept[8], kept_feed[5])):
                kept_f[i, where, :] = value
            kept_u[where, :] = kept_feed[3]
            for pair in range(3):
                kept_p[chunk, pair] = kept[7][pair]
            for frame in range(2):
                for part in range(2):
                    start = frame * 64 + part * 32
                    h1[chunk, part, frame * 32 : frame * 32 + 32, :] = out[start : start + 32]
            return carry

        lax.fori_loop(0, count, step, 0)
        for copy in residuals(count - 1):
            copy.start()
        for chunk in range(count):
            for copy in residuals(chunk):
                copy.wait()


def last_kernel(
    role, half, tok, mq, vec, wa, wb, wf, in_b, in_f, in_u, in_p, dh, dkv, extra, grads_t, dmod_t,
    acts, actf, actw, dkvb, dy, vect, dmod, grads, kept_b, kept_f, kept_u, kept_p, ksem,
):
    @pl.when(role[0] == 0)
    def _():
        grads[...] = jnp.zeros_like(grads)
        dmod[...] = jnp.zeros_like(dmod)
        count = dh.shape[0]
        residuals = residual_copies((in_b, in_f, in_u, in_p), (kept_b, kept_f, kept_u, kept_p), ksem)
        for chunk in range(count):
            for copy in residuals(chunk):
                copy.start()

        def step(chunk, carry):
            for copy in residuals(chunk):
                copy.wait()
            m = mod_rows(mq, vec, 19, (half[0] * count + chunk) // 2)
            where = pl.ds(pl.multiple_of(chunk * 128, 128), 128)
            tokens = tok[where, :]
            h0, q, k, v, o = (kept_b[i, where, :] for i in range(5))
            x1, branch, branch_f = (kept_f[i, where, :] for i in range(3))
            normed, inv = norm(h0.astype(f32))
            a = low(normed * (1.0 + m[1]) + m[0])
            probs = [kept_p[chunk, pair] for pair in range(3)]
            kept = (normed, inv, a, q, k, v, o, probs, branch)
            normed_f, inv_f = norm(x1)
            c = low(normed_f * (1.0 + m[4]) + m[3])
            kept_feed = (normed_f, inv_f, c, kept_u[where, :], None, branch_f)
            parts = []
            for frame in range(2):
                for part in range(2):
                    parts.append(dh[chunk, part, frame * 32 : frame * 32 + 32, :])
            dx = jnp.concatenate(parts, axis=0).astype(f32)
            dx, dm_f, db_f, act_f = feed_backward(dx, kept_feed, m, wf)
            dx, dm_a, db_a, act_a = self_backward(dx, kept, m, wa)
            dh0 = low(dx)
            for i, value in enumerate(act_a):
                acts[i, where, :] = value
            for i in range(2):
                actf[i, where, :] = act_f[i]
                actw[i, where, :] = act_f[2 + i]
            mods = dm_a + dm_f
            dmod[chunk, 0:6, :] = jnp.concatenate(mods, axis=0)
            grads[...] += tn(tokens, dh0)
            grads[0:1] += col_sum(dh0)
            for i in range(3):
                grads[11 + i : 12 + i] += db_a[i]
            for i in range(4):
                grads[14 + i : 15 + i] += db_f[0][:, i * 384 : i * 384 + 384]
            grads[18:19] += db_f[1]
            for i in range(6):
                grads[19 + i : 20 + i] += mods[i]
            return carry

        lax.fori_loop(0, count, step, 0)

    @pl.when(role[0] == 1)
    def _():
        grads[...] = grads_t[...]
        dmod[...] = dmod_t[...]
        dy[...] = jnp.zeros_like(dy)
        dkvb[...] = jnp.zeros_like(dkvb)
        ncl = dy.shape[0]
        for c in range(ncl):

            @pl.when(jnp.logical_or(half[0] == 0, c > 0))
            def _():
                pieces = []
                for i in range(2):
                    value = dkv[i, c]
                    if c == ncl - 1:
                        value = value + jnp.where(half[0] == 0, extra[i], 0.0)
                    pieces.append(low(value))
                dkvb[0, c], dkvb[1, c] = pieces
                back = low(nn(pieces[0], wb[1]) + nn(pieces[1], wb[2]))
                dy[c] = back
                grads[40:41] += col_sum(pieces[1])
                grads[10:11] += col_sum(back)

    vect[...] = jnp.transpose(grads[...])


def temporal_kernel(
    role, half, rank, lens, errw, h1, timing, mq, vec, temb, wa, wb, wf, gq, rgq, y2p, target,
    dh1, acts, actf, actw, ybuf, dkv, grads, dmod, loss, kx, vx,
):
    @pl.when(role[0] == 0)
    def _():
        loss[...] = jnp.zeros_like(loss)

    @pl.when(role[0] == 1)
    def _():
        allowed = pair_mask(1)
        count = h1.shape[0]
        ncl = ybuf.shape[0]
        for ref in (kx, vx, dkv, grads, loss):
            ref[...] = jnp.zeros_like(ref)
        first_clip = (half[0] * count) // 2

        def features(c, carry):
            clip = jnp.minimum(first_clip + c, gq.shape[0] - 1)
            y = nt(gq[clip], y2p[half[0]]) + nt(rgq[clip], y2p[1 - half[0]])
            y = low(y + vec[10:11])
            ybuf[c] = y
            kx[c, 0:LP, :] = low(nt(y, wb[1]))
            vx[c, 0:LP, :] = low(nt(y, wb[2]) + vec[40:41])
            return carry

        lax.fori_loop(0, ncl, features, 0)
        bu = up_bias(vec, 28)
        lane = lax.broadcasted_iota(jnp.int32, (1, 128), 1)
        real = jnp.logical_and(lane >= HEAD0, lane < HEAD0 + 16)
        bias_h = pltpu.roll(jnp.broadcast_to(vec[44:45, 0:128], (8, 128)), HEAD0, 1)[0:1]
        head = low(vec[...])

        def step(chunk, carry):
            clip = (half[0] * count + chunk) // 2
            here = clip - first_clip
            m = mod_rows(mq, vec, 33, clip)
            emb = temb[pl.ds(rank[0] * 8 + clip, 1), :]
            m6, m7 = vec[42:43] + emb, vec[43:44] + emb
            h = jnp.concatenate([h1[chunk, 0], h1[chunk, 1]], axis=0)
            x = h.astype(f32) + jnp.concatenate(
                [jnp.broadcast_to(timing[i : i + 1], (32, h.shape[1])) for i in range(4)], axis=0
            )
            x, kept = self_forward(x, m, wa, (vec[25:26], vec[26:27], vec[27:28]), allowed)
            xb = low(x)
            cq = low(nt(xb, wb[0]) + vec[39:40])
            keys, values = kx[here], vx[here]
            seen = lax.broadcasted_iota(jnp.int32, (1, KP), 1) < lens[clip]
            co, probs = attend(cq, keys, values, seen)
            x = x + (nt(co, wb[3]) + vec[41:42])
            x, kept_f = feed_forward(x, m, wf, bu, vec[32:33])
            h2 = low(x).astype(f32)
            normed, inv = norm(h2)
            cf = low(normed * (1.0 + m7) + m6)
            where = pl.ds(pl.multiple_of(chunk * 128, 128), 128)
            diff = jnp.where(real, nt(cf, head) + bias_h - target[where, :], 0.0)
            scale = errw[pl.ds(clip, 1), 0:1]
            loss[...] += col_sum(diff * diff) * scale
            dpred = low(diff * (2.0 * scale))
            dcf = nn(dpred, head)
            grads[...] += tn(dpred, cf)
            dbh = pltpu.roll(jnp.broadcast_to(col_sum(dpred), (8, 128)), 128 - HEAD0, 1)[0:1]
            grads[44:45, 0:128] += dbh
            dm7, dm6 = col_sum(dcf * normed), col_sum(dcf)
            dx = low(norm_back(dcf * (1.0 + m7), normed, inv)).astype(f32)
            dx, dm_f, db_f, act_f = feed_backward(dx, kept_f, m, wf)
            dcbr = low(dx)
            dco = low(nn(dcbr, wb[3]))
            dcq, dck, dcv = attend_back(dco, cq, keys, values, probs)
            dcq = low(dcq)
            dkv[0, here] += dck[0:LP]
            dkv[1, here] += dcv[0:LP]
            dx = dx + nn(dcq, wb[0])
            dx, dm_a, db_a, act_a = self_backward(dx, kept, m, wa)
            out = low(dx)
            dh1[chunk, 0] = out[0:64]
            dh1[chunk, 1] = out[64:128]
            for i, value in enumerate(act_a + (xb, dcq, co, dcbr)):
                acts[i, where, :] = value
            for i in range(2):
                actf[i, where, :] = act_f[i]
                actw[i, where, :] = act_f[2 + i]
            mods = dm_a + dm_f + (dm6, dm7)
            dmod[chunk] = jnp.concatenate(mods, axis=0)
            for i in range(3):
                grads[25 + i : 26 + i] += db_a[i]
            for i in range(4):
                grads[28 + i : 29 + i] += db_f[0][:, i * 384 : i * 384 + 384]
            grads[32:33] += db_f[1]
            for i in range(6):
                grads[33 + i : 34 + i] += mods[i]
            grads[39:40] += col_sum(dcq)
            grads[41:42] += col_sum(dcbr)
            grads[42:43] += dm6
            grads[43:44] += dm7
            return carry

        lax.fori_loop(0, count, step, 0)


def weight_grad_kernel(
    role, half, rank, acts_s, acts_t, racts, actf_s, actf_t, ractf, actw_s, actw_t, ractw,
    ybuf, rybuf, dkvb, rdkvb, dy, rdy, gq, rgq, hq, y2p, captions,
    own, snd, text_out, la, lf, lw, cap, square, turned, sums, sems,
):
    tokens = acts_s.shape[1]
    line, cols = own.shape[1], own.shape[2]
    odd = lax.rem(rank[0], 2) == 1
    near, far = pl.ds(0, tokens), pl.ds(tokens, tokens)

    def copies(r, h):
        if h == 0:
            local = acts_s if r == 0 else acts_t
            size = pl.ds(0, local.shape[0])
            return [(local, la.at[size, near], 0), (racts.at[size], la.at[size, far], 1)]
        thin, wide = ((actf_s, actw_s), (actf_t, actw_t))[r]
        return [
            (thin, lf.at[:, near], 0), (ractf, lf.at[:, far], 1),
            (wide, lw.at[:, near], 2), (ractw, lw.at[:, far], 3),
        ]

    def text():
        return [(captions.at[c], cap.at[c], 4 + c) for c in range(captions.shape[0])]

    def run(group, finish):
        for src, dst, i in group:
            copy = pltpu.make_async_copy(src, dst, sems.at[i])
            copy.wait() if finish else copy.start()

    for r in range(2):
        for h in range(2):

            @pl.when(jnp.logical_and(role[0] == r, half[0] == h))
            def _():
                run(copies(r, h), False)
                if r == 1:
                    run(text(), False)
                run(copies(r, h), True)

    def keep(unit, at, first, second):
        own[unit, at] = jnp.where(odd, second, first)
        snd[unit, at] = low(jnp.where(odd, first, second))

    def keep_square(unit, value):
        for p in range(line):
            cut = 2 * p * cols
            keep(unit, p, value[cut : cut + cols], value[cut + cols : cut + 2 * cols])

    def matrix(unit, left, right):
        keep_square(unit, tn(la[left], la[right]))

    @pl.when(half[0] == 0)
    def _():
        def square(i, carry):
            left = jnp.where(i < 3, i + 1, 2 * i - 1)
            right = jnp.where(i < 3, 0, 2 * i - 2)
            matrix(jnp.where(i < 5, i, 7), left, right)
            return carry

        lax.fori_loop(0, 4 + 2 * role[0], square, 0)

        @pl.when(role[0] == 1)
        def _():
            def cross(i, carry):
                total = tn(dkvb[i, 0], ybuf[0]) + tn(rdkvb[i, 0], rybuf[0])
                for c in range(1, ybuf.shape[0]):
                    total = total + tn(dkvb[i, c], ybuf[c]) + tn(rdkvb[i, c], rybuf[c])
                keep_square(5 + i, total)
                return carry

            lax.fori_loop(0, 2, cross, 0)

    @pl.when(half[0] == 1)
    def _():
        side = la.shape[2]
        tiles = lw.shape[2] // side
        block = 4 * cols
        per = side // (2 * block)

        def feed(i, carry):
            pair, tile = i // tiles, lax.rem(i, tiles)
            lanes = pl.ds(pl.multiple_of(tile * side, 128), side)
            value = tn(lw[pair, :, lanes], lf[pair])
            for p in range(per):
                for j in range(4):
                    at = 2 * p * block + j * cols
                    keep(
                        4 * pair + j, tile * per + p, value[at : at + cols],
                        value[at + block : at + block + cols],
                    )
            return carry

        lax.fori_loop(0, 2 * tiles, feed, 0)

    @pl.when(role[0] == 1)
    def _():
        clips = captions.shape[0]
        rows = captions.shape[1]
        def dy_of(c):
            h = (2 * c) // clips
            at = c - (h * clips) // 2
            return jnp.where(half[0] == h, dy[at].astype(f32), rdy[at].astype(f32)).astype(bf16)

        @pl.when(half[0] == 1)
        def _():
            shape = (y2p.shape[2], y2p.shape[1], cols)
            mine, theirs = units_of(1, *shape), units_of(0, *shape)
            square[...] = jnp.zeros_like(square)

            def one(c, carry):
                plain = low(nn(gq[c], mine) + nn(rgq[c], theirs))
                square[...] += tn(dy_of(c), plain)
                return carry

            lax.fori_loop(0, clips, one, 0)
            keep_square(8, square[...])

        units = text_out.shape[2]

        def keep_text(lanes, value):
            for p in range(line):
                for q in range(2):
                    cut = (2 * p + q) * units
                    text_out[p, q, :, lanes] = low(value[cut : cut + units])

        ones = jnp.ones((LP, 128), bf16)
        sums[...] = jnp.zeros_like(sums)

        def turn(c, carry):
            back = nn(dy_of(c), y2p[half[0]]) * gelu_both(hq[c])[1]
            turned[c] = low(jnp.transpose(back))
            sums[...] += nn(turned[c], ones)
            return carry

        lax.fori_loop(0, clips, turn, 0)
        run(text(), True)

        def text_tile(t, carry):
            lanes = pl.ds(pl.multiple_of(t * 512, 512), 512)
            total = nn(turned[0, :, 0:rows], cap[0, :, lanes])
            for c in range(1, clips):
                total = total + nn(turned[c, :, 0:rows], cap[c, :, lanes])
            keep_text(lanes, total)
            return carry

        lax.fori_loop(0, captions.shape[2] // 512, text_tile, 0)
        keep_text(pl.ds(captions.shape[2], 128), sums[...])


def halves(value):
    first = low(value)
    return first, low(value - first.astype(f32))


def lefts(value, axis=1):
    first, second = halves(value)
    return jnp.concatenate([first, first, second], axis=axis)


def rights(value, axis=0):
    first, second = halves(value)
    return jnp.concatenate([first, second, first], axis=axis)


def gram_of(value, dot):
    first, second = halves(value)
    both = dot(first, first), dot(first, second)
    return both[0] + (both[1] + jnp.transpose(both[1]))


def muon_kernel(half, ua, uf, xa, xf, gram, whole):
    @pl.when(half[0] == 0)
    def _():
        u = ua[...]
        whole[...] = u / (jnp.sqrt(jnp.sum(u * u)) + 1e-07)

        def sweep(i, carry):
            x = whole[...]
            square = gram_of(x, nt)
            poly = coef_b * square + coef_c * gram_of(square, nt)
            whole[...] = coef_a * x + nn(lefts(poly), rights(x))
            return carry

        lax.fori_loop(0, 5, sweep, 0)
        xa[...] = low(whole[...])

    @pl.when(half[0] == 1)
    def _():
        width = uf.shape[1]
        tiles = uf.shape[0] // width
        gram[...] = jnp.zeros_like(gram)

        def rows(t):
            return pl.ds(pl.multiple_of(t * width, 128), width)

        def first(t, carry):
            piece = uf[rows(t), :]
            gram[...] += gram_of(piece, tn)
            return carry

        lax.fori_loop(0, tiles, first, 0)
        row = lax.broadcasted_iota(jnp.int32, (width, width), 0)
        col = lax.broadcasted_iota(jnp.int32, (width, width), 1)
        eye = jnp.where(row == col, 1.0, 0.0)
        start = gram[...]
        inv = 1.0 / (jnp.sqrt(jnp.sum(start * eye)) + 1e-07)
        gram[...] = start * (inv * inv)
        whole[...] = eye * inv

        def poly_of(a):
            return coef_a * eye + coef_b * a + coef_c * nn(lefts(a), rights(a))

        def sweep(i, carry):
            a = gram[...]
            left = lefts(poly_of(a))
            both = nn(left, rights(jnp.concatenate([a, whole[...]], axis=1)))
            whole[...] = both[:, width:]

            @pl.when(i < 4)
            def _():
                gram[...] = nn(left, rights(both[:, :width]))

            return carry

        lax.fori_loop(0, 5, sweep, 0)
        last = rights(whole[...])

        def apply(t, carry):
            xf[rows(t), :] = low(nn(lefts(uf[rows(t), :]), last))
            return carry

        lax.fori_loop(0, tiles, apply, 0)


def local_call(kernel, out_shape, in_specs, args, scratch=(), out_specs=None):
    return pl.pallas_call(
        kernel,
        out_shape=out_shape,
        in_specs=in_specs,
        out_specs=jax.tree.map(lambda _: VM, out_shape) if out_specs is None else out_specs,
        scratch_shapes=scratch,
        compiler_params=pltpu.CompilerParams(vmem_limit_bytes=VMEM_LIMIT),
    )(*args)


def here():
    return lax.axis_index("dp"), lax.axis_index("segment")


def dev(d, s):
    return {"dp": d, "segment": s}


def remote(src, dst, send, recv, target):
    return pltpu.make_async_remote_copy(
        src_ref=src, dst_ref=dst, send_sem=send, recv_sem=recv, device_id=target,
        device_id_type=MESH,
    )


def greet(targets):
    barrier = pltpu.get_barrier_semaphore()
    for target in targets:
        pl.semaphore_signal(barrier, inc=1, device_id=target, device_id_type=MESH)
    pl.semaphore_wait(barrier, len(targets))


def greet_dp(n, extra=()):
    d, s = here()
    barrier = pltpu.get_barrier_semaphore()

    def step(k, carry):
        pl.semaphore_signal(
            barrier, inc=1, device_id=dev(lax.rem(d + k, n), s), device_id_type=MESH
        )
        return carry

    lax.fori_loop(1, n, step, 0)
    for target in extra:
        pl.semaphore_signal(barrier, inc=1, device_id=target, device_id_type=MESH)
    pl.semaphore_wait(barrier, n - 1 + len(extra))


def comm_call(kernel, cid, args, out_shape, sems, out_specs=None, scratch=(), in_specs=None):
    if out_specs is None:
        out_specs = jax.tree.map(lambda _: ANY, out_shape)
    return pl.pallas_call(
        kernel,
        out_shape=out_shape,
        in_specs=[ANY] * len(args) if in_specs is None else in_specs,
        out_specs=out_specs,
        scratch_shapes=list(scratch) + [pltpu.SemaphoreType.DMA(shape) for shape in sems],
        compiler_params=pltpu.CompilerParams(
            collective_id=cid, has_side_effects=True, vmem_limit_bytes=VMEM_LIMIT
        ),
    )(*args)


def gather_kernel(n, pa, pb, pf, pw, py, pm, pt, wa, wb, wf, ww, wy, wm, wt,
                  send, recv, crecv, own):
    pair = 2 if n % 2 == 0 else 1
    line = n // pair
    d, s = here()
    role, half = s // 2, lax.rem(s, 2)
    a, x = d // pair, lax.rem(d, pair)
    mate = dev(d, role * 2 + 1 - half)
    above, below = dev(d + pair, s), dev(d - pair, s)
    across = dev(a * pair + (pair - 1 - x), s)
    barrier = pltpu.get_barrier_semaphore()

    def signal(target):
        pl.semaphore_signal(barrier, inc=1, device_id=target, device_id_type=MESH)

    signal(mate)
    if pair == 2:
        signal(across)

    @pl.when(a < line - 1)
    def _():
        signal(above)

    @pl.when(a > 0)
    def _():
        signal(below)

    pl.semaphore_wait(barrier, pair + jnp.minimum(a, 1) + jnp.minimum(line - 1 - a, 1))

    def two(i, ref, out):
        return [
            (i, ref.at[pl.ds(0, 2)], out.at[pl.ds(0, 2)], 2),
            (i + 1, ref.at[pl.ds(2, 2)], out.at[pl.ds(2, 2)], 2),
        ]

    first, last = half == 0, role == 1
    both = jnp.logical_and(first, last)
    shared = [((2, pw, ww, 0), first, True)]
    shared += [(item, first, True) for item in two(0, pa, wa)]
    shared += [(item, both, last) for item in two(5, pb, wb)]
    for m in range(2):
        item = (m, pf.at[pl.ds(m, 1)], wf.at[pl.ds(m, 1)], 1)
        shared.append((item, jnp.logical_not(first), True))
    alone = [((3, pt, wt, 0), True), ((4, pm, wm, 0), role == 0), ((4, py, wy, 0), role == 1)]
    parts = [(item, when, True) for item, when, _ in shared]
    parts += [(item, when, False) for item, when in alone]

    def slot(ref, lead, o):
        return ref.at[:, o] if lead else ref.at[o]

    def given(when, act):
        if when is True:
            act()
        else:
            pl.when(when)(act)

    def move(item, way, o, target, is_own=False):
        i, src, dst, lead = item
        there = slot(dst, lead, o)
        sem = crecv if way == 3 else recv
        return remote(src if is_own else there, there, send.at[way, i, o], sem.at[i, o], target)

    def forward(o, up, down, side, wait):
        is_own = not wait
        for item, when, common in parts:

            def act(item=item, common=common):
                if wait:
                    move(item, 0, o, across).wait_recv()

                def go(way, target):
                    move(item, way, o, target, is_own).start()

                if side and pair == 2:
                    go(2, across)
                if up is not None:
                    pl.when(up)(functools.partial(go, 0, above))
                if down is not None:
                    pl.when(down)(functools.partial(go, 1, below))
                if common:
                    go(3, mate)

            given(when, act)

    def keep(finish):
        for item, when, common in parts:

            def act(item=item):
                i, src, dst, lead = item
                copy = pltpu.make_async_copy(src, slot(dst, lead, d), own.at[i])
                copy.wait() if finish else copy.start()

            given(when, act)

    forward(d, a < line - 1, a > 0, True, False)
    keep(False)
    other = pair - 1 - x

    def sweep():
        def step(k, carry):
            @pl.when(a - k >= 0)
            def _():
                forward((a - k) * pair + x, a < line - 1, None, True, True)

            @pl.when(a + k < line)
            def _():
                forward((a + k) * pair + x, None, a > 0, True, True)

            if pair == 2:

                def from_side(o, carry):
                    forward(o * pair + other, None, None, False, True)
                    return carry

                @pl.when(a - (k - 1) >= 0)
                def _():
                    from_side(a - (k - 1), 0)

                @pl.when(jnp.logical_and(k > 1, a + (k - 1) < line))
                def _():
                    from_side(a + (k - 1), 0)

            return carry

        lax.fori_loop(1, line + 1, step, 0)

    sweep()

    def drain(o, carry):
        there, column = o // pair, lax.rem(o, pair)
        mine = column == x
        sent = (
            (0, jnp.logical_and(mine, jnp.logical_and(there <= a, a < line - 1)), above),
            (1, jnp.logical_and(mine, jnp.logical_and(there >= a, a > 0)), below),
            (2, mine, across),
        )
        for item, when, common in parts:

            def act(item=item, common=common):
                for way, yes, target in sent:
                    if way == 2 and pair == 1:
                        continue
                    pl.when(yes)(lambda: move(item, way, o, target).wait_send())
                if common:
                    move(item, 3, o, mate).wait_send()

            given(when, act)
        return carry

    lax.fori_loop(0, n, drain, 0)
    keep(True)

    def collect(o, carry):
        for item, when, arrives in shared:
            mine = when if when is not both else first

            def act(item=item):
                i, src, dst, lead = item
                there = slot(dst, lead, o)
                remote(there, there, send.at[3, i, o], crecv.at[i, o], mate).wait_recv()

            given(jnp.logical_and(jnp.logical_not(mine), arrives), act)
        return carry

    lax.fori_loop(0, n, collect, 0)


def mate_kernel(src, dst, send, recv, own):
    d, s = here()
    role, half = s // 2, lax.rem(s, 2)
    mate = dev(d, role * 2 + 1 - half)

    @pl.when(role == 0)
    def _():
        greet([mate])
        pltpu.make_async_copy(src, dst.at[half], own.at[0]).start()
        remote(src, dst.at[half], send.at[0], recv.at[0], mate).start()
        pltpu.make_async_copy(src, dst.at[half], own.at[0]).wait()
        remote(src, dst.at[1 - half], send.at[0], recv.at[0], mate).wait()


def forward_kernel(count, h1s, gq, mq, h1t, gqs, mqt, send, recv, msend, mrecv, qsend, qrecv):
    relay_half_clips(
        count, 0, h1s, h1t, send, recv, swap=(gq, gqs, msend, mrecv), rows=(mq, mqt, qsend, qrecv)
    )


def relay_half_clips(count, from_role, src, dst, send, recv, extra=None, swap=None, rows=None):
    d, s = here()
    role, half = s // 2, lax.rem(s, 2)
    peers = [dev(d, (1 - role) * 2), dev(d, (1 - role) * 2 + 1)]
    mate = dev(d, role * 2 + 1 - half)
    peers.append(mate)
    greet(peers)

    def unit(i, part):
        there = half * count + i
        clip, own = there // 2, lax.rem(there, 2)
        other = 2 * clip + part
        return own, other // count, lax.rem(other, count)

    def copy(i, part):
        own, to, slot = unit(i, part)
        return remote(
            src.at[i, part], dst.at[slot, own], send.at[i, part], recv.at[slot, own],
            dev(d, (1 - from_role) * 2 + to),
        )

    def row_copy(to, finish):
        value, there, qsend, qrecv = rows
        slot = there.at[half] if from_role == 1 else there
        copy = remote(value, slot, qsend.at[to], qrecv.at[half], dev(d, (1 - from_role) * 2 + to))
        copy.wait_send() if finish else copy.start()

    def row_sends(finish):
        if rows is None:
            return

        @pl.when(role == from_role)
        def _():
            if from_role == 0:
                for to in range(2):
                    pl.when(half == to)(functools.partial(row_copy, to, finish))
            else:
                for to in range(2):
                    row_copy(to, finish)

    row_sends(False)
    if swap is not None:
        mine, both, msend, mrecv = swap

        @pl.when(role == 1)
        def _():
            remote(mine, both, msend.at[0], mrecv.at[0], mate).start()

    if extra is not None:
        own_src, own_dst, esend, erecv = extra

        @pl.when(jnp.logical_and(role == 1, half == 1))
        def _():
            remote(own_src, own_dst, esend.at[0], erecv.at[0], dev(d, 2)).start()

    @pl.when(role == from_role)
    def _():
        for i in range(count):
            for part in range(2):
                copy(i, part).start()
        for i in range(count):
            for part in range(2):
                copy(i, part).wait_send()

    @pl.when(role == 1 - from_role)
    def _():
        for i in range(count):
            for part in range(2):
                remote(
                    src.at[i, part], dst.at[i, part], send.at[i, part], recv.at[i, part],
                    dev(d, from_role * 2),
                ).wait_recv()

    row_sends(True)
    if rows is not None:
        value, there, qsend, qrecv = rows

        @pl.when(role == 1 - from_role)
        def _():
            if from_role == 0:
                remote(value, there, qsend.at[0], qrecv.at[half], mate).wait_recv()
            else:
                for o in range(2):
                    remote(value, there.at[o], qsend.at[0], qrecv.at[o], mate).wait_recv()

    if swap is not None:

        @pl.when(role == 1)
        def _():
            remote(mine, both, msend.at[0], mrecv.at[0], mate).wait()

    if extra is not None:

        @pl.when(jnp.logical_and(role == 1, half == 1))
        def _():
            remote(own_src, own_dst, esend.at[0], erecv.at[0], dev(d, 2)).wait_send()

        @pl.when(jnp.logical_and(role == 1, half == 0))
        def _():
            remote(own_src, own_dst, esend.at[0], erecv.at[0], dev(d, 2)).wait_recv()


def backward_kernel(count, dh1, dkv, dmod, dhs, extra, dmods, send, recv, esend, erecv, qsend,
                    qrecv):
    relay_half_clips(
        count, 1, dh1, dhs, send, recv, extra=(dkv.at[:, 0], extra, esend, erecv),
        rows=(dmod, dmods, qsend, qrecv),
    )


def swap_kernel(acts_s, acts_t, actf_s, actf_t, actw_s, actw_t, ybuf, dkvb, dy, dmod,
                racts, ractf, ractw, rybuf, rdkvb, rdy, rdmod, send, recv):
    d, s = here()
    role, half = s // 2, lax.rem(s, 2)
    mate = dev(d, role * 2 + 1 - half)
    greet([mate])
    six = acts_s.shape[0]
    gives = {
        (0, 0): [(0, actf_s, ractf), (1, actw_s, ractw), (4, dmod, rdmod)],
        (0, 1): [(0, acts_s, racts.at[pl.ds(0, six)]), (4, dmod, rdmod)],
        (1, 0): [(0, actf_t, ractf), (1, actw_t, ractw), (2, dy, rdy)],
        (1, 1): [(0, acts_t, racts), (1, ybuf, rybuf), (3, dkvb, rdkvb), (2, dy, rdy)],
    }
    for (r, h), mine in gives.items():

        @pl.when(jnp.logical_and(role == r, half == h))
        def _():
            for i, src, dst in mine:
                remote(src, dst, send.at[i], recv.at[i], mate).start()
            for i, src, dst in mine:
                remote(src, dst, send.at[i], recv.at[i], mate).wait_send()
            for i, src, dst in gives[(r, 1 - h)]:
                remote(src, dst, send.at[i], recv.at[i], mate).wait_recv()


TEXT_CUTS = 11


def scatter_kernel(n, own_in, snd, text_in, dm, vec, loss, wm, temb, ww, hid, wt,
                   summed, text, vsum, squares, gm, g2, g1,
                   own, rx, up, down, sx, rz, tin, trx, tsx, trz, rv, rm, dtembs,
                   osem, send1, recv1, send2, recv2, usend, urecv, dsend, drecv,
                   ssend, srecv, sown, tsend, trecv, esend, erecv):
    line = n // 2
    d, s = here()
    role, half = s // 2, lax.rem(s, 2)
    a, x = d // 2, lax.rem(d, 2)
    across = dev(a * 2 + 1 - x, s)
    other = dev(d, (1 - role) * 2 + half)
    count = 8 - 4 * (1 - role) * (1 - half)
    greet_dp(n, [other])
    squares[...] = jnp.zeros_like(squares)
    squares[1:2, 0:128] = loss[...]
    step = text.shape[1] // TEXT_CUTS
    is_text, is_last, is_time = role == 0, s == 3, s == 0
    clip_rows = dm.shape[0]

    def first_copies(u):
        return (
            remote(snd.at[u], rx.at[u], send1.at[u], recv1.at[u], across),
            pltpu.make_async_copy(own_in.at[u], own.at[u], osem.at[u]),
        )

    def text_hop(k):
        lanes = pl.ds(pl.multiple_of(k * step, 128), step)
        return remote(text_in.at[:, :, :, lanes], tin.at[k], tsend.at[k], trecv.at[k], other)

    def text_across(k):
        return remote(tin.at[k, :, 1 - x], trx.at[k], send1.at[9 + k], recv1.at[9 + k], across)

    def begin(u, carry):
        for copy in first_copies(u):
            copy.start()
        return carry

    def rows_at(o):
        return rm.at[pl.ds(pl.multiple_of(o * clip_rows, 8), clip_rows)]

    def small(i, finish):
        src, dst = (
            (lambda p: vec.at[p], lambda o: rv.at[o]) if i else (lambda p: dm, rows_at)
        )

        def each(k, carry):
            to, o = lax.rem(d + k, n), lax.rem(d + n - k, n)
            if finish:
                remote(src(o), dst(o), ssend.at[i, k], srecv.at[i, k], dev(o, s)).wait()
            else:
                remote(src(to), dst(d), ssend.at[i, k], srecv.at[i, k], dev(to, s)).start()
            return carry

        lax.fori_loop(1, n, each, 0)
        copy = pltpu.make_async_copy(src(d), dst(d), sown.at[i])
        copy.wait() if finish else copy.start()

    pl.when(is_time)(lambda: small(0, False))
    lax.fori_loop(0, 1, begin, 0)
    small(1, False)
    lax.fori_loop(1, count, begin, 0)

    @pl.when(is_last)
    def _():
        begin(8, 0)

    @pl.when(role == 1)
    def _():
        lax.fori_loop(0, TEXT_CUTS, lambda k, c: (text_hop(k).start(), c)[1], 0)

    def embeds(finish):
        def each(k, carry):
            to, o = lax.rem(d + k, n), lax.rem(d + n - k, n)
            if finish:
                remote(dtembs.at[o], dtembs.at[o], esend.at[k], erecv.at[k], dev(o, s)).wait()
            else:
                remote(dtembs.at[d], dtembs.at[d], esend.at[k], erecv.at[k], dev(to, s)).start()
            return carry

        lax.fori_loop(1, n, each, 0)

    def upward(u, p):
        return remote(up.at[u, p], up.at[u, p], usend.at[u, p], urecv.at[u, p], dev(d + 2, s))

    def downward(u, p):
        return remote(
            down.at[u, p], down.at[u, p], dsend.at[u, p], drecv.at[u, p], dev(d - 2, s)
        )

    def along_up(u):
        def add(i, carry):
            p = line - 1 - i

            @pl.when(a == 0)
            def _():
                up[u, p] = own[u, p]

            @pl.when(a > 0)
            def _():
                upward(u, p).wait_recv()
                up[u, p] = up[u, p] + own[u, p]

            return carry

        def send(i, carry):
            upward(u, line - 1 - i).start()
            return carry

        lax.fori_loop(0, line - 1 - a, add, 0)
        lax.fori_loop(0, line - 1 - a, send, 0)

    def along_down(u):
        def add(p, carry):
            @pl.when(a == line - 1)
            def _():
                down[u, p] = own[u, p]

            @pl.when(a < line - 1)
            def _():
                downward(u, p).wait_recv()
                down[u, p] = down[u, p] + own[u, p]

            return carry

        def send(p, carry):
            downward(u, p).start()
            return carry

        lax.fori_loop(0, a, add, 0)
        lax.fori_loop(0, a, send, 0)

    def pairs(u):
        for copy in first_copies(u):
            copy.wait()
        own[u] = own[u] + rx[u].astype(f32)

    def direct(i, total, line_in, finish):
        def each(k, carry):
            to, o = lax.rem(a + k, line), lax.rem(a + line - k, line)
            if finish:
                remote(
                    total.at[o], line_in.at[o], send2.at[i, k], recv2.at[i, k], dev(o * 2 + x, s)
                ).wait()
            else:
                remote(
                    total.at[to], line_in.at[a], send2.at[i, k], recv2.at[i, k],
                    dev(to * 2 + x, s),
                ).start()
            return carry

        lax.fori_loop(1, line, each, 0)

    def round_trip(i, carry):
        @pl.when(i < count)
        def _():
            pairs(i)

        @pl.when(jnp.logical_and(is_time, i == 1))
        def _():
            small(0, True)
            time_back([d], rm, wm, temb, dtembs.at[d])

        pl.when(jnp.logical_and(is_time, i == 2))(lambda: embeds(False))

        @pl.when(is_text)
        def _():
            def cut_at(delay, act):
                k = i - delay
                pl.when(jnp.logical_and(k >= 0, k < TEXT_CUTS))(lambda: act(k))

            def arrive(k):
                text_hop(k).wait_recv()
                text_across(k).start()

            def add(k):
                text_across(k).wait()
                tsx[k] = low(tin[k, :, x].astype(f32) + trx[k].astype(f32))

            cut_at(4, lambda k: direct(k, tsx.at[k], trz.at[k], False))
            cut_at(1, arrive)
            cut_at(3, add)

        k = i - count

        @pl.when(jnp.logical_and(is_last, k == 0))
        def _():
            pairs(8)
            sx[...] = low(own[8])

        @pl.when(jnp.logical_and(is_last, k == 1))
        def _():
            direct(TEXT_CUTS, sx, rz, False)

        later = i - 1 - a

        @pl.when(jnp.logical_and(later >= 0, later < count))
        def _():
            along_up(later)

        other = i - line + a

        @pl.when(jnp.logical_and(other >= 0, other < count))
        def _():
            along_down(other)

        return carry

    lax.fori_loop(0, jnp.maximum(count + line, TEXT_CUTS + 4), round_trip, 0)
    small(1, True)
    vsum[...] = lax.fori_loop(0, n, lambda o, total: total + rv[o], jnp.zeros(vsum.shape, f32))

    @pl.when(is_time)
    def _():
        embeds(True)
        time_grad([d], rm, dtembs, ww, temb, hid, wt, gm, g2, g1, vsum, squares)

    @pl.when(role == 1)
    def _():
        lax.fori_loop(0, TEXT_CUTS, lambda k, c: (text_hop(k).wait_send(), c)[1], 0)

    def collect(u, carry):
        @pl.when(a > 0)
        def _():
            upward(u, a).wait_recv()
            own[u, a] = own[u, a] + up[u, a]

        @pl.when(a < line - 1)
        def _():
            downward(u, a).wait_recv()
            own[u, a] = own[u, a] + down[u, a]

        whole = own[u, a]
        summed[u] = whole
        squares[0:1, :] += col_sum(whole * whole)
        return carry

    lax.fori_loop(0, count, collect, 0)

    def drain(u, carry):
        def one(i, c):
            upward(u, line - 1 - i).wait_send()
            return c

        def two(p, c):
            downward(u, p).wait_send()
            return c

        lax.fori_loop(0, line - 1 - a, one, 0)
        lax.fori_loop(0, a, two, 0)
        return carry

    lax.fori_loop(0, count, drain, 0)

    def others(line_in, whole):
        return lax.fori_loop(
            1, line, lambda k, acc: acc + line_in[lax.rem(a + k, line)].astype(f32), whole
        )

    @pl.when(is_last)
    def _():
        direct(TEXT_CUTS, sx, rz, True)
        whole = others(rz, own[8, a])
        summed[8] = whole
        squares[0:1, :] += col_sum(whole * whole)

    @pl.when(is_text)
    def _():
        def whole_cut(k, carry):
            direct(k, tsx.at[k], trz.at[k], True)
            whole = others(trz.at[k], tin[k, a, x].astype(f32) + trx[k, a].astype(f32))
            text[:, pl.ds(pl.multiple_of(k * step, 128), step)] = low(whole)
            lane = lax.broadcasted_iota(jnp.int32, (1, step), 1)
            spare = jnp.logical_and(k == TEXT_CUTS - 1, lane > step - 128)
            counted = jnp.where(spare, 0.0, whole)
            squares[0:1, :] += col_sum(counted * counted)
            return carry

        lax.fori_loop(0, TEXT_CUTS, whole_cut, 0)


def three(value):
    first = low(value)
    rest = value - first.astype(f32)
    second = low(rest)
    return first, second, low(rest - second.astype(f32))


def nn3(left, right):
    return sum(nn(piece, right) for piece in three(left))


def nt3(left, right):
    return sum(nt(piece, right) for piece in three(left))


def tn3(left, right):
    return sum(tn(left, piece) for piece in three(right))


def own_columns(rank, width, cols):
    row = lax.broadcasted_iota(jnp.int32, (width, 128), 0)
    col = lax.broadcasted_iota(jnp.int32, (width, 128), 1)
    return low(jnp.where(jnp.logical_and(row == rank * cols + col, col < cols), 1.0, 0.0))


def clip_groups(clips, rows):
    per = 8 * (rows // (clips // 8) // 8)
    left = lax.broadcasted_iota(jnp.int32, (clips, rows), 0)
    right = lax.broadcasted_iota(jnp.int32, (clips, rows), 1)
    match = (right // per) * 8 + (right % per) // 8 == left
    return low(jnp.where(match, 1.0, 0.0))


def silu_back(value):
    gate = jax.nn.sigmoid(value)
    return gate * (1.0 + value * (1.0 - gate))


def time_back(rank, rm, wm, temb, dtemb):
    cols, width = wm.shape[0], rm.shape[1]
    rows, clips = rm.shape[0], temb.shape[0]
    pick = own_columns(rank[0], width, cols)
    kind = lax.broadcasted_iota(jnp.int32, (rows, 1), 0) % 8
    value = rm[...]
    pieces = three(value)
    total = jnp.where(kind >= 6, nn3(value, pick), 0.0)
    zeros = jnp.zeros((128 - cols, width), bf16)

    def one(r, total):
        lanes = pl.ds(pl.multiple_of(r * width, 128), width)
        weight = jnp.concatenate([wm[:, lanes], zeros], axis=0)
        back = nt(pieces[0], weight) + nt(pieces[1], weight) + nt(pieces[2], weight)
        return total + jnp.where(kind == r, back, 0.0)

    total = lax.fori_loop(0, 6, one, total)
    slope = silu_back(nn3(temb[...], pick))
    group = clip_groups(clips, rows)

    def collapse(part):
        first, second, third = three(part)
        return nn(group, first) + nn(group, second) + nn(group, third)

    dtemb[...] = collapse(jnp.where(kind < 6, total, 0.0)) * slope + collapse(
        jnp.where(kind >= 6, total, 0.0)
    )


def time_grad(rank, rm, dtembs, ww, temb, hid, wt, gm, g2, g1, vout, tout):
    width, cols = rm.shape[1], vout.shape[0]
    rows, clips = rm.shape[0], temb.shape[0]
    n = dtembs.shape[0]
    pick = own_columns(rank[0], width, cols)
    kind = lax.broadcasted_iota(jnp.int32, (rows, 1), 0) % 8
    value = rm[...]
    hidden = hid[...]
    own_hid, own_temb = nn3(hidden, pick), nn3(temb[...], pick)
    gates = low(own_temb * jax.nn.sigmoid(own_temb))
    spread = low(tn(clip_groups(clips, rows), gates))
    pieces = three(value)
    count = jnp.zeros((1, 1), f32)

    def squared(block):
        return jnp.sum(jnp.sum(block * block, axis=1, keepdims=True), axis=0, keepdims=True)

    def one(r, count):
        masked = jnp.where(kind == r, spread.astype(f32), 0.0).astype(bf16)
        block = sum(tn(masked, piece) for piece in pieces)[0:cols]
        gm[:, pl.ds(pl.multiple_of(r * width, 128), width)] = block
        return count + squared(block)

    count = lax.fori_loop(0, 6, one, count)
    mine = dtembs[rank[0]]
    mine_pieces = three(mine)
    act = low(hidden * jax.nn.sigmoid(hidden))
    block = sum(tn(piece, act) for piece in mine_pieces)[0:cols]
    g2[...] = block
    count = count + squared(block)
    back = jnp.zeros((clips, 128), f32)
    zeros = jnp.zeros((128 - cols, 128), bf16)
    picked = low(nn(ww[:, 256 : 256 + width], pick))
    for o in range(n):
        weight = picked[o * cols : o * cols + cols]
        back = back + nn3(dtembs[o], jnp.concatenate([weight, zeros], axis=0))
    dhid = back * silu_back(own_hid)
    dhid_pieces = three(dhid)
    feature = low(wt[:, 0:256])
    block = sum(tn(piece, feature) for piece in dhid_pieces)[0:cols]
    g1[...] = block
    count = count + squared(block)
    at = lax.broadcasted_iota(jnp.int32, (clips, 128), 1)
    first = low(jnp.where(at == 1, 1.0, 0.0))
    second = low(jnp.where(at == 2, 1.0, 0.0))
    total = sum(tn(piece, first) for piece in dhid_pieces)
    total = total + sum(tn(piece, second) for piece in mine_pieces)
    row_kind = lax.broadcasted_iota(jnp.int32, (rows, 128), 0) % 8
    row_lane = lax.broadcasted_iota(jnp.int32, (rows, 128), 1)
    put = jnp.logical_and(row_lane == row_kind + 3, row_kind < 6)
    put = low(jnp.where(put, 1.0, 0.0))
    total = total + sum(tn(piece, put) for piece in three(nn3(value, pick)))

    vout[...] += total[0:cols]
    lane = lax.broadcasted_iota(jnp.int32, (1, 128), 1)
    tout[0:1, 0:128] += jnp.where(lane == 0, count, 0.0)


class Relay:
    def __init__(self, send, recv):
        self.d, self.s = here()
        self.role, self.half = self.s // 2, lax.rem(self.s, 2)
        self.other = dev(self.d, (1 - self.role) * 2 + self.half)
        self.mate = dev(self.d, self.role * 2 + 1 - self.half)
        self.send, self.recv = send, recv

    def at(self, r, h):
        return jnp.logical_and(self.role == r, self.half == h)

    def copy(self, i, leg, src, dst):
        target = self.other if leg == 0 else self.mate
        return remote(src, dst, self.send.at[i, leg], self.recv.at[i, leg], target)

    def start(self, i, src, dst):
        self.copy(i, 0, src, dst).start()
        self.copy(i, 1, src, dst).start()

    def middle(self, i, dst):
        self.copy(i, 0, dst, dst).wait_recv()
        self.copy(i, 2, dst, dst).start()

    def finish(self, r, h, items):
        @pl.when(self.at(r, h))
        def _():
            for i, src, dst in items:
                self.copy(i, 0, src, dst).wait_send()
                self.copy(i, 1, src, dst).wait_send()

        @pl.when(self.at(1 - r, h))
        def _():
            for i, src, dst in items:
                self.copy(i, 2, dst, dst).wait_send()

        @pl.when(self.at(r, 1 - h))
        def _():
            for i, src, dst in items:
                self.copy(i, 1, dst, dst).wait_recv()

        @pl.when(self.at(1 - r, 1 - h))
        def _():
            for i, src, dst in items:
                self.copy(i, 2, dst, dst).wait_recv()


def owner_first(role, mat):
    return 2 * mat + mat % 2 if role == 0 else mat


def owner_second(mat):
    return 2 + 3 * mat


def settle_kernel(n, vsum, tile, summed, att_m, feed_m, gm, g2, g1,
                  oa, of, xa, xf, xm, x2, x1, gv, stat,
                  vecs, tiles, mine, totals, look, mom,
                  msem, send, recv, own, gsend, grecv, gown, ssend, srecv, tsend, trecv):
    relay = Relay(gsend, grecv)
    d, s, role, half = relay.d, relay.s, relay.role, relay.half
    peers = [dev(d, lax.rem(s + k, 4)) for k in range(1, 4)]
    greet_dp(n, peers)
    four, eight = pl.ds(0, 4), pl.ds(0, 8)
    shared = {
        (0, 0): [(0, summed.at[four], xa.at[four]), (4, gm, xm), (5, g2, x2), (6, g1, x1)],
        (0, 1): [(1, summed.at[eight], xf.at[eight])],
        (1, 0): [(2, summed.at[eight], xa.at[pl.ds(4, 8)])],
        (1, 1): [(3, summed.at[eight], xf.at[pl.ds(8, 8)])],
    }
    def momentum(finish):
        sources = {
            (0, 0): (att_m.at[four], mom.at[four]),
            (0, 1): (feed_m.at[eight], mom),
            (1, 0): (att_m.at[pl.ds(4, 8)], mom),
            (1, 1): (feed_m.at[pl.ds(8, 8)], mom),
        }
        for (r, h), (src, dst) in sources.items():

            @pl.when(relay.at(r, h))
            def _():
                copy = pltpu.make_async_copy(src, dst, msem.at[0])
                copy.wait() if finish else copy.start()

    momentum(False)
    small = [(0, vsum, vecs), (1, tile, tiles)]
    for i, src, dst in small:
        for k in range(1, 4):
            remote(src, dst.at[s], ssend.at[i, k], srecv.at[i, k], peers[k - 1]).start()
    for (r, h), items in shared.items():

        @pl.when(relay.at(r, h))
        def _():
            for i, src, dst in items:
                pltpu.make_async_copy(src, dst, gown.at[i]).start()
                relay.start(i, src, dst)

    total, squares, losses = vsum[...], tile[0:1, :], tile[1:2, :]
    for k in range(1, 4):
        o = lax.rem(s + 4 - k, 4)
        for i, src, dst in small:
            remote(src, dst.at[o], ssend.at[i, k], srecv.at[i, k], dev(d, o)).wait()
        total = total + vecs[o]
        squares = squares + tiles[o, 0:1, :]
        losses = losses + tiles[o, 1:2, :]
    lane = lax.broadcasted_iota(jnp.int32, (1, 128), 1)
    total = jnp.where(jnp.logical_or(lane == 9, lane >= 77), 0.0, total)
    gv[...] = total

    def whole(block):
        return jnp.sum(jnp.sum(block, axis=1, keepdims=True), axis=0, keepdims=True)

    row = lax.broadcasted_iota(jnp.int32, (8, 128), 0)
    mine[...] = jnp.where(row < 4, whole(squares) + whole(total * total), whole(losses[:, 0:128]))
    so_far = mine[...]

    def start(k, carry):
        remote(mine, totals.at[d], tsend.at[k], trecv.at[k], dev(lax.rem(d + k, n), s)).start()
        return carry

    lax.fori_loop(1, n, start, 0)

    def finish(k, carry):
        o = lax.rem(d + n - k, n)
        remote(mine, totals.at[o], tsend.at[k], trecv.at[k], dev(o, s)).wait()
        return carry + totals[o]

    lax.fori_loop(1, n, lambda k, c: (finish(k, so_far), c)[1], 0)
    totals[d] = so_far
    so_far = lax.fori_loop(0, n, lambda o, c: c + totals[o], jnp.zeros((8, 128), f32))
    stat[...] = so_far
    factor = jnp.minimum(1.0, max_norm / (jnp.sqrt(so_far[0:1, 0:1]) + 1e-06))
    scale = factor * (1.0 + momentum_decay)

    momentum(True)

    def update(m, carry):
        look[m] = summed[m] * scale + mom[m] * (momentum_decay * momentum_decay)
        return carry

    lax.fori_loop(0, 8, update, 0)
    groups = []
    for r in range(2):
        mats = 4 if r == 0 else 8
        groups.append((r, 0, [(m, owner_first(r, m), look.at[m], oa) for m in range(mats)]))
        groups.append((
            r, 1, [(m, owner_second(m), look.at[pl.ds(4 * m, 4)], of) for m in range(2)]
        ))
    for r, h, mats in groups:

        @pl.when(relay.at(r, h))
        def _():
            for m, o, src, dst in mats:

                @pl.when(d == o)
                def _():
                    pltpu.make_async_copy(src, dst.at[d], own.at[0]).start()

                @pl.when(d != o)
                def _():
                    remote(src, dst.at[d], send.at[m], recv.at[d], dev(o, s)).start()

    for (r, h), items in shared.items():

        @pl.when(relay.at(1 - r, h))
        def _():
            for i, src, dst in items:
                relay.middle(i, dst)

    for r, h, mats in groups:

        @pl.when(relay.at(r, h))
        def _():
            for i, src, dst in shared[(r, h)]:
                pltpu.make_async_copy(src, dst, gown.at[i]).wait()
            for m, o, src, dst in mats:

                @pl.when(d == o)
                def _():
                    pltpu.make_async_copy(src, dst.at[d], own.at[0]).wait()

                    def arrived(k, carry):
                        p = lax.rem(d + n - k, n)
                        remote(src, dst.at[p], send.at[m], recv.at[p], dev(p, s)).wait_recv()
                        return carry

                    lax.fori_loop(1, n, arrived, 0)

                @pl.when(d != o)
                def _():
                    remote(src, dst.at[d], send.at[m], recv.at[d], dev(o, s)).wait_send()

    for (r, h), items in shared.items():
        relay.finish(r, h, items)


def spread_kernel(n, xa, xf, gy1, summed, oa, of, xy1, xy2, send, recv, rsend, rrecv, own, gown):
    relay = Relay(rsend, rrecv)
    d, s, role, half = relay.d, relay.s, relay.role, relay.half
    greet_dp(n, [relay.other, relay.mate])
    groups = []
    for r in range(2):
        mats = 4 if r == 0 else 8
        groups.append((r, 0, mats, functools.partial(owner_first, r), xa, oa, 10 * r, 4))
        groups.append((r, 1, 2, owner_second, xf, of, 10 * r + 8, 2))
    text = {
        (0, 0): [(20, gy1, xy1.at[0])],
        (0, 1): [(21, gy1, xy1.at[1])],
        (1, 1): [(22, summed.at[8], xy2)],
    }
    for (r, h), items in text.items():

        @pl.when(relay.at(r, h))
        def _():
            for i, src, dst in items:
                pltpu.make_async_copy(src, dst, gown.at[i - 20]).start()
                relay.start(i, src, dst)

    for r, h, mats, owner, src, dst, base, per in groups:

        @pl.when(relay.at(r, h))
        def _():
            for m in range(mats):

                @pl.when(d == owner(m))
                def _():
                    pltpu.make_async_copy(src.at[d], dst.at[per * r + m], own.at[m]).start()

                    def start(k, carry):
                        to = lax.rem(d + k, n)
                        remote(
                            src.at[to], dst.at[per * r + m], send.at[k], recv.at[m], dev(to, s)
                        ).start()
                        return carry

                    lax.fori_loop(1, n, start, 0)

            for m in range(mats):

                @pl.when(d == owner(m))
                def _():
                    pltpu.make_async_copy(src.at[d], dst.at[per * r + m], own.at[m]).wait()

                @pl.when(d != owner(m))
                def _():
                    remote(
                        src.at[d], dst.at[per * r + m], send.at[1], recv.at[m], dev(owner(m), s)
                    ).wait_recv()

                relay.start(base + m, dst.at[per * r + m], dst.at[per * r + m])

    for (r, h), items in text.items():

        @pl.when(relay.at(1 - r, h))
        def _():
            for i, src, dst in items:
                relay.middle(i, dst)

    for r, h, mats, owner, src, dst, base, per in groups:

        @pl.when(relay.at(1 - r, h))
        def _():
            for m in range(mats):
                relay.middle(base + m, dst.at[per * r + m])

    for r, h, mats, owner, src, dst, base, per in groups:

        @pl.when(relay.at(r, h))
        def _():
            for m in range(mats):

                @pl.when(d == owner(m))
                def _():
                    def finish(k, carry):
                        to = lax.rem(d + k, n)
                        remote(
                            src.at[to], dst.at[per * r + m], send.at[k], recv.at[m], dev(to, s)
                        ).wait_send()
                        return carry

                    lax.fori_loop(1, n, finish, 0)

        relay.finish(r, h, [(base + m, dst.at[per * r + m], dst.at[per * r + m]) for m in range(mats)])

    for (r, h), items in text.items():

        @pl.when(relay.at(r, h))
        def _():
            for i, src, dst in items:
                pltpu.make_async_copy(src, dst, gown.at[i - 20]).wait()

        relay.finish(r, h, items)


def adamw_update(weight, first, second, grad, fix_one, fix_two):
    first = beta_one * first + (1.0 - beta_one) * grad
    second = beta_two * second + (1.0 - beta_two) * grad * grad
    first_hat = first / fix_one
    second_hat = second / fix_two
    weight = weight - adam_rate * (
        first_hat / (jnp.sqrt(second_hat) + 1e-08) + weight_decay * weight
    )
    return (weight, first, second)


def update_kernel(
    rates, pieces, scal, stat,
    aw, am, ag, ax, fw, fm, fg, fx, sw, s1, s2, gv, g1, g2, gt, gy2, gm, vw, v1, v2, gvall, gtall,
    aw_, am_, ab_, fw_, fm_, fb_, sw_, s1_, s2_, sb_, vw_, v1_, v2_, vb_, loss_, norm_,
):
    grad_norm = jnp.sqrt(stat[0:1, 0:1])
    factor = jnp.minimum(1.0, max_norm / (grad_norm + 1e-06))
    fix_one, fix_two = scal[0], scal[1]
    loss_[...] = stat[4:5, 0:1]
    norm_[...] = grad_norm
    shrink = 1.0 - muon_rate * weight_decay
    for rate, (w, m, g, x, w_, m_, b_) in zip(
        rates, ((aw, am, ag, ax, aw_, am_, ab_), (fw, fm, fg, fx, fw_, fm_, fb_))
    ):
        m_[...] = momentum_decay * m[...] + g[...] * factor
        fresh = w[...] * shrink - rate * x[...].astype(f32)
        w_[...] = fresh
        b_[...] = low(fresh)
    text = gt.shape[1] - 128
    shards = {
        "embed": gv[:, EMB0 : EMB0 + 16],
        "time": g1[...],
        "time2": g2[...],
        "text": None,
        "text2": gy2[...],
        "head": gv[:, HEAD0 : HEAD0 + 16],
        "mod": gm[...],
    }
    for name, at, size in pieces:
        stride = size if name != "text" else 512
        for start in range(0, size, stride):
            cut = slice(at + start, at + start + stride)
            grad = gt[:, start : start + stride].astype(f32) if name == "text" else shards[name]
            fresh, one, two = adamw_update(
                sw[:, cut], s1[:, cut], s2[:, cut], grad * factor, fix_one, fix_two
            )
            sw_[:, cut], s1_[:, cut], s2_[:, cut] = fresh, one, two
            sb_[:, cut] = low(fresh)

    @pl.when(pl.program_id(0) == 0)
    def _():
        lane = lax.broadcasted_iota(jnp.int32, (1, 128), 1)
        column = gtall[:, text : text + 128].astype(f32)
        whole = jnp.where(lane == 9, column, gvall[...])
        rows = vw.shape[0]
        grad = jnp.transpose(whole)[0:rows, :] * factor
        fresh, one, two = adamw_update(vw[...], v1[...], v2[...], grad, fix_one, fix_two)
        vw_[...], v1_[...], v2_[...] = fresh, one, two
        vb_[...] = low(fresh)


def body(
    latents,
    noise_draw,
    timesteps,
    captions,
    caption_len,
    attention_weights,
    feed_weights,
    side_weights,
    vector_weights,
    attention_momentum,
    feed_momentum,
    side_first,
    side_second,
    vector_first,
    vector_second,
    step_count,
):
    n = lax.axis_size("dp")
    d, s = here()
    role, half = s // 2, lax.rem(s, 2)
    count = latents.shape[0]
    frames = latents.shape[1]
    width = attention_weights.shape[1]
    cols, feed_cols = attention_weights.shape[2], feed_weights.shape[2]
    hidden = n * feed_cols
    text = captions.shape[2]
    sds = jax.ShapeDtypeStruct
    role_s, half_s = role.reshape(1).astype(jnp.int32), half.reshape(1).astype(jnp.int32)

    o_time = 16
    o_text = o_time + 256 + width
    o_text2 = o_text + text
    o_head = o_text2 + width
    o_mod = o_head + 16
    six = 6 * width
    own_rows = -(-cols // 2)
    lanes = n * own_rows

    att_t = jnp.swapaxes(attention_weights, 1, 2)
    feed_t = jnp.swapaxes(feed_weights, 1, 2)
    side_t = side_weights.T
    pa, pb, pf, pw, py, pm, wm_own = local_call(
        lambda role, half, *refs: pack_kernel(
            role, half, (o_time, o_text, o_text2, o_head, o_mod), *refs
        ),
        [
            sds((4, cols, width), bf16),
            sds((4, cols, width), bf16),
            sds((2, feed_cols, width), bf16),
            sds((cols, 1152), bf16),
            sds((own_rows, text), bf16),
            sds((cols, 3 * width), bf16),
            sds((cols, six), bf16),
        ],
        [SM] * 2 + [VM] * 4,
        (role_s, half_s, att_t, feed_t, side_t, vector_weights.T),
    )
    freqs = jnp.exp(-math.log(10000.0) * jnp.arange(128, dtype=f32) / 128)
    angles = timesteps.astype(f32)[:, None] * freqs[None, :]
    level, snr = snr_weight(timesteps.astype(f32))
    pt = jnp.concatenate([jnp.cos(angles), jnp.sin(angles), snr[:, None]], axis=1)
    pt = jnp.pad(pt, ((0, 8 - count), (0, width - 257)))

    wa, wb, wf, ww, wy, wm, wt = comm_call(
        functools.partial(gather_kernel, n),
        1,
        (pa, pb, pf, pw, py, pm, pt),
        [
            sds((4, n, cols, width), bf16),
            sds((4, n, cols, width), bf16),
            sds((2, n, feed_cols, width), bf16),
            sds((n, cols, 1152), bf16),
            sds((n, own_rows, text), bf16),
            sds((n, cols, 3 * width), bf16),
            sds((n, 8, width), f32),
        ],
        [(4, 7, n), (7, n), (7, n), (7,)],
    )
    wa = wa.reshape(4, width, width)
    wb = wb.reshape(4, width, width)
    wf = wf.reshape(2, hidden, width)
    ww = ww.reshape(width, 1152)
    wy = wy.reshape(lanes, text)
    wm = wm.reshape(width, 3 * width)
    rank_s = d.reshape(1).astype(jnp.int32)
    per_clip = frames * (latents.shape[3] // 2) * (latents.shape[4] // 2)
    vec, hid, temb, mq_own, y2p, errs = local_call(
        functools.partial(condition_kernel, per_clip=per_clip, cols=cols),
        [
            sds((128, width), f32),
            sds((n * 8, width), f32),
            sds((n * 8, width), f32),
            sds((8, 3 * width), f32),
            sds((2, width, lanes), bf16),
            sds((8, 128), f32),
        ],
        [SM] + [VM] * 3,
        (rank_s, wt.reshape(n * 8, width), ww, wm),
    )
    mq = comm_call(
        mate_kernel, 2, (mq_own,), sds((2, 8, 3 * width), f32), [(1,), (1,), (1,)]
    )

    half_tokens = count * per_clip // 2

    def own_rows_of(value):
        return lax.dynamic_slice_in_dim(
            value.reshape(count * per_clip, 16), half * half_tokens, half_tokens, 0
        )

    def tokens(clean, noise):
        mix = level[:, None, None, None, None]
        noisy = low(jnp.sqrt(mix) * clean + jnp.sqrt(1.0 - mix) * noise)
        return jnp.pad(own_rows_of(patchify(noisy)), ((0, 0), (EMB0, 112 - EMB0)))

    def targets(noise):
        value = patchify(noise).reshape(count, frames, 2, 32, 16).transpose(0, 2, 1, 3, 4)
        return jnp.pad(own_rows_of(value), ((0, 0), (HEAD0, 112 - HEAD0)))

    tok = lax.cond(
        role == 0,
        tokens,
        lambda clean, noise: jnp.zeros((half_tokens, 128), bf16),
        latents,
        noise_draw,
    )
    places = np.arange(per_clip // frames)
    edge = latents.shape[3] // 2
    pos = np.concatenate(
        [sincos(places // edge, width // 2), sincos(places % edge, width // 2)], axis=1
    )
    pos = jnp.asarray(pos)
    timing = jnp.asarray(sincos(np.arange(frames), width))

    clip_rows = captions.shape[1]
    residuals = [
        sds((5, half_tokens, width), bf16),
        sds((3, half_tokens, width), f32),
        sds((half_tokens, hidden), f32),
        sds((count, 3, 256, 128), f32),
    ]
    residual_scratch = [pltpu.VMEM(v.shape, v.dtype) for v in residuals]
    h1s, hq, gq_own, kept_b, kept_f, kept_u, kept_p = local_call(
        functools.partial(first_kernel, cols),
        [
            sds((count, 2, 64, width), bf16),
            sds((count, LP, lanes), f32),
            sds((count, LP, lanes), bf16),
        ]
        + residuals,
        [SM] * 2 + [VM] * 7 + [ANY],
        (role_s, half_s, tok, pos, mq, vec, wa, wf, wy, captions),
        residual_scratch
        + [
            pltpu.VMEM((count, clip_rows, text), bf16),
            pltpu.SemaphoreType.DMA((count,)),
            pltpu.SemaphoreType.DMA((count, 4)),
        ],
        [VM] * 3 + [ANY] * 4,
    )
    later_noise, gq_own = lax.optimization_barrier((noise_draw, gq_own))
    target = lax.cond(
        role == 1,
        targets,
        lambda noise: jnp.zeros((half_tokens, 128), f32),
        later_noise,
    )
    target, h1s = lax.optimization_barrier((target, h1s))
    h1t, rgq, mqt = comm_call(
        functools.partial(forward_kernel, count),
        3,
        (h1s, gq_own, mq),
        [
            sds((count, 2, 64, width), bf16),
            sds((count, LP, lanes), bf16),
            sds((2, 8, 3 * width), f32),
        ],
        [(count, 2), (count, 2), (1,), (1,), (2,), (2,)],
    )

    ncl = (count + 1) // 2
    wide = sds((2, half_tokens, hidden), bf16)
    thin = sds((2, half_tokens, width), bf16)
    cap_like = sds((ncl, LP, width), bf16)
    dh1, acts_t, actf_t, actw_t, ybuf, dkv, grads_t, dmod_t, loss_t = local_call(
        temporal_kernel,
        [
            sds((count, 2, 64, width), bf16),
            sds((10, half_tokens, width), bf16),
            thin,
            wide,
            cap_like,
            sds((2, ncl, LP, width), f32),
            sds((128, width), f32),
            sds((count, 8, width), f32),
            sds((1, 128), f32),
        ],
        [SM] * 4 + [VM] * 13,
        (
            role_s, half_s, rank_s, caption_len, errs, h1t, timing, mqt, vec, temb, wa, wb, wf,
            gq_own, rgq, y2p, target,
        ),
        [pltpu.VMEM((ncl, KP, width), bf16), pltpu.VMEM((ncl, KP, width), bf16)],
    )
    dhs, extra, dmods_t = comm_call(
        functools.partial(backward_kernel, count),
        4,
        (dh1, dkv, dmod_t),
        [
            sds((count, 2, 64, width), bf16),
            sds((2, LP, width), f32),
            sds((2, count, 8, width), f32),
        ],
        [(count, 2), (count, 2), (1,), (1,), (2,), (2,)],
    )
    acts_s, actf_s, actw_s, dkvb, dy, vect, dmod = local_call(
        last_kernel,
        [
            sds((6, half_tokens, width), bf16),
            thin,
            wide,
            sds((2, ncl, LP, width), bf16),
            cap_like,
            sds((width, 128), f32),
            sds((count, 8, width), f32),
        ],
        [SM] * 2 + [VM] * 6 + [ANY] * 4 + [VM] * 5,
        (
            role_s, half_s, tok, mq, vec, wa, wb, wf, kept_b, kept_f, kept_u, kept_p, dhs, dkv,
            extra, grads_t, dmod_t,
        ),
        [pltpu.VMEM((128, width), f32)]
        + residual_scratch
        + [pltpu.SemaphoreType.DMA((count, 4))],
    )
    racts, ractf, ractw, rybuf, rdkvb, rdy, rdmod = comm_call(
        swap_kernel,
        5,
        (acts_s, acts_t, actf_s, actf_t, actw_s, actw_t, ybuf, dkvb, dy, dmod),
        [
            sds((10, half_tokens, width), bf16),
            thin,
            wide,
            cap_like,
            sds((2, ncl, LP, width), bf16),
            cap_like,
            sds((count, 8, width), f32),
        ],
        [(5,), (5,)],
    )
    line = n // 2
    wide_text = text + 128
    cut_text = wide_text // TEXT_CUTS
    block = (9, line, cols, width)
    tokens2 = 2 * half_tokens
    grad_own, grad_snd, text_part = local_call(
        weight_grad_kernel,
        [
            sds(block, f32),
            sds(block, bf16),
            sds((line, 2, own_rows, wide_text), bf16),
        ],
        [SM] * 3 + [ANY] * 9 + [VM] * 10 + [ANY],
        (
            role_s, half_s, rank_s, acts_s, acts_t, racts, actf_s, actf_t, ractf, actw_s, actw_t,
            ractw, ybuf, rybuf, dkvb, rdkvb, dy, rdy, gq_own, rgq, hq, y2p, captions,
        ),
        [
            pltpu.VMEM((10, tokens2, width), bf16),
            pltpu.VMEM((2, tokens2, width), bf16),
            pltpu.VMEM((2, tokens2, hidden), bf16),
            pltpu.VMEM((count, clip_rows, text), bf16),
            pltpu.VMEM((width, width), f32),
            pltpu.VMEM((count, lanes, LP), bf16),
            pltpu.VMEM((lanes, 128), f32),
            pltpu.SemaphoreType.DMA((4 + count,)),
        ],
    )

    mine0 = jnp.where(half == 0, dmod, rdmod)
    mine1 = jnp.where(half == 0, rdmod, dmod)
    sources = (mine0, mine1, dmods_t[0], dmods_t[1])
    dm_clip = []
    for clip in range(count):
        total = 0.0
        for seg in range(4):
            for i in range(count):
                if ((seg % 2) * count + i) // 2 == clip:
                    total = total + sources[seg][i]
        dm_clip.append(total)
    dm = jnp.concatenate(dm_clip, axis=0)

    whole_clips = n * 8
    text_block = (TEXT_CUTS, line, own_rows, cut_text)
    summed, text_sum, vsum, tile, grad_mod, grad_time2, grad_time1 = comm_call(
        functools.partial(scatter_kernel, n),
        6,
        (
            grad_own, grad_snd, text_part, dm, vect.reshape(n, cols, 128), loss_t,
            wm_own, temb, ww, hid, wt.reshape(whole_clips, width),
        ),
        [
            sds((9, cols, width), f32),
            sds((own_rows, wide_text), bf16),
            sds((cols, 128), f32),
            sds((8, width), f32),
            sds((cols, six), f32),
            sds((cols, width), f32),
            sds((cols, 256), f32),
        ],
        [(9,), (9 + TEXT_CUTS,), (9 + TEXT_CUTS,)]
        + [(TEXT_CUTS + 1, line)] * 2
        + [(8, line)] * 4
        + [(2, n), (2, n), (2,), (TEXT_CUTS,), (TEXT_CUTS,), (n,), (n,)],
        [VM] * 7,
        in_specs=[ANY] * 5 + [VM] * 6,
        scratch=[
            pltpu.VMEM(block, f32),
            pltpu.VMEM(block, bf16),
            pltpu.VMEM((8,) + block[1:], f32),
            pltpu.VMEM((8,) + block[1:], f32),
            pltpu.VMEM(block[1:], bf16),
            pltpu.VMEM(block[1:], bf16),
            pltpu.VMEM((TEXT_CUTS, line, 2, own_rows, cut_text), bf16),
        ]
        + [pltpu.VMEM(text_block, bf16)] * 3
        + [
            pltpu.VMEM((n, cols, 128), f32),
            pltpu.VMEM((n * 8 * count, width), f32),
            pltpu.VMEM((n, whole_clips, 128), f32),
        ],
    )

    att_m = jnp.swapaxes(attention_momentum, 1, 2)
    feed_m = jnp.swapaxes(feed_momentum, 1, 2)
    ua, uf, ga2, gf2, grad_mod, grad_time2, grad_time1, grad_v, stat = comm_call(
        functools.partial(settle_kernel, n),
        8,
        (
            vsum, tile, summed, att_m, feed_m.reshape(16, cols, width), grad_mod, grad_time2,
            grad_time1,
        ),
        [
            sds((n, cols, width), f32),
            sds((n, 4, cols, width), f32),
            sds((12, cols, width), f32),
            sds((16, cols, width), f32),
            sds((cols, six), f32),
            sds((cols, width), f32),
            sds((cols, 256), f32),
            sds((cols, 128), f32),
            sds((8, 128), f32),
        ],
        [(1,), (8,), (n,), (1,), (7, 3), (7, 3), (7,), (2, 4), (2, 4), (n,), (n,)],
        [ANY] * 7 + [VM] * 2,
        in_specs=[VM] * 3 + [ANY] * 5,
        scratch=[
            pltpu.VMEM((4, cols, 128), f32),
            pltpu.VMEM((4, 8, width), f32),
            pltpu.VMEM((8, 128), f32),
            pltpu.VMEM((n, 8, 128), f32),
            pltpu.VMEM((8, cols, width), f32),
            pltpu.VMEM((8, cols, width), f32),
        ],
    )
    xa, xf = local_call(
        muon_kernel,
        [sds((width, width), bf16), sds((hidden, width), bf16)],
        [SM] + [VM] * 2,
        (half_s, ua.reshape(width, width), uf.reshape(hidden, width)),
        [pltpu.VMEM((width, width), f32), pltpu.VMEM((width, width), f32)],
    )
    xa_all, xf_all, gy12, gy22 = comm_call(
        functools.partial(spread_kernel, n),
        10,
        (xa.reshape(n, cols, width), xf.reshape(n, feed_cols, width), text_sum, summed),
        [
            sds((12, cols, width), bf16),
            sds((4, feed_cols, width), bf16),
            sds((2, own_rows, wide_text), bf16),
            sds((cols, width), f32),
        ],
        [(n,), (8,), (23, 3), (23, 3), (8,), (3,)],
    )

    clock = step_count[0].astype(f32)
    scal = jnp.stack([1.0 - jnp.power(beta_one, clock), 1.0 - jnp.power(beta_two, clock)])
    text_grad = gy12.reshape(2 * own_rows, wide_text)[:cols]
    side_m, side_v = side_first.T, side_second.T
    side_rows = side_t.shape[1]
    pieces = (
        ("embed", 0, 16),
        ("time", o_time, 256),
        ("time2", o_time + 256, width),
        ("text", o_text, text),
        ("text2", o_text2, width),
        ("head", o_head, 16),
        ("mod", o_mod, six),
    )
    rates = tuple(
        muon_rate * 0.2 * math.sqrt(columns) for columns in (n * cols, n * feed_cols)
    )
    grid = cols // 8 if cols % 8 == 0 else 1

    def by_rows(value):
        return value.reshape(-1, value.shape[-1])

    def rows_spec(value):
        return pl.BlockSpec((value.shape[0] // grid, value.shape[1]), lambda i: (i, 0))

    def whole_spec(value):
        return pl.BlockSpec(value.shape, lambda i: (0, 0))

    cutup = [by_rows(v) for v in (att_t, att_m, ga2, xa_all, feed_t, feed_m, gf2, xf_all)] + [
        side_t, side_m, side_v, grad_v, grad_time1, grad_time2, text_grad, gy22, grad_mod,
    ]
    fixed = [vector_weights, vector_first, vector_second, grad_v, text_grad]
    a_like, f_like, s_like = (sds(v.shape, f32) for v in (cutup[0], cutup[4], side_t))
    v_like = sds(vector_weights.shape, f32)

    def low_of(like):
        return sds(like.shape, bf16)

    row_outs = [
        a_like, a_like, low_of(a_like), f_like, f_like, low_of(f_like), s_like, s_like, s_like,
        low_of(s_like),
    ]
    whole_outs = [v_like, v_like, v_like, low_of(v_like), sds((1, 1), f32), sds((1, 1), f32)]
    (
        att_new, att_moment, att_low, feed_new, feed_moment, feed_low, side_new, side_first_new,
        side_second_new, side_low, vector_new, vector_first_new, vector_second_new, vector_low,
        loss_value, grad_norm,
    ) = pl.pallas_call(
        functools.partial(update_kernel, rates, pieces),
        grid=(grid,),
        out_shape=row_outs + whole_outs,
        in_specs=[SM, whole_spec(stat)] + [rows_spec(v) for v in cutup] + [whole_spec(v) for v in fixed],
        out_specs=[rows_spec(v) for v in row_outs] + [whole_spec(v) for v in whole_outs],
        compiler_params=pltpu.CompilerParams(vmem_limit_bytes=VMEM_LIMIT),
    )(scal, stat, *cutup, *fixed)

    def att(value):
        return value.reshape(att_t.shape)

    def feed(value):
        return value.reshape(feed_t.shape)

    def back(value):
        return jnp.swapaxes(value, -1, -2)

    return (
        loss_value[0, 0],
        grad_norm[0, 0],
        back(att(att_new)),
        back(att(att_moment)),
        back(feed(feed_new)),
        back(feed(feed_moment)),
        back(side_new),
        back(side_first_new),
        back(side_second_new),
        vector_new,
        vector_first_new,
        vector_second_new,
        back(att(att_low)),
        back(feed(feed_low)),
        back(side_low),
        vector_low,
    )


def solution(mesh):
    column = P(None, "dp")
    matrix = P(None, None, "dp")
    return jax.shard_map(
        body,
        mesh=mesh,
        in_specs=(
            P("dp", None, None, None, None),
            P("dp", None, None, None, None),
            P("dp"),
            P("dp", None, None),
            P("dp"),
            matrix,
            matrix,
            column,
            column,
            matrix,
            matrix,
            column,
            column,
            column,
            column,
            P(),
        ),
        out_specs=(
            P(),
            P(),
            matrix,
            matrix,
            matrix,
            matrix,
            column,
            column,
            column,
            column,
            column,
            column,
            matrix,
            matrix,
            column,
            column,
        ),
        check_vma=False,
    )
```

```python
import functools
import math

import jax
import jax.numpy as jnp
import numpy as np
from jax import lax
from jax.experimental import pallas as pl
from jax.experimental.pallas import tpu as pltpu
from jax.sharding import PartitionSpec as P

HEADS = 6
HEAD = 64
LP = 304
KP = 384

highest = lax.Precision.HIGHEST
snr_gamma = 5.0
max_norm = 0.005
momentum_decay = 0.95
muon_rate = 0.05
adam_rate = 0.02
beta_one = 0.9
beta_two = 0.999
weight_decay = 0.01
coef_a = 3.4445
coef_b = -4.775
coef_c = 2.0315

f32, bf16 = jnp.float32, jnp.bfloat16
MESH = pl.DeviceIdType.MESH
ANY = pl.BlockSpec(memory_space=pl.ANY)
VM = pl.BlockSpec(memory_space=pltpu.VMEM)
SM = pl.BlockSpec(memory_space=pltpu.SMEM)
VMEM_LIMIT = 60000 * 1024


def low(value):
    return value.astype(bf16)


def nt(left, right):
    return lax.dot_general(left, right, (((1,), (1,)), ((), ())), preferred_element_type=f32)


def nn(left, right):
    return lax.dot_general(left, right, (((1,), (0,)), ((), ())), preferred_element_type=f32)


def tn(left, right):
    return lax.dot_general(left, right, (((0,), (0,)), ((), ())), preferred_element_type=f32)


def snr_weight(steps_t):
    level = jnp.cos((steps_t / 1000.0 + 0.008) / 1.008 * (math.pi / 2)) ** 2
    ratio = level / (1.0 - level)
    return level, jnp.minimum(ratio, snr_gamma) / ratio


def patchify(frames):
    clips, count, channels, height, breadth = frames.shape
    grid = frames.reshape(clips, count, channels, height // 2, 2, breadth // 2, 2)
    grid = grid.transpose(0, 1, 3, 5, 4, 6, 2)
    return grid.reshape(clips, count, (height // 2) * (breadth // 2), 4 * channels)


def sincos(places, model_width):
    half_width = model_width // 2
    freqs = np.exp(-math.log(10000.0) * np.arange(half_width) / half_width)
    angles = places[:, None] * freqs[None, :]
    return np.concatenate([np.sin(angles), np.cos(angles)], axis=1).astype(np.float32)


def col_sum(value):
    return jnp.sum(value.astype(f32), axis=0, keepdims=True)


def norm(value):
    centred = value - jnp.mean(value, axis=-1, keepdims=True)
    inv = lax.rsqrt(jnp.mean(centred * centred, axis=-1, keepdims=True) + 1e-06)
    return centred * inv, inv


def norm_back(grad, normed, inv):
    return inv * (
        grad
        - jnp.mean(grad, axis=-1, keepdims=True)
        - normed * jnp.mean(grad * normed, axis=-1, keepdims=True)
    )


GELU_C = math.sqrt(2.0 / math.pi)


def gelu(value):
    inner = GELU_C * (value + 0.044715 * (value * value * value))
    return value * (0.5 * (1.0 + jnp.tanh(inner)))


def gelu_both(value):
    square = value * value
    tanh = jnp.tanh(GELU_C * (value + 0.044715 * (square * value)))
    cdf = 0.5 * (1.0 + tanh)
    slope = 0.5 * (1.0 - tanh * tanh) * (GELU_C * (1.0 + 3 * 0.044715 * square))
    return value * cdf, cdf + value * slope


def lanes_low():
    lane = lax.broadcasted_iota(jnp.int32, (1, 128), 1)
    first = jnp.where(lane < HEAD, 1.0, 0.0)
    return low(first), low(1.0 - first), lane < HEAD


def stack_heads(pair, first, second):
    return jnp.concatenate([pair * first, pair * second], axis=0)


def attend(queries, keys, values, allowed):
    first, second, lower = lanes_low()
    rows = queries.shape[0]
    mixed, probs = [], []
    for pair in range(HEADS // 2):
        cut = slice(pair * 128, pair * 128 + 128)
        scores = nt(stack_heads(queries[:, cut], first, second), keys[:, cut]) * 0.125
        scores = jnp.where(allowed, scores, -1e30)
        weight = jnp.exp(scores - jnp.max(scores, axis=-1, keepdims=True))
        prob = weight / jnp.sum(weight, axis=-1, keepdims=True)
        probs.append(prob)
        out = nn(low(prob), values[:, cut])
        mixed.append(jnp.where(lower, out[:rows], out[rows:]))
    return low(jnp.concatenate(mixed, axis=1)), probs


def attend_back(grad, queries, keys, values, probs):
    first, second, lower = lanes_low()
    rows = queries.shape[0]
    dq, dk, dv = [], [], []
    for pair in range(HEADS // 2):
        cut = slice(pair * 128, pair * 128 + 128)
        stacked = stack_heads(grad[:, cut], first, second)
        prob = probs[pair]
        dv.append(tn(low(prob), stacked))
        dprob = nt(stacked, values[:, cut])
        dscore = low(prob * (dprob - jnp.sum(prob * dprob, axis=-1, keepdims=True)))
        part = nn(dscore, keys[:, cut])
        dq.append(jnp.where(lower, part[:rows], part[rows:]) * 0.125)
        dk.append(tn(dscore, stack_heads(queries[:, cut], first, second)) * 0.125)
    return tuple(jnp.concatenate(piece, axis=1) for piece in (dq, dk, dv))


def self_forward(x, mods, weights, bias, allowed):
    normed, inv = norm(x)
    a = low(normed * (1.0 + mods[1]) + mods[0])
    q = low(nt(a, weights[0]) + bias[0])
    k = low(nt(a, weights[1]))
    v = low(nt(a, weights[2]) + bias[1])
    o, probs = attend(q, k, v, allowed)
    branch = nt(o, weights[3]) + bias[2]
    return x + mods[2] * branch, (normed, inv, a, q, k, v, o, probs, branch)


def self_backward(dx, kept, mods, weights):
    normed, inv, a, q, k, v, o, probs, branch = kept
    dm2 = col_sum(dx * branch)
    dbr = low(dx * mods[2])
    do = low(nn(dbr, weights[3]))
    dq, dk, dv = (low(piece) for piece in attend_back(do, q, k, v, probs))
    da = nn(dq, weights[0]) + nn(dk, weights[1]) + nn(dv, weights[2])
    dm1, dm0 = col_sum(da * normed), col_sum(da)
    dx = dx + norm_back(da * (1.0 + mods[1]), normed, inv)
    return dx, (dm0, dm1, dm2), (col_sum(dq), col_sum(dv), col_sum(dbr)), (a, dq, dk, dv, o, dbr)


def feed_forward(x, mods, feed, bias_up, bias_down):
    normed, inv = norm(x)
    c = low(normed * (1.0 + mods[4]) + mods[3])
    u = nt(c, feed[0]) + bias_up
    g = low(gelu(u))
    branch = nn(g, feed[1]) + bias_down
    return x + mods[5] * branch, (normed, inv, c, u, g, branch)


def feed_backward(dx, kept, mods, feed):
    normed, inv, c, u, g, branch = kept
    dm5 = col_sum(dx * branch)
    dbr = low(dx * mods[5])
    value, slope = gelu_both(u)
    g = low(value)
    du = low(nt(dbr, feed[1]) * slope)
    dc = nn(du, feed[0])
    dm4, dm3 = col_sum(dc * normed), col_sum(dc)
    dx = dx + norm_back(dc * (1.0 + mods[4]), normed, inv)
    return dx, (dm3, dm4, dm5), (col_sum(du), col_sum(dbr)), (c, dbr, du, g)


def pair_mask(kind):
    row = lax.broadcasted_iota(jnp.int32, (256, 128), 0) % 128
    col = lax.broadcasted_iota(jnp.int32, (256, 128), 1)
    if kind == 0:
        return row // 64 == col // 64
    return row % 32 == col % 32


VEC0, EMB0, HEAD0 = 0, 45, 61


def mod_rows(mq, vec, table, clip):
    rows = []
    for r in range(6):
        at = (r % 3) * 384
        rows.append(
            mq[r // 3, pl.ds(clip, 1), at : at + 384]
            + vec[3 + r : 4 + r]
            + vec[table + r : table + r + 1]
        )
    return rows


def up_bias(vec, start):
    return jnp.concatenate([vec[start + i : start + i + 1] for i in range(4)], axis=1)


def pack_kernel(role, half, offsets, att, feed, side, vec, pa, pb, pf, pw, py, pm, wm):
    time, text, text2, head, mod = offsets
    width, per, rows = att.shape[2], pf.shape[0], py.shape[0]

    def rounded(at, size):
        return low(side[:, at : at + size])

    first = text - time
    pw[:, 0:first] = rounded(time, first)
    pw[:, first : first + width] = rounded(text2, width)
    cols = pw.shape[0]
    pw[:, first + width :] = low(jnp.concatenate(
        [jnp.transpose(vec[...]), side[:, 0:16], side[:, head : head + 16], jnp.zeros((cols, 51), f32)], axis=1
    ))
    wm[...] = rounded(mod, 6 * width)
    for r in range(2):

        @pl.when(role[0] == r)
        def _():
            pa[...] = low(att[4 * r : 4 * r + 4])
            pf[...] = low(feed[per * r : per * r + per])
            if r == 1:
                pb[...] = low(att[8:12])

    for h in range(2):

        @pl.when(half[0] == h)
        def _():
            pm[...] = rounded(mod + h * 3 * width, 3 * width)
            top = min((h + 1) * rows, cols)
            py[0 : top - h * rows, :] = low(side[h * rows : top, text : text + py.shape[1]])


def units_of(hand, lanes, width, cols):
    per = -(-cols // 2)
    unit = lax.broadcasted_iota(jnp.int32, (lanes, width), 0)
    column = lax.broadcasted_iota(jnp.int32, (lanes, width), 1)
    inside = hand * per + unit % per
    match = jnp.logical_and((unit // per) * cols + inside == column, inside < cols)
    return low(jnp.where(match, 1.0, 0.0))


def condition_kernel(rank, wt, ww, wm, vec, hid, temb, mq, y2p, errs, *, per_clip, cols):
    turned = jnp.transpose(ww[:, 1024:1152].astype(f32))
    vec[...] = turned
    feature = low(wt[:, 0:256])
    first = nt(feature, ww[:, 0:256]) + turned[1:2]
    hid[...] = first
    second = nt(low(first * jax.nn.sigmoid(first)), ww[:, 256:640]) + turned[2:3]
    temb[...] = second
    own = temb[pl.ds(pl.multiple_of(rank[0] * 8, 8), 8), :]
    mq[...] = nn(low(own * jax.nn.sigmoid(own)), wm[...])
    for h in range(2):
        y2p[h] = low(nt(ww[:, 640:1024], units_of(h, y2p.shape[2], y2p.shape[1], cols)))
    total = jnp.sum(wt[:, 256:257], axis=0, keepdims=True)
    weight = wt[pl.ds(pl.multiple_of(rank[0] * 8, 8), 8), 256:257] / (total * (per_clip * 16.0))
    errs[...] = jnp.broadcast_to(weight, errs.shape)


def embed_chunk(tok_ref, vec, pos_ref, chunk):
    tokens = tok_ref[pl.ds(pl.multiple_of(chunk * 128, 128), 128), :]
    places = pos_ref[...] + vec[0:1]
    return low(nn(tokens, low(vec[...])) + jnp.concatenate([places, places], axis=0)), tokens


def spatial_bias(vec):
    return (vec[11:12], vec[12:13], vec[13:14])


def residual_copies(sources, targets, sems):
    def of(chunk):
        rows = pl.ds(pl.multiple_of(chunk * 128, 128), 128)
        cuts = [lambda r: r.at[:, rows], lambda r: r.at[:, rows], lambda r: r.at[rows],
                lambda r: r.at[chunk]]
        return [
            pltpu.make_async_copy(cut(src), cut(dst), sems.at[chunk, i])
            for i, (cut, src, dst) in enumerate(zip(cuts, sources, targets))
        ]

    return of


def first_kernel(
    cols, role, half, tok, pos, mq, vec, wa, wf, wy, captions,
    h1, hq, gq, out_b, out_f, out_u, out_p, kept_b, kept_f, kept_u, kept_p, cap, sems, ksem,
):
    @pl.when(role[0] == 1)
    def _():
        clips = captions.shape[0]
        for c in range(clips):
            pltpu.make_async_copy(captions.at[c], cap.at[c], sems.at[c]).start()
        bias = nt(low(vec[9:10]), units_of(half[0], wy.shape[0], vec.shape[1], cols))
        def layer(c, carry):
            pltpu.make_async_copy(captions.at[c], cap.at[c], sems.at[c]).wait()
            value = nt(cap[c], wy[...]) + bias
            rows = value.shape[0]
            pad = jnp.zeros((LP - rows, value.shape[1]), f32)
            hq[c] = jnp.concatenate([value, pad], axis=0)
            gq[c] = low(jnp.concatenate([gelu(value), pad], axis=0))
            return carry

        lax.fori_loop(0, clips, layer, 0)

    @pl.when(role[0] == 0)
    def _():
        allowed = pair_mask(0)
        count = h1.shape[0]
        bu = up_bias(vec, 14)
        residuals = residual_copies((kept_b, kept_f, kept_u, kept_p), (out_b, out_f, out_u, out_p), ksem)

        def step(chunk, carry):
            @pl.when(chunk > 0)
            def _():
                for copy in residuals(chunk - 1):
                    copy.start()

            m = mod_rows(mq, vec, 19, (half[0] * count + chunk) // 2)
            h0, _ = embed_chunk(tok, vec, pos, chunk)
            x1, kept = self_forward(h0.astype(f32), m, wa, spatial_bias(vec), allowed)
            x, kept_feed = feed_forward(x1, m, wf, bu, vec[18:19])
            out = low(x)
            where = pl.ds(pl.multiple_of(chunk * 128, 128), 128)
            for i, value in enumerate((h0,) + kept[3:7]):
                kept_b[i, where, :] = value
            for i, value in enumerate((x1, kept[8], kept_feed[5])):
                kept_f[i, where, :] = value
            kept_u[where, :] = kept_feed[3]
            for pair in range(3):
                kept_p[chunk, pair] = kept[7][pair]
            for frame in range(2):
                for part in range(2):
                    start = frame * 64 + part * 32
                    h1[chunk, part, frame * 32 : frame * 32 + 32, :] = out[start : start + 32]
            return carry

        lax.fori_loop(0, count, step, 0)
        for copy in residuals(count - 1):
            copy.start()
        for chunk in range(count):
            for copy in residuals(chunk):
                copy.wait()


def last_kernel(
    role, half, tok, mq, vec, wa, wb, wf, in_b, in_f, in_u, in_p, dh, dkv, extra, grads_t, dmod_t,
    acts, actf, actw, dkvb, dy, vect, dmod, grads, kept_b, kept_f, kept_u, kept_p, ksem,
):
    @pl.when(role[0] == 0)
    def _():
        grads[...] = jnp.zeros_like(grads)
        dmod[...] = jnp.zeros_like(dmod)
        count = dh.shape[0]
        residuals = residual_copies((in_b, in_f, in_u, in_p), (kept_b, kept_f, kept_u, kept_p), ksem)
        for chunk in range(count):
            for copy in residuals(chunk):
                copy.start()

        def step(chunk, carry):
            for copy in residuals(chunk):
                copy.wait()
            m = mod_rows(mq, vec, 19, (half[0] * count + chunk) // 2)
            where = pl.ds(pl.multiple_of(chunk * 128, 128), 128)
            tokens = tok[where, :]
            h0, q, k, v, o = (kept_b[i, where, :] for i in range(5))
            x1, branch, branch_f = (kept_f[i, where, :] for i in range(3))
            normed, inv = norm(h0.astype(f32))
            a = low(normed * (1.0 + m[1]) + m[0])
            probs = [kept_p[chunk, pair] for pair in range(3)]
            kept = (normed, inv, a, q, k, v, o, probs, branch)
            normed_f, inv_f = norm(x1)
            c = low(normed_f * (1.0 + m[4]) + m[3])
            kept_feed = (normed_f, inv_f, c, kept_u[where, :], None, branch_f)
            parts = []
            for frame in range(2):
                for part in range(2):
                    parts.append(dh[chunk, part, frame * 32 : frame * 32 + 32, :])
            dx = jnp.concatenate(parts, axis=0).astype(f32)
            dx, dm_f, db_f, act_f = feed_backward(dx, kept_feed, m, wf)
            dx, dm_a, db_a, act_a = self_backward(dx, kept, m, wa)
            dh0 = low(dx)
            for i, value in enumerate(act_a):
                acts[i, where, :] = value
            for i in range(2):
                actf[i, where, :] = act_f[i]
                actw[i, where, :] = act_f[2 + i]
            mods = dm_a + dm_f
            dmod[chunk, 0:6, :] = jnp.concatenate(mods, axis=0)
            grads[...] += tn(tokens, dh0)
            grads[0:1] += col_sum(dh0)
            for i in range(3):
                grads[11 + i : 12 + i] += db_a[i]
            for i in range(4):
                grads[14 + i : 15 + i] += db_f[0][:, i * 384 : i * 384 + 384]
            grads[18:19] += db_f[1]
            for i in range(6):
                grads[19 + i : 20 + i] += mods[i]
            return carry

        lax.fori_loop(0, count, step, 0)

    @pl.when(role[0] == 1)
    def _():
        grads[...] = grads_t[...]
        dmod[...] = dmod_t[...]
        dy[...] = jnp.zeros_like(dy)
        dkvb[...] = jnp.zeros_like(dkvb)
        ncl = dy.shape[0]
        for c in range(ncl):

            @pl.when(jnp.logical_or(half[0] == 0, c > 0))
            def _():
                pieces = []
                for i in range(2):
                    value = dkv[i, c]
                    if c == ncl - 1:
                        value = value + jnp.where(half[0] == 0, extra[i], 0.0)
                    pieces.append(low(value))
                dkvb[0, c], dkvb[1, c] = pieces
                back = low(nn(pieces[0], wb[1]) + nn(pieces[1], wb[2]))
                dy[c] = back
                grads[40:41] += col_sum(pieces[1])
                grads[10:11] += col_sum(back)

    vect[...] = jnp.transpose(grads[...])


def temporal_kernel(
    role, half, rank, lens, errw, h1, timing, mq, vec, temb, wa, wb, wf, gq, rgq, y2p, target,
    dh1, acts, actf, actw, ybuf, dkv, grads, dmod, loss, kx, vx,
):
    @pl.when(role[0] == 0)
    def _():
        loss[...] = jnp.zeros_like(loss)

    @pl.when(role[0] == 1)
    def _():
        allowed = pair_mask(1)
        count = h1.shape[0]
        ncl = ybuf.shape[0]
        for ref in (kx, vx, dkv, grads, loss):
            ref[...] = jnp.zeros_like(ref)
        first_clip = (half[0] * count) // 2

        def features(c, carry):
            clip = jnp.minimum(first_clip + c, gq.shape[0] - 1)
            y = nt(gq[clip], y2p[half[0]]) + nt(rgq[clip], y2p[1 - half[0]])
            y = low(y + vec[10:11])
            ybuf[c] = y
            kx[c, 0:LP, :] = low(nt(y, wb[1]))
            vx[c, 0:LP, :] = low(nt(y, wb[2]) + vec[40:41])
            return carry

        lax.fori_loop(0, ncl, features, 0)
        bu = up_bias(vec, 28)
        lane = lax.broadcasted_iota(jnp.int32, (1, 128), 1)
        real = jnp.logical_and(lane >= HEAD0, lane < HEAD0 + 16)
        bias_h = pltpu.roll(jnp.broadcast_to(vec[44:45, 0:128], (8, 128)), HEAD0, 1)[0:1]
        head = low(vec[...])

        def step(chunk, carry):
            clip = (half[0] * count + chunk) // 2
            here = clip - first_clip
            m = mod_rows(mq, vec, 33, clip)
            emb = temb[pl.ds(rank[0] * 8 + clip, 1), :]
            m6, m7 = vec[42:43] + emb, vec[43:44] + emb
            h = jnp.concatenate([h1[chunk, 0], h1[chunk, 1]], axis=0)
            x = h.astype(f32) + jnp.concatenate(
                [jnp.broadcast_to(timing[i : i + 1], (32, h.shape[1])) for i in range(4)], axis=0
            )
            x, kept = self_forward(x, m, wa, (vec[25:26], vec[26:27], vec[27:28]), allowed)
            xb = low(x)
            cq = low(nt(xb, wb[0]) + vec[39:40])
            keys, values = kx[here], vx[here]
            seen = lax.broadcasted_iota(jnp.int32, (1, KP), 1) < lens[clip]
            co, probs = attend(cq, keys, values, seen)
            x = x + (nt(co, wb[3]) + vec[41:42])
            x, kept_f = feed_forward(x, m, wf, bu, vec[32:33])
            h2 = low(x).astype(f32)
            normed, inv = norm(h2)
            cf = low(normed * (1.0 + m7) + m6)
            where = pl.ds(pl.multiple_of(chunk * 128, 128), 128)
            diff = jnp.where(real, nt(cf, head) + bias_h - target[where, :], 0.0)
            scale = errw[pl.ds(clip, 1), 0:1]
            loss[...] += col_sum(diff * diff) * scale
            dpred = low(diff * (2.0 * scale))
            dcf = nn(dpred, head)
            grads[...] += tn(dpred, cf)
            dbh = pltpu.roll(jnp.broadcast_to(col_sum(dpred), (8, 128)), 128 - HEAD0, 1)[0:1]
            grads[44:45, 0:128] += dbh
            dm7, dm6 = col_sum(dcf * normed), col_sum(dcf)
            dx = low(norm_back(dcf * (1.0 + m7), normed, inv)).astype(f32)
            dx, dm_f, db_f, act_f = feed_backward(dx, kept_f, m, wf)
            dcbr = low(dx)
            dco = low(nn(dcbr, wb[3]))
            dcq, dck, dcv = attend_back(dco, cq, keys, values, probs)
            dcq = low(dcq)
            dkv[0, here] += dck[0:LP]
            dkv[1, here] += dcv[0:LP]
            dx = dx + nn(dcq, wb[0])
            dx, dm_a, db_a, act_a = self_backward(dx, kept, m, wa)
            out = low(dx)
            dh1[chunk, 0] = out[0:64]
            dh1[chunk, 1] = out[64:128]
            for i, value in enumerate(act_a + (xb, dcq, co, dcbr)):
                acts[i, where, :] = value
            for i in range(2):
                actf[i, where, :] = act_f[i]
                actw[i, where, :] = act_f[2 + i]
            mods = dm_a + dm_f + (dm6, dm7)
            dmod[chunk] = jnp.concatenate(mods, axis=0)
            for i in range(3):
                grads[25 + i : 26 + i] += db_a[i]
            for i in range(4):
                grads[28 + i : 29 + i] += db_f[0][:, i * 384 : i * 384 + 384]
            grads[32:33] += db_f[1]
            for i in range(6):
                grads[33 + i : 34 + i] += mods[i]
            grads[39:40] += col_sum(dcq)
            grads[41:42] += col_sum(dcbr)
            grads[42:43] += dm6
            grads[43:44] += dm7
            return carry

        lax.fori_loop(0, count, step, 0)


def weight_grad_kernel(
    role, half, rank, acts_s, acts_t, racts, actf_s, actf_t, ractf, actw_s, actw_t, ractw,
    ybuf, rybuf, dkvb, rdkvb, dy, rdy, gq, rgq, hq, y2p, captions,
    own, snd, text_out, la, lf, lw, cap, square, turned, sums, sems,
):
    tokens = acts_s.shape[1]
    line, cols = own.shape[1], own.shape[2]
    odd = lax.rem(rank[0], 2) == 1
    near, far = pl.ds(0, tokens), pl.ds(tokens, tokens)

    def copies(r, h):
        if h == 0:
            local = acts_s if r == 0 else acts_t
            size = pl.ds(0, local.shape[0])
            return [(local, la.at[size, near], 0), (racts.at[size], la.at[size, far], 1)]
        thin, wide = ((actf_s, actw_s), (actf_t, actw_t))[r]
        return [
            (thin, lf.at[:, near], 0), (ractf, lf.at[:, far], 1),
            (wide, lw.at[:, near], 2), (ractw, lw.at[:, far], 3),
        ]

    def text():
        return [(captions.at[c], cap.at[c], 4 + c) for c in range(captions.shape[0])]

    def run(group, finish):
        for src, dst, i in group:
            copy = pltpu.make_async_copy(src, dst, sems.at[i])
            copy.wait() if finish else copy.start()

    for r in range(2):
        for h in range(2):

            @pl.when(jnp.logical_and(role[0] == r, half[0] == h))
            def _():
                run(copies(r, h), False)
                if r == 1:
                    run(text(), False)
                run(copies(r, h), True)

    def keep(unit, at, first, second):
        own[unit, at] = jnp.where(odd, second, first)
        snd[unit, at] = low(jnp.where(odd, first, second))

    def keep_square(unit, value):
        for p in range(line):
            cut = 2 * p * cols
            keep(unit, p, value[cut : cut + cols], value[cut + cols : cut + 2 * cols])

    def matrix(unit, left, right):
        keep_square(unit, tn(la[left], la[right]))

    @pl.when(half[0] == 0)
    def _():
        def square(i, carry):
            left = jnp.where(i < 3, i + 1, 2 * i - 1)
            right = jnp.where(i < 3, 0, 2 * i - 2)
            matrix(jnp.where(i < 5, i, 7), left, right)
            return carry

        lax.fori_loop(0, 4 + 2 * role[0], square, 0)

        @pl.when(role[0] == 1)
        def _():
            def cross(i, carry):
                total = tn(dkvb[i, 0], ybuf[0]) + tn(rdkvb[i, 0], rybuf[0])
                for c in range(1, ybuf.shape[0]):
                    total = total + tn(dkvb[i, c], ybuf[c]) + tn(rdkvb[i, c], rybuf[c])
                keep_square(5 + i, total)
                return carry

            lax.fori_loop(0, 2, cross, 0)

    @pl.when(half[0] == 1)
    def _():
        side = la.shape[2]
        tiles = lw.shape[2] // side
        block = 4 * cols
        per = side // (2 * block)

        def feed(i, carry):
            pair, tile = i // tiles, lax.rem(i, tiles)
            lanes = pl.ds(pl.multiple_of(tile * side, 128), side)
            value = tn(lw[pair, :, lanes], lf[pair])
            for p in range(per):
                for j in range(4):
                    at = 2 * p * block + j * cols
                    keep(
                        4 * pair + j, tile * per + p, value[at : at + cols],
                        value[at + block : at + block + cols],
                    )
            return carry

        lax.fori_loop(0, 2 * tiles, feed, 0)

    @pl.when(role[0] == 1)
    def _():
        clips = captions.shape[0]
        rows = captions.shape[1]
        def dy_of(c):
            h = (2 * c) // clips
            at = c - (h * clips) // 2
            return jnp.where(half[0] == h, dy[at].astype(f32), rdy[at].astype(f32)).astype(bf16)

        @pl.when(half[0] == 1)
        def _():
            shape = (y2p.shape[2], y2p.shape[1], cols)
            mine, theirs = units_of(1, *shape), units_of(0, *shape)
            square[...] = jnp.zeros_like(square)

            def one(c, carry):
                plain = low(nn(gq[c], mine) + nn(rgq[c], theirs))
                square[...] += tn(dy_of(c), plain)
                return carry

            lax.fori_loop(0, clips, one, 0)
            keep_square(8, square[...])

        units = text_out.shape[2]

        def keep_text(lanes, value):
            for p in range(line):
                for q in range(2):
                    cut = (2 * p + q) * units
                    text_out[p, q, :, lanes] = low(value[cut : cut + units])

        ones = jnp.ones((LP, 128), bf16)
        sums[...] = jnp.zeros_like(sums)

        def turn(c, carry):
            back = nn(dy_of(c), y2p[half[0]]) * gelu_both(hq[c])[1]
            turned[c] = low(jnp.transpose(back))
            sums[...] += nn(turned[c], ones)
            return carry

        lax.fori_loop(0, clips, turn, 0)
        run(text(), True)

        def text_tile(t, carry):
            lanes = pl.ds(pl.multiple_of(t * 512, 512), 512)
            total = nn(turned[0, :, 0:rows], cap[0, :, lanes])
            for c in range(1, clips):
                total = total + nn(turned[c, :, 0:rows], cap[c, :, lanes])
            keep_text(lanes, total)
            return carry

        lax.fori_loop(0, captions.shape[2] // 512, text_tile, 0)
        keep_text(pl.ds(captions.shape[2], 128), sums[...])


def halves(value):
    first = low(value)
    return first, low(value - first.astype(f32))


def lefts(value, axis=1):
    first, second = halves(value)
    return jnp.concatenate([first, first, second], axis=axis)


def rights(value, axis=0):
    first, second = halves(value)
    return jnp.concatenate([first, second, first], axis=axis)


def gram_of(value, dot):
    first, second = halves(value)
    both = dot(first, first), dot(first, second)
    return both[0] + (both[1] + jnp.transpose(both[1]))


def muon_kernel(half, ua, uf, xa, xf, gram, whole):
    @pl.when(half[0] == 0)
    def _():
        u = ua[...]
        whole[...] = u / (jnp.sqrt(jnp.sum(u * u)) + 1e-07)

        def sweep(i, carry):
            x = whole[...]
            square = gram_of(x, nt)
            poly = coef_b * square + coef_c * gram_of(square, nt)
            whole[...] = coef_a * x + nn(lefts(poly), rights(x))
            return carry

        lax.fori_loop(0, 5, sweep, 0)
        xa[...] = low(whole[...])

    @pl.when(half[0] == 1)
    def _():
        width = uf.shape[1]
        tiles = uf.shape[0] // width
        gram[...] = jnp.zeros_like(gram)

        def rows(t):
            return pl.ds(pl.multiple_of(t * width, 128), width)

        def first(t, carry):
            piece = uf[rows(t), :]
            gram[...] += gram_of(piece, tn)
            return carry

        lax.fori_loop(0, tiles, first, 0)
        row = lax.broadcasted_iota(jnp.int32, (width, width), 0)
        col = lax.broadcasted_iota(jnp.int32, (width, width), 1)
        eye = jnp.where(row == col, 1.0, 0.0)
        start = gram[...]
        inv = 1.0 / (jnp.sqrt(jnp.sum(start * eye)) + 1e-07)
        gram[...] = start * (inv * inv)
        whole[...] = eye * inv

        def poly_of(a):
            return coef_a * eye + coef_b * a + coef_c * nn(lefts(a), rights(a))

        def sweep(i, carry):
            a = gram[...]
            left = lefts(poly_of(a))
            both = nn(left, rights(jnp.concatenate([a, whole[...]], axis=1)))
            whole[...] = both[:, width:]

            @pl.when(i < 4)
            def _():
                gram[...] = nn(left, rights(both[:, :width]))

            return carry

        lax.fori_loop(0, 5, sweep, 0)
        last = rights(whole[...])

        def apply(t, carry):
            xf[rows(t), :] = low(nn(lefts(uf[rows(t), :]), last))
            return carry

        lax.fori_loop(0, tiles, apply, 0)


def local_call(kernel, out_shape, in_specs, args, scratch=(), out_specs=None):
    return pl.pallas_call(
        kernel,
        out_shape=out_shape,
        in_specs=in_specs,
        out_specs=jax.tree.map(lambda _: VM, out_shape) if out_specs is None else out_specs,
        scratch_shapes=scratch,
        compiler_params=pltpu.CompilerParams(vmem_limit_bytes=VMEM_LIMIT),
    )(*args)


def here():
    return lax.axis_index("dp"), lax.axis_index("segment")


def dev(d, s):
    return {"dp": d, "segment": s}


def remote(src, dst, send, recv, target):
    return pltpu.make_async_remote_copy(
        src_ref=src, dst_ref=dst, send_sem=send, recv_sem=recv, device_id=target,
        device_id_type=MESH,
    )


def greet(targets):
    barrier = pltpu.get_barrier_semaphore()
    for target in targets:
        pl.semaphore_signal(barrier, inc=1, device_id=target, device_id_type=MESH)
    pl.semaphore_wait(barrier, len(targets))


def greet_dp(n, extra=()):
    d, s = here()
    barrier = pltpu.get_barrier_semaphore()

    def step(k, carry):
        pl.semaphore_signal(
            barrier, inc=1, device_id=dev(lax.rem(d + k, n), s), device_id_type=MESH
        )
        return carry

    lax.fori_loop(1, n, step, 0)
    for target in extra:
        pl.semaphore_signal(barrier, inc=1, device_id=target, device_id_type=MESH)
    pl.semaphore_wait(barrier, n - 1 + len(extra))


def comm_call(kernel, cid, args, out_shape, sems, out_specs=None, scratch=(), in_specs=None):
    if out_specs is None:
        out_specs = jax.tree.map(lambda _: ANY, out_shape)
    return pl.pallas_call(
        kernel,
        out_shape=out_shape,
        in_specs=[ANY] * len(args) if in_specs is None else in_specs,
        out_specs=out_specs,
        scratch_shapes=list(scratch) + [pltpu.SemaphoreType.DMA(shape) for shape in sems],
        compiler_params=pltpu.CompilerParams(
            collective_id=cid, has_side_effects=True, vmem_limit_bytes=VMEM_LIMIT
        ),
    )(*args)


ACROSS_FIRST = 2


def gather_kernel(n, pa, pb, pf, pw, py, pm, pt, wa, wb, wf, ww, wy, wm, wt,
                  send, recv, crecv, own):
    pair = 2 if n % 2 == 0 else 1
    line = n // pair
    d, s = here()
    role, half = s // 2, lax.rem(s, 2)
    a, x = d // pair, lax.rem(d, pair)
    mate = dev(d, role * 2 + 1 - half)
    above, below = dev(d + pair, s), dev(d - pair, s)
    across = dev(a * pair + (pair - 1 - x), s)
    barrier = pltpu.get_barrier_semaphore()

    def signal(target):
        pl.semaphore_signal(barrier, inc=1, device_id=target, device_id_type=MESH)

    signal(mate)
    if pair == 2:
        signal(across)

    @pl.when(a < line - 1)
    def _():
        signal(above)

    @pl.when(a > 0)
    def _():
        signal(below)

    pl.semaphore_wait(barrier, pair + jnp.minimum(a, 1) + jnp.minimum(line - 1 - a, 1))

    def two(i, ref, out):
        return [
            (i, ref.at[pl.ds(0, 2)], out.at[pl.ds(0, 2)], 2),
            (i + 1, ref.at[pl.ds(2, 2)], out.at[pl.ds(2, 2)], 2),
        ]

    first, last = half == 0, role == 1
    both = jnp.logical_and(first, last)
    shared = [((2, pw, ww, 0), first, True)]
    shared += [(item, first, True) for item in two(0, pa, wa)]
    shared += [(item, both, last) for item in two(5, pb, wb)]
    for m in range(2):
        item = (m, pf.at[pl.ds(m, 1)], wf.at[pl.ds(m, 1)], 1)
        shared.append((item, jnp.logical_not(first), True))
    alone = [((3, pt, wt, 0), True), ((4, pm, wm, 0), role == 0), ((4, py, wy, 0), role == 1)]
    parts = [(item, when, True) for item, when, _ in shared]
    parts += [(item, when, False) for item, when in alone]

    def slot(ref, lead, o):
        return ref.at[:, o] if lead else ref.at[o]

    def given(when, act):
        if when is True:
            act()
        else:
            pl.when(when)(act)

    def move(item, way, o, target, is_own=False):
        i, src, dst, lead = item
        there = slot(dst, lead, o)
        sem = crecv if way == 3 else recv
        return remote(src if is_own else there, there, send.at[way, i, o], sem.at[i, o], target)

    def forward(o, up, down, side, wait, ways=None):
        is_own = not wait
        for item, when, common in parts:

            def act(item=item, common=common, up=up, down=down, side=side):
                if item[0] == ACROSS_FIRST and pair == 2:
                    side = is_own
                    up, down = (up, down) if ways is None else ways
                if wait:
                    move(item, 0, o, across).wait_recv()

                def go(way, target):
                    move(item, way, o, target, is_own).start()

                if side and pair == 2:
                    go(2, across)
                if up is not None:
                    pl.when(up)(functools.partial(go, 0, above))
                if down is not None:
                    pl.when(down)(functools.partial(go, 1, below))
                if common:
                    go(3, mate)

            given(when, act)

    def keep(finish):
        for item, when, common in parts:

            def act(item=item):
                i, src, dst, lead = item
                copy = pltpu.make_async_copy(src, slot(dst, lead, d), own.at[i])
                copy.wait() if finish else copy.start()

            given(when, act)

    forward(d, a < line - 1, a > 0, True, False)
    keep(False)
    other = pair - 1 - x

    def sweep():
        def step(k, carry):
            @pl.when(a - k >= 0)
            def _():
                forward((a - k) * pair + x, a < line - 1, None, True, True)

            @pl.when(a + k < line)
            def _():
                forward((a + k) * pair + x, None, a > 0, True, True)

            if pair == 2:

                def from_side(o, up, down):
                    forward(o * pair + other, None, None, False, True, (up, down))

                @pl.when(a - (k - 1) >= 0)
                def _():
                    from_side(
                        a - (k - 1), a < line - 1, jnp.logical_and(k == 1, a > 0)
                    )

                @pl.when(jnp.logical_and(k > 1, a + (k - 1) < line))
                def _():
                    from_side(a + (k - 1), None, a > 0)

            return carry

        lax.fori_loop(1, line + 1, step, 0)

    sweep()

    def drain(o, carry):
        there, column = o // pair, lax.rem(o, pair)
        mine = column == x
        up = jnp.logical_and(there <= a, a < line - 1)
        down = jnp.logical_and(there >= a, a > 0)
        for item, when, common in parts:

            def act(item=item, common=common):
                lines_first = item[0] != ACROSS_FIRST or pair == 1
                sent = (
                    (0, jnp.logical_and(mine, up) if lines_first else up, above),
                    (1, jnp.logical_and(mine, down) if lines_first else down, below),
                    (2, mine if lines_first else o == d, across),
                )
                for way, yes, target in sent:
                    if way == 2 and pair == 1:
                        continue
                    pl.when(yes)(lambda: move(item, way, o, target).wait_send())
                if common:
                    move(item, 3, o, mate).wait_send()

            given(when, act)
        return carry

    lax.fori_loop(0, n, drain, 0)
    keep(True)

    def collect(o, carry):
        for item, when, arrives in shared:
            mine = when if when is not both else first

            def act(item=item):
                i, src, dst, lead = item
                there = slot(dst, lead, o)
                remote(there, there, send.at[3, i, o], crecv.at[i, o], mate).wait_recv()

            given(jnp.logical_and(jnp.logical_not(mine), arrives), act)
        return carry

    lax.fori_loop(0, n, collect, 0)


def mate_kernel(src, dst, send, recv, own):
    d, s = here()
    role, half = s // 2, lax.rem(s, 2)
    mate = dev(d, role * 2 + 1 - half)

    @pl.when(role == 0)
    def _():
        greet([mate])
        pltpu.make_async_copy(src, dst.at[half], own.at[0]).start()
        remote(src, dst.at[half], send.at[0], recv.at[0], mate).start()
        pltpu.make_async_copy(src, dst.at[half], own.at[0]).wait()
        remote(src, dst.at[1 - half], send.at[0], recv.at[0], mate).wait()


def forward_kernel(count, h1s, gq, mq, h1t, gqs, mqt, send, recv, msend, mrecv, qsend, qrecv):
    relay_half_clips(
        count, 0, h1s, h1t, send, recv, swap=(gq, gqs, msend, mrecv), rows=(mq, mqt, qsend, qrecv)
    )


def relay_half_clips(count, from_role, src, dst, send, recv, extra=None, swap=None, rows=None):
    d, s = here()
    role, half = s // 2, lax.rem(s, 2)
    peers = [dev(d, (1 - role) * 2), dev(d, (1 - role) * 2 + 1)]
    mate = dev(d, role * 2 + 1 - half)
    peers.append(mate)
    greet(peers)

    def unit(i, part):
        there = half * count + i
        clip, own = there // 2, lax.rem(there, 2)
        other = 2 * clip + part
        return own, other // count, lax.rem(other, count)

    def copy(i, part):
        own, to, slot = unit(i, part)
        return remote(
            src.at[i, part], dst.at[slot, own], send.at[i, part], recv.at[slot, own],
            dev(d, (1 - from_role) * 2 + to),
        )

    def row_copy(to, finish):
        value, there, qsend, qrecv = rows
        copy = remote(value, there, qsend.at[to], qrecv.at[half], dev(d, (1 - from_role) * 2 + to))
        copy.wait_send() if finish else copy.start()

    def row_sends(finish):
        if rows is None:
            return

        @pl.when(role == from_role)
        def _():
            for to in range(2):
                pl.when(half == to)(functools.partial(row_copy, to, finish))

    row_sends(False)
    if swap is not None:
        mine, both, msend, mrecv = swap

        @pl.when(role == 1)
        def _():
            remote(mine, both, msend.at[0], mrecv.at[0], mate).start()

    if extra is not None:
        own_src, own_dst, esend, erecv = extra

        @pl.when(jnp.logical_and(role == 1, half == 1))
        def _():
            remote(own_src, own_dst, esend.at[0], erecv.at[0], dev(d, 2)).start()

    @pl.when(role == from_role)
    def _():
        for i in range(count):
            for part in range(2):
                copy(i, part).start()
        for i in range(count):
            for part in range(2):
                copy(i, part).wait_send()

    @pl.when(role == 1 - from_role)
    def _():
        for i in range(count):
            for part in range(2):
                remote(
                    src.at[i, part], dst.at[i, part], send.at[i, part], recv.at[i, part],
                    dev(d, from_role * 2),
                ).wait_recv()

    row_sends(True)
    if rows is not None:
        value, there, qsend, qrecv = rows

        @pl.when(role == 1 - from_role)
        def _():
            remote(value, there, qsend.at[0], qrecv.at[half], mate).wait_recv()

    if swap is not None:

        @pl.when(role == 1)
        def _():
            remote(mine, both, msend.at[0], mrecv.at[0], mate).wait()

    if extra is not None:

        @pl.when(jnp.logical_and(role == 1, half == 1))
        def _():
            remote(own_src, own_dst, esend.at[0], erecv.at[0], dev(d, 2)).wait_send()

        @pl.when(jnp.logical_and(role == 1, half == 0))
        def _():
            remote(own_src, own_dst, esend.at[0], erecv.at[0], dev(d, 2)).wait_recv()


def backward_kernel(count, dh1, dkv, dhs, extra, send, recv, esend, erecv):
    relay_half_clips(count, 1, dh1, dhs, send, recv, extra=(dkv.at[:, 0], extra, esend, erecv))


def swap_kernel(acts_s, acts_t, actf_s, actf_t, actw_s, actw_t, ybuf, dkvb, dy, dmod,
                racts, ractf, ractw, rybuf, rdkvb, rdy, rdmod, send, recv):
    d, s = here()
    role, half = s // 2, lax.rem(s, 2)
    mate = dev(d, role * 2 + 1 - half)
    greet([mate])
    six = acts_s.shape[0]
    gives = {
        (0, 0): [(0, actf_s, ractf), (1, actw_s, ractw), (4, dmod, rdmod)],
        (0, 1): [(0, acts_s, racts.at[pl.ds(0, six)]), (4, dmod, rdmod)],
        (1, 0): [(0, actf_t, ractf), (1, actw_t, ractw), (2, dy, rdy), (4, dmod, rdmod)],
        (1, 1): [
            (0, acts_t, racts), (1, ybuf, rybuf), (3, dkvb, rdkvb), (2, dy, rdy), (4, dmod, rdmod)
        ],
    }
    for (r, h), mine in gives.items():

        @pl.when(jnp.logical_and(role == r, half == h))
        def _():
            for i, src, dst in mine:
                remote(src, dst, send.at[i], recv.at[i], mate).start()
            for i, src, dst in mine:
                remote(src, dst, send.at[i], recv.at[i], mate).wait_send()
            for i, src, dst in gives[(r, 1 - h)]:
                remote(src, dst, send.at[i], recv.at[i], mate).wait_recv()


TEXT_CUTS = 11


def scatter_kernel(n, own_in, snd, text_in, vec, dmod, rdmod, loss, wm, temb, ww, hid, wt,
                   summed, text, vsum, squares, gm, g2, g1,
                   own, rx, up, down, sx, rz, tin, trx, tsx, trz, rv, rm, dtembs, dm, dmt,
                   osem, send1, recv1, send2, recv2, usend, urecv, dsend, drecv,
                   ssend, srecv, sown, tsend, trecv, esend, erecv, psend, precv):
    line = n // 2
    d, s = here()
    role, half = s // 2, lax.rem(s, 2)
    a, x = d // 2, lax.rem(d, 2)
    across = dev(a * 2 + 1 - x, s)
    other = dev(d, (1 - role) * 2 + half)
    count = 8 - 4 * (1 - role) * (1 - half)
    greet_dp(n, [other])
    squares[...] = jnp.zeros_like(squares)
    squares[1:2, 0:128] = loss[...]
    step = text.shape[1] // TEXT_CUTS
    is_text, is_last, is_time = role == 0, s == 3, s == 0
    clip_rows = dm.shape[0]

    def clip_sums():
        clips = dmod.shape[0]
        sources = (dmod, rdmod)
        for clip in range(clips):
            total = None
            for h in range(2):
                for i in range(clips):
                    if (h * clips + i) // 2 == clip:
                        part = sources[h][i]
                        total = part if total is None else total + part
            dm[8 * clip : 8 * clip + 8] = total

    pl.when(half == 0)(clip_sums)
    partial = remote(dm, dmt, psend.at[0], precv.at[0], other)

    def first_copies(u):
        return (
            remote(snd.at[u], rx.at[u], send1.at[u], recv1.at[u], across),
            pltpu.make_async_copy(own_in.at[u], own.at[u], osem.at[u]),
        )

    def text_hop(k):
        lanes = pl.ds(pl.multiple_of(k * step, 128), step)
        return remote(text_in.at[:, :, :, lanes], tin.at[k], tsend.at[k], trecv.at[k], other)

    def text_across(k):
        return remote(tin.at[k, :, 1 - x], trx.at[k], send1.at[9 + k], recv1.at[9 + k], across)

    def begin(u, carry):
        for copy in first_copies(u):
            copy.start()
        return carry

    def rows_at(o):
        return rm.at[pl.ds(pl.multiple_of(o * clip_rows, 8), clip_rows)]

    def small(i, finish):
        src, dst = (
            (lambda p: vec.at[p], lambda o: rv.at[o]) if i else (lambda p: dm, rows_at)
        )

        def each(k, carry):
            to, o = lax.rem(d + k, n), lax.rem(d + n - k, n)
            if finish:
                remote(src(o), dst(o), ssend.at[i, k], srecv.at[i, k], dev(o, s)).wait()
            else:
                remote(src(to), dst(d), ssend.at[i, k], srecv.at[i, k], dev(to, s)).start()
            return carry

        lax.fori_loop(1, n, each, 0)
        copy = pltpu.make_async_copy(src(d), dst(d), sown.at[i])
        copy.wait() if finish else copy.start()

    lax.fori_loop(0, 1, begin, 0)
    small(1, False)

    @pl.when(is_time)
    def _():
        partial.wait_recv()
        dm[...] = dm[...] + dmt[...]

    lax.fori_loop(1, count, begin, 0)

    @pl.when(is_last)
    def _():
        begin(8, 0)

    @pl.when(role == 1)
    def _():
        pl.when(half == 0)(lambda: partial.start())
        lax.fori_loop(0, TEXT_CUTS, lambda k, c: (text_hop(k).start(), c)[1], 0)

    def embeds(finish):
        def each(k, carry):
            to, o = lax.rem(d + k, n), lax.rem(d + n - k, n)
            if finish:
                remote(dtembs.at[o], dtembs.at[o], esend.at[k], erecv.at[k], dev(o, s)).wait()
            else:
                remote(dtembs.at[d], dtembs.at[d], esend.at[k], erecv.at[k], dev(to, s)).start()
            return carry

        lax.fori_loop(1, n, each, 0)

    def upward(u, p):
        return remote(up.at[u, p], up.at[u, p], usend.at[u, p], urecv.at[u, p], dev(d + 2, s))

    def downward(u, p):
        return remote(
            down.at[u, p], down.at[u, p], dsend.at[u, p], drecv.at[u, p], dev(d - 2, s)
        )

    def along_up(u):
        def add(i, carry):
            p = line - 1 - i

            @pl.when(a == 0)
            def _():
                up[u, p] = own[u, p]

            @pl.when(a > 0)
            def _():
                upward(u, p).wait_recv()
                up[u, p] = up[u, p] + own[u, p]

            return carry

        def send(i, carry):
            upward(u, line - 1 - i).start()
            return carry

        lax.fori_loop(0, line - 1 - a, add, 0)
        lax.fori_loop(0, line - 1 - a, send, 0)

    def along_down(u):
        def add(p, carry):
            @pl.when(a == line - 1)
            def _():
                down[u, p] = own[u, p]

            @pl.when(a < line - 1)
            def _():
                downward(u, p).wait_recv()
                down[u, p] = down[u, p] + own[u, p]

            return carry

        def send(p, carry):
            downward(u, p).start()
            return carry

        lax.fori_loop(0, a, add, 0)
        lax.fori_loop(0, a, send, 0)

    def pairs(u):
        for copy in first_copies(u):
            copy.wait()
        own[u] = own[u] + rx[u].astype(f32)

    def direct(i, total, line_in, finish):
        def each(k, carry):
            to, o = lax.rem(a + k, line), lax.rem(a + line - k, line)
            if finish:
                remote(
                    total.at[o], line_in.at[o], send2.at[i, k], recv2.at[i, k], dev(o * 2 + x, s)
                ).wait()
            else:
                remote(
                    total.at[to], line_in.at[a], send2.at[i, k], recv2.at[i, k],
                    dev(to * 2 + x, s),
                ).start()
            return carry

        lax.fori_loop(1, line, each, 0)

    def round_trip(i, carry):
        @pl.when(i < count)
        def _():
            pairs(i)

        pl.when(jnp.logical_and(is_time, i == 0))(lambda: small(0, False))

        @pl.when(jnp.logical_and(is_time, i == 1))
        def _():
            small(0, True)
            time_back([d], rm, wm, temb, dtembs.at[d])

        pl.when(jnp.logical_and(is_time, i == 2))(lambda: embeds(False))

        @pl.when(is_text)
        def _():
            def cut_at(delay, act):
                for j in range(2):
                    k = 2 * (i - delay) + j
                    pl.when(jnp.logical_and(k >= 0, k < TEXT_CUTS))(functools.partial(act, k))

            def arrive(k):
                text_hop(k).wait_recv()
                text_across(k).start()

            def add(k):
                text_across(k).wait()
                tsx[k] = low(tin[k, :, x].astype(f32) + trx[k].astype(f32))

            cut_at(5, lambda k: direct(k, tsx.at[k], trz.at[k], False))
            cut_at(3, arrive)
            cut_at(4, add)

        k = i - count

        @pl.when(jnp.logical_and(is_last, k == 0))
        def _():
            pairs(8)
            sx[...] = low(own[8])

        @pl.when(jnp.logical_and(is_last, k == 1))
        def _():
            direct(TEXT_CUTS, sx, rz, False)

        later = i - 1 - a

        @pl.when(jnp.logical_and(later >= 0, later < count))
        def _():
            along_up(later)

        other = i - line + a

        @pl.when(jnp.logical_and(other >= 0, other < count))
        def _():
            along_down(other)

        return carry

    lax.fori_loop(0, jnp.maximum(count + line, TEXT_CUTS // 2 + 6), round_trip, 0)
    small(1, True)
    vsum[...] = lax.fori_loop(0, n, lambda o, total: total + rv[o], jnp.zeros(vsum.shape, f32))

    @pl.when(is_time)
    def _():
        embeds(True)
        time_grad([d], rm, dtembs, ww, temb, hid, wt, gm, g2, g1, vsum, squares)

    @pl.when(role == 1)
    def _():
        pl.when(half == 0)(lambda: partial.wait_send())
        lax.fori_loop(0, TEXT_CUTS, lambda k, c: (text_hop(k).wait_send(), c)[1], 0)

    def collect(u, carry):
        @pl.when(a > 0)
        def _():
            upward(u, a).wait_recv()
            own[u, a] = own[u, a] + up[u, a]

        @pl.when(a < line - 1)
        def _():
            downward(u, a).wait_recv()
            own[u, a] = own[u, a] + down[u, a]

        whole = own[u, a]
        summed[u] = whole
        squares[0:1, :] += col_sum(whole * whole)
        return carry

    lax.fori_loop(0, count, collect, 0)

    def drain(u, carry):
        def one(i, c):
            upward(u, line - 1 - i).wait_send()
            return c

        def two(p, c):
            downward(u, p).wait_send()
            return c

        lax.fori_loop(0, line - 1 - a, one, 0)
        lax.fori_loop(0, a, two, 0)
        return carry

    lax.fori_loop(0, count, drain, 0)

    def others(line_in, whole):
        return lax.fori_loop(
            1, line, lambda k, acc: acc + line_in[lax.rem(a + k, line)].astype(f32), whole
        )

    @pl.when(is_last)
    def _():
        direct(TEXT_CUTS, sx, rz, True)
        whole = others(rz, own[8, a])
        summed[8] = whole
        squares[0:1, :] += col_sum(whole * whole)

    @pl.when(is_text)
    def _():
        def whole_cut(k, carry):
            direct(k, tsx.at[k], trz.at[k], True)
            whole = others(trz.at[k], tin[k, a, x].astype(f32) + trx[k, a].astype(f32))
            text[:, pl.ds(pl.multiple_of(k * step, 128), step)] = low(whole)
            lane = lax.broadcasted_iota(jnp.int32, (1, step), 1)
            spare = jnp.logical_and(k == TEXT_CUTS - 1, lane > step - 128)
            counted = jnp.where(spare, 0.0, whole)
            squares[0:1, :] += col_sum(counted * counted)
            return carry

        lax.fori_loop(0, TEXT_CUTS, whole_cut, 0)


def three(value):
    first = low(value)
    rest = value - first.astype(f32)
    second = low(rest)
    return first, second, low(rest - second.astype(f32))


def nn3(left, right):
    return sum(nn(piece, right) for piece in three(left))


def nt3(left, right):
    return sum(nt(piece, right) for piece in three(left))


def tn3(left, right):
    return sum(tn(left, piece) for piece in three(right))


def own_columns(rank, width, cols):
    row = lax.broadcasted_iota(jnp.int32, (width, 128), 0)
    col = lax.broadcasted_iota(jnp.int32, (width, 128), 1)
    return low(jnp.where(jnp.logical_and(row == rank * cols + col, col < cols), 1.0, 0.0))


def clip_groups(clips, rows):
    per = 8 * (rows // (clips // 8) // 8)
    left = lax.broadcasted_iota(jnp.int32, (clips, rows), 0)
    right = lax.broadcasted_iota(jnp.int32, (clips, rows), 1)
    match = (right // per) * 8 + (right % per) // 8 == left
    return low(jnp.where(match, 1.0, 0.0))


def silu_back(value):
    gate = jax.nn.sigmoid(value)
    return gate * (1.0 + value * (1.0 - gate))


def time_back(rank, rm, wm, temb, dtemb):
    cols, width = wm.shape[0], rm.shape[1]
    rows, clips = rm.shape[0], temb.shape[0]
    pick = own_columns(rank[0], width, cols)
    kind = lax.broadcasted_iota(jnp.int32, (rows, 1), 0) % 8
    value = rm[...]
    pieces = three(value)
    total = jnp.where(kind >= 6, nn3(value, pick), 0.0)
    zeros = jnp.zeros((128 - cols, width), bf16)

    def one(r, total):
        lanes = pl.ds(pl.multiple_of(r * width, 128), width)
        weight = jnp.concatenate([wm[:, lanes], zeros], axis=0)
        back = nt(pieces[0], weight) + nt(pieces[1], weight) + nt(pieces[2], weight)
        return total + jnp.where(kind == r, back, 0.0)

    total = lax.fori_loop(0, 6, one, total)
    slope = silu_back(nn3(temb[...], pick))
    group = clip_groups(clips, rows)

    def collapse(part):
        first, second, third = three(part)
        return nn(group, first) + nn(group, second) + nn(group, third)

    dtemb[...] = collapse(jnp.where(kind < 6, total, 0.0)) * slope + collapse(
        jnp.where(kind >= 6, total, 0.0)
    )


def time_grad(rank, rm, dtembs, ww, temb, hid, wt, gm, g2, g1, vout, tout):
    width, cols = rm.shape[1], vout.shape[0]
    rows, clips = rm.shape[0], temb.shape[0]
    n = dtembs.shape[0]
    pick = own_columns(rank[0], width, cols)
    kind = lax.broadcasted_iota(jnp.int32, (rows, 1), 0) % 8
    value = rm[...]
    hidden = hid[...]
    own_hid, own_temb = nn3(hidden, pick), nn3(temb[...], pick)
    gates = low(own_temb * jax.nn.sigmoid(own_temb))
    spread = low(tn(clip_groups(clips, rows), gates))
    pieces = three(value)
    count = jnp.zeros((1, 1), f32)

    def squared(block):
        return jnp.sum(jnp.sum(block * block, axis=1, keepdims=True), axis=0, keepdims=True)

    def one(r, count):
        masked = jnp.where(kind == r, spread.astype(f32), 0.0).astype(bf16)
        block = sum(tn(masked, piece) for piece in pieces)[0:cols]
        gm[:, pl.ds(pl.multiple_of(r * width, 128), width)] = block
        return count + squared(block)

    count = lax.fori_loop(0, 6, one, count)
    mine = dtembs[rank[0]]
    mine_pieces = three(mine)
    act = low(hidden * jax.nn.sigmoid(hidden))
    block = sum(tn(piece, act) for piece in mine_pieces)[0:cols]
    g2[...] = block
    count = count + squared(block)
    back = jnp.zeros((clips, 128), f32)
    zeros = jnp.zeros((128 - cols, 128), bf16)
    picked = low(nn(ww[:, 256 : 256 + width], pick))
    for o in range(n):
        weight = picked[o * cols : o * cols + cols]
        back = back + nn3(dtembs[o], jnp.concatenate([weight, zeros], axis=0))
    dhid = back * silu_back(own_hid)
    dhid_pieces = three(dhid)
    feature = low(wt[:, 0:256])
    block = sum(tn(piece, feature) for piece in dhid_pieces)[0:cols]
    g1[...] = block
    count = count + squared(block)
    at = lax.broadcasted_iota(jnp.int32, (clips, 128), 1)
    first = low(jnp.where(at == 1, 1.0, 0.0))
    second = low(jnp.where(at == 2, 1.0, 0.0))
    total = sum(tn(piece, first) for piece in dhid_pieces)
    total = total + sum(tn(piece, second) for piece in mine_pieces)
    row_kind = lax.broadcasted_iota(jnp.int32, (rows, 128), 0) % 8
    row_lane = lax.broadcasted_iota(jnp.int32, (rows, 128), 1)
    put = jnp.logical_and(row_lane == row_kind + 3, row_kind < 6)
    put = low(jnp.where(put, 1.0, 0.0))
    total = total + sum(tn(piece, put) for piece in three(nn3(value, pick)))

    vout[...] += total[0:cols]
    lane = lax.broadcasted_iota(jnp.int32, (1, 128), 1)
    tout[0:1, 0:128] += jnp.where(lane == 0, count, 0.0)


class Relay:
    def __init__(self, send, recv):
        self.d, self.s = here()
        self.role, self.half = self.s // 2, lax.rem(self.s, 2)
        self.other = dev(self.d, (1 - self.role) * 2 + self.half)
        self.mate = dev(self.d, self.role * 2 + 1 - self.half)
        self.send, self.recv = send, recv

    def at(self, r, h):
        return jnp.logical_and(self.role == r, self.half == h)

    def copy(self, i, leg, src, dst):
        target = self.other if leg == 0 else self.mate
        return remote(src, dst, self.send.at[i, leg], self.recv.at[i, leg], target)

    def start(self, i, src, dst):
        self.copy(i, 0, src, dst).start()
        self.copy(i, 1, src, dst).start()

    def middle(self, i, dst):
        self.copy(i, 0, dst, dst).wait_recv()
        self.copy(i, 2, dst, dst).start()

    def finish(self, r, h, items):
        @pl.when(self.at(r, h))
        def _():
            for i, src, dst in items:
                self.copy(i, 0, src, dst).wait_send()
                self.copy(i, 1, src, dst).wait_send()

        @pl.when(self.at(1 - r, h))
        def _():
            for i, src, dst in items:
                self.copy(i, 2, dst, dst).wait_send()

        @pl.when(self.at(r, 1 - h))
        def _():
            for i, src, dst in items:
                self.copy(i, 1, dst, dst).wait_recv()

        @pl.when(self.at(1 - r, 1 - h))
        def _():
            for i, src, dst in items:
                self.copy(i, 2, dst, dst).wait_recv()


def owner_first(role, mat):
    return 2 * mat + mat % 2 if role == 0 else mat


def owner_second(mat):
    return 2 + 3 * mat


def settle_kernel(n, vsum, tile, summed, att_m, feed_m, gm, g2, g1,
                  oa, of, xa, xf, xm, x2, x1, gv, stat,
                  vecs, tiles, mine, totals, look, mom,
                  msem, send, recv, own, gsend, grecv, gown, ssend, srecv, tsend, trecv):
    relay = Relay(gsend, grecv)
    d, s, role, half = relay.d, relay.s, relay.role, relay.half
    peers = [dev(d, lax.rem(s + k, 4)) for k in range(1, 4)]
    greet_dp(n, peers)
    four, eight = pl.ds(0, 4), pl.ds(0, 8)
    shared = {
        (0, 0): [(0, summed.at[four], xa.at[four]), (4, gm, xm), (5, g2, x2), (6, g1, x1)],
        (0, 1): [(1, summed.at[eight], xf.at[eight])],
        (1, 0): [(2, summed.at[eight], xa.at[pl.ds(4, 8)])],
        (1, 1): [(3, summed.at[eight], xf.at[pl.ds(8, 8)])],
    }
    def momentum(finish):
        sources = {
            (0, 0): (att_m.at[four], mom.at[four]),
            (0, 1): (feed_m.at[eight], mom),
            (1, 0): (att_m.at[pl.ds(4, 8)], mom),
            (1, 1): (feed_m.at[pl.ds(8, 8)], mom),
        }
        for (r, h), (src, dst) in sources.items():

            @pl.when(relay.at(r, h))
            def _():
                copy = pltpu.make_async_copy(src, dst, msem.at[0])
                copy.wait() if finish else copy.start()

    momentum(False)
    small = [(0, vsum, vecs), (1, tile, tiles)]
    for i, src, dst in small:
        for k in range(1, 4):
            remote(src, dst.at[s], ssend.at[i, k], srecv.at[i, k], peers[k - 1]).start()
    for (r, h), items in shared.items():

        @pl.when(relay.at(r, h))
        def _():
            for i, src, dst in items:
                pltpu.make_async_copy(src, dst, gown.at[i]).start()
                relay.start(i, src, dst)

    total, squares, losses = vsum[...], tile[0:1, :], tile[1:2, :]
    for k in range(1, 4):
        o = lax.rem(s + 4 - k, 4)
        for i, src, dst in small:
            remote(src, dst.at[o], ssend.at[i, k], srecv.at[i, k], dev(d, o)).wait()
        total = total + vecs[o]
        squares = squares + tiles[o, 0:1, :]
        losses = losses + tiles[o, 1:2, :]
    lane = lax.broadcasted_iota(jnp.int32, (1, 128), 1)
    total = jnp.where(jnp.logical_or(lane == 9, lane >= 77), 0.0, total)
    gv[...] = total

    def whole(block):
        return jnp.sum(jnp.sum(block, axis=1, keepdims=True), axis=0, keepdims=True)

    row = lax.broadcasted_iota(jnp.int32, (8, 128), 0)
    mine[...] = jnp.where(row < 4, whole(squares) + whole(total * total), whole(losses[:, 0:128]))
    so_far = mine[...]

    def start(k, carry):
        remote(mine, totals.at[d], tsend.at[k], trecv.at[k], dev(lax.rem(d + k, n), s)).start()
        return carry

    lax.fori_loop(1, n, start, 0)

    def finish(k, carry):
        o = lax.rem(d + n - k, n)
        remote(mine, totals.at[o], tsend.at[k], trecv.at[k], dev(o, s)).wait()
        return carry + totals[o]

    lax.fori_loop(1, n, lambda k, c: (finish(k, so_far), c)[1], 0)
    totals[d] = so_far
    so_far = lax.fori_loop(0, n, lambda o, c: c + totals[o], jnp.zeros((8, 128), f32))
    stat[...] = so_far
    factor = jnp.minimum(1.0, max_norm / (jnp.sqrt(so_far[0:1, 0:1]) + 1e-06))
    scale = factor * (1.0 + momentum_decay)

    momentum(True)

    def update(m, carry):
        look[m] = summed[m] * scale + mom[m] * (momentum_decay * momentum_decay)
        return carry

    lax.fori_loop(0, 8, update, 0)
    groups = []
    for r in range(2):
        mats = 4 if r == 0 else 8
        groups.append((r, 0, [(m, owner_first(r, m), look.at[m], oa) for m in range(mats)]))
        groups.append((
            r, 1, [(m, owner_second(m), look.at[pl.ds(4 * m, 4)], of) for m in range(2)]
        ))
    for r, h, mats in groups:

        @pl.when(relay.at(r, h))
        def _():
            for m, o, src, dst in mats:

                @pl.when(d == o)
                def _():
                    pltpu.make_async_copy(src, dst.at[d], own.at[0]).start()

                @pl.when(d != o)
                def _():
                    remote(src, dst.at[d], send.at[m], recv.at[d], dev(o, s)).start()

    for (r, h), items in shared.items():

        @pl.when(relay.at(1 - r, h))
        def _():
            for i, src, dst in items:
                relay.middle(i, dst)

    for r, h, mats in groups:

        @pl.when(relay.at(r, h))
        def _():
            for i, src, dst in shared[(r, h)]:
                pltpu.make_async_copy(src, dst, gown.at[i]).wait()
            for m, o, src, dst in mats:

                @pl.when(d == o)
                def _():
                    pltpu.make_async_copy(src, dst.at[d], own.at[0]).wait()

                    def arrived(k, carry):
                        p = lax.rem(d + n - k, n)
                        remote(src, dst.at[p], send.at[m], recv.at[p], dev(p, s)).wait_recv()
                        return carry

                    lax.fori_loop(1, n, arrived, 0)

                @pl.when(d != o)
                def _():
                    remote(src, dst.at[d], send.at[m], recv.at[d], dev(o, s)).wait_send()

    for (r, h), items in shared.items():
        relay.finish(r, h, items)


def spread_kernel(n, xa, xf, gy1, summed, oa, of, xy1, xy2, send, recv, rsend, rrecv, own, gown):
    relay = Relay(rsend, rrecv)
    d, s, role, half = relay.d, relay.s, relay.role, relay.half
    greet_dp(n, [relay.other, relay.mate])
    groups = []
    for r in range(2):
        mats = 4 if r == 0 else 8
        groups.append((r, 0, mats, functools.partial(owner_first, r), xa, oa, 10 * r, 4))
        groups.append((r, 1, 2, owner_second, xf, of, 10 * r + 8, 2))
    text = {
        (0, 0): [(20, gy1, xy1.at[0])],
        (0, 1): [(21, gy1, xy1.at[1])],
        (1, 1): [(22, summed.at[8], xy2)],
    }
    for (r, h), items in text.items():

        @pl.when(relay.at(r, h))
        def _():
            for i, src, dst in items:
                pltpu.make_async_copy(src, dst, gown.at[i - 20]).start()
                relay.start(i, src, dst)

    for r, h, mats, owner, src, dst, base, per in groups:

        @pl.when(relay.at(r, h))
        def _():
            for m in range(mats):

                @pl.when(d == owner(m))
                def _():
                    pltpu.make_async_copy(src.at[d], dst.at[per * r + m], own.at[m]).start()

                    def start(k, carry):
                        to = lax.rem(d + k, n)
                        remote(
                            src.at[to], dst.at[per * r + m], send.at[k], recv.at[m], dev(to, s)
                        ).start()
                        return carry

                    lax.fori_loop(1, n, start, 0)

            for m in range(mats):

                @pl.when(d == owner(m))
                def _():
                    pltpu.make_async_copy(src.at[d], dst.at[per * r + m], own.at[m]).wait()

                @pl.when(d != owner(m))
                def _():
                    remote(
                        src.at[d], dst.at[per * r + m], send.at[1], recv.at[m], dev(owner(m), s)
                    ).wait_recv()

                relay.start(base + m, dst.at[per * r + m], dst.at[per * r + m])

    for (r, h), items in text.items():

        @pl.when(relay.at(1 - r, h))
        def _():
            for i, src, dst in items:
                relay.middle(i, dst)

    for r, h, mats, owner, src, dst, base, per in groups:

        @pl.when(relay.at(1 - r, h))
        def _():
            for m in range(mats):
                relay.middle(base + m, dst.at[per * r + m])

    for r, h, mats, owner, src, dst, base, per in groups:

        @pl.when(relay.at(r, h))
        def _():
            for m in range(mats):

                @pl.when(d == owner(m))
                def _():
                    def finish(k, carry):
                        to = lax.rem(d + k, n)
                        remote(
                            src.at[to], dst.at[per * r + m], send.at[k], recv.at[m], dev(to, s)
                        ).wait_send()
                        return carry

                    lax.fori_loop(1, n, finish, 0)

        relay.finish(r, h, [(base + m, dst.at[per * r + m], dst.at[per * r + m]) for m in range(mats)])

    for (r, h), items in text.items():

        @pl.when(relay.at(r, h))
        def _():
            for i, src, dst in items:
                pltpu.make_async_copy(src, dst, gown.at[i - 20]).wait()

        relay.finish(r, h, items)


def adamw_update(weight, first, second, grad, fix_one, fix_two):
    first = beta_one * first + (1.0 - beta_one) * grad
    second = beta_two * second + (1.0 - beta_two) * grad * grad
    first_hat = first * fix_one
    second_hat = second * fix_two
    weight = weight - adam_rate * (
        first_hat / (jnp.sqrt(second_hat) + 1e-08) + weight_decay * weight
    )
    return (weight, first, second)


def update_kernel(
    rates, pieces, scal, stat,
    aw, am, ag, ax, fw, fm, fg, fx, sw, s1, s2, gv, g1, g2, gt, gy2, gm, vw, v1, v2, gvall, gtall,
    aw_, am_, ab_, fw_, fm_, fb_, sw_, s1_, s2_, sb_, vw_, v1_, v2_, vb_, loss_, norm_, powers,
):
    grad_norm = jnp.sqrt(stat[0:1, 0:1])
    factor = jnp.minimum(1.0, max_norm / (grad_norm + 1e-06))

    @pl.when(pl.program_id(0) == 0)
    def _():
        for i, beta in enumerate((beta_one, beta_two)):
            powers[i] = lax.fori_loop(0, scal[0], lambda _, value: value * beta, jnp.float32(1.0))

    fix_one, fix_two = (1.0 / (1.0 - jnp.full((1, 1), powers[i])) for i in range(2))
    loss_[...] = stat[4:5, 0:1]
    norm_[...] = grad_norm
    shrink = 1.0 - muon_rate * weight_decay
    for rate, (w, m, g, x, w_, m_, b_) in zip(
        rates, ((aw, am, ag, ax, aw_, am_, ab_), (fw, fm, fg, fx, fw_, fm_, fb_))
    ):
        m_[...] = momentum_decay * m[...] + g[...] * factor
        fresh = w[...] * shrink - rate * x[...].astype(f32)
        w_[...] = fresh
        b_[...] = low(fresh)
    text = gt.shape[1] - 128
    shards = {
        "embed": gv[:, EMB0 : EMB0 + 16],
        "time": g1[...],
        "time2": g2[...],
        "text": None,
        "text2": gy2[...],
        "head": gv[:, HEAD0 : HEAD0 + 16],
        "mod": gm[...],
    }
    for name, at, size in pieces:
        stride = size if name != "text" else 512
        for start in range(0, size, stride):
            cut = slice(at + start, at + start + stride)
            grad = gt[:, start : start + stride].astype(f32) if name == "text" else shards[name]
            fresh, one, two = adamw_update(
                sw[:, cut], s1[:, cut], s2[:, cut], grad * factor, fix_one, fix_two
            )
            sw_[:, cut], s1_[:, cut], s2_[:, cut] = fresh, one, two
            sb_[:, cut] = low(fresh)

    @pl.when(pl.program_id(0) == 0)
    def _():
        lane = lax.broadcasted_iota(jnp.int32, (1, 128), 1)
        column = gtall[:, text : text + 128].astype(f32)
        whole = jnp.where(lane == 9, column, gvall[...])
        rows = vw.shape[0]
        grad = jnp.transpose(whole)[0:rows, :] * factor
        fresh, one, two = adamw_update(vw[...], v1[...], v2[...], grad, fix_one, fix_two)
        vw_[...], v1_[...], v2_[...] = fresh, one, two
        vb_[...] = low(fresh)


def body(
    latents,
    noise_draw,
    timesteps,
    captions,
    caption_len,
    attention_weights,
    feed_weights,
    side_weights,
    vector_weights,
    attention_momentum,
    feed_momentum,
    side_first,
    side_second,
    vector_first,
    vector_second,
    step_count,
):
    n = lax.axis_size("dp")
    d, s = here()
    role, half = s // 2, lax.rem(s, 2)
    count = latents.shape[0]
    frames = latents.shape[1]
    width = attention_weights.shape[1]
    cols, feed_cols = attention_weights.shape[2], feed_weights.shape[2]
    hidden = n * feed_cols
    text = captions.shape[2]
    sds = jax.ShapeDtypeStruct
    role_s, half_s = role.reshape(1).astype(jnp.int32), half.reshape(1).astype(jnp.int32)

    o_time = 16
    o_text = o_time + 256 + width
    o_text2 = o_text + text
    o_head = o_text2 + width
    o_mod = o_head + 16
    six = 6 * width
    own_rows = -(-cols // 2)
    lanes = n * own_rows

    att_t = jnp.swapaxes(attention_weights, 1, 2)
    feed_t = jnp.swapaxes(feed_weights, 1, 2)
    side_t = side_weights.T
    pa, pb, pf, pw, py, pm, wm_own = local_call(
        lambda role, half, *refs: pack_kernel(
            role, half, (o_time, o_text, o_text2, o_head, o_mod), *refs
        ),
        [
            sds((4, cols, width), bf16),
            sds((4, cols, width), bf16),
            sds((2, feed_cols, width), bf16),
            sds((cols, 1152), bf16),
            sds((own_rows, text), bf16),
            sds((cols, 3 * width), bf16),
            sds((cols, six), bf16),
        ],
        [SM] * 2 + [VM] * 4,
        (role_s, half_s, att_t, feed_t, side_t, vector_weights),
    )
    freqs = jnp.exp(-math.log(10000.0) * jnp.arange(128, dtype=f32) / 128)
    angles = timesteps.astype(f32)[:, None] * freqs[None, :]
    level, snr = snr_weight(timesteps.astype(f32))
    pt = jnp.concatenate([jnp.cos(angles), jnp.sin(angles), snr[:, None]], axis=1)
    pt = jnp.pad(pt, ((0, 8 - count), (0, width - 257)))

    wa, wb, wf, ww, wy, wm, wt = comm_call(
        functools.partial(gather_kernel, n),
        1,
        (pa, pb, pf, pw, py, pm, pt),
        [
            sds((4, n, cols, width), bf16),
            sds((4, n, cols, width), bf16),
            sds((2, n, feed_cols, width), bf16),
            sds((n, cols, 1152), bf16),
            sds((n, own_rows, text), bf16),
            sds((n, cols, 3 * width), bf16),
            sds((n, 8, width), f32),
        ],
        [(4, 7, n), (7, n), (7, n), (7,)],
    )
    wa = wa.reshape(4, width, width)
    wb = wb.reshape(4, width, width)
    wf = wf.reshape(2, hidden, width)
    ww = ww.reshape(width, 1152)
    wy = wy.reshape(lanes, text)
    wm = wm.reshape(width, 3 * width)
    rank_s = d.reshape(1).astype(jnp.int32)
    per_clip = frames * (latents.shape[3] // 2) * (latents.shape[4] // 2)
    vec, hid, temb, mq_own, y2p, errs = local_call(
        functools.partial(condition_kernel, per_clip=per_clip, cols=cols),
        [
            sds((128, width), f32),
            sds((n * 8, width), f32),
            sds((n * 8, width), f32),
            sds((8, 3 * width), f32),
            sds((2, width, lanes), bf16),
            sds((8, 128), f32),
        ],
        [SM] + [VM] * 3,
        (rank_s, wt.reshape(n * 8, width), ww, wm),
    )
    mq = comm_call(
        mate_kernel, 2, (mq_own,), sds((2, 8, 3 * width), f32), [(1,), (1,), (1,)]
    )

    half_tokens = count * per_clip // 2

    def own_rows_of(value):
        return lax.dynamic_slice_in_dim(
            value.reshape(count * per_clip, 16), half * half_tokens, half_tokens, 0
        )

    def tokens(clean, noise):
        mix = level[:, None, None, None, None]
        noisy = low(jnp.sqrt(mix) * clean + jnp.sqrt(1.0 - mix) * noise)
        return jnp.pad(own_rows_of(patchify(noisy)), ((0, 0), (EMB0, 112 - EMB0)))

    def targets(noise):
        value = patchify(noise).reshape(count, frames, 2, 32, 16).transpose(0, 2, 1, 3, 4)
        return jnp.pad(own_rows_of(value), ((0, 0), (HEAD0, 112 - HEAD0)))

    tok = lax.cond(
        role == 0,
        tokens,
        lambda clean, noise: jnp.zeros((half_tokens, 128), bf16),
        latents,
        noise_draw,
    )
    places = np.arange(per_clip // frames)
    edge = latents.shape[3] // 2
    pos = np.concatenate(
        [sincos(places // edge, width // 2), sincos(places % edge, width // 2)], axis=1
    )
    pos = jnp.asarray(pos)
    timing = jnp.asarray(sincos(np.arange(frames), width))

    clip_rows = captions.shape[1]
    residuals = [
        sds((5, half_tokens, width), bf16),
        sds((3, half_tokens, width), f32),
        sds((half_tokens, hidden), f32),
        sds((count, 3, 256, 128), f32),
    ]
    residual_scratch = [pltpu.VMEM(v.shape, v.dtype) for v in residuals]
    h1s, hq, gq_own, kept_b, kept_f, kept_u, kept_p = local_call(
        functools.partial(first_kernel, cols),
        [
            sds((count, 2, 64, width), bf16),
            sds((count, LP, lanes), f32),
            sds((count, LP, lanes), bf16),
        ]
        + residuals,
        [SM] * 2 + [VM] * 7 + [ANY],
        (role_s, half_s, tok, pos, mq, vec, wa, wf, wy, captions),
        residual_scratch
        + [
            pltpu.VMEM((count, clip_rows, text), bf16),
            pltpu.SemaphoreType.DMA((count,)),
            pltpu.SemaphoreType.DMA((count, 4)),
        ],
        [VM] * 3 + [ANY] * 4,
    )
    later_noise, gq_own = lax.optimization_barrier((noise_draw, gq_own))
    target = lax.cond(
        role == 1,
        targets,
        lambda noise: jnp.zeros((half_tokens, 128), f32),
        later_noise,
    )
    target, h1s = lax.optimization_barrier((target, h1s))
    h1t, rgq, mqt = comm_call(
        functools.partial(forward_kernel, count),
        3,
        (h1s, gq_own, mq),
        [
            sds((count, 2, 64, width), bf16),
            sds((count, LP, lanes), bf16),
            sds((2, 8, 3 * width), f32),
        ],
        [(count, 2), (count, 2), (1,), (1,), (2,), (2,)],
    )

    ncl = (count + 1) // 2
    wide = sds((2, half_tokens, hidden), bf16)
    thin = sds((2, half_tokens, width), bf16)
    cap_like = sds((ncl, LP, width), bf16)
    dh1, acts_t, actf_t, actw_t, ybuf, dkv, grads_t, dmod_t, loss_t = local_call(
        temporal_kernel,
        [
            sds((count, 2, 64, width), bf16),
            sds((10, half_tokens, width), bf16),
            thin,
            wide,
            cap_like,
            sds((2, ncl, LP, width), f32),
            sds((128, width), f32),
            sds((count, 8, width), f32),
            sds((1, 128), f32),
        ],
        [SM] * 4 + [VM] * 13,
        (
            role_s, half_s, rank_s, caption_len, errs, h1t, timing, mqt, vec, temb, wa, wb, wf,
            gq_own, rgq, y2p, target,
        ),
        [pltpu.VMEM((ncl, KP, width), bf16), pltpu.VMEM((ncl, KP, width), bf16)],
    )
    dhs, extra = comm_call(
        functools.partial(backward_kernel, count),
        4,
        (dh1, dkv),
        [sds((count, 2, 64, width), bf16), sds((2, LP, width), f32)],
        [(count, 2), (count, 2), (1,), (1,)],
    )
    acts_s, actf_s, actw_s, dkvb, dy, vect, dmod = local_call(
        last_kernel,
        [
            sds((6, half_tokens, width), bf16),
            thin,
            wide,
            sds((2, ncl, LP, width), bf16),
            cap_like,
            sds((width, 128), f32),
            sds((count, 8, width), f32),
        ],
        [SM] * 2 + [VM] * 6 + [ANY] * 4 + [VM] * 5,
        (
            role_s, half_s, tok, mq, vec, wa, wb, wf, kept_b, kept_f, kept_u, kept_p, dhs, dkv,
            extra, grads_t, dmod_t,
        ),
        [pltpu.VMEM((128, width), f32)]
        + residual_scratch
        + [pltpu.SemaphoreType.DMA((count, 4))],
    )
    racts, ractf, ractw, rybuf, rdkvb, rdy, rdmod = comm_call(
        swap_kernel,
        5,
        (acts_s, acts_t, actf_s, actf_t, actw_s, actw_t, ybuf, dkvb, dy, dmod),
        [
            sds((10, half_tokens, width), bf16),
            thin,
            wide,
            cap_like,
            sds((2, ncl, LP, width), bf16),
            cap_like,
            sds((count, 8, width), f32),
        ],
        [(5,), (5,)],
    )
    line = n // 2
    wide_text = text + 128
    cut_text = wide_text // TEXT_CUTS
    block = (9, line, cols, width)
    tokens2 = 2 * half_tokens
    grad_own, grad_snd, text_part = local_call(
        weight_grad_kernel,
        [
            sds(block, f32),
            sds(block, bf16),
            sds((line, 2, own_rows, wide_text), bf16),
        ],
        [SM] * 3 + [ANY] * 9 + [VM] * 10 + [ANY],
        (
            role_s, half_s, rank_s, acts_s, acts_t, racts, actf_s, actf_t, ractf, actw_s, actw_t,
            ractw, ybuf, rybuf, dkvb, rdkvb, dy, rdy, gq_own, rgq, hq, y2p, captions,
        ),
        [
            pltpu.VMEM((10, tokens2, width), bf16),
            pltpu.VMEM((2, tokens2, width), bf16),
            pltpu.VMEM((2, tokens2, hidden), bf16),
            pltpu.VMEM((count, clip_rows, text), bf16),
            pltpu.VMEM((width, width), f32),
            pltpu.VMEM((count, lanes, LP), bf16),
            pltpu.VMEM((lanes, 128), f32),
            pltpu.SemaphoreType.DMA((4 + count,)),
        ],
    )

    whole_clips = n * 8
    text_block = (TEXT_CUTS, line, own_rows, cut_text)
    summed, text_sum, vsum, tile, grad_mod, grad_time2, grad_time1 = comm_call(
        functools.partial(scatter_kernel, n),
        6,
        (
            grad_own, grad_snd, text_part, vect.reshape(n, cols, 128), dmod, rdmod, loss_t,
            wm_own, temb, ww, hid, wt.reshape(whole_clips, width),
        ),
        [
            sds((9, cols, width), f32),
            sds((own_rows, wide_text), bf16),
            sds((cols, 128), f32),
            sds((8, width), f32),
            sds((cols, six), f32),
            sds((cols, width), f32),
            sds((cols, 256), f32),
        ],
        [(9,), (9 + TEXT_CUTS,), (9 + TEXT_CUTS,)]
        + [(TEXT_CUTS + 1, line)] * 2
        + [(8, line)] * 4
        + [(2, n), (2, n), (2,), (TEXT_CUTS,), (TEXT_CUTS,), (n,), (n,), (1,), (1,)],
        [VM] * 7,
        in_specs=[ANY] * 4 + [VM] * 8,
        scratch=[
            pltpu.VMEM(block, f32),
            pltpu.VMEM(block, bf16),
            pltpu.VMEM((8,) + block[1:], f32),
            pltpu.VMEM((8,) + block[1:], f32),
            pltpu.VMEM(block[1:], bf16),
            pltpu.VMEM(block[1:], bf16),
            pltpu.VMEM((TEXT_CUTS, line, 2, own_rows, cut_text), bf16),
        ]
        + [pltpu.VMEM(text_block, bf16)] * 3
        + [
            pltpu.VMEM((n, cols, 128), f32),
            pltpu.VMEM((n * 8 * count, width), f32),
            pltpu.VMEM((n, whole_clips, 128), f32),
            pltpu.VMEM((8 * count, width), f32),
            pltpu.VMEM((8 * count, width), f32),
        ],
    )

    att_m = jnp.swapaxes(attention_momentum, 1, 2)
    feed_m = jnp.swapaxes(feed_momentum, 1, 2)
    ua, uf, ga2, gf2, grad_mod, grad_time2, grad_time1, grad_v, stat = comm_call(
        functools.partial(settle_kernel, n),
        8,
        (
            vsum, tile, summed, att_m, feed_m.reshape(16, cols, width), grad_mod, grad_time2,
            grad_time1,
        ),
        [
            sds((n, cols, width), f32),
            sds((n, 4, cols, width), f32),
            sds((12, cols, width), f32),
            sds((16, cols, width), f32),
            sds((cols, six), f32),
            sds((cols, width), f32),
            sds((cols, 256), f32),
            sds((cols, 128), f32),
            sds((8, 128), f32),
        ],
        [(1,), (8,), (n,), (1,), (7, 3), (7, 3), (7,), (2, 4), (2, 4), (n,), (n,)],
        [ANY] * 7 + [VM] * 2,
        in_specs=[VM] * 3 + [ANY] * 5,
        scratch=[
            pltpu.VMEM((4, cols, 128), f32),
            pltpu.VMEM((4, 8, width), f32),
            pltpu.VMEM((8, 128), f32),
            pltpu.VMEM((n, 8, 128), f32),
            pltpu.VMEM((8, cols, width), f32),
            pltpu.VMEM((8, cols, width), f32),
        ],
    )
    xa, xf = local_call(
        muon_kernel,
        [sds((width, width), bf16), sds((hidden, width), bf16)],
        [SM] + [VM] * 2,
        (half_s, ua.reshape(width, width), uf.reshape(hidden, width)),
        [pltpu.VMEM((width, width), f32), pltpu.VMEM((width, width), f32)],
    )
    xa_all, xf_all, gy12, gy22 = comm_call(
        functools.partial(spread_kernel, n),
        10,
        (xa.reshape(n, cols, width), xf.reshape(n, feed_cols, width), text_sum, summed),
        [
            sds((12, cols, width), bf16),
            sds((4, feed_cols, width), bf16),
            sds((2, own_rows, wide_text), bf16),
            sds((cols, width), f32),
        ],
        [(n,), (8,), (23, 3), (23, 3), (8,), (3,)],
    )

    text_grad = gy12.reshape(2 * own_rows, wide_text)[:cols]
    side_m, side_v = side_first.T, side_second.T
    side_rows = side_t.shape[1]
    pieces = (
        ("embed", 0, 16),
        ("time", o_time, 256),
        ("time2", o_time + 256, width),
        ("text", o_text, text),
        ("text2", o_text2, width),
        ("head", o_head, 16),
        ("mod", o_mod, six),
    )
    rates = tuple(
        muon_rate * 0.2 * math.sqrt(columns) for columns in (n * cols, n * feed_cols)
    )
    grid = cols // 8 if cols % 8 == 0 else 1

    def by_rows(value):
        return value.reshape(-1, value.shape[-1])

    def rows_spec(value):
        return pl.BlockSpec((value.shape[0] // grid, value.shape[1]), lambda i: (i, 0))

    def whole_spec(value):
        return pl.BlockSpec(value.shape, lambda i: (0, 0))

    cutup = [by_rows(v) for v in (att_t, att_m, ga2, xa_all, feed_t, feed_m, gf2, xf_all)] + [
        side_t, side_m, side_v, grad_v, grad_time1, grad_time2, text_grad, gy22, grad_mod,
    ]
    fixed = [vector_weights, vector_first, vector_second, grad_v, text_grad]
    a_like, f_like, s_like = (sds(v.shape, f32) for v in (cutup[0], cutup[4], side_t))
    v_like = sds(vector_weights.shape, f32)

    def low_of(like):
        return sds(like.shape, bf16)

    row_outs = [
        a_like, a_like, low_of(a_like), f_like, f_like, low_of(f_like), s_like, s_like, s_like,
        low_of(s_like),
    ]
    whole_outs = [v_like, v_like, v_like, low_of(v_like), sds((1, 1), f32), sds((1, 1), f32)]
    (
        att_new, att_moment, att_low, feed_new, feed_moment, feed_low, side_new, side_first_new,
        side_second_new, side_low, vector_new, vector_first_new, vector_second_new, vector_low,
        loss_value, grad_norm,
    ) = pl.pallas_call(
        functools.partial(update_kernel, rates, pieces),
        grid=(grid,),
        out_shape=row_outs + whole_outs,
        in_specs=[SM, whole_spec(stat)] + [rows_spec(v) for v in cutup] + [whole_spec(v) for v in fixed],
        out_specs=[rows_spec(v) for v in row_outs] + [whole_spec(v) for v in whole_outs],
        scratch_shapes=[pltpu.SMEM((2,), f32)],
        compiler_params=pltpu.CompilerParams(vmem_limit_bytes=VMEM_LIMIT),
    )(step_count, stat, *cutup, *fixed)

    def att(value):
        return value.reshape(att_t.shape)

    def feed(value):
        return value.reshape(feed_t.shape)

    def back(value):
        return jnp.swapaxes(value, -1, -2)

    return (
        loss_value[0, 0],
        grad_norm[0, 0],
        back(att(att_new)),
        back(att(att_moment)),
        back(feed(feed_new)),
        back(feed(feed_moment)),
        back(side_new),
        back(side_first_new),
        back(side_second_new),
        vector_new,
        vector_first_new,
        vector_second_new,
        back(att(att_low)),
        back(feed(feed_low)),
        back(side_low),
        vector_low,
    )


def solution(mesh):
    column = P(None, "dp")
    matrix = P(None, None, "dp")
    return jax.shard_map(
        body,
        mesh=mesh,
        in_specs=(
            P("dp", None, None, None, None),
            P("dp", None, None, None, None),
            P("dp"),
            P("dp", None, None),
            P("dp"),
            matrix,
            matrix,
            column,
            column,
            matrix,
            matrix,
            column,
            column,
            column,
            column,
            P(),
        ),
        out_specs=(
            P(),
            P(),
            matrix,
            matrix,
            matrix,
            matrix,
            column,
            column,
            column,
            column,
            column,
            column,
            matrix,
            matrix,
            column,
            column,
        ),
        check_vma=False,
    )
```

```python
import functools
import math

import jax
import jax.numpy as jnp
import numpy as np
from jax import lax
from jax.experimental import pallas as pl
from jax.experimental.pallas import tpu as pltpu
from jax.sharding import PartitionSpec as P

HEADS = 6
HEAD = 64
LP = 304
KP = 384

highest = lax.Precision.HIGHEST
snr_gamma = 5.0
max_norm = 0.005
momentum_decay = 0.95
muon_rate = 0.05
adam_rate = 0.02
beta_one = 0.9
beta_two = 0.999
weight_decay = 0.01
coef_a = 3.4445
coef_b = -4.775
coef_c = 2.0315

f32, bf16 = jnp.float32, jnp.bfloat16
MESH = pl.DeviceIdType.MESH
ANY = pl.BlockSpec(memory_space=pl.ANY)
VM = pl.BlockSpec(memory_space=pltpu.VMEM)
SM = pl.BlockSpec(memory_space=pltpu.SMEM)
VMEM_LIMIT = 60000 * 1024


def low(value):
    return value.astype(bf16)


def nt(left, right):
    return lax.dot_general(left, right, (((1,), (1,)), ((), ())), preferred_element_type=f32)


def nn(left, right):
    return lax.dot_general(left, right, (((1,), (0,)), ((), ())), preferred_element_type=f32)


def tn(left, right):
    return lax.dot_general(left, right, (((0,), (0,)), ((), ())), preferred_element_type=f32)


def snr_weight(steps_t):
    level = jnp.cos((steps_t / 1000.0 + 0.008) / 1.008 * (math.pi / 2)) ** 2
    ratio = level / (1.0 - level)
    return level, jnp.minimum(ratio, snr_gamma) / ratio


def sincos(places, model_width):
    half_width = model_width // 2
    freqs = np.exp(-math.log(10000.0) * np.arange(half_width) / half_width)
    angles = places[:, None] * freqs[None, :]
    return np.concatenate([np.sin(angles), np.cos(angles)], axis=1).astype(np.float32)


def col_sum(value):
    return jnp.sum(value.astype(f32), axis=0, keepdims=True)


def norm(value):
    centred = value - jnp.mean(value, axis=-1, keepdims=True)
    inv = lax.rsqrt(jnp.mean(centred * centred, axis=-1, keepdims=True) + 1e-06)
    return centred * inv, inv


def norm_back(grad, normed, inv):
    return inv * (
        grad
        - jnp.mean(grad, axis=-1, keepdims=True)
        - normed * jnp.mean(grad * normed, axis=-1, keepdims=True)
    )


GELU_C = math.sqrt(2.0 / math.pi)


def gelu(value):
    inner = GELU_C * (value + 0.044715 * (value * value * value))
    return value * (0.5 * (1.0 + jnp.tanh(inner)))


def gelu_both(value):
    square = value * value
    tanh = jnp.tanh(GELU_C * (value + 0.044715 * (square * value)))
    cdf = 0.5 * (1.0 + tanh)
    slope = 0.5 * (1.0 - tanh * tanh) * (GELU_C * (1.0 + 3 * 0.044715 * square))
    return value * cdf, cdf + value * slope


def lanes_low():
    lane = lax.broadcasted_iota(jnp.int32, (1, 128), 1)
    first = jnp.where(lane < HEAD, 1.0, 0.0)
    return low(first), low(1.0 - first), lane < HEAD


def stack_heads(pair, first, second):
    return jnp.concatenate([pair * first, pair * second], axis=0)


def attend(queries, keys, values, allowed):
    first, second, lower = lanes_low()
    rows = queries.shape[0]
    mixed, probs = [], []
    for pair in range(HEADS // 2):
        cut = slice(pair * 128, pair * 128 + 128)
        scores = nt(stack_heads(queries[:, cut], first, second), keys[:, cut]) * 0.125
        scores = jnp.where(allowed, scores, -1e30)
        weight = jnp.exp(scores - jnp.max(scores, axis=-1, keepdims=True))
        prob = weight / jnp.sum(weight, axis=-1, keepdims=True)
        probs.append(prob)
        out = nn(low(prob), values[:, cut])
        mixed.append(jnp.where(lower, out[:rows], out[rows:]))
    return low(jnp.concatenate(mixed, axis=1)), probs


def attend_back(grad, queries, keys, values, probs):
    first, second, lower = lanes_low()
    rows = queries.shape[0]
    dq, dk, dv = [], [], []
    for pair in range(HEADS // 2):
        cut = slice(pair * 128, pair * 128 + 128)
        stacked = stack_heads(grad[:, cut], first, second)
        prob = probs[pair]
        dv.append(tn(low(prob), stacked))
        dprob = nt(stacked, values[:, cut])
        dscore = low(prob * (dprob - jnp.sum(prob * dprob, axis=-1, keepdims=True)))
        part = nn(dscore, keys[:, cut])
        dq.append(jnp.where(lower, part[:rows], part[rows:]) * 0.125)
        dk.append(tn(dscore, stack_heads(queries[:, cut], first, second)) * 0.125)
    return tuple(jnp.concatenate(piece, axis=1) for piece in (dq, dk, dv))


def self_forward(x, mods, weights, bias, allowed):
    normed, inv = norm(x)
    a = low(normed * (1.0 + mods[1]) + mods[0])
    q = low(nt(a, weights[0]) + bias[0])
    k = low(nt(a, weights[1]))
    v = low(nt(a, weights[2]) + bias[1])
    o, probs = attend(q, k, v, allowed)
    branch = nt(o, weights[3]) + bias[2]
    return x + mods[2] * branch, (normed, inv, a, q, k, v, o, probs, branch)


def self_backward(dx, kept, mods, weights):
    normed, inv, a, q, k, v, o, probs, branch = kept
    dm2 = col_sum(dx * branch)
    dbr = low(dx * mods[2])
    do = low(nn(dbr, weights[3]))
    dq, dk, dv = (low(piece) for piece in attend_back(do, q, k, v, probs))
    da = nn(dq, weights[0]) + nn(dk, weights[1]) + nn(dv, weights[2])
    dm1, dm0 = col_sum(da * normed), col_sum(da)
    dx = dx + norm_back(da * (1.0 + mods[1]), normed, inv)
    return dx, (dm0, dm1, dm2), (col_sum(dq), col_sum(dv), col_sum(dbr)), (a, dq, dk, dv, o, dbr)


def feed_forward(x, mods, feed, bias_up, bias_down):
    normed, inv = norm(x)
    c = low(normed * (1.0 + mods[4]) + mods[3])
    u = nt(c, feed[0]) + bias_up
    g = low(gelu(u))
    branch = nn(g, feed[1]) + bias_down
    return x + mods[5] * branch, (normed, inv, c, u, g, branch)


def feed_backward(dx, kept, mods, feed):
    normed, inv, c, u, g, branch = kept
    dm5 = col_sum(dx * branch)
    dbr = low(dx * mods[5])
    value, slope = gelu_both(u)
    g = low(value)
    du = low(nt(dbr, feed[1]) * slope)
    dc = nn(du, feed[0])
    dm4, dm3 = col_sum(dc * normed), col_sum(dc)
    dx = dx + norm_back(dc * (1.0 + mods[4]), normed, inv)
    return dx, (dm3, dm4, dm5), (col_sum(du), col_sum(dbr)), (c, dbr, du, g)


def pair_mask(kind):
    row = lax.broadcasted_iota(jnp.int32, (256, 128), 0) % 128
    col = lax.broadcasted_iota(jnp.int32, (256, 128), 1)
    if kind == 0:
        return row // 64 == col // 64
    return row % 32 == col % 32


VEC0, EMB0, HEAD0 = 0, 45, 61


def mod_rows(mq, vec, table, clip):
    rows = []
    for r in range(6):
        at = (r % 3) * 384
        rows.append(
            mq[r // 3, pl.ds(clip, 1), at : at + 384]
            + vec[3 + r : 4 + r]
            + vec[table + r : table + r + 1]
        )
    return rows


def up_bias(vec, start):
    return jnp.concatenate([vec[start + i : start + i + 1] for i in range(4)], axis=1)


def pack_kernel(role, half, offsets, att, feed, side, vec, pa, pb, pf, pw, py, pm, wm):
    time, text, text2, head, mod = offsets
    width, per, rows = att.shape[2], pf.shape[0], py.shape[0]

    def rounded(at, size):
        return low(side[:, at : at + size])

    first = text - time
    pw[:, 0:first] = rounded(time, first)
    pw[:, first : first + width] = rounded(text2, width)
    cols = pw.shape[0]
    pw[:, first + width :] = low(jnp.concatenate(
        [jnp.transpose(vec[...]), side[:, 0:16], side[:, head : head + 16], jnp.zeros((cols, 51), f32)], axis=1
    ))
    wm[...] = rounded(mod, 6 * width)
    for r in range(2):

        @pl.when(role[0] == r)
        def _():
            pa[...] = low(att[4 * r : 4 * r + 4])
            pf[...] = low(feed[per * r : per * r + per])
            if r == 1:
                pb[...] = low(att[8:12])

    for h in range(2):

        @pl.when(half[0] == h)
        def _():
            pm[...] = rounded(mod + h * 3 * width, 3 * width)
            top = min((h + 1) * rows, cols)
            py[0 : top - h * rows, :] = low(side[h * rows : top, text : text + py.shape[1]])


def units_of(hand, lanes, width, cols):
    per = -(-cols // 2)
    unit = lax.broadcasted_iota(jnp.int32, (lanes, width), 0)
    column = lax.broadcasted_iota(jnp.int32, (lanes, width), 1)
    inside = hand * per + unit % per
    match = jnp.logical_and((unit // per) * cols + inside == column, inside < cols)
    return low(jnp.where(match, 1.0, 0.0))


def condition_kernel(rank, wt, ww, wm, vec, hid, temb, mq, y2p, errs, *, per_clip, cols):
    turned = jnp.transpose(ww[:, 1024:1152].astype(f32))
    vec[...] = turned
    feature = low(wt[:, 0:256])
    first = nt(feature, ww[:, 0:256]) + turned[1:2]
    hid[...] = first
    second = nt(low(first * jax.nn.sigmoid(first)), ww[:, 256:640]) + turned[2:3]
    temb[...] = second
    own = temb[pl.ds(pl.multiple_of(rank[0] * 8, 8), 8), :]
    mq[...] = nn(low(own * jax.nn.sigmoid(own)), wm[...])
    for h in range(2):
        y2p[h] = low(nt(ww[:, 640:1024], units_of(h, y2p.shape[2], y2p.shape[1], cols)))
    total = jnp.sum(wt[:, 256:257], axis=0, keepdims=True)
    weight = wt[pl.ds(pl.multiple_of(rank[0] * 8, 8), 8), 256:257] / (total * (per_clip * 16.0))
    errs[...] = jnp.broadcast_to(weight, errs.shape)


class Patches:
    def __init__(self, rows, first, lane0):
        place = lax.broadcasted_iota(jnp.int32, (rows, 16), 0)
        col = lax.broadcasted_iota(jnp.int32, (rows, 16), 1)
        self.pick = [low(jnp.where(col == 2 * (place % 8) + q, 1.0, 0.0)) for q in range(2)]
        place = lax.broadcasted_iota(jnp.int32, (rows, 64), 0)
        line = lax.broadcasted_iota(jnp.int32, (rows, 64), 1) % 16
        self.keep = [line == 2 * (first + place // 8) + p for p in range(2)]
        channel = lax.broadcasted_iota(jnp.int32, (64, 128), 0) // 16
        lane = lax.broadcasted_iota(jnp.int32, (64, 128), 1) - lane0
        self.put = [
            [low(jnp.where(lane == p * 8 + q * 4 + channel, 1.0, 0.0)) for q in range(2)]
            for p in range(2)
        ]

    def of(self, pieces):
        total = None
        for piece in pieces:
            for q in range(2):
                columns = nt(self.pick[q], piece)
                for p in range(2):
                    part = nn(low(jnp.where(self.keep[p], columns, 0.0)), self.put[p][q])
                    total = part if total is None else total + part
        return total


def embed_chunk(tokens, vec, pos_ref):
    places = pos_ref[...] + vec[0:1]
    return low(nn(tokens, low(vec[...])) + jnp.concatenate([places, places], axis=0))


def spatial_bias(vec):
    return (vec[11:12], vec[12:13], vec[13:14])


def residual_copies(sources, targets, sems):
    def of(chunk):
        rows = pl.ds(pl.multiple_of(chunk * 128, 128), 128)
        cuts = [lambda r: r.at[:, rows], lambda r: r.at[:, rows], lambda r: r.at[rows],
                lambda r: r.at[chunk]]
        return [
            pltpu.make_async_copy(cut(src), cut(dst), sems.at[chunk, i])
            for i, (cut, src, dst) in enumerate(zip(cuts, sources, targets))
        ]

    return of


def first_kernel(
    cols, role, half, clean, noise, pt, pos, mq, vec, wa, wf, wy, captions,
    h1, hq, gq, tok, out_b, out_f, out_u, out_p, kept_b, kept_f, kept_u, kept_p, cap, sems, ksem,
):
    @pl.when(role[0] == 1)
    def _():
        clips = captions.shape[0]
        for c in range(clips):
            pltpu.make_async_copy(captions.at[c], cap.at[c], sems.at[c]).start()
        bias = nt(low(vec[9:10]), units_of(half[0], wy.shape[0], vec.shape[1], cols))
        def layer(c, carry):
            pltpu.make_async_copy(captions.at[c], cap.at[c], sems.at[c]).wait()
            value = nt(cap[c], wy[...]) + bias
            rows = value.shape[0]
            pad = jnp.zeros((LP - rows, value.shape[1]), f32)
            hq[c] = jnp.concatenate([value, pad], axis=0)
            gq[c] = low(jnp.concatenate([gelu(value), pad], axis=0))
            return carry

        lax.fori_loop(0, clips, layer, 0)

    @pl.when(role[0] == 0)
    def _():
        allowed = pair_mask(0)
        count = h1.shape[0]
        bu = up_bias(vec, 14)
        patches = Patches(64, 0, EMB0)
        residuals = residual_copies((kept_b, kept_f, kept_u, kept_p), (out_b, out_f, out_u, out_p), ksem)

        def step(chunk, carry):
            @pl.when(chunk > 0)
            def _():
                for copy in residuals(chunk - 1):
                    copy.start()

            there = half[0] * count + chunk
            clip = there // 2
            m = mod_rows(mq, vec, 19, clip)
            mix = pt[pl.ds(clip, 1), :][:, 256:384]
            frames = []
            for f in range(2):
                frame = 2 * lax.rem(there, 2) + f
                one, two = (ref[clip, frame].reshape(64, 16) for ref in (clean, noise))
                frames.append(patches.of([low(mix[:, 1:2] * one + mix[:, 2:3] * two)]))
            tokens = low(jnp.concatenate(frames, axis=0))
            tok[pl.ds(pl.multiple_of(chunk * 128, 128), 128), :] = tokens
            h0 = embed_chunk(tokens, vec, pos)
            x1, kept = self_forward(h0.astype(f32), m, wa, spatial_bias(vec), allowed)
            x, kept_feed = feed_forward(x1, m, wf, bu, vec[18:19])
            out = low(x)
            where = pl.ds(pl.multiple_of(chunk * 128, 128), 128)
            for i, value in enumerate((h0,) + kept[3:7]):
                kept_b[i, where, :] = value
            for i, value in enumerate((x1, kept[8], kept_feed[5])):
                kept_f[i, where, :] = value
            kept_u[where, :] = kept_feed[3]
            for pair in range(3):
                kept_p[chunk, pair] = kept[7][pair]
            for frame in range(2):
                for part in range(2):
                    start = frame * 64 + part * 32
                    h1[chunk, part, frame * 32 : frame * 32 + 32, :] = out[start : start + 32]
            return carry

        lax.fori_loop(0, count, step, 0)
        for copy in residuals(count - 1):
            copy.start()
        for chunk in range(count):
            for copy in residuals(chunk):
                copy.wait()


def last_kernel(
    role, half, tok, mq, vec, wa, wb, wf, in_b, in_f, in_u, in_p, dh, dkv, extra, grads_t, dmod_t,
    acts, actf, actw, dkvb, dy, vect, dmod, grads, kept_b, kept_f, kept_u, kept_p, ksem,
):
    @pl.when(role[0] == 0)
    def _():
        grads[...] = jnp.zeros_like(grads)
        dmod[...] = jnp.zeros_like(dmod)
        count = dh.shape[0]
        residuals = residual_copies((in_b, in_f, in_u, in_p), (kept_b, kept_f, kept_u, kept_p), ksem)
        for chunk in range(count):
            for copy in residuals(chunk):
                copy.start()

        def step(chunk, carry):
            for copy in residuals(chunk):
                copy.wait()
            m = mod_rows(mq, vec, 19, (half[0] * count + chunk) // 2)
            where = pl.ds(pl.multiple_of(chunk * 128, 128), 128)
            tokens = tok[where, :]
            h0, q, k, v, o = (kept_b[i, where, :] for i in range(5))
            x1, branch, branch_f = (kept_f[i, where, :] for i in range(3))
            normed, inv = norm(h0.astype(f32))
            a = low(normed * (1.0 + m[1]) + m[0])
            probs = [kept_p[chunk, pair] for pair in range(3)]
            kept = (normed, inv, a, q, k, v, o, probs, branch)
            normed_f, inv_f = norm(x1)
            c = low(normed_f * (1.0 + m[4]) + m[3])
            kept_feed = (normed_f, inv_f, c, kept_u[where, :], None, branch_f)
            parts = []
            for frame in range(2):
                for part in range(2):
                    parts.append(dh[chunk, part, frame * 32 : frame * 32 + 32, :])
            dx = jnp.concatenate(parts, axis=0).astype(f32)
            dx, dm_f, db_f, act_f = feed_backward(dx, kept_feed, m, wf)
            dx, dm_a, db_a, act_a = self_backward(dx, kept, m, wa)
            dh0 = low(dx)
            for i, value in enumerate(act_a):
                acts[i, where, :] = value
            for i in range(2):
                actf[i, where, :] = act_f[i]
                actw[i, where, :] = act_f[2 + i]
            mods = dm_a + dm_f
            dmod[chunk, 0:6, :] = jnp.concatenate(mods, axis=0)
            grads[...] += tn(tokens, dh0)
            grads[0:1] += col_sum(dh0)
            for i in range(3):
                grads[11 + i : 12 + i] += db_a[i]
            for i in range(4):
                grads[14 + i : 15 + i] += db_f[0][:, i * 384 : i * 384 + 384]
            grads[18:19] += db_f[1]
            for i in range(6):
                grads[19 + i : 20 + i] += mods[i]
            return carry

        lax.fori_loop(0, count, step, 0)

    @pl.when(role[0] == 1)
    def _():
        grads[...] = grads_t[...]
        dmod[...] = dmod_t[...]
        dy[...] = jnp.zeros_like(dy)
        dkvb[...] = jnp.zeros_like(dkvb)
        ncl = dy.shape[0]
        for c in range(ncl):

            @pl.when(jnp.logical_or(half[0] == 0, c > 0))
            def _():
                pieces = []
                for i in range(2):
                    value = dkv[i, c]
                    if c == ncl - 1:
                        value = value + jnp.where(half[0] == 0, extra[i], 0.0)
                    pieces.append(low(value))
                dkvb[0, c], dkvb[1, c] = pieces
                back = low(nn(pieces[0], wb[1]) + nn(pieces[1], wb[2]))
                dy[c] = back
                grads[40:41] += col_sum(pieces[1])
                grads[10:11] += col_sum(back)

    vect[...] = jnp.transpose(grads[...])


def temporal_kernel(
    role, half, rank, lens, errw, h1, timing, mq, vec, temb, wa, wb, wf, gq, rgq, y2p, noise,
    dh1, acts, actf, actw, ybuf, dkv, grads, dmod, loss, kx, vx,
):
    @pl.when(role[0] == 0)
    def _():
        loss[...] = jnp.zeros_like(loss)

    @pl.when(role[0] == 1)
    def _():
        allowed = pair_mask(1)
        count = h1.shape[0]
        ncl = ybuf.shape[0]
        for ref in (kx, vx, dkv, grads, loss):
            ref[...] = jnp.zeros_like(ref)
        first_clip = (half[0] * count) // 2

        def features(c, carry):
            clip = jnp.minimum(first_clip + c, gq.shape[0] - 1)
            y = nt(gq[clip], y2p[half[0]]) + nt(rgq[clip], y2p[1 - half[0]])
            y = low(y + vec[10:11])
            ybuf[c] = y
            kx[c, 0:LP, :] = low(nt(y, wb[1]))
            vx[c, 0:LP, :] = low(nt(y, wb[2]) + vec[40:41])
            return carry

        lax.fori_loop(0, ncl, features, 0)
        bu = up_bias(vec, 28)
        lane = lax.broadcasted_iota(jnp.int32, (1, 128), 1)
        real = jnp.logical_and(lane >= HEAD0, lane < HEAD0 + 16)
        bias_h = pltpu.roll(jnp.broadcast_to(vec[44:45, 0:128], (8, 128)), HEAD0, 1)[0:1]
        head = low(vec[...])

        def step(chunk, carry):
            clip = (half[0] * count + chunk) // 2
            here = clip - first_clip
            m = mod_rows(mq, vec, 33, clip)
            emb = temb[pl.ds(rank[0] * 8 + clip, 1), :]
            m6, m7 = vec[42:43] + emb, vec[43:44] + emb
            h = jnp.concatenate([h1[chunk, 0], h1[chunk, 1]], axis=0)
            x = h.astype(f32) + jnp.concatenate(
                [jnp.broadcast_to(timing[i : i + 1], (32, h.shape[1])) for i in range(4)], axis=0
            )
            x, kept = self_forward(x, m, wa, (vec[25:26], vec[26:27], vec[27:28]), allowed)
            xb = low(x)
            cq = low(nt(xb, wb[0]) + vec[39:40])
            keys, values = kx[here], vx[here]
            seen = lax.broadcasted_iota(jnp.int32, (1, KP), 1) < lens[clip]
            co, probs = attend(cq, keys, values, seen)
            x = x + (nt(co, wb[3]) + vec[41:42])
            x, kept_f = feed_forward(x, m, wf, bu, vec[32:33])
            h2 = low(x).astype(f32)
            normed, inv = norm(h2)
            cf = low(normed * (1.0 + m7) + m6)
            where = pl.ds(pl.multiple_of(chunk * 128, 128), 128)
            patches = Patches(32, 4 * lax.rem(half[0] * count + chunk, 2), HEAD0)
            target = jnp.concatenate(
                [
                    patches.of(three(noise[clip, frame].reshape(64, 16)))
                    for frame in range(noise.shape[1])
                ],
                axis=0,
            )
            diff = jnp.where(real, nt(cf, head) + bias_h - target, 0.0)
            scale = errw[pl.ds(clip, 1), 0:1]
            loss[...] += col_sum(diff * diff) * scale
            dpred = low(diff * (2.0 * scale))
            dcf = nn(dpred, head)
            grads[...] += tn(dpred, cf)
            dbh = pltpu.roll(jnp.broadcast_to(col_sum(dpred), (8, 128)), 128 - HEAD0, 1)[0:1]
            grads[44:45, 0:128] += dbh
            dm7, dm6 = col_sum(dcf * normed), col_sum(dcf)
            dx = low(norm_back(dcf * (1.0 + m7), normed, inv)).astype(f32)
            dx, dm_f, db_f, act_f = feed_backward(dx, kept_f, m, wf)
            dcbr = low(dx)
            dco = low(nn(dcbr, wb[3]))
            dcq, dck, dcv = attend_back(dco, cq, keys, values, probs)
            dcq = low(dcq)
            dkv[0, here] += dck[0:LP]
            dkv[1, here] += dcv[0:LP]
            dx = dx + nn(dcq, wb[0])
            dx, dm_a, db_a, act_a = self_backward(dx, kept, m, wa)
            out = low(dx)
            dh1[chunk, 0] = out[0:64]
            dh1[chunk, 1] = out[64:128]
            for i, value in enumerate(act_a + (xb, dcq, co, dcbr)):
                acts[i, where, :] = value
            for i in range(2):
                actf[i, where, :] = act_f[i]
                actw[i, where, :] = act_f[2 + i]
            mods = dm_a + dm_f + (dm6, dm7)
            dmod[chunk] = jnp.concatenate(mods, axis=0)
            for i in range(3):
                grads[25 + i : 26 + i] += db_a[i]
            for i in range(4):
                grads[28 + i : 29 + i] += db_f[0][:, i * 384 : i * 384 + 384]
            grads[32:33] += db_f[1]
            for i in range(6):
                grads[33 + i : 34 + i] += mods[i]
            grads[39:40] += col_sum(dcq)
            grads[41:42] += col_sum(dcbr)
            grads[42:43] += dm6
            grads[43:44] += dm7
            return carry

        lax.fori_loop(0, count, step, 0)


def weight_grad_kernel(
    role, half, rank, acts_s, acts_t, racts, actf_s, actf_t, ractf, actw_s, actw_t, ractw,
    ybuf, rybuf, dkvb, rdkvb, dy, rdy, gq, rgq, hq, y2p, captions,
    own, snd, text_out, la, lf, lw, cap, square, turned, sums, sems,
):
    tokens = acts_s.shape[1]
    line, cols = own.shape[1], own.shape[2]
    odd = lax.rem(rank[0], 2) == 1
    near, far = pl.ds(0, tokens), pl.ds(tokens, tokens)

    def copies(r, h):
        if h == 0:
            local = acts_s if r == 0 else acts_t
            size = pl.ds(0, local.shape[0])
            return [(local, la.at[size, near], 0), (racts.at[size], la.at[size, far], 1)]
        thin, wide = ((actf_s, actw_s), (actf_t, actw_t))[r]
        return [
            (thin, lf.at[:, near], 0), (ractf, lf.at[:, far], 1),
            (wide, lw.at[:, near], 2), (ractw, lw.at[:, far], 3),
        ]

    def text():
        return [(captions.at[c], cap.at[c], 4 + c) for c in range(captions.shape[0])]

    def run(group, finish):
        for src, dst, i in group:
            copy = pltpu.make_async_copy(src, dst, sems.at[i])
            copy.wait() if finish else copy.start()

    for r in range(2):
        for h in range(2):

            @pl.when(jnp.logical_and(role[0] == r, half[0] == h))
            def _():
                run(copies(r, h), False)
                if r == 1:
                    run(text(), False)
                run(copies(r, h), True)

    def keep(unit, at, first, second):
        own[unit, at] = jnp.where(odd, second, first)
        snd[unit, at] = low(jnp.where(odd, first, second))

    def keep_square(unit, value):
        for p in range(line):
            cut = 2 * p * cols
            keep(unit, p, value[cut : cut + cols], value[cut + cols : cut + 2 * cols])

    def matrix(unit, left, right):
        keep_square(unit, tn(la[left], la[right]))

    @pl.when(half[0] == 0)
    def _():
        def square(i, carry):
            left = jnp.where(i < 3, i + 1, 2 * i - 1)
            right = jnp.where(i < 3, 0, 2 * i - 2)
            matrix(jnp.where(i < 5, i, 7), left, right)
            return carry

        lax.fori_loop(0, 4 + 2 * role[0], square, 0)

        @pl.when(role[0] == 1)
        def _():
            def cross(i, carry):
                total = tn(dkvb[i, 0], ybuf[0]) + tn(rdkvb[i, 0], rybuf[0])
                for c in range(1, ybuf.shape[0]):
                    total = total + tn(dkvb[i, c], ybuf[c]) + tn(rdkvb[i, c], rybuf[c])
                keep_square(5 + i, total)
                return carry

            lax.fori_loop(0, 2, cross, 0)

    @pl.when(half[0] == 1)
    def _():
        side = la.shape[2]
        tiles = lw.shape[2] // side
        block = 4 * cols
        per = side // (2 * block)

        def feed(i, carry):
            pair, tile = i // tiles, lax.rem(i, tiles)
            lanes = pl.ds(pl.multiple_of(tile * side, 128), side)
            value = tn(lw[pair, :, lanes], lf[pair])
            for p in range(per):
                for j in range(4):
                    at = 2 * p * block + j * cols
                    keep(
                        4 * pair + j, tile * per + p, value[at : at + cols],
                        value[at + block : at + block + cols],
                    )
            return carry

        lax.fori_loop(0, 2 * tiles, feed, 0)

    @pl.when(role[0] == 1)
    def _():
        clips = captions.shape[0]
        rows = captions.shape[1]
        def dy_of(c):
            h = (2 * c) // clips
            at = c - (h * clips) // 2
            return jnp.where(half[0] == h, dy[at].astype(f32), rdy[at].astype(f32)).astype(bf16)

        @pl.when(half[0] == 1)
        def _():
            shape = (y2p.shape[2], y2p.shape[1], cols)
            mine, theirs = units_of(1, *shape), units_of(0, *shape)
            square[...] = jnp.zeros_like(square)

            def one(c, carry):
                plain = low(nn(gq[c], mine) + nn(rgq[c], theirs))
                square[...] += tn(dy_of(c), plain)
                return carry

            lax.fori_loop(0, clips, one, 0)
            keep_square(8, square[...])

        units = text_out.shape[2]

        def keep_text(lanes, value):
            for p in range(line):
                for q in range(2):
                    cut = (2 * p + q) * units
                    text_out[p, q, :, lanes] = low(value[cut : cut + units])

        ones = jnp.ones((LP, 128), bf16)
        sums[...] = jnp.zeros_like(sums)

        def turn(c, carry):
            back = nn(dy_of(c), y2p[half[0]]) * gelu_both(hq[c])[1]
            turned[c] = low(jnp.transpose(back))
            sums[...] += nn(turned[c], ones)
            return carry

        lax.fori_loop(0, clips, turn, 0)
        run(text(), True)

        def text_tile(t, carry):
            lanes = pl.ds(pl.multiple_of(t * 512, 512), 512)
            total = nn(turned[0, :, 0:rows], cap[0, :, lanes])
            for c in range(1, clips):
                total = total + nn(turned[c, :, 0:rows], cap[c, :, lanes])
            keep_text(lanes, total)
            return carry

        lax.fori_loop(0, captions.shape[2] // 512, text_tile, 0)
        keep_text(pl.ds(captions.shape[2], 128), sums[...])


def halves(value):
    first = low(value)
    return first, low(value - first.astype(f32))


def lefts(value, axis=1):
    first, second = halves(value)
    return jnp.concatenate([first, first, second], axis=axis)


def rights(value, axis=0):
    first, second = halves(value)
    return jnp.concatenate([first, second, first], axis=axis)


def gram_of(value, dot):
    first, second = halves(value)
    both = dot(first, first), dot(first, second)
    return both[0] + (both[1] + jnp.transpose(both[1]))


def muon_kernel(half, ua, uf, xa, xf, gram, whole):
    @pl.when(half[0] == 0)
    def _():
        u = ua[...]
        whole[...] = u / (jnp.sqrt(jnp.sum(u * u)) + 1e-07)

        def sweep(i, carry):
            x = whole[...]
            square = gram_of(x, nt)
            poly = coef_b * square + coef_c * gram_of(square, nt)
            whole[...] = coef_a * x + nn(lefts(poly), rights(x))
            return carry

        lax.fori_loop(0, 5, sweep, 0)
        xa[...] = low(whole[...])

    @pl.when(half[0] == 1)
    def _():
        width = uf.shape[1]
        tiles = uf.shape[0] // width
        gram[...] = jnp.zeros_like(gram)

        def rows(t):
            return pl.ds(pl.multiple_of(t * width, 128), width)

        def first(t, carry):
            piece = uf[rows(t), :]
            gram[...] += gram_of(piece, tn)
            return carry

        lax.fori_loop(0, tiles, first, 0)
        row = lax.broadcasted_iota(jnp.int32, (width, width), 0)
        col = lax.broadcasted_iota(jnp.int32, (width, width), 1)
        eye = jnp.where(row == col, 1.0, 0.0)
        start = gram[...]
        inv = 1.0 / (jnp.sqrt(jnp.sum(start * eye)) + 1e-07)
        gram[...] = start * (inv * inv)
        whole[...] = eye * inv

        def poly_of(a):
            return coef_a * eye + coef_b * a + coef_c * nn(lefts(a), rights(a))

        def sweep(i, carry):
            a = gram[...]
            left = lefts(poly_of(a))
            both = nn(left, rights(jnp.concatenate([a, whole[...]], axis=1)))
            whole[...] = both[:, width:]
            gram[...] = nn(left, rights(both[:, :width]))
            return carry

        lax.fori_loop(0, 4, sweep, 0)
        last = rights(nn(lefts(poly_of(gram[...])), rights(whole[...])))

        def apply(t, carry):
            xf[rows(t), :] = low(nn(lefts(uf[rows(t), :]), last))
            return carry

        lax.fori_loop(0, tiles, apply, 0)


def local_call(kernel, out_shape, in_specs, args, scratch=(), out_specs=None):
    return pl.pallas_call(
        kernel,
        out_shape=out_shape,
        in_specs=in_specs,
        out_specs=jax.tree.map(lambda _: VM, out_shape) if out_specs is None else out_specs,
        scratch_shapes=scratch,
        compiler_params=pltpu.CompilerParams(vmem_limit_bytes=VMEM_LIMIT),
    )(*args)


def here():
    return lax.axis_index("dp"), lax.axis_index("segment")


def dev(d, s):
    return {"dp": d, "segment": s}


def remote(src, dst, send, recv, target):
    return pltpu.make_async_remote_copy(
        src_ref=src, dst_ref=dst, send_sem=send, recv_sem=recv, device_id=target,
        device_id_type=MESH,
    )


def greet(targets):
    barrier = pltpu.get_barrier_semaphore()
    for target in targets:
        pl.semaphore_signal(barrier, inc=1, device_id=target, device_id_type=MESH)
    pl.semaphore_wait(barrier, len(targets))


def greet_dp(n, extra=()):
    d, s = here()
    barrier = pltpu.get_barrier_semaphore()

    def step(k, carry):
        pl.semaphore_signal(
            barrier, inc=1, device_id=dev(lax.rem(d + k, n), s), device_id_type=MESH
        )
        return carry

    lax.fori_loop(1, n, step, 0)
    for target in extra:
        pl.semaphore_signal(barrier, inc=1, device_id=target, device_id_type=MESH)
    pl.semaphore_wait(barrier, n - 1 + len(extra))


def comm_call(kernel, cid, args, out_shape, sems, out_specs=None, scratch=(), in_specs=None):
    if out_specs is None:
        out_specs = jax.tree.map(lambda _: ANY, out_shape)
    return pl.pallas_call(
        kernel,
        out_shape=out_shape,
        in_specs=[ANY] * len(args) if in_specs is None else in_specs,
        out_specs=out_specs,
        scratch_shapes=list(scratch) + [pltpu.SemaphoreType.DMA(shape) for shape in sems],
        compiler_params=pltpu.CompilerParams(
            collective_id=cid, has_side_effects=True, vmem_limit_bytes=VMEM_LIMIT
        ),
    )(*args)


ACROSS_FIRST = (2, 5)


def gather_kernel(n, pa, pb, pf, pw, py, pm, pt, wa, wb, wf, ww, wy, wm, wt,
                  send, recv, crecv, own):
    pair = 2 if n % 2 == 0 else 1
    line = n // pair
    d, s = here()
    role, half = s // 2, lax.rem(s, 2)
    a, x = d // pair, lax.rem(d, pair)
    mate = dev(d, role * 2 + 1 - half)
    above, below = dev(d + pair, s), dev(d - pair, s)
    across = dev(a * pair + (pair - 1 - x), s)
    barrier = pltpu.get_barrier_semaphore()

    def signal(target):
        pl.semaphore_signal(barrier, inc=1, device_id=target, device_id_type=MESH)

    signal(mate)
    if pair == 2:
        signal(across)

    @pl.when(a < line - 1)
    def _():
        signal(above)

    @pl.when(a > 0)
    def _():
        signal(below)

    pl.semaphore_wait(barrier, pair + jnp.minimum(a, 1) + jnp.minimum(line - 1 - a, 1))

    def two(i, ref, out):
        return [
            (i, ref.at[pl.ds(0, 2)], out.at[pl.ds(0, 2)], 2),
            (i + 1, ref.at[pl.ds(2, 2)], out.at[pl.ds(2, 2)], 2),
        ]

    first, last = half == 0, role == 1
    both = jnp.logical_and(first, last)
    shared = [((2, pw, ww, 0), first, True)]
    shared += [(item, first, True) for item in two(0, pa, wa)]
    shared += [(item, both, last) for item in two(5, pb, wb)]
    for m in range(2):
        item = (m, pf.at[pl.ds(m, 1)], wf.at[pl.ds(m, 1)], 1)
        shared.append((item, jnp.logical_not(first), True))
    alone = [((3, pt, wt, 0), True), ((4, pm, wm, 0), role == 0), ((4, py, wy, 0), role == 1)]
    parts = [(item, when, True) for item, when, _ in shared]
    parts += [(item, when, False) for item, when in alone]

    def slot(ref, lead, o):
        return ref.at[:, o] if lead else ref.at[o]

    def given(when, act):
        if when is True:
            act()
        else:
            pl.when(when)(act)

    def move(item, way, o, target, is_own=False):
        i, src, dst, lead = item
        there = slot(dst, lead, o)
        sem = crecv if way == 3 else recv
        return remote(src if is_own else there, there, send.at[way, i, o], sem.at[i, o], target)

    def forward(o, up, down, side, wait, ways=None):
        is_own = not wait
        for item, when, common in parts:

            def act(item=item, common=common, up=up, down=down, side=side):
                if item[0] in ACROSS_FIRST and pair == 2:
                    side = is_own
                    up, down = (up, down) if ways is None else ways
                if wait:
                    move(item, 0, o, across).wait_recv()

                def go(way, target):
                    move(item, way, o, target, is_own).start()

                if side and pair == 2:
                    go(2, across)
                if up is not None:
                    pl.when(up)(functools.partial(go, 0, above))
                if down is not None:
                    pl.when(down)(functools.partial(go, 1, below))
                if common:
                    go(3, mate)

            given(when, act)

    def keep(finish):
        for item, when, common in parts:

            def act(item=item):
                i, src, dst, lead = item
                copy = pltpu.make_async_copy(src, slot(dst, lead, d), own.at[i])
                copy.wait() if finish else copy.start()

            given(when, act)

    forward(d, a < line - 1, a > 0, True, False)
    keep(False)
    other = pair - 1 - x

    def sweep():
        def step(k, carry):
            @pl.when(a - k >= 0)
            def _():
                forward((a - k) * pair + x, a < line - 1, None, True, True)

            @pl.when(a + k < line)
            def _():
                forward((a + k) * pair + x, None, a > 0, True, True)

            if pair == 2:

                def from_side(o, up, down):
                    forward(o * pair + other, None, None, False, True, (up, down))

                @pl.when(a - (k - 1) >= 0)
                def _():
                    from_side(
                        a - (k - 1), a < line - 1, jnp.logical_and(k == 1, a > 0)
                    )

                @pl.when(jnp.logical_and(k > 1, a + (k - 1) < line))
                def _():
                    from_side(a + (k - 1), None, a > 0)

            return carry

        lax.fori_loop(1, line + 1, step, 0)

    sweep()

    def drain(o, carry):
        there, column = o // pair, lax.rem(o, pair)
        mine = column == x
        up = jnp.logical_and(there <= a, a < line - 1)
        down = jnp.logical_and(there >= a, a > 0)
        for item, when, common in parts:

            def act(item=item, common=common):
                lines_first = item[0] not in ACROSS_FIRST or pair == 1
                sent = (
                    (0, jnp.logical_and(mine, up) if lines_first else up, above),
                    (1, jnp.logical_and(mine, down) if lines_first else down, below),
                    (2, mine if lines_first else o == d, across),
                )
                for way, yes, target in sent:
                    if way == 2 and pair == 1:
                        continue
                    pl.when(yes)(lambda: move(item, way, o, target).wait_send())
                if common:
                    move(item, 3, o, mate).wait_send()

            given(when, act)
        return carry

    lax.fori_loop(0, n, drain, 0)
    keep(True)

    def collect(o, carry):
        for item, when, arrives in shared:
            mine = when if when is not both else first

            def act(item=item):
                i, src, dst, lead = item
                there = slot(dst, lead, o)
                remote(there, there, send.at[3, i, o], crecv.at[i, o], mate).wait_recv()

            given(jnp.logical_and(jnp.logical_not(mine), arrives), act)
        return carry

    lax.fori_loop(0, n, collect, 0)


def mate_kernel(src, dst, send, recv, own):
    d, s = here()
    role, half = s // 2, lax.rem(s, 2)
    mate = dev(d, role * 2 + 1 - half)

    @pl.when(role == 0)
    def _():
        greet([mate])
        pltpu.make_async_copy(src, dst.at[half], own.at[0]).start()
        remote(src, dst.at[half], send.at[0], recv.at[0], mate).start()
        pltpu.make_async_copy(src, dst.at[half], own.at[0]).wait()
        remote(src, dst.at[1 - half], send.at[0], recv.at[0], mate).wait()


def forward_kernel(count, h1s, gq, mq, h1t, gqs, mqt, send, recv, msend, mrecv, qsend, qrecv):
    relay_half_clips(
        count, 0, h1s, h1t, send, recv, swap=(gq, gqs, msend, mrecv), rows=(mq, mqt, qsend, qrecv)
    )


def relay_half_clips(count, from_role, src, dst, send, recv, extra=None, swap=None, rows=None):
    d, s = here()
    role, half = s // 2, lax.rem(s, 2)
    peers = [dev(d, (1 - role) * 2), dev(d, (1 - role) * 2 + 1)]
    mate = dev(d, role * 2 + 1 - half)
    peers.append(mate)
    greet(peers)

    def unit(i, part):
        there = half * count + i
        clip, own = there // 2, lax.rem(there, 2)
        other = 2 * clip + part
        return own, other // count, lax.rem(other, count)

    def copy(i, part):
        own, to, slot = unit(i, part)
        return remote(
            src.at[i, part], dst.at[slot, own], send.at[i, part], recv.at[slot, own],
            dev(d, (1 - from_role) * 2 + to),
        )

    def row_copy(to, finish):
        value, there, qsend, qrecv = rows
        copy = remote(value, there, qsend.at[to], qrecv.at[half], dev(d, (1 - from_role) * 2 + to))
        copy.wait_send() if finish else copy.start()

    def row_sends(finish):
        if rows is None:
            return

        @pl.when(role == from_role)
        def _():
            for to in range(2):
                pl.when(half == to)(functools.partial(row_copy, to, finish))

    row_sends(False)
    if swap is not None:
        mine, both, msend, mrecv = swap

        @pl.when(role == 1)
        def _():
            remote(mine, both, msend.at[0], mrecv.at[0], mate).start()

    if extra is not None:
        own_src, own_dst, esend, erecv = extra

        @pl.when(jnp.logical_and(role == 1, half == 1))
        def _():
            remote(own_src, own_dst, esend.at[0], erecv.at[0], dev(d, 2)).start()

    @pl.when(role == from_role)
    def _():
        for i in range(count):
            for part in range(2):
                copy(i, part).start()
        for i in range(count):
            for part in range(2):
                copy(i, part).wait_send()

    @pl.when(role == 1 - from_role)
    def _():
        for i in range(count):
            for part in range(2):
                remote(
                    src.at[i, part], dst.at[i, part], send.at[i, part], recv.at[i, part],
                    dev(d, from_role * 2),
                ).wait_recv()

    row_sends(True)
    if rows is not None:
        value, there, qsend, qrecv = rows

        @pl.when(role == 1 - from_role)
        def _():
            remote(value, there, qsend.at[0], qrecv.at[half], mate).wait_recv()

    if swap is not None:

        @pl.when(role == 1)
        def _():
            remote(mine, both, msend.at[0], mrecv.at[0], mate).wait()

    if extra is not None:

        @pl.when(jnp.logical_and(role == 1, half == 1))
        def _():
            remote(own_src, own_dst, esend.at[0], erecv.at[0], dev(d, 2)).wait_send()

        @pl.when(jnp.logical_and(role == 1, half == 0))
        def _():
            remote(own_src, own_dst, esend.at[0], erecv.at[0], dev(d, 2)).wait_recv()


def backward_kernel(count, dh1, dkv, dhs, extra, send, recv, esend, erecv):
    relay_half_clips(count, 1, dh1, dhs, send, recv, extra=(dkv.at[:, 0], extra, esend, erecv))


def swap_kernel(acts_s, acts_t, actf_s, actf_t, actw_s, actw_t, ybuf, dkvb, dy, dmod,
                racts, ractf, ractw, rybuf, rdkvb, rdy, rdmod, send, recv):
    d, s = here()
    role, half = s // 2, lax.rem(s, 2)
    mate = dev(d, role * 2 + 1 - half)
    greet([mate])
    six = acts_s.shape[0]
    gives = {
        (0, 0): [(0, actf_s, ractf), (1, actw_s, ractw), (4, dmod, rdmod)],
        (0, 1): [(0, acts_s, racts.at[pl.ds(0, six)]), (4, dmod, rdmod)],
        (1, 0): [(0, actf_t, ractf), (1, actw_t, ractw), (2, dy, rdy), (4, dmod, rdmod)],
        (1, 1): [
            (0, acts_t, racts), (1, ybuf, rybuf), (3, dkvb, rdkvb), (2, dy, rdy), (4, dmod, rdmod)
        ],
    }
    for (r, h), mine in gives.items():

        @pl.when(jnp.logical_and(role == r, half == h))
        def _():
            for i, src, dst in mine:
                remote(src, dst, send.at[i], recv.at[i], mate).start()
            for i, src, dst in mine:
                remote(src, dst, send.at[i], recv.at[i], mate).wait_send()
            for i, src, dst in gives[(r, 1 - h)]:
                remote(src, dst, send.at[i], recv.at[i], mate).wait_recv()


TEXT_CUTS = 11


def scatter_kernel(n, own_in, snd, text_in, vec, dmod, rdmod, loss, wm, temb, ww, hid, wt,
                   summed, text, vsum, squares, gm, g2, g1,
                   own, rx, up, down, sx, rz, tin, trx, tsx, trz, rv, rm, dtembs, dm, dmt,
                   osem, send1, recv1, send2, recv2, usend, urecv, dsend, drecv,
                   ssend, srecv, sown, tsend, trecv, esend, erecv, psend, precv):
    line = n // 2
    d, s = here()
    role, half = s // 2, lax.rem(s, 2)
    a, x = d // 2, lax.rem(d, 2)
    across = dev(a * 2 + 1 - x, s)
    other = dev(d, (1 - role) * 2 + half)
    count = 8 - 4 * (1 - role) * (1 - half)
    greet_dp(n, [other])
    squares[...] = jnp.zeros_like(squares)
    squares[1:2, 0:128] = loss[...]
    step = text.shape[1] // TEXT_CUTS
    is_text, is_last, is_time = role == 0, s == 3, s == 0
    clip_rows = dm.shape[0]

    def clip_sums():
        clips = dmod.shape[0]
        sources = (dmod, rdmod)
        for clip in range(clips):
            total = None
            for h in range(2):
                for i in range(clips):
                    if (h * clips + i) // 2 == clip:
                        part = sources[h][i]
                        total = part if total is None else total + part
            dm[8 * clip : 8 * clip + 8] = total

    pl.when(half == 0)(clip_sums)
    partial = remote(dm, dmt, psend.at[0], precv.at[0], other)

    def first_copies(u):
        return (
            remote(snd.at[u], rx.at[u], send1.at[u], recv1.at[u], across),
            pltpu.make_async_copy(own_in.at[u], own.at[u], osem.at[u]),
        )

    def text_hop(k):
        lanes = pl.ds(pl.multiple_of(k * step, 128), step)
        return remote(text_in.at[:, :, :, lanes], tin.at[k], tsend.at[k], trecv.at[k], other)

    def text_across(k):
        return remote(tin.at[k, :, 1 - x], trx.at[k], send1.at[9 + k], recv1.at[9 + k], across)

    def begin(u, carry):
        for copy in first_copies(u):
            copy.start()
        return carry

    def rows_at(o):
        return rm.at[pl.ds(pl.multiple_of(o * clip_rows, 8), clip_rows)]

    def small(i, finish):
        src, dst = (
            (lambda p: vec.at[p], lambda o: rv.at[o]) if i else (lambda p: dm, rows_at)
        )

        def each(k, carry):
            to, o = lax.rem(d + k, n), lax.rem(d + n - k, n)
            if finish:
                remote(src(o), dst(o), ssend.at[i, k], srecv.at[i, k], dev(o, s)).wait()
            else:
                remote(src(to), dst(d), ssend.at[i, k], srecv.at[i, k], dev(to, s)).start()
            return carry

        lax.fori_loop(1, n, each, 0)
        copy = pltpu.make_async_copy(src(d), dst(d), sown.at[i])
        copy.wait() if finish else copy.start()

    lax.fori_loop(0, 1, begin, 0)
    small(1, False)

    @pl.when(is_time)
    def _():
        partial.wait_recv()
        dm[...] = dm[...] + dmt[...]

    lax.fori_loop(1, count, begin, 0)

    @pl.when(is_last)
    def _():
        begin(8, 0)

    @pl.when(role == 1)
    def _():
        pl.when(half == 0)(lambda: partial.start())
        lax.fori_loop(0, TEXT_CUTS, lambda k, c: (text_hop(k).start(), c)[1], 0)

    def embeds(finish):
        def each(k, carry):
            to, o = lax.rem(d + k, n), lax.rem(d + n - k, n)
            if finish:
                remote(dtembs.at[o], dtembs.at[o], esend.at[k], erecv.at[k], dev(o, s)).wait()
            else:
                remote(dtembs.at[d], dtembs.at[d], esend.at[k], erecv.at[k], dev(to, s)).start()
            return carry

        lax.fori_loop(1, n, each, 0)

    def upward(u, p):
        return remote(up.at[u, p], up.at[u, p], usend.at[u, p], urecv.at[u, p], dev(d + 2, s))

    def downward(u, p):
        return remote(
            down.at[u, p], down.at[u, p], dsend.at[u, p], drecv.at[u, p], dev(d - 2, s)
        )

    def along_up(u):
        def add(i, carry):
            p = line - 1 - i

            @pl.when(a == 0)
            def _():
                up[u, p] = own[u, p]

            @pl.when(a > 0)
            def _():
                upward(u, p).wait_recv()
                up[u, p] = up[u, p] + own[u, p]

            return carry

        def send(i, carry):
            upward(u, line - 1 - i).start()
            return carry

        lax.fori_loop(0, line - 1 - a, add, 0)
        lax.fori_loop(0, line - 1 - a, send, 0)

    def along_down(u):
        def add(p, carry):
            @pl.when(a == line - 1)
            def _():
                down[u, p] = own[u, p]

            @pl.when(a < line - 1)
            def _():
                downward(u, p).wait_recv()
                down[u, p] = down[u, p] + own[u, p]

            return carry

        def send(p, carry):
            downward(u, p).start()
            return carry

        lax.fori_loop(0, a, add, 0)
        lax.fori_loop(0, a, send, 0)

    def pairs(u):
        for copy in first_copies(u):
            copy.wait()
        own[u] = own[u] + rx[u].astype(f32)

    def direct(i, total, line_in, finish):
        def each(k, carry):
            to, o = lax.rem(a + k, line), lax.rem(a + line - k, line)
            if finish:
                remote(
                    total.at[o], line_in.at[o], send2.at[i, k], recv2.at[i, k], dev(o * 2 + x, s)
                ).wait()
            else:
                remote(
                    total.at[to], line_in.at[a], send2.at[i, k], recv2.at[i, k],
                    dev(to * 2 + x, s),
                ).start()
            return carry

        lax.fori_loop(1, line, each, 0)

    def round_trip(i, carry):
        @pl.when(i < count)
        def _():
            pairs(i)

        pl.when(jnp.logical_and(is_time, i == 0))(lambda: small(0, False))

        @pl.when(jnp.logical_and(is_time, i == 1))
        def _():
            small(0, True)
            time_back([d], rm, wm, temb, dtembs.at[d])

        pl.when(jnp.logical_and(is_time, i == 2))(lambda: embeds(False))

        @pl.when(is_text)
        def _():
            def cut_at(delay, act):
                for j in range(2):
                    k = 2 * (i - delay) + j
                    pl.when(jnp.logical_and(k >= 0, k < TEXT_CUTS))(functools.partial(act, k))

            def arrive(k):
                text_hop(k).wait_recv()
                text_across(k).start()

            def add(k):
                text_across(k).wait()
                tsx[k] = low(tin[k, :, x].astype(f32) + trx[k].astype(f32))

            cut_at(5, lambda k: direct(k, tsx.at[k], trz.at[k], False))
            cut_at(3, arrive)
            cut_at(4, add)

        k = i - count

        @pl.when(jnp.logical_and(is_last, k == 0))
        def _():
            pairs(8)
            sx[...] = low(own[8])

        @pl.when(jnp.logical_and(is_last, k == 1))
        def _():
            direct(TEXT_CUTS, sx, rz, False)

        later = i - 1 - a

        @pl.when(jnp.logical_and(later >= 0, later < count))
        def _():
            along_up(later)

        other = i - line + a

        @pl.when(jnp.logical_and(other >= 0, other < count))
        def _():
            along_down(other)

        return carry

    lax.fori_loop(0, jnp.maximum(count + line, TEXT_CUTS // 2 + 6), round_trip, 0)
    small(1, True)
    vsum[...] = lax.fori_loop(0, n, lambda o, total: total + rv[o], jnp.zeros(vsum.shape, f32))

    @pl.when(is_time)
    def _():
        embeds(True)
        time_grad([d], rm, dtembs, ww, temb, hid, wt, gm, g2, g1, vsum, squares)

    @pl.when(role == 1)
    def _():
        pl.when(half == 0)(lambda: partial.wait_send())
        lax.fori_loop(0, TEXT_CUTS, lambda k, c: (text_hop(k).wait_send(), c)[1], 0)

    def collect(u, carry):
        @pl.when(a > 0)
        def _():
            upward(u, a).wait_recv()
            own[u, a] = own[u, a] + up[u, a]

        @pl.when(a < line - 1)
        def _():
            downward(u, a).wait_recv()
            own[u, a] = own[u, a] + down[u, a]

        whole = own[u, a]
        summed[u] = whole
        squares[0:1, :] += col_sum(whole * whole)
        return carry

    lax.fori_loop(0, count, collect, 0)

    def drain(u, carry):
        def one(i, c):
            upward(u, line - 1 - i).wait_send()
            return c

        def two(p, c):
            downward(u, p).wait_send()
            return c

        lax.fori_loop(0, line - 1 - a, one, 0)
        lax.fori_loop(0, a, two, 0)
        return carry

    lax.fori_loop(0, count, drain, 0)

    def others(line_in, whole):
        return lax.fori_loop(
            1, line, lambda k, acc: acc + line_in[lax.rem(a + k, line)].astype(f32), whole
        )

    @pl.when(is_last)
    def _():
        direct(TEXT_CUTS, sx, rz, True)
        whole = others(rz, own[8, a])
        summed[8] = whole
        squares[0:1, :] += col_sum(whole * whole)

    @pl.when(is_text)
    def _():
        def whole_cut(k, carry):
            direct(k, tsx.at[k], trz.at[k], True)
            whole = others(trz.at[k], tin[k, a, x].astype(f32) + trx[k, a].astype(f32))
            text[:, pl.ds(pl.multiple_of(k * step, 128), step)] = low(whole)
            lane = lax.broadcasted_iota(jnp.int32, (1, step), 1)
            spare = jnp.logical_and(k == TEXT_CUTS - 1, lane > step - 128)
            counted = jnp.where(spare, 0.0, whole)
            squares[0:1, :] += col_sum(counted * counted)
            return carry

        lax.fori_loop(0, TEXT_CUTS, whole_cut, 0)


def three(value):
    first = low(value)
    rest = value - first.astype(f32)
    second = low(rest)
    return first, second, low(rest - second.astype(f32))


def nn3(left, right):
    return sum(nn(piece, right) for piece in three(left))


def nt3(left, right):
    return sum(nt(piece, right) for piece in three(left))


def tn3(left, right):
    return sum(tn(left, piece) for piece in three(right))


def own_columns(rank, width, cols):
    row = lax.broadcasted_iota(jnp.int32, (width, 128), 0)
    col = lax.broadcasted_iota(jnp.int32, (width, 128), 1)
    return low(jnp.where(jnp.logical_and(row == rank * cols + col, col < cols), 1.0, 0.0))


def clip_groups(clips, rows):
    per = 8 * (rows // (clips // 8) // 8)
    left = lax.broadcasted_iota(jnp.int32, (clips, rows), 0)
    right = lax.broadcasted_iota(jnp.int32, (clips, rows), 1)
    match = (right // per) * 8 + (right % per) // 8 == left
    return low(jnp.where(match, 1.0, 0.0))


def silu_back(value):
    gate = jax.nn.sigmoid(value)
    return gate * (1.0 + value * (1.0 - gate))


def time_back(rank, rm, wm, temb, dtemb):
    cols, width = wm.shape[0], rm.shape[1]
    rows, clips = rm.shape[0], temb.shape[0]
    pick = own_columns(rank[0], width, cols)
    kind = lax.broadcasted_iota(jnp.int32, (rows, 1), 0) % 8
    value = rm[...]
    pieces = three(value)
    total = jnp.where(kind >= 6, nn3(value, pick), 0.0)
    zeros = jnp.zeros((128 - cols, width), bf16)

    def one(r, total):
        lanes = pl.ds(pl.multiple_of(r * width, 128), width)
        weight = jnp.concatenate([wm[:, lanes], zeros], axis=0)
        back = nt(pieces[0], weight) + nt(pieces[1], weight) + nt(pieces[2], weight)
        return total + jnp.where(kind == r, back, 0.0)

    total = lax.fori_loop(0, 6, one, total)
    slope = silu_back(nn3(temb[...], pick))
    group = clip_groups(clips, rows)

    def collapse(part):
        first, second, third = three(part)
        return nn(group, first) + nn(group, second) + nn(group, third)

    dtemb[...] = collapse(jnp.where(kind < 6, total, 0.0)) * slope + collapse(
        jnp.where(kind >= 6, total, 0.0)
    )


def time_grad(rank, rm, dtembs, ww, temb, hid, wt, gm, g2, g1, vout, tout):
    width, cols = rm.shape[1], vout.shape[0]
    rows, clips = rm.shape[0], temb.shape[0]
    n = dtembs.shape[0]
    pick = own_columns(rank[0], width, cols)
    kind = lax.broadcasted_iota(jnp.int32, (rows, 1), 0) % 8
    value = rm[...]
    hidden = hid[...]
    own_hid, own_temb = nn3(hidden, pick), nn3(temb[...], pick)
    gates = low(own_temb * jax.nn.sigmoid(own_temb))
    spread = low(tn(clip_groups(clips, rows), gates))
    pieces = three(value)
    count = jnp.zeros((1, 1), f32)

    def squared(block):
        return jnp.sum(jnp.sum(block * block, axis=1, keepdims=True), axis=0, keepdims=True)

    def one(r, count):
        masked = jnp.where(kind == r, spread.astype(f32), 0.0).astype(bf16)
        block = sum(tn(masked, piece) for piece in pieces)[0:cols]
        gm[:, pl.ds(pl.multiple_of(r * width, 128), width)] = block
        return count + squared(block)

    count = lax.fori_loop(0, 6, one, count)
    mine = dtembs[rank[0]]
    mine_pieces = three(mine)
    act = low(hidden * jax.nn.sigmoid(hidden))
    block = sum(tn(piece, act) for piece in mine_pieces)[0:cols]
    g2[...] = block
    count = count + squared(block)
    back = jnp.zeros((clips, 128), f32)
    zeros = jnp.zeros((128 - cols, 128), bf16)
    picked = low(nn(ww[:, 256 : 256 + width], pick))
    for o in range(n):
        weight = picked[o * cols : o * cols + cols]
        back = back + nn3(dtembs[o], jnp.concatenate([weight, zeros], axis=0))
    dhid = back * silu_back(own_hid)
    dhid_pieces = three(dhid)
    feature = low(wt[:, 0:256])
    block = sum(tn(piece, feature) for piece in dhid_pieces)[0:cols]
    g1[...] = block
    count = count + squared(block)
    at = lax.broadcasted_iota(jnp.int32, (clips, 128), 1)
    first = low(jnp.where(at == 1, 1.0, 0.0))
    second = low(jnp.where(at == 2, 1.0, 0.0))
    total = sum(tn(piece, first) for piece in dhid_pieces)
    total = total + sum(tn(piece, second) for piece in mine_pieces)
    row_kind = lax.broadcasted_iota(jnp.int32, (rows, 128), 0) % 8
    row_lane = lax.broadcasted_iota(jnp.int32, (rows, 128), 1)
    put = jnp.logical_and(row_lane == row_kind + 3, row_kind < 6)
    put = low(jnp.where(put, 1.0, 0.0))
    total = total + sum(tn(piece, put) for piece in three(nn3(value, pick)))

    vout[...] += total[0:cols]
    lane = lax.broadcasted_iota(jnp.int32, (1, 128), 1)
    tout[0:1, 0:128] += jnp.where(lane == 0, count, 0.0)


class Relay:
    def __init__(self, send, recv):
        self.d, self.s = here()
        self.role, self.half = self.s // 2, lax.rem(self.s, 2)
        self.other = dev(self.d, (1 - self.role) * 2 + self.half)
        self.mate = dev(self.d, self.role * 2 + 1 - self.half)
        self.send, self.recv = send, recv

    def at(self, r, h):
        return jnp.logical_and(self.role == r, self.half == h)

    def copy(self, i, leg, src, dst):
        target = self.other if leg == 0 else self.mate
        return remote(src, dst, self.send.at[i, leg], self.recv.at[i, leg], target)

    def start(self, i, src, dst):
        self.copy(i, 0, src, dst).start()
        self.copy(i, 1, src, dst).start()

    def middle(self, i, dst):
        self.copy(i, 0, dst, dst).wait_recv()
        self.copy(i, 2, dst, dst).start()

    def finish(self, r, h, items):
        @pl.when(self.at(r, h))
        def _():
            for i, src, dst in items:
                self.copy(i, 0, src, dst).wait_send()
                self.copy(i, 1, src, dst).wait_send()

        @pl.when(self.at(1 - r, h))
        def _():
            for i, src, dst in items:
                self.copy(i, 2, dst, dst).wait_send()

        @pl.when(self.at(r, 1 - h))
        def _():
            for i, src, dst in items:
                self.copy(i, 1, dst, dst).wait_recv()

        @pl.when(self.at(1 - r, 1 - h))
        def _():
            for i, src, dst in items:
                self.copy(i, 2, dst, dst).wait_recv()


def owner_first(role, mat):
    return 2 * mat + mat % 2 if role == 0 else mat


def owner_second(mat):
    return 2 + 3 * mat


def settle_kernel(n, vsum, tile, summed, att_m, feed_m, gm, g2, g1,
                  oa, of, xa, xf, xm, x2, x1, gv, stat,
                  vecs, tiles, mine, totals, look, mom,
                  msem, send, recv, own, gsend, grecv, gown, ssend, srecv, tsend, trecv):
    relay = Relay(gsend, grecv)
    d, s, role, half = relay.d, relay.s, relay.role, relay.half
    peers = [dev(d, lax.rem(s + k, 4)) for k in range(1, 4)]
    greet_dp(n, peers)
    four, eight = pl.ds(0, 4), pl.ds(0, 8)
    shared = {
        (0, 0): [(0, summed.at[four], xa.at[four]), (4, gm, xm), (5, g2, x2), (6, g1, x1)],
        (0, 1): [(1, summed.at[eight], xf.at[eight])],
        (1, 0): [(2, summed.at[eight], xa.at[pl.ds(4, 8)])],
        (1, 1): [(3, summed.at[eight], xf.at[pl.ds(8, 8)])],
    }
    def momentum(finish):
        sources = {
            (0, 0): (att_m.at[four], mom.at[four]),
            (0, 1): (feed_m.at[eight], mom),
            (1, 0): (att_m.at[pl.ds(4, 8)], mom),
            (1, 1): (feed_m.at[pl.ds(8, 8)], mom),
        }
        for (r, h), (src, dst) in sources.items():

            @pl.when(relay.at(r, h))
            def _():
                copy = pltpu.make_async_copy(src, dst, msem.at[0])
                copy.wait() if finish else copy.start()

    momentum(False)
    small = [(0, vsum, vecs), (1, tile, tiles)]
    for i, src, dst in small:
        for k in range(1, 4):
            remote(src, dst.at[s], ssend.at[i, k], srecv.at[i, k], peers[k - 1]).start()
    for (r, h), items in shared.items():

        @pl.when(relay.at(r, h))
        def _():
            for i, src, dst in items:
                pltpu.make_async_copy(src, dst, gown.at[i]).start()
                relay.start(i, src, dst)

    total, squares, losses = vsum[...], tile[0:1, :], tile[1:2, :]
    for k in range(1, 4):
        o = lax.rem(s + 4 - k, 4)
        for i, src, dst in small:
            remote(src, dst.at[o], ssend.at[i, k], srecv.at[i, k], dev(d, o)).wait()
        total = total + vecs[o]
        squares = squares + tiles[o, 0:1, :]
        losses = losses + tiles[o, 1:2, :]
    lane = lax.broadcasted_iota(jnp.int32, (1, 128), 1)
    total = jnp.where(jnp.logical_or(lane == 9, lane >= 77), 0.0, total)
    gv[...] = total

    def whole(block):
        return jnp.sum(jnp.sum(block, axis=1, keepdims=True), axis=0, keepdims=True)

    row = lax.broadcasted_iota(jnp.int32, (8, 128), 0)
    mine[...] = jnp.where(row < 4, whole(squares) + whole(total * total), whole(losses[:, 0:128]))
    so_far = mine[...]

    def start(k, carry):
        remote(mine, totals.at[d], tsend.at[k], trecv.at[k], dev(lax.rem(d + k, n), s)).start()
        return carry

    lax.fori_loop(1, n, start, 0)

    def finish(k, carry):
        o = lax.rem(d + n - k, n)
        remote(mine, totals.at[o], tsend.at[k], trecv.at[k], dev(o, s)).wait()
        return carry + totals[o]

    lax.fori_loop(1, n, lambda k, c: (finish(k, so_far), c)[1], 0)
    totals[d] = so_far
    so_far = lax.fori_loop(0, n, lambda o, c: c + totals[o], jnp.zeros((8, 128), f32))
    stat[...] = so_far
    factor = jnp.minimum(1.0, max_norm / (jnp.sqrt(so_far[0:1, 0:1]) + 1e-06))
    scale = factor * (1.0 + momentum_decay)

    momentum(True)

    def update(m, carry):
        look[m] = summed[m] * scale + mom[m] * (momentum_decay * momentum_decay)
        return carry

    lax.fori_loop(0, 8, update, 0)
    groups = []
    for r in range(2):
        mats = 4 if r == 0 else 8
        groups.append((r, 0, [(m, owner_first(r, m), look.at[m], oa) for m in range(mats)]))
        groups.append((
            r, 1, [(m, owner_second(m), look.at[pl.ds(4 * m, 4)], of) for m in range(2)]
        ))
    for r, h, mats in groups:

        @pl.when(relay.at(r, h))
        def _():
            for m, o, src, dst in mats:

                @pl.when(d == o)
                def _():
                    pltpu.make_async_copy(src, dst.at[d], own.at[0]).start()

                @pl.when(d != o)
                def _():
                    remote(src, dst.at[d], send.at[m], recv.at[d], dev(o, s)).start()

    for (r, h), items in shared.items():

        @pl.when(relay.at(1 - r, h))
        def _():
            for i, src, dst in items:
                relay.middle(i, dst)

    for r, h, mats in groups:

        @pl.when(relay.at(r, h))
        def _():
            for i, src, dst in shared[(r, h)]:
                pltpu.make_async_copy(src, dst, gown.at[i]).wait()
            for m, o, src, dst in mats:

                @pl.when(d == o)
                def _():
                    pltpu.make_async_copy(src, dst.at[d], own.at[0]).wait()

                    def arrived(k, carry):
                        p = lax.rem(d + n - k, n)
                        remote(src, dst.at[p], send.at[m], recv.at[p], dev(p, s)).wait_recv()
                        return carry

                    lax.fori_loop(1, n, arrived, 0)

                @pl.when(d != o)
                def _():
                    remote(src, dst.at[d], send.at[m], recv.at[d], dev(o, s)).wait_send()

    for (r, h), items in shared.items():
        relay.finish(r, h, items)


def spread_kernel(n, xa, xf, gy1, summed, oa, of, xy1, xy2, send, recv, rsend, rrecv, own, gown):
    relay = Relay(rsend, rrecv)
    d, s, role, half = relay.d, relay.s, relay.role, relay.half
    greet_dp(n, [relay.other, relay.mate])
    groups = []
    for r in range(2):
        mats = 4 if r == 0 else 8
        groups.append((r, 0, mats, functools.partial(owner_first, r), xa, oa, 10 * r, 4))
        groups.append((r, 1, 2, owner_second, xf, of, 10 * r + 8, 2))
    text = {
        (0, 0): [(20, gy1, xy1.at[0])],
        (0, 1): [(21, gy1, xy1.at[1])],
        (1, 1): [(22, summed.at[8], xy2)],
    }
    for (r, h), items in text.items():

        @pl.when(relay.at(r, h))
        def _():
            for i, src, dst in items:
                pltpu.make_async_copy(src, dst, gown.at[i - 20]).start()
                relay.start(i, src, dst)

    for r, h, mats, owner, src, dst, base, per in groups:

        @pl.when(relay.at(r, h))
        def _():
            for m in range(mats):

                @pl.when(d == owner(m))
                def _():
                    pltpu.make_async_copy(src.at[d], dst.at[per * r + m], own.at[m]).start()

                    def start(k, carry):
                        to = lax.rem(d + k, n)
                        remote(
                            src.at[to], dst.at[per * r + m], send.at[k], recv.at[m], dev(to, s)
                        ).start()
                        return carry

                    lax.fori_loop(1, n, start, 0)

            for m in range(mats):

                @pl.when(d == owner(m))
                def _():
                    pltpu.make_async_copy(src.at[d], dst.at[per * r + m], own.at[m]).wait()

                @pl.when(d != owner(m))
                def _():
                    remote(
                        src.at[d], dst.at[per * r + m], send.at[1], recv.at[m], dev(owner(m), s)
                    ).wait_recv()

                relay.start(base + m, dst.at[per * r + m], dst.at[per * r + m])

    for (r, h), items in text.items():

        @pl.when(relay.at(1 - r, h))
        def _():
            for i, src, dst in items:
                relay.middle(i, dst)

    for r, h, mats, owner, src, dst, base, per in groups:

        @pl.when(relay.at(1 - r, h))
        def _():
            for m in range(mats):
                relay.middle(base + m, dst.at[per * r + m])

    for r, h, mats, owner, src, dst, base, per in groups:

        @pl.when(relay.at(r, h))
        def _():
            for m in range(mats):

                @pl.when(d == owner(m))
                def _():
                    def finish(k, carry):
                        to = lax.rem(d + k, n)
                        remote(
                            src.at[to], dst.at[per * r + m], send.at[k], recv.at[m], dev(to, s)
                        ).wait_send()
                        return carry

                    lax.fori_loop(1, n, finish, 0)

        relay.finish(r, h, [(base + m, dst.at[per * r + m], dst.at[per * r + m]) for m in range(mats)])

    for (r, h), items in text.items():

        @pl.when(relay.at(r, h))
        def _():
            for i, src, dst in items:
                pltpu.make_async_copy(src, dst, gown.at[i - 20]).wait()

        relay.finish(r, h, items)


def adamw_update(weight, first, second, grad, fix_one, fix_two):
    first = beta_one * first + (1.0 - beta_one) * grad
    second = beta_two * second + (1.0 - beta_two) * grad * grad
    first_hat = first * fix_one
    second_hat = second * fix_two
    weight = weight - adam_rate * (
        first_hat / (jnp.sqrt(second_hat) + 1e-08) + weight_decay * weight
    )
    return (weight, first, second)


def update_kernel(
    rates, pieces, scal, stat,
    aw, am, ag, ax, fw, fm, fg, fx, sw, s1, s2, gv, g1, g2, gt, gy2, gm, vw, v1, v2, gvall, gtall,
    aw_, am_, ab_, fw_, fm_, fb_, sw_, s1_, s2_, sb_, vw_, v1_, v2_, vb_, loss_, norm_, powers,
):
    grad_norm = jnp.sqrt(stat[0:1, 0:1])
    factor = jnp.minimum(1.0, max_norm / (grad_norm + 1e-06))

    @pl.when(pl.program_id(0) == 0)
    def _():
        for i, beta in enumerate((beta_one, beta_two)):
            powers[i] = lax.fori_loop(0, scal[0], lambda _, value: value * beta, jnp.float32(1.0))

    fix_one, fix_two = (1.0 / (1.0 - jnp.full((1, 1), powers[i])) for i in range(2))
    loss_[...] = stat[4:5, 0:1]
    norm_[...] = grad_norm
    shrink = 1.0 - muon_rate * weight_decay
    for rate, (w, m, g, x, w_, m_, b_) in zip(
        rates, ((aw, am, ag, ax, aw_, am_, ab_), (fw, fm, fg, fx, fw_, fm_, fb_))
    ):
        m_[...] = momentum_decay * m[...] + g[...] * factor
        fresh = w[...] * shrink - rate * x[...].astype(f32)
        w_[...] = fresh
        b_[...] = low(fresh)
    text = gt.shape[1] - 128
    shards = {
        "embed": gv[:, EMB0 : EMB0 + 16],
        "time": g1[...],
        "time2": g2[...],
        "text": None,
        "text2": gy2[...],
        "head": gv[:, HEAD0 : HEAD0 + 16],
        "mod": gm[...],
    }
    for name, at, size in pieces:
        stride = size if name != "text" else 512
        for start in range(0, size, stride):
            cut = slice(at + start, at + start + stride)
            grad = gt[:, start : start + stride].astype(f32) if name == "text" else shards[name]
            fresh, one, two = adamw_update(
                sw[:, cut], s1[:, cut], s2[:, cut], grad * factor, fix_one, fix_two
            )
            sw_[:, cut], s1_[:, cut], s2_[:, cut] = fresh, one, two
            sb_[:, cut] = low(fresh)

    @pl.when(pl.program_id(0) == 0)
    def _():
        lane = lax.broadcasted_iota(jnp.int32, (1, 128), 1)
        column = gtall[:, text : text + 128].astype(f32)
        whole = jnp.where(lane == 9, column, gvall[...])
        rows = vw.shape[0]
        grad = jnp.transpose(whole)[0:rows, :] * factor
        fresh, one, two = adamw_update(vw[...], v1[...], v2[...], grad, fix_one, fix_two)
        vw_[...], v1_[...], v2_[...] = fresh, one, two
        vb_[...] = low(fresh)


def body(
    latents,
    noise_draw,
    timesteps,
    captions,
    caption_len,
    attention_weights,
    feed_weights,
    side_weights,
    vector_weights,
    attention_momentum,
    feed_momentum,
    side_first,
    side_second,
    vector_first,
    vector_second,
    step_count,
):
    n = lax.axis_size("dp")
    d, s = here()
    role, half = s // 2, lax.rem(s, 2)
    count = latents.shape[0]
    frames = latents.shape[1]
    width = attention_weights.shape[1]
    cols, feed_cols = attention_weights.shape[2], feed_weights.shape[2]
    hidden = n * feed_cols
    text = captions.shape[2]
    sds = jax.ShapeDtypeStruct
    role_s, half_s = role.reshape(1).astype(jnp.int32), half.reshape(1).astype(jnp.int32)

    o_time = 16
    o_text = o_time + 256 + width
    o_text2 = o_text + text
    o_head = o_text2 + width
    o_mod = o_head + 16
    six = 6 * width
    own_rows = -(-cols // 2)
    lanes = n * own_rows

    att_t = jnp.swapaxes(attention_weights, 1, 2)
    feed_t = jnp.swapaxes(feed_weights, 1, 2)
    side_t = side_weights.T
    pa, pb, pf, pw, py, pm, wm_own = local_call(
        lambda role, half, *refs: pack_kernel(
            role, half, (o_time, o_text, o_text2, o_head, o_mod), *refs
        ),
        [
            sds((4, cols, width), bf16),
            sds((4, cols, width), bf16),
            sds((2, feed_cols, width), bf16),
            sds((cols, 1152), bf16),
            sds((own_rows, text), bf16),
            sds((cols, 3 * width), bf16),
            sds((cols, six), bf16),
        ],
        [SM] * 2 + [VM] * 4,
        (role_s, half_s, att_t, feed_t, side_t, vector_weights),
    )
    freqs = jnp.exp(-math.log(10000.0) * jnp.arange(128, dtype=f32) / 128)
    angles = timesteps.astype(f32)[:, None] * freqs[None, :]
    level, snr = snr_weight(timesteps.astype(f32))
    mix = jnp.stack([snr, jnp.sqrt(level), jnp.sqrt(1.0 - level)], axis=1)
    pt = jnp.concatenate([jnp.cos(angles), jnp.sin(angles), mix], axis=1)
    pt = jnp.pad(pt, ((0, 8 - count), (0, width - 259)))

    wa, wb, wf, ww, wy, wm, wt = comm_call(
        functools.partial(gather_kernel, n),
        1,
        (pa, pb, pf, pw, py, pm, pt),
        [
            sds((4, n, cols, width), bf16),
            sds((4, n, cols, width), bf16),
            sds((2, n, feed_cols, width), bf16),
            sds((n, cols, 1152), bf16),
            sds((n, own_rows, text), bf16),
            sds((n, cols, 3 * width), bf16),
            sds((n, 8, width), f32),
        ],
        [(4, 7, n), (7, n), (7, n), (7,)],
    )
    wa = wa.reshape(4, width, width)
    wb = wb.reshape(4, width, width)
    wf = wf.reshape(2, hidden, width)
    ww = ww.reshape(width, 1152)
    wy = wy.reshape(lanes, text)
    wm = wm.reshape(width, 3 * width)
    rank_s = d.reshape(1).astype(jnp.int32)
    per_clip = frames * (latents.shape[3] // 2) * (latents.shape[4] // 2)
    vec, hid, temb, mq_own, y2p, errs = local_call(
        functools.partial(condition_kernel, per_clip=per_clip, cols=cols),
        [
            sds((128, width), f32),
            sds((n * 8, width), f32),
            sds((n * 8, width), f32),
            sds((8, 3 * width), f32),
            sds((2, width, lanes), bf16),
            sds((8, 128), f32),
        ],
        [SM] + [VM] * 3,
        (rank_s, wt.reshape(n * 8, width), ww, wm),
    )
    mq = comm_call(
        mate_kernel, 2, (mq_own,), sds((2, 8, 3 * width), f32), [(1,), (1,), (1,)]
    )

    half_tokens = count * per_clip // 2
    places = np.arange(per_clip // frames)
    edge = latents.shape[3] // 2
    pos = np.concatenate(
        [sincos(places // edge, width // 2), sincos(places % edge, width // 2)], axis=1
    )
    pos = jnp.asarray(pos)
    timing = jnp.asarray(sincos(np.arange(frames), width))

    clip_rows = captions.shape[1]
    residuals = [
        sds((5, half_tokens, width), bf16),
        sds((3, half_tokens, width), f32),
        sds((half_tokens, hidden), f32),
        sds((count, 3, 256, 128), f32),
    ]
    residual_scratch = [pltpu.VMEM(v.shape, v.dtype) for v in residuals]
    h1s, hq, gq_own, tok, kept_b, kept_f, kept_u, kept_p = local_call(
        functools.partial(first_kernel, cols),
        [
            sds((count, 2, 64, width), bf16),
            sds((count, LP, lanes), f32),
            sds((count, LP, lanes), bf16),
            sds((half_tokens, 128), bf16),
        ]
        + residuals,
        [SM] * 2 + [VM] * 9 + [ANY],
        (role_s, half_s, latents, noise_draw, pt, pos, mq, vec, wa, wf, wy, captions),
        residual_scratch
        + [
            pltpu.VMEM((count, clip_rows, text), bf16),
            pltpu.SemaphoreType.DMA((count,)),
            pltpu.SemaphoreType.DMA((count, 4)),
        ],
        [VM] * 4 + [ANY] * 4,
    )
    h1t, rgq, mqt = comm_call(
        functools.partial(forward_kernel, count),
        3,
        (h1s, gq_own, mq),
        [
            sds((count, 2, 64, width), bf16),
            sds((count, LP, lanes), bf16),
            sds((2, 8, 3 * width), f32),
        ],
        [(count, 2), (count, 2), (1,), (1,), (2,), (2,)],
    )

    ncl = (count + 1) // 2
    wide = sds((2, half_tokens, hidden), bf16)
    thin = sds((2, half_tokens, width), bf16)
    cap_like = sds((ncl, LP, width), bf16)
    dh1, acts_t, actf_t, actw_t, ybuf, dkv, grads_t, dmod_t, loss_t = local_call(
        temporal_kernel,
        [
            sds((count, 2, 64, width), bf16),
            sds((10, half_tokens, width), bf16),
            thin,
            wide,
            cap_like,
            sds((2, ncl, LP, width), f32),
            sds((128, width), f32),
            sds((count, 8, width), f32),
            sds((1, 128), f32),
        ],
        [SM] * 4 + [VM] * 13,
        (
            role_s, half_s, rank_s, caption_len, errs, h1t, timing, mqt, vec, temb, wa, wb, wf,
            gq_own, rgq, y2p, noise_draw,
        ),
        [pltpu.VMEM((ncl, KP, width), bf16), pltpu.VMEM((ncl, KP, width), bf16)],
    )
    dhs, extra = comm_call(
        functools.partial(backward_kernel, count),
        4,
        (dh1, dkv),
        [sds((count, 2, 64, width), bf16), sds((2, LP, width), f32)],
        [(count, 2), (count, 2), (1,), (1,)],
    )
    acts_s, actf_s, actw_s, dkvb, dy, vect, dmod = local_call(
        last_kernel,
        [
            sds((6, half_tokens, width), bf16),
            thin,
            wide,
            sds((2, ncl, LP, width), bf16),
            cap_like,
            sds((width, 128), f32),
            sds((count, 8, width), f32),
        ],
        [SM] * 2 + [VM] * 6 + [ANY] * 4 + [VM] * 5,
        (
            role_s, half_s, tok, mq, vec, wa, wb, wf, kept_b, kept_f, kept_u, kept_p, dhs, dkv,
            extra, grads_t, dmod_t,
        ),
        [pltpu.VMEM((128, width), f32)]
        + residual_scratch
        + [pltpu.SemaphoreType.DMA((count, 4))],
    )
    racts, ractf, ractw, rybuf, rdkvb, rdy, rdmod = comm_call(
        swap_kernel,
        5,
        (acts_s, acts_t, actf_s, actf_t, actw_s, actw_t, ybuf, dkvb, dy, dmod),
        [
            sds((10, half_tokens, width), bf16),
            thin,
            wide,
            cap_like,
            sds((2, ncl, LP, width), bf16),
            cap_like,
            sds((count, 8, width), f32),
        ],
        [(5,), (5,)],
    )
    line = n // 2
    wide_text = text + 128
    cut_text = wide_text // TEXT_CUTS
    block = (9, line, cols, width)
    tokens2 = 2 * half_tokens
    grad_own, grad_snd, text_part = local_call(
        weight_grad_kernel,
        [
            sds(block, f32),
            sds(block, bf16),
            sds((line, 2, own_rows, wide_text), bf16),
        ],
        [SM] * 3 + [ANY] * 9 + [VM] * 10 + [ANY],
        (
            role_s, half_s, rank_s, acts_s, acts_t, racts, actf_s, actf_t, ractf, actw_s, actw_t,
            ractw, ybuf, rybuf, dkvb, rdkvb, dy, rdy, gq_own, rgq, hq, y2p, captions,
        ),
        [
            pltpu.VMEM((10, tokens2, width), bf16),
            pltpu.VMEM((2, tokens2, width), bf16),
            pltpu.VMEM((2, tokens2, hidden), bf16),
            pltpu.VMEM((count, clip_rows, text), bf16),
            pltpu.VMEM((width, width), f32),
            pltpu.VMEM((count, lanes, LP), bf16),
            pltpu.VMEM((lanes, 128), f32),
            pltpu.SemaphoreType.DMA((4 + count,)),
        ],
    )

    whole_clips = n * 8
    text_block = (TEXT_CUTS, line, own_rows, cut_text)
    summed, text_sum, vsum, tile, grad_mod, grad_time2, grad_time1 = comm_call(
        functools.partial(scatter_kernel, n),
        6,
        (
            grad_own, grad_snd, text_part, vect.reshape(n, cols, 128), dmod, rdmod, loss_t,
            wm_own, temb, ww, hid, wt.reshape(whole_clips, width),
        ),
        [
            sds((9, cols, width), f32),
            sds((own_rows, wide_text), bf16),
            sds((cols, 128), f32),
            sds((8, width), f32),
            sds((cols, six), f32),
            sds((cols, width), f32),
            sds((cols, 256), f32),
        ],
        [(9,), (9 + TEXT_CUTS,), (9 + TEXT_CUTS,)]
        + [(TEXT_CUTS + 1, line)] * 2
        + [(8, line)] * 4
        + [(2, n), (2, n), (2,), (TEXT_CUTS,), (TEXT_CUTS,), (n,), (n,), (1,), (1,)],
        [VM] * 7,
        in_specs=[ANY] * 4 + [VM] * 8,
        scratch=[
            pltpu.VMEM(block, f32),
            pltpu.VMEM(block, bf16),
            pltpu.VMEM((8,) + block[1:], f32),
            pltpu.VMEM((8,) + block[1:], f32),
            pltpu.VMEM(block[1:], bf16),
            pltpu.VMEM(block[1:], bf16),
            pltpu.VMEM((TEXT_CUTS, line, 2, own_rows, cut_text), bf16),
        ]
        + [pltpu.VMEM(text_block, bf16)] * 3
        + [
            pltpu.VMEM((n, cols, 128), f32),
            pltpu.VMEM((n * 8 * count, width), f32),
            pltpu.VMEM((n, whole_clips, 128), f32),
            pltpu.VMEM((8 * count, width), f32),
            pltpu.VMEM((8 * count, width), f32),
        ],
    )

    att_m = jnp.swapaxes(attention_momentum, 1, 2)
    feed_m = jnp.swapaxes(feed_momentum, 1, 2)
    ua, uf, ga2, gf2, grad_mod, grad_time2, grad_time1, grad_v, stat = comm_call(
        functools.partial(settle_kernel, n),
        8,
        (
            vsum, tile, summed, att_m, feed_m.reshape(16, cols, width), grad_mod, grad_time2,
            grad_time1,
        ),
        [
            sds((n, cols, width), f32),
            sds((n, 4, cols, width), f32),
            sds((12, cols, width), f32),
            sds((16, cols, width), f32),
            sds((cols, six), f32),
            sds((cols, width), f32),
            sds((cols, 256), f32),
            sds((cols, 128), f32),
            sds((8, 128), f32),
        ],
        [(1,), (8,), (n,), (1,), (7, 3), (7, 3), (7,), (2, 4), (2, 4), (n,), (n,)],
        [ANY] * 7 + [VM] * 2,
        in_specs=[VM] * 3 + [ANY] * 5,
        scratch=[
            pltpu.VMEM((4, cols, 128), f32),
            pltpu.VMEM((4, 8, width), f32),
            pltpu.VMEM((8, 128), f32),
            pltpu.VMEM((n, 8, 128), f32),
            pltpu.VMEM((8, cols, width), f32),
            pltpu.VMEM((8, cols, width), f32),
        ],
    )
    xa, xf = local_call(
        muon_kernel,
        [sds((width, width), bf16), sds((hidden, width), bf16)],
        [SM] + [VM] * 2,
        (half_s, ua.reshape(width, width), uf.reshape(hidden, width)),
        [pltpu.VMEM((width, width), f32), pltpu.VMEM((width, width), f32)],
    )
    xa_all, xf_all, gy12, gy22 = comm_call(
        functools.partial(spread_kernel, n),
        10,
        (xa.reshape(n, cols, width), xf.reshape(n, feed_cols, width), text_sum, summed),
        [
            sds((12, cols, width), bf16),
            sds((4, feed_cols, width), bf16),
            sds((2, own_rows, wide_text), bf16),
            sds((cols, width), f32),
        ],
        [(n,), (8,), (23, 3), (23, 3), (8,), (3,)],
    )

    text_grad = gy12.reshape(2 * own_rows, wide_text)[:cols]
    side_m, side_v = side_first.T, side_second.T
    side_rows = side_t.shape[1]
    pieces = (
        ("embed", 0, 16),
        ("time", o_time, 256),
        ("time2", o_time + 256, width),
        ("text", o_text, text),
        ("text2", o_text2, width),
        ("head", o_head, 16),
        ("mod", o_mod, six),
    )
    rates = tuple(
        muon_rate * 0.2 * math.sqrt(columns) for columns in (n * cols, n * feed_cols)
    )
    grid = cols // 8 if cols % 8 == 0 else 1

    def by_rows(value):
        return value.reshape(-1, value.shape[-1])

    def rows_spec(value):
        return pl.BlockSpec((value.shape[0] // grid, value.shape[1]), lambda i: (i, 0))

    def whole_spec(value):
        return pl.BlockSpec(value.shape, lambda i: (0, 0))

    cutup = [by_rows(v) for v in (att_t, att_m, ga2, xa_all, feed_t, feed_m, gf2, xf_all)] + [
        side_t, side_m, side_v, grad_v, grad_time1, grad_time2, text_grad, gy22, grad_mod,
    ]
    fixed = [vector_weights, vector_first, vector_second, grad_v, text_grad]
    a_like, f_like, s_like = (sds(v.shape, f32) for v in (cutup[0], cutup[4], side_t))
    v_like = sds(vector_weights.shape, f32)

    def low_of(like):
        return sds(like.shape, bf16)

    row_outs = [
        a_like, a_like, low_of(a_like), f_like, f_like, low_of(f_like), s_like, s_like, s_like,
        low_of(s_like),
    ]
    whole_outs = [v_like, v_like, v_like, low_of(v_like), sds((1, 1), f32), sds((1, 1), f32)]
    (
        att_new, att_moment, att_low, feed_new, feed_moment, feed_low, side_new, side_first_new,
        side_second_new, side_low, vector_new, vector_first_new, vector_second_new, vector_low,
        loss_value, grad_norm,
    ) = pl.pallas_call(
        functools.partial(update_kernel, rates, pieces),
        grid=(grid,),
        out_shape=row_outs + whole_outs,
        in_specs=[SM, whole_spec(stat)] + [rows_spec(v) for v in cutup] + [whole_spec(v) for v in fixed],
        out_specs=[rows_spec(v) for v in row_outs] + [whole_spec(v) for v in whole_outs],
        scratch_shapes=[pltpu.SMEM((2,), f32)],
        compiler_params=pltpu.CompilerParams(vmem_limit_bytes=VMEM_LIMIT),
    )(step_count, stat, *cutup, *fixed)

    def att(value):
        return value.reshape(att_t.shape)

    def feed(value):
        return value.reshape(feed_t.shape)

    def back(value):
        return jnp.swapaxes(value, -1, -2)

    return (
        loss_value[0, 0],
        grad_norm[0, 0],
        back(att(att_new)),
        back(att(att_moment)),
        back(feed(feed_new)),
        back(feed(feed_moment)),
        back(side_new),
        back(side_first_new),
        back(side_second_new),
        vector_new,
        vector_first_new,
        vector_second_new,
        back(att(att_low)),
        back(feed(feed_low)),
        back(side_low),
        vector_low,
    )


def solution(mesh):
    column = P(None, "dp")
    matrix = P(None, None, "dp")
    return jax.shard_map(
        body,
        mesh=mesh,
        in_specs=(
            P("dp", None, None, None, None),
            P("dp", None, None, None, None),
            P("dp"),
            P("dp", None, None),
            P("dp"),
            matrix,
            matrix,
            column,
            column,
            matrix,
            matrix,
            column,
            column,
            column,
            column,
            P(),
        ),
        out_specs=(
            P(),
            P(),
            matrix,
            matrix,
            matrix,
            matrix,
            column,
            column,
            column,
            column,
            column,
            column,
            matrix,
            matrix,
            column,
            column,
        ),
        check_vma=False,
    )
```

```python
import functools
import math

import jax
import jax.numpy as jnp
import numpy as np
from jax import lax
from jax.experimental import pallas as pl
from jax.experimental.pallas import tpu as pltpu
from jax.sharding import PartitionSpec as P

HEADS = 6
HEAD = 64
LP = 304
KP = 384

highest = lax.Precision.HIGHEST
snr_gamma = 5.0
max_norm = 0.005
momentum_decay = 0.95
muon_rate = 0.05
adam_rate = 0.02
beta_one = 0.9
beta_two = 0.999
weight_decay = 0.01
coef_a = 3.4445
coef_b = -4.775
coef_c = 2.0315

f32, bf16 = jnp.float32, jnp.bfloat16
MESH = pl.DeviceIdType.MESH
ANY = pl.BlockSpec(memory_space=pl.ANY)
VM = pl.BlockSpec(memory_space=pltpu.VMEM)
SM = pl.BlockSpec(memory_space=pltpu.SMEM)
VMEM_LIMIT = 60000 * 1024


def low(value):
    return value.astype(bf16)


def nt(left, right):
    return lax.dot_general(left, right, (((1,), (1,)), ((), ())), preferred_element_type=f32)


def nn(left, right):
    return lax.dot_general(left, right, (((1,), (0,)), ((), ())), preferred_element_type=f32)


def tn(left, right):
    return lax.dot_general(left, right, (((0,), (0,)), ((), ())), preferred_element_type=f32)


def snr_weight(steps_t):
    level = jnp.cos((steps_t / 1000.0 + 0.008) / 1.008 * (math.pi / 2)) ** 2
    ratio = level / (1.0 - level)
    return level, jnp.minimum(ratio, snr_gamma) / ratio


def sincos(places, model_width):
    half_width = model_width // 2
    freqs = np.exp(-math.log(10000.0) * np.arange(half_width) / half_width)
    angles = places[:, None] * freqs[None, :]
    return np.concatenate([np.sin(angles), np.cos(angles)], axis=1).astype(np.float32)


def col_sum(value):
    return jnp.sum(value.astype(f32), axis=0, keepdims=True)


def norm(value):
    centred = value - jnp.mean(value, axis=-1, keepdims=True)
    inv = lax.rsqrt(jnp.mean(centred * centred, axis=-1, keepdims=True) + 1e-06)
    return centred * inv, inv


def norm_back(grad, normed, inv):
    return inv * (
        grad
        - jnp.mean(grad, axis=-1, keepdims=True)
        - normed * jnp.mean(grad * normed, axis=-1, keepdims=True)
    )


GELU_C = math.sqrt(2.0 / math.pi)


def gelu(value):
    inner = GELU_C * (value + 0.044715 * (value * value * value))
    return value * (0.5 * (1.0 + jnp.tanh(inner)))


def gelu_both(value):
    square = value * value
    tanh = jnp.tanh(GELU_C * (value + 0.044715 * (square * value)))
    cdf = 0.5 * (1.0 + tanh)
    slope = 0.5 * (1.0 - tanh * tanh) * (GELU_C * (1.0 + 3 * 0.044715 * square))
    return value * cdf, cdf + value * slope


def lanes_low():
    lane = lax.broadcasted_iota(jnp.int32, (1, 128), 1)
    first = jnp.where(lane < HEAD, 1.0, 0.0)
    return low(first), low(1.0 - first), lane < HEAD


def stack_heads(pair, first, second):
    return jnp.concatenate([pair * first, pair * second], axis=0)


def attend(queries, keys, values, allowed):
    first, second, lower = lanes_low()
    rows = queries.shape[0]
    mixed, probs = [], []
    for pair in range(HEADS // 2):
        cut = slice(pair * 128, pair * 128 + 128)
        scores = nt(stack_heads(queries[:, cut], first, second), keys[:, cut]) * 0.125
        scores = jnp.where(allowed, scores, -1e30)
        weight = jnp.exp(scores - jnp.max(scores, axis=-1, keepdims=True))
        prob = weight / jnp.sum(weight, axis=-1, keepdims=True)
        probs.append(prob)
        out = nn(low(prob), values[:, cut])
        mixed.append(jnp.where(lower, out[:rows], out[rows:]))
    return low(jnp.concatenate(mixed, axis=1)), probs


def attend_back(grad, queries, keys, values, probs):
    first, second, lower = lanes_low()
    rows = queries.shape[0]
    dq, dk, dv = [], [], []
    for pair in range(HEADS // 2):
        cut = slice(pair * 128, pair * 128 + 128)
        stacked = stack_heads(grad[:, cut], first, second)
        prob = probs[pair]
        dv.append(tn(low(prob), stacked))
        dprob = nt(stacked, values[:, cut])
        dscore = low(prob * (dprob - jnp.sum(prob * dprob, axis=-1, keepdims=True)))
        part = nn(dscore, keys[:, cut])
        dq.append(jnp.where(lower, part[:rows], part[rows:]) * 0.125)
        dk.append(tn(dscore, stack_heads(queries[:, cut], first, second)) * 0.125)
    return tuple(jnp.concatenate(piece, axis=1) for piece in (dq, dk, dv))


def self_forward(x, mods, weights, bias, allowed):
    normed, inv = norm(x)
    a = low(normed * (1.0 + mods[1]) + mods[0])
    q = low(nt(a, weights[0]) + bias[0])
    k = low(nt(a, weights[1]))
    v = low(nt(a, weights[2]) + bias[1])
    o, probs = attend(q, k, v, allowed)
    branch = nt(o, weights[3]) + bias[2]
    return x + mods[2] * branch, (normed, inv, a, q, k, v, o, probs, branch)


def self_backward(dx, kept, mods, weights):
    normed, inv, a, q, k, v, o, probs, branch = kept
    dm2 = col_sum(dx * branch)
    dbr = low(dx * mods[2])
    do = low(nn(dbr, weights[3]))
    dq, dk, dv = (low(piece) for piece in attend_back(do, q, k, v, probs))
    da = nn(dq, weights[0]) + nn(dk, weights[1]) + nn(dv, weights[2])
    dm1, dm0 = col_sum(da * normed), col_sum(da)
    dx = dx + norm_back(da * (1.0 + mods[1]), normed, inv)
    return dx, (dm0, dm1, dm2), (col_sum(dq), col_sum(dv), col_sum(dbr)), (a, dq, dk, dv, o, dbr)


def feed_forward(x, mods, feed, bias_up, bias_down):
    normed, inv = norm(x)
    c = low(normed * (1.0 + mods[4]) + mods[3])
    u = nt(c, feed[0]) + bias_up
    g = low(gelu(u))
    branch = nn(g, feed[1]) + bias_down
    return x + mods[5] * branch, (normed, inv, c, u, g, branch)


def feed_backward(dx, kept, mods, feed):
    normed, inv, c, u, g, branch = kept
    dm5 = col_sum(dx * branch)
    dbr = low(dx * mods[5])
    value, slope = gelu_both(u)
    g = low(value)
    du = low(nt(dbr, feed[1]) * slope)
    dc = nn(du, feed[0])
    dm4, dm3 = col_sum(dc * normed), col_sum(dc)
    dx = dx + norm_back(dc * (1.0 + mods[4]), normed, inv)
    return dx, (dm3, dm4, dm5), (col_sum(du), col_sum(dbr)), (c, dbr, du, g)


def pair_mask(kind):
    row = lax.broadcasted_iota(jnp.int32, (256, 128), 0) % 128
    col = lax.broadcasted_iota(jnp.int32, (256, 128), 1)
    if kind == 0:
        return row // 64 == col // 64
    return row % 32 == col % 32


VEC0, EMB0, HEAD0 = 0, 45, 61


def mod_rows(mq, vec, table, clip):
    rows = []
    for r in range(6):
        at = (r % 3) * 384
        rows.append(
            mq[r // 3, pl.ds(clip, 1), at : at + 384]
            + vec[3 + r : 4 + r]
            + vec[table + r : table + r + 1]
        )
    return rows


def up_bias(vec, start):
    return jnp.concatenate([vec[start + i : start + i + 1] for i in range(4)], axis=1)


def pack_kernel(role, half, offsets, att, feed, side, vec, pa, pb, pf, pw, py, pm, wm):
    time, text, text2, head, mod = offsets
    width, per, rows = att.shape[2], pf.shape[0], py.shape[0]

    def rounded(at, size):
        return low(side[:, at : at + size])

    first = text - time
    pw[:, 0:first] = rounded(time, first)
    pw[:, first : first + width] = rounded(text2, width)
    cols = pw.shape[0]
    pw[:, first + width :] = low(jnp.concatenate(
        [jnp.transpose(vec[...]), side[:, 0:16], side[:, head : head + 16], jnp.zeros((cols, 51), f32)], axis=1
    ))
    wm[...] = rounded(mod, 6 * width)
    for r in range(2):

        @pl.when(role[0] == r)
        def _():
            pa[...] = low(att[4 * r : 4 * r + 4])
            pf[...] = low(feed[per * r : per * r + per])
            if r == 1:
                pb[...] = low(att[8:12])

    for h in range(2):

        @pl.when(half[0] == h)
        def _():
            pm[...] = rounded(mod + h * 3 * width, 3 * width)
            top = min((h + 1) * rows, cols)
            py[0 : top - h * rows, :] = low(side[h * rows : top, text : text + py.shape[1]])


def units_of(hand, lanes, width, cols):
    per = -(-cols // 2)
    unit = lax.broadcasted_iota(jnp.int32, (lanes, width), 0)
    column = lax.broadcasted_iota(jnp.int32, (lanes, width), 1)
    inside = hand * per + unit % per
    match = jnp.logical_and((unit // per) * cols + inside == column, inside < cols)
    return low(jnp.where(match, 1.0, 0.0))


def condition_kernel(rank, wt, ww, wm, vec, hid, temb, mq, y2p, errs, *, per_clip, cols):
    turned = jnp.transpose(ww[:, 1024:1152].astype(f32))
    vec[...] = turned
    feature = low(wt[:, 0:256])
    first = nt(feature, ww[:, 0:256]) + turned[1:2]
    hid[...] = first
    second = nt(low(first * jax.nn.sigmoid(first)), ww[:, 256:640]) + turned[2:3]
    temb[...] = second
    own = temb[pl.ds(pl.multiple_of(rank[0] * 8, 8), 8), :]
    mq[...] = nn(low(own * jax.nn.sigmoid(own)), wm[...])
    for h in range(2):
        y2p[h] = low(nt(ww[:, 640:1024], units_of(h, y2p.shape[2], y2p.shape[1], cols)))
    total = jnp.sum(wt[:, 256:257], axis=0, keepdims=True)
    weight = wt[pl.ds(pl.multiple_of(rank[0] * 8, 8), 8), 256:257] / (total * (per_clip * 16.0))
    errs[...] = jnp.broadcast_to(weight, errs.shape)


class Patches:
    def __init__(self, rows, first, lane0):
        place = lax.broadcasted_iota(jnp.int32, (rows, 16), 0)
        col = lax.broadcasted_iota(jnp.int32, (rows, 16), 1)
        self.pick = [low(jnp.where(col == 2 * (place % 8) + q, 1.0, 0.0)) for q in range(2)]
        place = lax.broadcasted_iota(jnp.int32, (rows, 64), 0)
        line = lax.broadcasted_iota(jnp.int32, (rows, 64), 1) % 16
        self.keep = [line == 2 * (first + place // 8) + p for p in range(2)]
        channel = lax.broadcasted_iota(jnp.int32, (64, 128), 0) // 16
        lane = lax.broadcasted_iota(jnp.int32, (64, 128), 1) - lane0
        self.put = [
            [low(jnp.where(lane == p * 8 + q * 4 + channel, 1.0, 0.0)) for q in range(2)]
            for p in range(2)
        ]

    def of(self, pieces):
        total = None
        for piece in pieces:
            for q in range(2):
                columns = nt(self.pick[q], piece)
                for p in range(2):
                    part = nn(low(jnp.where(self.keep[p], columns, 0.0)), self.put[p][q])
                    total = part if total is None else total + part
        return total


def embed_chunk(tokens, vec, pos_ref):
    places = pos_ref[...] + vec[0:1]
    return low(nn(tokens, low(vec[...])) + jnp.concatenate([places, places], axis=0))


def spatial_bias(vec):
    return (vec[11:12], vec[12:13], vec[13:14])


def residual_copies(sources, targets, sems):
    def of(chunk):
        rows = pl.ds(pl.multiple_of(chunk * 128, 128), 128)
        cuts = [lambda r: r.at[:, rows], lambda r: r.at[:, rows], lambda r: r.at[rows],
                lambda r: r.at[chunk]]
        return [
            pltpu.make_async_copy(cut(src), cut(dst), sems.at[chunk, i])
            for i, (cut, src, dst) in enumerate(zip(cuts, sources, targets))
        ]

    return of


def first_kernel(
    cols, role, half, clean, noise, pt, pos, mq, vec, wa, wf, wy, captions,
    h1, hq, gq, tok, out_b, out_f, out_u, out_p, kept_b, kept_f, kept_u, kept_p, cap, sems, ksem,
):
    @pl.when(role[0] == 1)
    def _():
        clips = captions.shape[0]
        for c in range(clips):
            pltpu.make_async_copy(captions.at[c], cap.at[c], sems.at[c]).start()
        bias = nt(low(vec[9:10]), units_of(half[0], wy.shape[0], vec.shape[1], cols))
        def layer(c, carry):
            pltpu.make_async_copy(captions.at[c], cap.at[c], sems.at[c]).wait()
            value = nt(cap[c], wy[...]) + bias
            rows = value.shape[0]
            pad = jnp.zeros((LP - rows, value.shape[1]), f32)
            hq[c] = jnp.concatenate([value, pad], axis=0)
            gq[c] = low(jnp.concatenate([gelu(value), pad], axis=0))
            return carry

        lax.fori_loop(0, clips, layer, 0)

    @pl.when(role[0] == 0)
    def _():
        allowed = pair_mask(0)
        count = h1.shape[0]
        bu = up_bias(vec, 14)
        patches = Patches(64, 0, EMB0)
        residuals = residual_copies((kept_b, kept_f, kept_u, kept_p), (out_b, out_f, out_u, out_p), ksem)

        def step(chunk, carry):
            @pl.when(chunk > 0)
            def _():
                for copy in residuals(chunk - 1):
                    copy.start()

            there = half[0] * count + chunk
            clip = there // 2
            m = mod_rows(mq, vec, 19, clip)
            mix = pt[pl.ds(clip, 1), :][:, 256:384]
            frames = []
            for f in range(2):
                frame = 2 * lax.rem(there, 2) + f
                one, two = (ref[clip, frame].reshape(64, 16) for ref in (clean, noise))
                frames.append(patches.of([low(mix[:, 1:2] * one + mix[:, 2:3] * two)]))
            tokens = low(jnp.concatenate(frames, axis=0))
            tok[pl.ds(pl.multiple_of(chunk * 128, 128), 128), :] = tokens
            h0 = embed_chunk(tokens, vec, pos)
            x1, kept = self_forward(h0.astype(f32), m, wa, spatial_bias(vec), allowed)
            x, kept_feed = feed_forward(x1, m, wf, bu, vec[18:19])
            out = low(x)
            where = pl.ds(pl.multiple_of(chunk * 128, 128), 128)
            for i, value in enumerate((h0,) + kept[3:7]):
                kept_b[i, where, :] = value
            for i, value in enumerate((x1, kept[8], kept_feed[5])):
                kept_f[i, where, :] = value
            kept_u[where, :] = kept_feed[3]
            for pair in range(3):
                kept_p[chunk, pair] = kept[7][pair]
            for frame in range(2):
                for part in range(2):
                    start = frame * 64 + part * 32
                    h1[chunk, part, frame * 32 : frame * 32 + 32, :] = out[start : start + 32]
            return carry

        lax.fori_loop(0, count, step, 0)
        for copy in residuals(count - 1):
            copy.start()
        for chunk in range(count):
            for copy in residuals(chunk):
                copy.wait()


def last_kernel(
    role, half, tok, mq, vec, wa, wb, wf, in_b, in_f, in_u, in_p, dh, dkv, extra, grads_t, dmod_t,
    acts, actf, actw, dkvb, dy, vect, dmod, grads, kept_b, kept_f, kept_u, kept_p, ksem,
):
    @pl.when(role[0] == 0)
    def _():
        grads[...] = jnp.zeros_like(grads)
        dmod[...] = jnp.zeros_like(dmod)
        count = dh.shape[0]
        residuals = residual_copies((in_b, in_f, in_u, in_p), (kept_b, kept_f, kept_u, kept_p), ksem)
        for chunk in range(count):
            for copy in residuals(chunk):
                copy.start()

        def step(chunk, carry):
            for copy in residuals(chunk):
                copy.wait()
            m = mod_rows(mq, vec, 19, (half[0] * count + chunk) // 2)
            where = pl.ds(pl.multiple_of(chunk * 128, 128), 128)
            tokens = tok[where, :]
            h0, q, k, v, o = (kept_b[i, where, :] for i in range(5))
            x1, branch, branch_f = (kept_f[i, where, :] for i in range(3))
            normed, inv = norm(h0.astype(f32))
            a = low(normed * (1.0 + m[1]) + m[0])
            probs = [kept_p[chunk, pair] for pair in range(3)]
            kept = (normed, inv, a, q, k, v, o, probs, branch)
            normed_f, inv_f = norm(x1)
            c = low(normed_f * (1.0 + m[4]) + m[3])
            kept_feed = (normed_f, inv_f, c, kept_u[where, :], None, branch_f)
            parts = []
            for frame in range(2):
                for part in range(2):
                    parts.append(dh[chunk, part, frame * 32 : frame * 32 + 32, :])
            dx = jnp.concatenate(parts, axis=0).astype(f32)
            dx, dm_f, db_f, act_f = feed_backward(dx, kept_feed, m, wf)
            dx, dm_a, db_a, act_a = self_backward(dx, kept, m, wa)
            dh0 = low(dx)
            for i, value in enumerate(act_a):
                acts[i, where, :] = value
            for i in range(2):
                actf[i, where, :] = act_f[i]
                actw[i, where, :] = act_f[2 + i]
            mods = dm_a + dm_f
            dmod[chunk, 0:6, :] = jnp.concatenate(mods, axis=0)
            grads[...] += tn(tokens, dh0)
            grads[0:1] += col_sum(dh0)
            for i in range(3):
                grads[11 + i : 12 + i] += db_a[i]
            for i in range(4):
                grads[14 + i : 15 + i] += db_f[0][:, i * 384 : i * 384 + 384]
            grads[18:19] += db_f[1]
            for i in range(6):
                grads[19 + i : 20 + i] += mods[i]
            return carry

        lax.fori_loop(0, count, step, 0)

    @pl.when(role[0] == 1)
    def _():
        grads[...] = grads_t[...]
        dmod[...] = dmod_t[...]
        dy[...] = jnp.zeros_like(dy)
        dkvb[...] = jnp.zeros_like(dkvb)
        ncl = dy.shape[0]
        for c in range(ncl):

            @pl.when(jnp.logical_or(half[0] == 0, c > 0))
            def _():
                pieces = []
                for i in range(2):
                    value = dkv[i, c]
                    if c == ncl - 1:
                        value = value + jnp.where(half[0] == 0, extra[i], 0.0)
                    pieces.append(low(value))
                dkvb[0, c], dkvb[1, c] = pieces
                back = low(nn(pieces[0], wb[1]) + nn(pieces[1], wb[2]))
                dy[c] = back
                grads[40:41] += col_sum(pieces[1])
                grads[10:11] += col_sum(back)

    vect[...] = jnp.transpose(grads[...])


def temporal_kernel(
    role, half, rank, lens, errw, h1, timing, mq, vec, temb, wa, wb, wf, gq, rgq, y2p, noise,
    dh1, acts, actf, actw, ybuf, dkv, grads, dmod, loss, kx, vx,
):
    @pl.when(role[0] == 0)
    def _():
        loss[...] = jnp.zeros_like(loss)

    @pl.when(role[0] == 1)
    def _():
        allowed = pair_mask(1)
        count = h1.shape[0]
        ncl = ybuf.shape[0]
        for ref in (kx, vx, dkv, grads, loss):
            ref[...] = jnp.zeros_like(ref)
        first_clip = (half[0] * count) // 2

        def features(c, carry):
            clip = jnp.minimum(first_clip + c, gq.shape[0] - 1)
            y = nt(gq[clip], y2p[half[0]]) + nt(rgq[clip], y2p[1 - half[0]])
            y = low(y + vec[10:11])
            ybuf[c] = y
            kx[c, 0:LP, :] = low(nt(y, wb[1]))
            vx[c, 0:LP, :] = low(nt(y, wb[2]) + vec[40:41])
            return carry

        lax.fori_loop(0, ncl, features, 0)
        bu = up_bias(vec, 28)
        lane = lax.broadcasted_iota(jnp.int32, (1, 128), 1)
        real = jnp.logical_and(lane >= HEAD0, lane < HEAD0 + 16)
        bias_h = pltpu.roll(jnp.broadcast_to(vec[44:45, 0:128], (8, 128)), HEAD0, 1)[0:1]
        head = low(vec[...])

        def step(chunk, carry):
            clip = (half[0] * count + chunk) // 2
            here = clip - first_clip
            m = mod_rows(mq, vec, 33, clip)
            emb = temb[pl.ds(rank[0] * 8 + clip, 1), :]
            m6, m7 = vec[42:43] + emb, vec[43:44] + emb
            h = jnp.concatenate([h1[chunk, 0], h1[chunk, 1]], axis=0)
            x = h.astype(f32) + jnp.concatenate(
                [jnp.broadcast_to(timing[i : i + 1], (32, h.shape[1])) for i in range(4)], axis=0
            )
            x, kept = self_forward(x, m, wa, (vec[25:26], vec[26:27], vec[27:28]), allowed)
            xb = low(x)
            cq = low(nt(xb, wb[0]) + vec[39:40])
            keys, values = kx[here], vx[here]
            seen = lax.broadcasted_iota(jnp.int32, (1, KP), 1) < lens[clip]
            co, probs = attend(cq, keys, values, seen)
            x = x + (nt(co, wb[3]) + vec[41:42])
            x, kept_f = feed_forward(x, m, wf, bu, vec[32:33])
            h2 = low(x).astype(f32)
            normed, inv = norm(h2)
            cf = low(normed * (1.0 + m7) + m6)
            where = pl.ds(pl.multiple_of(chunk * 128, 128), 128)
            patches = Patches(32, 4 * lax.rem(half[0] * count + chunk, 2), HEAD0)
            target = jnp.concatenate(
                [
                    patches.of(three(noise[clip, frame].reshape(64, 16)))
                    for frame in range(noise.shape[1])
                ],
                axis=0,
            )
            diff = jnp.where(real, nt(cf, head) + bias_h - target, 0.0)
            scale = errw[pl.ds(clip, 1), 0:1]
            loss[...] += col_sum(diff * diff) * scale
            dpred = low(diff * (2.0 * scale))
            dcf = nn(dpred, head)
            grads[...] += tn(dpred, cf)
            dbh = pltpu.roll(jnp.broadcast_to(col_sum(dpred), (8, 128)), 128 - HEAD0, 1)[0:1]
            grads[44:45, 0:128] += dbh
            dm7, dm6 = col_sum(dcf * normed), col_sum(dcf)
            dx = low(norm_back(dcf * (1.0 + m7), normed, inv)).astype(f32)
            dx, dm_f, db_f, act_f = feed_backward(dx, kept_f, m, wf)
            dcbr = low(dx)
            dco = low(nn(dcbr, wb[3]))
            dcq, dck, dcv = attend_back(dco, cq, keys, values, probs)
            dcq = low(dcq)
            dkv[0, here] += dck[0:LP]
            dkv[1, here] += dcv[0:LP]
            dx = dx + nn(dcq, wb[0])
            dx, dm_a, db_a, act_a = self_backward(dx, kept, m, wa)
            out = low(dx)
            dh1[chunk, 0] = out[0:64]
            dh1[chunk, 1] = out[64:128]
            for i, value in enumerate(act_a + (xb, dcq, co, dcbr)):
                acts[i, where, :] = value
            for i in range(2):
                actf[i, where, :] = act_f[i]
                actw[i, where, :] = act_f[2 + i]
            mods = dm_a + dm_f + (dm6, dm7)
            dmod[chunk] = jnp.concatenate(mods, axis=0)
            for i in range(3):
                grads[25 + i : 26 + i] += db_a[i]
            for i in range(4):
                grads[28 + i : 29 + i] += db_f[0][:, i * 384 : i * 384 + 384]
            grads[32:33] += db_f[1]
            for i in range(6):
                grads[33 + i : 34 + i] += mods[i]
            grads[39:40] += col_sum(dcq)
            grads[41:42] += col_sum(dcbr)
            grads[42:43] += dm6
            grads[43:44] += dm7
            return carry

        lax.fori_loop(0, count, step, 0)


def weight_grad_kernel(
    role, half, rank, acts_s, acts_t, racts, actf_s, actf_t, ractf, actw_s, actw_t, ractw,
    ybuf, rybuf, dkvb, rdkvb, dy, rdy, gq, rgq, hq, y2p, captions,
    own, snd, text_out, la, lf, lw, cap, square, turned, sums, sems,
):
    tokens = acts_s.shape[1]
    line, cols = own.shape[1], own.shape[2]
    odd = lax.rem(rank[0], 2) == 1
    near, far = pl.ds(0, tokens), pl.ds(tokens, tokens)

    def copies(r, h):
        if h == 0:
            local = acts_s if r == 0 else acts_t
            size = pl.ds(0, local.shape[0])
            return [(local, la.at[size, near], 0), (racts.at[size], la.at[size, far], 1)]
        thin, wide = ((actf_s, actw_s), (actf_t, actw_t))[r]
        return [
            (thin, lf.at[:, near], 0), (ractf, lf.at[:, far], 1),
            (wide, lw.at[:, near], 2), (ractw, lw.at[:, far], 3),
        ]

    def text():
        return [(captions.at[c], cap.at[c], 4 + c) for c in range(captions.shape[0])]

    def run(group, finish):
        for src, dst, i in group:
            copy = pltpu.make_async_copy(src, dst, sems.at[i])
            copy.wait() if finish else copy.start()

    for r in range(2):
        for h in range(2):

            @pl.when(jnp.logical_and(role[0] == r, half[0] == h))
            def _():
                run(copies(r, h), False)
                if r == 1:
                    run(text(), False)
                run(copies(r, h), True)

    def keep(unit, at, first, second):
        own[unit, at] = jnp.where(odd, second, first)
        snd[unit, at] = low(jnp.where(odd, first, second))

    def keep_square(unit, value):
        for p in range(line):
            cut = 2 * p * cols
            keep(unit, p, value[cut : cut + cols], value[cut + cols : cut + 2 * cols])

    def matrix(unit, left, right):
        keep_square(unit, tn(la[left], la[right]))

    @pl.when(half[0] == 0)
    def _():
        def square(i, carry):
            left = jnp.where(i < 3, i + 1, 2 * i - 1)
            right = jnp.where(i < 3, 0, 2 * i - 2)
            matrix(jnp.where(i < 5, i, 7), left, right)
            return carry

        lax.fori_loop(0, 4 + 2 * role[0], square, 0)

        @pl.when(role[0] == 1)
        def _():
            def cross(i, carry):
                total = tn(dkvb[i, 0], ybuf[0]) + tn(rdkvb[i, 0], rybuf[0])
                for c in range(1, ybuf.shape[0]):
                    total = total + tn(dkvb[i, c], ybuf[c]) + tn(rdkvb[i, c], rybuf[c])
                keep_square(5 + i, total)
                return carry

            lax.fori_loop(0, 2, cross, 0)

    @pl.when(half[0] == 1)
    def _():
        side = la.shape[2]
        tiles = lw.shape[2] // side
        block = 4 * cols
        per = side // (2 * block)

        def feed(i, carry):
            pair, tile = i // tiles, lax.rem(i, tiles)
            lanes = pl.ds(pl.multiple_of(tile * side, 128), side)
            value = tn(lw[pair, :, lanes], lf[pair])
            for p in range(per):
                for j in range(4):
                    at = 2 * p * block + j * cols
                    keep(
                        4 * pair + j, tile * per + p, value[at : at + cols],
                        value[at + block : at + block + cols],
                    )
            return carry

        lax.fori_loop(0, 2 * tiles, feed, 0)

    @pl.when(role[0] == 1)
    def _():
        clips = captions.shape[0]
        rows = captions.shape[1]
        def dy_of(c):
            h = (2 * c) // clips
            at = c - (h * clips) // 2
            return jnp.where(half[0] == h, dy[at].astype(f32), rdy[at].astype(f32)).astype(bf16)

        @pl.when(half[0] == 1)
        def _():
            shape = (y2p.shape[2], y2p.shape[1], cols)
            mine, theirs = units_of(1, *shape), units_of(0, *shape)
            square[...] = jnp.zeros_like(square)

            def one(c, carry):
                plain = low(nn(gq[c], mine) + nn(rgq[c], theirs))
                square[...] += tn(dy_of(c), plain)
                return carry

            lax.fori_loop(0, clips, one, 0)
            keep_square(8, square[...])

        units = text_out.shape[2]

        def keep_text(lanes, value):
            for p in range(line):
                for q in range(2):
                    cut = (2 * p + q) * units
                    text_out[p, q, :, lanes] = low(value[cut : cut + units])

        ones = jnp.ones((LP, 128), bf16)
        sums[...] = jnp.zeros_like(sums)

        def turn(c, carry):
            back = nn(dy_of(c), y2p[half[0]]) * gelu_both(hq[c])[1]
            turned[c] = low(jnp.transpose(back))
            sums[...] += nn(turned[c], ones)
            return carry

        lax.fori_loop(0, clips, turn, 0)
        run(text(), True)

        def text_tile(t, carry):
            lanes = pl.ds(pl.multiple_of(t * 512, 512), 512)
            total = nn(turned[0, :, 0:rows], cap[0, :, lanes])
            for c in range(1, clips):
                total = total + nn(turned[c, :, 0:rows], cap[c, :, lanes])
            keep_text(lanes, total)
            return carry

        lax.fori_loop(0, captions.shape[2] // 512, text_tile, 0)
        keep_text(pl.ds(captions.shape[2], 128), sums[...])


def halves(value):
    first = low(value)
    return first, low(value - first.astype(f32))


def lefts(value, axis=1):
    first, second = halves(value)
    return jnp.concatenate([first, first, second], axis=axis)


def rights(value, axis=0):
    first, second = halves(value)
    return jnp.concatenate([first, second, first], axis=axis)


def gram_of(value, dot):
    first, second = halves(value)
    both = dot(first, first), dot(first, second)
    return both[0] + (both[1] + jnp.transpose(both[1]))


def muon_kernel(half, ua, uf, xa, xf, gram, whole):
    @pl.when(half[0] == 0)
    def _():
        u = ua[...]
        whole[...] = u / (jnp.sqrt(jnp.sum(u * u)) + 1e-07)

        def sweep(i, carry):
            x = whole[...]
            square = gram_of(x, nt)
            poly = coef_b * square + coef_c * gram_of(square, nt)
            whole[...] = coef_a * x + nn(lefts(poly), rights(x))
            return carry

        lax.fori_loop(0, 5, sweep, 0)
        xa[...] = low(whole[...])

    @pl.when(half[0] == 1)
    def _():
        width = uf.shape[1]
        tiles = uf.shape[0] // width
        gram[...] = jnp.zeros_like(gram)

        def rows(t):
            return pl.ds(pl.multiple_of(t * width, 128), width)

        def first(t, carry):
            piece = uf[rows(t), :]
            gram[...] += gram_of(piece, tn)
            return carry

        lax.fori_loop(0, tiles, first, 0)
        row = lax.broadcasted_iota(jnp.int32, (width, width), 0)
        col = lax.broadcasted_iota(jnp.int32, (width, width), 1)
        eye = jnp.where(row == col, 1.0, 0.0)
        start = gram[...]
        inv = 1.0 / (jnp.sqrt(jnp.sum(start * eye)) + 1e-07)
        gram[...] = start * (inv * inv)
        whole[...] = eye * inv

        def poly_of(a):
            return coef_a * eye + coef_b * a + coef_c * nn(lefts(a), rights(a))

        def sweep(i, carry):
            a = gram[...]
            left = lefts(poly_of(a))
            both = nn(left, rights(jnp.concatenate([a, whole[...]], axis=1)))
            whole[...] = both[:, width:]
            gram[...] = nn(left, rights(both[:, :width]))
            return carry

        lax.fori_loop(0, 4, sweep, 0)
        last = rights(nn(lefts(poly_of(gram[...])), rights(whole[...])))

        def apply(t, carry):
            xf[rows(t), :] = low(nn(lefts(uf[rows(t), :]), last))
            return carry

        lax.fori_loop(0, tiles, apply, 0)


def local_call(kernel, out_shape, in_specs, args, scratch=(), out_specs=None):
    return pl.pallas_call(
        kernel,
        out_shape=out_shape,
        in_specs=in_specs,
        out_specs=jax.tree.map(lambda _: VM, out_shape) if out_specs is None else out_specs,
        scratch_shapes=scratch,
        compiler_params=pltpu.CompilerParams(vmem_limit_bytes=VMEM_LIMIT),
    )(*args)


def here():
    return lax.axis_index("dp"), lax.axis_index("segment")


def dev(d, s):
    return {"dp": d, "segment": s}


def remote(src, dst, send, recv, target):
    return pltpu.make_async_remote_copy(
        src_ref=src, dst_ref=dst, send_sem=send, recv_sem=recv, device_id=target,
        device_id_type=MESH,
    )


def greet(targets):
    barrier = pltpu.get_barrier_semaphore()
    for target in targets:
        pl.semaphore_signal(barrier, inc=1, device_id=target, device_id_type=MESH)
    pl.semaphore_wait(barrier, len(targets))


def greet_dp(n, extra=()):
    d, s = here()
    barrier = pltpu.get_barrier_semaphore()

    def step(k, carry):
        pl.semaphore_signal(
            barrier, inc=1, device_id=dev(lax.rem(d + k, n), s), device_id_type=MESH
        )
        return carry

    lax.fori_loop(1, n, step, 0)
    for target in extra:
        pl.semaphore_signal(barrier, inc=1, device_id=target, device_id_type=MESH)
    pl.semaphore_wait(barrier, n - 1 + len(extra))


def comm_call(kernel, cid, args, out_shape, sems, out_specs=None, scratch=(), in_specs=None):
    if out_specs is None:
        out_specs = jax.tree.map(lambda _: ANY, out_shape)
    return pl.pallas_call(
        kernel,
        out_shape=out_shape,
        in_specs=[ANY] * len(args) if in_specs is None else in_specs,
        out_specs=out_specs,
        scratch_shapes=list(scratch) + [pltpu.SemaphoreType.DMA(shape) for shape in sems],
        compiler_params=pltpu.CompilerParams(
            collective_id=cid, has_side_effects=True, vmem_limit_bytes=VMEM_LIMIT
        ),
    )(*args)


ACROSS_FIRST = (2, 5)


def gather_kernel(n, pa, pb, pf, pw, py, pm, pt, wa, wb, wf, ww, wy, wm, wt,
                  send, recv, crecv, own):
    pair = 2 if n % 2 == 0 else 1
    line = n // pair
    d, s = here()
    role, half = s // 2, lax.rem(s, 2)
    a, x = d // pair, lax.rem(d, pair)
    mate = dev(d, role * 2 + 1 - half)
    above, below = dev(d + pair, s), dev(d - pair, s)
    across = dev(a * pair + (pair - 1 - x), s)
    barrier = pltpu.get_barrier_semaphore()

    def signal(target):
        pl.semaphore_signal(barrier, inc=1, device_id=target, device_id_type=MESH)

    signal(mate)
    if pair == 2:
        signal(across)

    @pl.when(a < line - 1)
    def _():
        signal(above)

    @pl.when(a > 0)
    def _():
        signal(below)

    pl.semaphore_wait(barrier, pair + jnp.minimum(a, 1) + jnp.minimum(line - 1 - a, 1))

    def two(i, ref, out):
        return [
            (i, ref.at[pl.ds(0, 2)], out.at[pl.ds(0, 2)], 2),
            (i + 1, ref.at[pl.ds(2, 2)], out.at[pl.ds(2, 2)], 2),
        ]

    first, last = half == 0, role == 1
    both = jnp.logical_and(first, last)
    shared = [((2, pw, ww, 0), first, True)]
    shared += [(item, first, True) for item in two(0, pa, wa)]
    shared += [(item, both, last) for item in two(5, pb, wb)]
    for m in range(2):
        item = (m, pf.at[pl.ds(m, 1)], wf.at[pl.ds(m, 1)], 1)
        shared.append((item, jnp.logical_not(first), True))
    alone = [((3, pt, wt, 0), True), ((4, pm, wm, 0), role == 0), ((4, py, wy, 0), role == 1)]
    parts = [(item, when, True) for item, when, _ in shared]
    parts += [(item, when, False) for item, when in alone]

    def slot(ref, lead, o):
        return ref.at[:, o] if lead else ref.at[o]

    def given(when, act):
        if when is True:
            act()
        else:
            pl.when(when)(act)

    def move(item, way, o, target, is_own=False):
        i, src, dst, lead = item
        there = slot(dst, lead, o)
        sem = crecv if way == 3 else recv
        return remote(src if is_own else there, there, send.at[way, i, o], sem.at[i, o], target)

    def forward(o, up, down, side, wait, ways=None):
        is_own = not wait
        for item, when, common in parts:

            def act(item=item, common=common, up=up, down=down, side=side):
                if item[0] in ACROSS_FIRST and pair == 2:
                    side = is_own
                    up, down = (up, down) if ways is None else ways
                if wait:
                    move(item, 0, o, across).wait_recv()

                def go(way, target):
                    move(item, way, o, target, is_own).start()

                if side and pair == 2:
                    go(2, across)
                if up is not None:
                    pl.when(up)(functools.partial(go, 0, above))
                if down is not None:
                    pl.when(down)(functools.partial(go, 1, below))
                if common:
                    go(3, mate)

            given(when, act)

    def keep(finish):
        for item, when, common in parts:

            def act(item=item):
                i, src, dst, lead = item
                copy = pltpu.make_async_copy(src, slot(dst, lead, d), own.at[i])
                copy.wait() if finish else copy.start()

            given(when, act)

    forward(d, a < line - 1, a > 0, True, False)
    keep(False)
    other = pair - 1 - x

    def sweep():
        def step(k, carry):
            @pl.when(a - k >= 0)
            def _():
                forward((a - k) * pair + x, a < line - 1, None, True, True)

            @pl.when(a + k < line)
            def _():
                forward((a + k) * pair + x, None, a > 0, True, True)

            if pair == 2:

                def from_side(o, up, down):
                    forward(o * pair + other, None, None, False, True, (up, down))

                @pl.when(a - (k - 1) >= 0)
                def _():
                    from_side(
                        a - (k - 1), a < line - 1, jnp.logical_and(k == 1, a > 0)
                    )

                @pl.when(jnp.logical_and(k > 1, a + (k - 1) < line))
                def _():
                    from_side(a + (k - 1), None, a > 0)

            return carry

        lax.fori_loop(1, line + 1, step, 0)

    sweep()

    def drain(o, carry):
        there, column = o // pair, lax.rem(o, pair)
        mine = column == x
        up = jnp.logical_and(there <= a, a < line - 1)
        down = jnp.logical_and(there >= a, a > 0)
        for item, when, common in parts:

            def act(item=item, common=common):
                lines_first = item[0] not in ACROSS_FIRST or pair == 1
                sent = (
                    (0, jnp.logical_and(mine, up) if lines_first else up, above),
                    (1, jnp.logical_and(mine, down) if lines_first else down, below),
                    (2, mine if lines_first else o == d, across),
                )
                for way, yes, target in sent:
                    if way == 2 and pair == 1:
                        continue
                    pl.when(yes)(lambda: move(item, way, o, target).wait_send())
                if common:
                    move(item, 3, o, mate).wait_send()

            given(when, act)
        return carry

    lax.fori_loop(0, n, drain, 0)
    keep(True)

    def collect(o, carry):
        for item, when, arrives in shared:
            mine = when if when is not both else first

            def act(item=item):
                i, src, dst, lead = item
                there = slot(dst, lead, o)
                remote(there, there, send.at[3, i, o], crecv.at[i, o], mate).wait_recv()

            given(jnp.logical_and(jnp.logical_not(mine), arrives), act)
        return carry

    lax.fori_loop(0, n, collect, 0)


def mate_kernel(src, dst, send, recv, own):
    d, s = here()
    role, half = s // 2, lax.rem(s, 2)
    mate = dev(d, role * 2 + 1 - half)

    @pl.when(role == 0)
    def _():
        greet([mate])
        pltpu.make_async_copy(src, dst.at[half], own.at[0]).start()
        remote(src, dst.at[half], send.at[0], recv.at[0], mate).start()
        pltpu.make_async_copy(src, dst.at[half], own.at[0]).wait()
        remote(src, dst.at[1 - half], send.at[0], recv.at[0], mate).wait()


def forward_kernel(count, h1s, gq, mq, h1t, gqs, mqt, send, recv, msend, mrecv, qsend, qrecv):
    relay_half_clips(
        count, 0, h1s, h1t, send, recv, swap=(gq, gqs, msend, mrecv), rows=(mq, mqt, qsend, qrecv)
    )


def relay_half_clips(count, from_role, src, dst, send, recv, extra=None, swap=None, rows=None):
    d, s = here()
    role, half = s // 2, lax.rem(s, 2)
    peers = [dev(d, (1 - role) * 2), dev(d, (1 - role) * 2 + 1)]
    mate = dev(d, role * 2 + 1 - half)
    peers.append(mate)
    greet(peers)

    def unit(i, part):
        there = half * count + i
        clip, own = there // 2, lax.rem(there, 2)
        other = 2 * clip + part
        return own, other // count, lax.rem(other, count)

    def copy(i, part):
        own, to, slot = unit(i, part)
        return remote(
            src.at[i, part], dst.at[slot, own], send.at[i, part], recv.at[slot, own],
            dev(d, (1 - from_role) * 2 + to),
        )

    def row_copy(to, finish):
        value, there, qsend, qrecv = rows
        copy = remote(value, there, qsend.at[to], qrecv.at[half], dev(d, (1 - from_role) * 2 + to))
        copy.wait_send() if finish else copy.start()

    def row_sends(finish):
        if rows is None:
            return

        @pl.when(role == from_role)
        def _():
            for to in range(2):
                pl.when(half == to)(functools.partial(row_copy, to, finish))

    @pl.when(role == from_role)
    def _():
        crossing = [(count - 1, 1), (0, 0)]
        rest = [(i, part) for i in range(count) for part in range(2)]
        for i, part in crossing + [unit_ for unit_ in rest if unit_ not in crossing]:
            copy(i, part).start()

    row_sends(False)
    if swap is not None:
        mine, both, msend, mrecv = swap

        @pl.when(role == 1)
        def _():
            remote(mine, both, msend.at[0], mrecv.at[0], mate).start()

    if extra is not None:
        own_src, own_dst, esend, erecv = extra

        @pl.when(jnp.logical_and(role == 1, half == 1))
        def _():
            remote(own_src, own_dst, esend.at[0], erecv.at[0], dev(d, 2)).start()

    @pl.when(role == from_role)
    def _():
        for i in range(count):
            for part in range(2):
                copy(i, part).wait_send()

    @pl.when(role == 1 - from_role)
    def _():
        for i in range(count):
            for part in range(2):
                remote(
                    src.at[i, part], dst.at[i, part], send.at[i, part], recv.at[i, part],
                    dev(d, from_role * 2),
                ).wait_recv()

    row_sends(True)
    if rows is not None:
        value, there, qsend, qrecv = rows

        @pl.when(role == 1 - from_role)
        def _():
            remote(value, there, qsend.at[0], qrecv.at[half], mate).wait_recv()

    if swap is not None:

        @pl.when(role == 1)
        def _():
            remote(mine, both, msend.at[0], mrecv.at[0], mate).wait()

    if extra is not None:

        @pl.when(jnp.logical_and(role == 1, half == 1))
        def _():
            remote(own_src, own_dst, esend.at[0], erecv.at[0], dev(d, 2)).wait_send()

        @pl.when(jnp.logical_and(role == 1, half == 0))
        def _():
            remote(own_src, own_dst, esend.at[0], erecv.at[0], dev(d, 2)).wait_recv()


def backward_kernel(count, dh1, dkv, dhs, extra, send, recv, esend, erecv):
    relay_half_clips(count, 1, dh1, dhs, send, recv, extra=(dkv.at[:, 0], extra, esend, erecv))


def swap_kernel(acts_s, acts_t, actf_s, actf_t, actw_s, actw_t, ybuf, dkvb, dy, dmod,
                racts, ractf, ractw, rybuf, rdkvb, rdy, rdmod, send, recv):
    d, s = here()
    role, half = s // 2, lax.rem(s, 2)
    mate = dev(d, role * 2 + 1 - half)
    greet([mate])
    six = acts_s.shape[0]
    gives = {
        (0, 0): [(0, actf_s, ractf), (1, actw_s, ractw), (4, dmod, rdmod)],
        (0, 1): [(0, acts_s, racts.at[pl.ds(0, six)]), (4, dmod, rdmod)],
        (1, 0): [(0, actf_t, ractf), (1, actw_t, ractw), (2, dy, rdy), (4, dmod, rdmod)],
        (1, 1): [
            (0, acts_t, racts), (1, ybuf, rybuf), (3, dkvb, rdkvb), (2, dy, rdy), (4, dmod, rdmod)
        ],
    }
    for (r, h), mine in gives.items():

        @pl.when(jnp.logical_and(role == r, half == h))
        def _():
            for i, src, dst in mine:
                remote(src, dst, send.at[i], recv.at[i], mate).start()
            for i, src, dst in mine:
                remote(src, dst, send.at[i], recv.at[i], mate).wait_send()
            for i, src, dst in gives[(r, 1 - h)]:
                remote(src, dst, send.at[i], recv.at[i], mate).wait_recv()


TEXT_CUTS = 11


def scatter_kernel(n, own_in, snd, text_in, vec, dmod, rdmod, loss, wm, temb, ww, hid, wt,
                   summed, text, vsum, squares, gm, g2, g1,
                   own, rx, up, down, sx, rz, tin, trx, tsx, trz, rv, rm, dtembs, dm, dmt,
                   osem, send1, recv1, send2, recv2, usend, urecv, dsend, drecv,
                   ssend, srecv, sown, tsend, trecv, esend, erecv, psend, precv):
    line = n // 2
    d, s = here()
    role, half = s // 2, lax.rem(s, 2)
    a, x = d // 2, lax.rem(d, 2)
    across = dev(a * 2 + 1 - x, s)
    other = dev(d, (1 - role) * 2 + half)
    count = 8 - 4 * (1 - role) * (1 - half)
    greet_dp(n, [other])
    squares[...] = jnp.zeros_like(squares)
    squares[1:2, 0:128] = loss[...]
    step = text.shape[1] // TEXT_CUTS
    is_text, is_last, is_time = role == 0, s == 3, s == 0
    clip_rows = dm.shape[0]

    def clip_sums():
        clips = dmod.shape[0]
        sources = (dmod, rdmod)
        for clip in range(clips):
            total = None
            for h in range(2):
                for i in range(clips):
                    if (h * clips + i) // 2 == clip:
                        part = sources[h][i]
                        total = part if total is None else total + part
            dm[8 * clip : 8 * clip + 8] = total

    pl.when(half == 0)(clip_sums)
    partial = remote(dm, dmt, psend.at[0], precv.at[0], other)

    def first_copies(u):
        return (
            remote(snd.at[u], rx.at[u], send1.at[u], recv1.at[u], across),
            pltpu.make_async_copy(own_in.at[u], own.at[u], osem.at[u]),
        )

    def text_hop(k):
        lanes = pl.ds(pl.multiple_of(k * step, 128), step)
        return remote(text_in.at[:, :, :, lanes], tin.at[k], tsend.at[k], trecv.at[k], other)

    def text_across(k):
        return remote(tin.at[k, :, 1 - x], trx.at[k], send1.at[9 + k], recv1.at[9 + k], across)

    def begin(u, carry):
        for copy in first_copies(u):
            copy.start()
        return carry

    def rows_at(o):
        return rm.at[pl.ds(pl.multiple_of(o * clip_rows, 8), clip_rows)]

    def small(i, finish):
        src, dst = (
            (lambda p: vec.at[p], lambda o: rv.at[o]) if i else (lambda p: dm, rows_at)
        )

        def each(k, carry):
            to, o = lax.rem(d + k, n), lax.rem(d + n - k, n)
            if finish:
                remote(src(o), dst(o), ssend.at[i, k], srecv.at[i, k], dev(o, s)).wait()
            else:
                remote(src(to), dst(d), ssend.at[i, k], srecv.at[i, k], dev(to, s)).start()
            return carry

        lax.fori_loop(1, n, each, 0)
        copy = pltpu.make_async_copy(src(d), dst(d), sown.at[i])
        copy.wait() if finish else copy.start()

    lax.fori_loop(0, 1, begin, 0)
    small(1, False)

    @pl.when(is_time)
    def _():
        partial.wait_recv()
        dm[...] = dm[...] + dmt[...]

    lax.fori_loop(1, count, begin, 0)

    @pl.when(is_last)
    def _():
        begin(8, 0)

    @pl.when(role == 1)
    def _():
        pl.when(half == 0)(lambda: partial.start())
        lax.fori_loop(0, TEXT_CUTS, lambda k, c: (text_hop(k).start(), c)[1], 0)

    def embeds(finish):
        def each(k, carry):
            to, o = lax.rem(d + k, n), lax.rem(d + n - k, n)
            if finish:
                remote(dtembs.at[o], dtembs.at[o], esend.at[k], erecv.at[k], dev(o, s)).wait()
            else:
                remote(dtembs.at[d], dtembs.at[d], esend.at[k], erecv.at[k], dev(to, s)).start()
            return carry

        lax.fori_loop(1, n, each, 0)

    def upward(u, p):
        return remote(up.at[u, p], up.at[u, p], usend.at[u, p], urecv.at[u, p], dev(d + 2, s))

    def downward(u, p):
        return remote(
            down.at[u, p], down.at[u, p], dsend.at[u, p], drecv.at[u, p], dev(d - 2, s)
        )

    def along_up(u):
        def add(i, carry):
            p = line - 1 - i

            @pl.when(a == 0)
            def _():
                up[u, p] = own[u, p]

            @pl.when(a > 0)
            def _():
                upward(u, p).wait_recv()
                up[u, p] = up[u, p] + own[u, p]

            return carry

        def send(i, carry):
            upward(u, line - 1 - i).start()
            return carry

        lax.fori_loop(0, line - 1 - a, add, 0)
        lax.fori_loop(0, line - 1 - a, send, 0)

    def along_down(u):
        def add(p, carry):
            @pl.when(a == line - 1)
            def _():
                down[u, p] = own[u, p]

            @pl.when(a < line - 1)
            def _():
                downward(u, p).wait_recv()
                down[u, p] = down[u, p] + own[u, p]

            return carry

        def send(p, carry):
            downward(u, p).start()
            return carry

        lax.fori_loop(0, a, add, 0)
        lax.fori_loop(0, a, send, 0)

    def pairs(u):
        for copy in first_copies(u):
            copy.wait()
        own[u] = own[u] + rx[u].astype(f32)

    def direct(i, total, line_in, finish):
        def each(k, carry):
            to, o = lax.rem(a + k, line), lax.rem(a + line - k, line)
            if finish:
                remote(
                    total.at[o], line_in.at[o], send2.at[i, k], recv2.at[i, k], dev(o * 2 + x, s)
                ).wait()
            else:
                remote(
                    total.at[to], line_in.at[a], send2.at[i, k], recv2.at[i, k],
                    dev(to * 2 + x, s),
                ).start()
            return carry

        lax.fori_loop(1, line, each, 0)

    def round_trip(i, carry):
        @pl.when(i < count)
        def _():
            pairs(i)

        pl.when(jnp.logical_and(is_time, i == 0))(lambda: small(0, False))

        @pl.when(jnp.logical_and(is_time, i == 1))
        def _():
            small(0, True)
            time_back([d], rm, wm, temb, dtembs.at[d])

        pl.when(jnp.logical_and(is_time, i == 2))(lambda: embeds(False))

        @pl.when(is_text)
        def _():
            def cut_at(delay, act):
                for j in range(2):
                    k = 2 * (i - delay) + j
                    pl.when(jnp.logical_and(k >= 0, k < TEXT_CUTS))(functools.partial(act, k))

            def arrive(k):
                text_hop(k).wait_recv()
                text_across(k).start()

            def add(k):
                text_across(k).wait()
                tsx[k] = low(tin[k, :, x].astype(f32) + trx[k].astype(f32))

            cut_at(5, lambda k: direct(k, tsx.at[k], trz.at[k], False))
            cut_at(3, arrive)
            cut_at(4, add)

        k = i - count

        @pl.when(jnp.logical_and(is_last, k == 0))
        def _():
            pairs(8)
            sx[...] = low(own[8])

        @pl.when(jnp.logical_and(is_last, k == 1))
        def _():
            direct(TEXT_CUTS, sx, rz, False)

        later = i - 1 - a

        @pl.when(jnp.logical_and(later >= 0, later < count))
        def _():
            along_up(later)

        other = i - line + a

        @pl.when(jnp.logical_and(other >= 0, other < count))
        def _():
            along_down(other)

        return carry

    lax.fori_loop(0, jnp.maximum(count + line, TEXT_CUTS // 2 + 6), round_trip, 0)
    small(1, True)
    vsum[...] = lax.fori_loop(0, n, lambda o, total: total + rv[o], jnp.zeros(vsum.shape, f32))

    @pl.when(is_time)
    def _():
        embeds(True)
        time_grad([d], rm, dtembs, ww, temb, hid, wt, gm, g2, g1, vsum, squares)

    @pl.when(role == 1)
    def _():
        pl.when(half == 0)(lambda: partial.wait_send())
        lax.fori_loop(0, TEXT_CUTS, lambda k, c: (text_hop(k).wait_send(), c)[1], 0)

    def collect(u, carry):
        @pl.when(a > 0)
        def _():
            upward(u, a).wait_recv()
            own[u, a] = own[u, a] + up[u, a]

        @pl.when(a < line - 1)
        def _():
            downward(u, a).wait_recv()
            own[u, a] = own[u, a] + down[u, a]

        whole = own[u, a]
        summed[u] = whole
        squares[0:1, :] += col_sum(whole * whole)
        return carry

    lax.fori_loop(0, count, collect, 0)

    def drain(u, carry):
        def one(i, c):
            upward(u, line - 1 - i).wait_send()
            return c

        def two(p, c):
            downward(u, p).wait_send()
            return c

        lax.fori_loop(0, line - 1 - a, one, 0)
        lax.fori_loop(0, a, two, 0)
        return carry

    lax.fori_loop(0, count, drain, 0)

    def others(line_in, whole):
        return lax.fori_loop(
            1, line, lambda k, acc: acc + line_in[lax.rem(a + k, line)].astype(f32), whole
        )

    @pl.when(is_last)
    def _():
        direct(TEXT_CUTS, sx, rz, True)
        whole = others(rz, own[8, a])
        summed[8] = whole
        squares[0:1, :] += col_sum(whole * whole)

    @pl.when(is_text)
    def _():
        def whole_cut(k, carry):
            direct(k, tsx.at[k], trz.at[k], True)
            whole = others(trz.at[k], tin[k, a, x].astype(f32) + trx[k, a].astype(f32))
            text[:, pl.ds(pl.multiple_of(k * step, 128), step)] = low(whole)
            lane = lax.broadcasted_iota(jnp.int32, (1, step), 1)
            spare = jnp.logical_and(k == TEXT_CUTS - 1, lane > step - 128)
            counted = jnp.where(spare, 0.0, whole)
            squares[0:1, :] += col_sum(counted * counted)
            return carry

        lax.fori_loop(0, TEXT_CUTS, whole_cut, 0)


def three(value):
    first = low(value)
    rest = value - first.astype(f32)
    second = low(rest)
    return first, second, low(rest - second.astype(f32))


def nn3(left, right):
    return sum(nn(piece, right) for piece in three(left))


def nt3(left, right):
    return sum(nt(piece, right) for piece in three(left))


def tn3(left, right):
    return sum(tn(left, piece) for piece in three(right))


def own_columns(rank, width, cols):
    row = lax.broadcasted_iota(jnp.int32, (width, 128), 0)
    col = lax.broadcasted_iota(jnp.int32, (width, 128), 1)
    return low(jnp.where(jnp.logical_and(row == rank * cols + col, col < cols), 1.0, 0.0))


def clip_groups(clips, rows):
    per = 8 * (rows // (clips // 8) // 8)
    left = lax.broadcasted_iota(jnp.int32, (clips, rows), 0)
    right = lax.broadcasted_iota(jnp.int32, (clips, rows), 1)
    match = (right // per) * 8 + (right % per) // 8 == left
    return low(jnp.where(match, 1.0, 0.0))


def silu_back(value):
    gate = jax.nn.sigmoid(value)
    return gate * (1.0 + value * (1.0 - gate))


def time_back(rank, rm, wm, temb, dtemb):
    cols, width = wm.shape[0], rm.shape[1]
    rows, clips = rm.shape[0], temb.shape[0]
    pick = own_columns(rank[0], width, cols)
    kind = lax.broadcasted_iota(jnp.int32, (rows, 1), 0) % 8
    value = rm[...]
    pieces = three(value)
    total = jnp.where(kind >= 6, nn3(value, pick), 0.0)
    zeros = jnp.zeros((128 - cols, width), bf16)

    def one(r, total):
        lanes = pl.ds(pl.multiple_of(r * width, 128), width)
        weight = jnp.concatenate([wm[:, lanes], zeros], axis=0)
        back = nt(pieces[0], weight) + nt(pieces[1], weight) + nt(pieces[2], weight)
        return total + jnp.where(kind == r, back, 0.0)

    total = lax.fori_loop(0, 6, one, total)
    slope = silu_back(nn3(temb[...], pick))
    group = clip_groups(clips, rows)

    def collapse(part):
        first, second, third = three(part)
        return nn(group, first) + nn(group, second) + nn(group, third)

    dtemb[...] = collapse(jnp.where(kind < 6, total, 0.0)) * slope + collapse(
        jnp.where(kind >= 6, total, 0.0)
    )


def time_grad(rank, rm, dtembs, ww, temb, hid, wt, gm, g2, g1, vout, tout):
    width, cols = rm.shape[1], vout.shape[0]
    rows, clips = rm.shape[0], temb.shape[0]
    n = dtembs.shape[0]
    pick = own_columns(rank[0], width, cols)
    kind = lax.broadcasted_iota(jnp.int32, (rows, 1), 0) % 8
    value = rm[...]
    hidden = hid[...]
    own_hid, own_temb = nn3(hidden, pick), nn3(temb[...], pick)
    gates = low(own_temb * jax.nn.sigmoid(own_temb))
    spread = low(tn(clip_groups(clips, rows), gates))
    pieces = three(value)
    count = jnp.zeros((1, 1), f32)

    def squared(block):
        return jnp.sum(jnp.sum(block * block, axis=1, keepdims=True), axis=0, keepdims=True)

    def one(r, count):
        masked = jnp.where(kind == r, spread.astype(f32), 0.0).astype(bf16)
        block = sum(tn(masked, piece) for piece in pieces)[0:cols]
        gm[:, pl.ds(pl.multiple_of(r * width, 128), width)] = block
        return count + squared(block)

    count = lax.fori_loop(0, 6, one, count)
    mine = dtembs[rank[0]]
    mine_pieces = three(mine)
    act = low(hidden * jax.nn.sigmoid(hidden))
    block = sum(tn(piece, act) for piece in mine_pieces)[0:cols]
    g2[...] = block
    count = count + squared(block)
    back = jnp.zeros((clips, 128), f32)
    zeros = jnp.zeros((128 - cols, 128), bf16)
    picked = low(nn(ww[:, 256 : 256 + width], pick))
    for o in range(n):
        weight = picked[o * cols : o * cols + cols]
        back = back + nn3(dtembs[o], jnp.concatenate([weight, zeros], axis=0))
    dhid = back * silu_back(own_hid)
    dhid_pieces = three(dhid)
    feature = low(wt[:, 0:256])
    block = sum(tn(piece, feature) for piece in dhid_pieces)[0:cols]
    g1[...] = block
    count = count + squared(block)
    at = lax.broadcasted_iota(jnp.int32, (clips, 128), 1)
    first = low(jnp.where(at == 1, 1.0, 0.0))
    second = low(jnp.where(at == 2, 1.0, 0.0))
    total = sum(tn(piece, first) for piece in dhid_pieces)
    total = total + sum(tn(piece, second) for piece in mine_pieces)
    row_kind = lax.broadcasted_iota(jnp.int32, (rows, 128), 0) % 8
    row_lane = lax.broadcasted_iota(jnp.int32, (rows, 128), 1)
    put = jnp.logical_and(row_lane == row_kind + 3, row_kind < 6)
    put = low(jnp.where(put, 1.0, 0.0))
    total = total + sum(tn(piece, put) for piece in three(nn3(value, pick)))

    vout[...] += total[0:cols]
    lane = lax.broadcasted_iota(jnp.int32, (1, 128), 1)
    tout[0:1, 0:128] += jnp.where(lane == 0, count, 0.0)


class Relay:
    def __init__(self, send, recv):
        self.d, self.s = here()
        self.role, self.half = self.s // 2, lax.rem(self.s, 2)
        self.other = dev(self.d, (1 - self.role) * 2 + self.half)
        self.mate = dev(self.d, self.role * 2 + 1 - self.half)
        self.send, self.recv = send, recv

    def at(self, r, h):
        return jnp.logical_and(self.role == r, self.half == h)

    def copy(self, i, leg, src, dst):
        target = self.other if leg == 0 else self.mate
        return remote(src, dst, self.send.at[i, leg], self.recv.at[i, leg], target)

    def start(self, i, src, dst):
        self.copy(i, 0, src, dst).start()
        self.copy(i, 1, src, dst).start()

    def middle(self, i, dst):
        self.copy(i, 0, dst, dst).wait_recv()
        self.copy(i, 2, dst, dst).start()

    def finish(self, r, h, items):
        @pl.when(self.at(r, h))
        def _():
            for i, src, dst in items:
                self.copy(i, 0, src, dst).wait_send()
                self.copy(i, 1, src, dst).wait_send()

        @pl.when(self.at(1 - r, h))
        def _():
            for i, src, dst in items:
                self.copy(i, 2, dst, dst).wait_send()

        @pl.when(self.at(r, 1 - h))
        def _():
            for i, src, dst in items:
                self.copy(i, 1, dst, dst).wait_recv()

        @pl.when(self.at(1 - r, 1 - h))
        def _():
            for i, src, dst in items:
                self.copy(i, 2, dst, dst).wait_recv()


def owner_first(role, mat):
    return 2 * mat + mat % 2 if role == 0 else mat


def owner_second(mat):
    return 2 + 3 * mat


def settle_kernel(n, vsum, tile, summed, att_m, feed_m, gm, g2, g1,
                  oa, of, xa, xf, xm, x2, x1, gv, stat,
                  vecs, tiles, mine, totals, look, mom,
                  msem, send, recv, own, gsend, grecv, gown, ssend, srecv, tsend, trecv):
    relay = Relay(gsend, grecv)
    d, s, role, half = relay.d, relay.s, relay.role, relay.half
    peers = [dev(d, lax.rem(s + k, 4)) for k in range(1, 4)]
    greet_dp(n, peers)
    four, eight = pl.ds(0, 4), pl.ds(0, 8)
    shared = {
        (0, 0): [(0, summed.at[four], xa.at[four]), (4, gm, xm), (5, g2, x2), (6, g1, x1)],
        (0, 1): [(1, summed.at[eight], xf.at[eight])],
        (1, 0): [(2, summed.at[eight], xa.at[pl.ds(4, 8)])],
        (1, 1): [(3, summed.at[eight], xf.at[pl.ds(8, 8)])],
    }
    def momentum(finish):
        sources = {
            (0, 0): (att_m.at[four], mom.at[four]),
            (0, 1): (feed_m.at[eight], mom),
            (1, 0): (att_m.at[pl.ds(4, 8)], mom),
            (1, 1): (feed_m.at[pl.ds(8, 8)], mom),
        }
        for (r, h), (src, dst) in sources.items():

            @pl.when(relay.at(r, h))
            def _():
                copy = pltpu.make_async_copy(src, dst, msem.at[0])
                copy.wait() if finish else copy.start()

    momentum(False)
    small = [(0, vsum, vecs), (1, tile, tiles)]
    for i, src, dst in small:
        for k in range(1, 4):
            remote(src, dst.at[s], ssend.at[i, k], srecv.at[i, k], peers[k - 1]).start()
    for (r, h), items in shared.items():

        @pl.when(relay.at(r, h))
        def _():
            for i, src, dst in items:
                pltpu.make_async_copy(src, dst, gown.at[i]).start()
                relay.start(i, src, dst)

    total, squares, losses = vsum[...], tile[0:1, :], tile[1:2, :]
    for k in range(1, 4):
        o = lax.rem(s + 4 - k, 4)
        for i, src, dst in small:
            remote(src, dst.at[o], ssend.at[i, k], srecv.at[i, k], dev(d, o)).wait()
        total = total + vecs[o]
        squares = squares + tiles[o, 0:1, :]
        losses = losses + tiles[o, 1:2, :]
    lane = lax.broadcasted_iota(jnp.int32, (1, 128), 1)
    total = jnp.where(jnp.logical_or(lane == 9, lane >= 77), 0.0, total)
    gv[...] = total

    def whole(block):
        return jnp.sum(jnp.sum(block, axis=1, keepdims=True), axis=0, keepdims=True)

    row = lax.broadcasted_iota(jnp.int32, (8, 128), 0)
    mine[...] = jnp.where(row < 4, whole(squares) + whole(total * total), whole(losses[:, 0:128]))
    so_far = mine[...]

    def start(k, carry):
        remote(mine, totals.at[d], tsend.at[k], trecv.at[k], dev(lax.rem(d + k, n), s)).start()
        return carry

    lax.fori_loop(1, n, start, 0)

    def finish(k, carry):
        o = lax.rem(d + n - k, n)
        remote(mine, totals.at[o], tsend.at[k], trecv.at[k], dev(o, s)).wait()
        return carry + totals[o]

    lax.fori_loop(1, n, lambda k, c: (finish(k, so_far), c)[1], 0)
    totals[d] = so_far
    so_far = lax.fori_loop(0, n, lambda o, c: c + totals[o], jnp.zeros((8, 128), f32))
    stat[...] = so_far
    factor = jnp.minimum(1.0, max_norm / (jnp.sqrt(so_far[0:1, 0:1]) + 1e-06))
    scale = factor * (1.0 + momentum_decay)

    momentum(True)

    def update(m, carry):
        look[m] = summed[m] * scale + mom[m] * (momentum_decay * momentum_decay)
        return carry

    lax.fori_loop(0, 8, update, 0)
    groups = []
    for r in range(2):
        mats = 4 if r == 0 else 8
        groups.append((r, 0, [(m, owner_first(r, m), look.at[m], oa) for m in range(mats)]))
        groups.append((
            r, 1, [(m, owner_second(m), look.at[pl.ds(4 * m, 4)], of) for m in range(2)]
        ))
    for r, h, mats in groups:

        @pl.when(relay.at(r, h))
        def _():
            for m, o, src, dst in mats:

                @pl.when(d == o)
                def _():
                    pltpu.make_async_copy(src, dst.at[d], own.at[0]).start()

                @pl.when(d != o)
                def _():
                    remote(src, dst.at[d], send.at[m], recv.at[d], dev(o, s)).start()

    for (r, h), items in shared.items():

        @pl.when(relay.at(1 - r, h))
        def _():
            for i, src, dst in items:
                relay.middle(i, dst)

    for r, h, mats in groups:

        @pl.when(relay.at(r, h))
        def _():
            for i, src, dst in shared[(r, h)]:
                pltpu.make_async_copy(src, dst, gown.at[i]).wait()
            for m, o, src, dst in mats:

                @pl.when(d == o)
                def _():
                    pltpu.make_async_copy(src, dst.at[d], own.at[0]).wait()

                    def arrived(k, carry):
                        p = lax.rem(d + n - k, n)
                        remote(src, dst.at[p], send.at[m], recv.at[p], dev(p, s)).wait_recv()
                        return carry

                    lax.fori_loop(1, n, arrived, 0)

                @pl.when(d != o)
                def _():
                    remote(src, dst.at[d], send.at[m], recv.at[d], dev(o, s)).wait_send()

    for (r, h), items in shared.items():
        relay.finish(r, h, items)


def spread_kernel(n, xa, xf, gy1, summed, oa, of, xy1, xy2, send, recv, rsend, rrecv, own, gown):
    relay = Relay(rsend, rrecv)
    d, s, role, half = relay.d, relay.s, relay.role, relay.half
    greet_dp(n, [relay.other, relay.mate])
    groups = []
    for r in range(2):
        mats = 4 if r == 0 else 8
        groups.append((r, 0, mats, functools.partial(owner_first, r), xa, oa, 10 * r, 4))
        groups.append((r, 1, 2, owner_second, xf, of, 10 * r + 8, 2))
    text = {
        (0, 0): [(20, gy1, xy1.at[0])],
        (0, 1): [(21, gy1, xy1.at[1])],
        (1, 1): [(22, summed.at[8], xy2)],
    }
    for (r, h), items in text.items():

        @pl.when(relay.at(r, h))
        def _():
            for i, src, dst in items:
                pltpu.make_async_copy(src, dst, gown.at[i - 20]).start()
                relay.start(i, src, dst)

    for r, h, mats, owner, src, dst, base, per in groups:

        @pl.when(relay.at(r, h))
        def _():
            for m in range(mats):

                @pl.when(d == owner(m))
                def _():
                    pltpu.make_async_copy(src.at[d], dst.at[per * r + m], own.at[m]).start()

                    def start(k, carry):
                        to = lax.rem(d + k, n)
                        remote(
                            src.at[to], dst.at[per * r + m], send.at[k], recv.at[m], dev(to, s)
                        ).start()
                        return carry

                    lax.fori_loop(1, n, start, 0)

            for m in range(mats):

                @pl.when(d == owner(m))
                def _():
                    pltpu.make_async_copy(src.at[d], dst.at[per * r + m], own.at[m]).wait()

                @pl.when(d != owner(m))
                def _():
                    remote(
                        src.at[d], dst.at[per * r + m], send.at[1], recv.at[m], dev(owner(m), s)
                    ).wait_recv()

                relay.start(base + m, dst.at[per * r + m], dst.at[per * r + m])

    for (r, h), items in text.items():

        @pl.when(relay.at(1 - r, h))
        def _():
            for i, src, dst in items:
                relay.middle(i, dst)

    for r, h, mats, owner, src, dst, base, per in groups:

        @pl.when(relay.at(1 - r, h))
        def _():
            for m in range(mats):
                relay.middle(base + m, dst.at[per * r + m])

    for r, h, mats, owner, src, dst, base, per in groups:

        @pl.when(relay.at(r, h))
        def _():
            for m in range(mats):

                @pl.when(d == owner(m))
                def _():
                    def finish(k, carry):
                        to = lax.rem(d + k, n)
                        remote(
                            src.at[to], dst.at[per * r + m], send.at[k], recv.at[m], dev(to, s)
                        ).wait_send()
                        return carry

                    lax.fori_loop(1, n, finish, 0)

        relay.finish(r, h, [(base + m, dst.at[per * r + m], dst.at[per * r + m]) for m in range(mats)])

    for (r, h), items in text.items():

        @pl.when(relay.at(r, h))
        def _():
            for i, src, dst in items:
                pltpu.make_async_copy(src, dst, gown.at[i - 20]).wait()

        relay.finish(r, h, items)


def adamw_update(weight, first, second, grad, fix_one, fix_two):
    first = beta_one * first + (1.0 - beta_one) * grad
    second = beta_two * second + (1.0 - beta_two) * grad * grad
    first_hat = first * fix_one
    second_hat = second * fix_two
    weight = weight - adam_rate * (
        first_hat / (jnp.sqrt(second_hat) + 1e-08) + weight_decay * weight
    )
    return (weight, first, second)


def update_kernel(
    rates, pieces, scal, stat,
    aw, am, ag, ax, fw, fm, fg, fx, sw, s1, s2, gv, g1, g2, gt, gy2, gm, vw, v1, v2, gvall, gtall,
    aw_, am_, ab_, fw_, fm_, fb_, sw_, s1_, s2_, sb_, vw_, v1_, v2_, vb_, loss_, norm_, powers,
):
    grad_norm = jnp.sqrt(stat[0:1, 0:1])
    factor = jnp.minimum(1.0, max_norm / (grad_norm + 1e-06))

    @pl.when(pl.program_id(0) == 0)
    def _():
        for i, beta in enumerate((beta_one, beta_two)):
            powers[i] = lax.fori_loop(0, scal[0], lambda _, value: value * beta, jnp.float32(1.0))

    fix_one, fix_two = (1.0 / (1.0 - jnp.full((1, 1), powers[i])) for i in range(2))
    loss_[...] = stat[4:5, 0:1]
    norm_[...] = grad_norm
    shrink = 1.0 - muon_rate * weight_decay
    for rate, (w, m, g, x, w_, m_, b_) in zip(
        rates, ((aw, am, ag, ax, aw_, am_, ab_), (fw, fm, fg, fx, fw_, fm_, fb_))
    ):
        m_[...] = momentum_decay * m[...] + g[...] * factor
        fresh = w[...] * shrink - rate * x[...].astype(f32)
        w_[...] = fresh
        b_[...] = low(fresh)
    text = gt.shape[1] - 128
    shards = {
        "embed": gv[:, EMB0 : EMB0 + 16],
        "time": g1[...],
        "time2": g2[...],
        "text": None,
        "text2": gy2[...],
        "head": gv[:, HEAD0 : HEAD0 + 16],
        "mod": gm[...],
    }
    for name, at, size in pieces:
        stride = size if name != "text" else 512
        for start in range(0, size, stride):
            cut = slice(at + start, at + start + stride)
            grad = gt[:, start : start + stride].astype(f32) if name == "text" else shards[name]
            fresh, one, two = adamw_update(
                sw[:, cut], s1[:, cut], s2[:, cut], grad * factor, fix_one, fix_two
            )
            sw_[:, cut], s1_[:, cut], s2_[:, cut] = fresh, one, two
            sb_[:, cut] = low(fresh)

    @pl.when(pl.program_id(0) == 0)
    def _():
        lane = lax.broadcasted_iota(jnp.int32, (1, 128), 1)
        column = gtall[:, text : text + 128].astype(f32)
        whole = jnp.where(lane == 9, column, gvall[...])
        rows = vw.shape[0]
        grad = jnp.transpose(whole)[0:rows, :] * factor
        fresh, one, two = adamw_update(vw[...], v1[...], v2[...], grad, fix_one, fix_two)
        vw_[...], v1_[...], v2_[...] = fresh, one, two
        vb_[...] = low(fresh)


def body(
    latents,
    noise_draw,
    timesteps,
    captions,
    caption_len,
    attention_weights,
    feed_weights,
    side_weights,
    vector_weights,
    attention_momentum,
    feed_momentum,
    side_first,
    side_second,
    vector_first,
    vector_second,
    step_count,
):
    n = lax.axis_size("dp")
    d, s = here()
    role, half = s // 2, lax.rem(s, 2)
    count = latents.shape[0]
    frames = latents.shape[1]
    width = attention_weights.shape[1]
    cols, feed_cols = attention_weights.shape[2], feed_weights.shape[2]
    hidden = n * feed_cols
    text = captions.shape[2]
    sds = jax.ShapeDtypeStruct
    role_s, half_s = role.reshape(1).astype(jnp.int32), half.reshape(1).astype(jnp.int32)

    o_time = 16
    o_text = o_time + 256 + width
    o_text2 = o_text + text
    o_head = o_text2 + width
    o_mod = o_head + 16
    six = 6 * width
    own_rows = -(-cols // 2)
    lanes = n * own_rows

    att_t = jnp.swapaxes(attention_weights, 1, 2)
    feed_t = jnp.swapaxes(feed_weights, 1, 2)
    side_t = side_weights.T
    pa, pb, pf, pw, py, pm, wm_own = local_call(
        lambda role, half, *refs: pack_kernel(
            role, half, (o_time, o_text, o_text2, o_head, o_mod), *refs
        ),
        [
            sds((4, cols, width), bf16),
            sds((4, cols, width), bf16),
            sds((2, feed_cols, width), bf16),
            sds((cols, 1152), bf16),
            sds((own_rows, text), bf16),
            sds((cols, 3 * width), bf16),
            sds((cols, six), bf16),
        ],
        [SM] * 2 + [VM] * 4,
        (role_s, half_s, att_t, feed_t, side_t, vector_weights),
    )
    freqs = jnp.exp(-math.log(10000.0) * jnp.arange(128, dtype=f32) / 128)
    angles = timesteps.astype(f32)[:, None] * freqs[None, :]
    level, snr = snr_weight(timesteps.astype(f32))
    mix = jnp.stack([snr, jnp.sqrt(level), jnp.sqrt(1.0 - level)], axis=1)
    pt = jnp.concatenate([jnp.cos(angles), jnp.sin(angles), mix], axis=1)
    pt = jnp.pad(pt, ((0, 8 - count), (0, width - 259)))

    wa, wb, wf, ww, wy, wm, wt = comm_call(
        functools.partial(gather_kernel, n),
        1,
        (pa, pb, pf, pw, py, pm, pt),
        [
            sds((4, n, cols, width), bf16),
            sds((4, n, cols, width), bf16),
            sds((2, n, feed_cols, width), bf16),
            sds((n, cols, 1152), bf16),
            sds((n, own_rows, text), bf16),
            sds((n, cols, 3 * width), bf16),
            sds((n, 8, width), f32),
        ],
        [(4, 7, n), (7, n), (7, n), (7,)],
    )
    wa = wa.reshape(4, width, width)
    wb = wb.reshape(4, width, width)
    wf = wf.reshape(2, hidden, width)
    ww = ww.reshape(width, 1152)
    wy = wy.reshape(lanes, text)
    wm = wm.reshape(width, 3 * width)
    rank_s = d.reshape(1).astype(jnp.int32)
    per_clip = frames * (latents.shape[3] // 2) * (latents.shape[4] // 2)
    vec, hid, temb, mq_own, y2p, errs = local_call(
        functools.partial(condition_kernel, per_clip=per_clip, cols=cols),
        [
            sds((128, width), f32),
            sds((n * 8, width), f32),
            sds((n * 8, width), f32),
            sds((8, 3 * width), f32),
            sds((2, width, lanes), bf16),
            sds((8, 128), f32),
        ],
        [SM] + [VM] * 3,
        (rank_s, wt.reshape(n * 8, width), ww, wm),
    )
    mq = comm_call(
        mate_kernel, 2, (mq_own,), sds((2, 8, 3 * width), f32), [(1,), (1,), (1,)]
    )

    half_tokens = count * per_clip // 2
    places = np.arange(per_clip // frames)
    edge = latents.shape[3] // 2
    pos = np.concatenate(
        [sincos(places // edge, width // 2), sincos(places % edge, width // 2)], axis=1
    )
    pos = jnp.asarray(pos)
    timing = jnp.asarray(sincos(np.arange(frames), width))

    clip_rows = captions.shape[1]
    residuals = [
        sds((5, half_tokens, width), bf16),
        sds((3, half_tokens, width), f32),
        sds((half_tokens, hidden), f32),
        sds((count, 3, 256, 128), f32),
    ]
    residual_scratch = [pltpu.VMEM(v.shape, v.dtype) for v in residuals]
    h1s, hq, gq_own, tok, kept_b, kept_f, kept_u, kept_p = local_call(
        functools.partial(first_kernel, cols),
        [
            sds((count, 2, 64, width), bf16),
            sds((count, LP, lanes), f32),
            sds((count, LP, lanes), bf16),
            sds((half_tokens, 128), bf16),
        ]
        + residuals,
        [SM] * 2 + [VM] * 9 + [ANY],
        (role_s, half_s, latents, noise_draw, pt, pos, mq, vec, wa, wf, wy, captions),
        residual_scratch
        + [
            pltpu.VMEM((count, clip_rows, text), bf16),
            pltpu.SemaphoreType.DMA((count,)),
            pltpu.SemaphoreType.DMA((count, 4)),
        ],
        [VM] * 4 + [ANY] * 4,
    )
    h1t, rgq, mqt = comm_call(
        functools.partial(forward_kernel, count),
        3,
        (h1s, gq_own, mq),
        [
            sds((count, 2, 64, width), bf16),
            sds((count, LP, lanes), bf16),
            sds((2, 8, 3 * width), f32),
        ],
        [(count, 2), (count, 2), (1,), (1,), (2,), (2,)],
    )

    ncl = (count + 1) // 2
    wide = sds((2, half_tokens, hidden), bf16)
    thin = sds((2, half_tokens, width), bf16)
    cap_like = sds((ncl, LP, width), bf16)
    dh1, acts_t, actf_t, actw_t, ybuf, dkv, grads_t, dmod_t, loss_t = local_call(
        temporal_kernel,
        [
            sds((count, 2, 64, width), bf16),
            sds((10, half_tokens, width), bf16),
            thin,
            wide,
            cap_like,
            sds((2, ncl, LP, width), f32),
            sds((128, width), f32),
            sds((count, 8, width), f32),
            sds((1, 128), f32),
        ],
        [SM] * 4 + [VM] * 13,
        (
            role_s, half_s, rank_s, caption_len, errs, h1t, timing, mqt, vec, temb, wa, wb, wf,
            gq_own, rgq, y2p, noise_draw,
        ),
        [pltpu.VMEM((ncl, KP, width), bf16), pltpu.VMEM((ncl, KP, width), bf16)],
    )
    dhs, extra = comm_call(
        functools.partial(backward_kernel, count),
        4,
        (dh1, dkv),
        [sds((count, 2, 64, width), bf16), sds((2, LP, width), f32)],
        [(count, 2), (count, 2), (1,), (1,)],
    )
    acts_s, actf_s, actw_s, dkvb, dy, vect, dmod = local_call(
        last_kernel,
        [
            sds((6, half_tokens, width), bf16),
            thin,
            wide,
            sds((2, ncl, LP, width), bf16),
            cap_like,
            sds((width, 128), f32),
            sds((count, 8, width), f32),
        ],
        [SM] * 2 + [VM] * 6 + [ANY] * 4 + [VM] * 5,
        (
            role_s, half_s, tok, mq, vec, wa, wb, wf, kept_b, kept_f, kept_u, kept_p, dhs, dkv,
            extra, grads_t, dmod_t,
        ),
        [pltpu.VMEM((128, width), f32)]
        + residual_scratch
        + [pltpu.SemaphoreType.DMA((count, 4))],
    )
    racts, ractf, ractw, rybuf, rdkvb, rdy, rdmod = comm_call(
        swap_kernel,
        5,
        (acts_s, acts_t, actf_s, actf_t, actw_s, actw_t, ybuf, dkvb, dy, dmod),
        [
            sds((10, half_tokens, width), bf16),
            thin,
            wide,
            cap_like,
            sds((2, ncl, LP, width), bf16),
            cap_like,
            sds((count, 8, width), f32),
        ],
        [(5,), (5,)],
    )
    line = n // 2
    wide_text = text + 128
    cut_text = wide_text // TEXT_CUTS
    block = (9, line, cols, width)
    tokens2 = 2 * half_tokens
    grad_own, grad_snd, text_part = local_call(
        weight_grad_kernel,
        [
            sds(block, f32),
            sds(block, bf16),
            sds((line, 2, own_rows, wide_text), bf16),
        ],
        [SM] * 3 + [ANY] * 9 + [VM] * 10 + [ANY],
        (
            role_s, half_s, rank_s, acts_s, acts_t, racts, actf_s, actf_t, ractf, actw_s, actw_t,
            ractw, ybuf, rybuf, dkvb, rdkvb, dy, rdy, gq_own, rgq, hq, y2p, captions,
        ),
        [
            pltpu.VMEM((10, tokens2, width), bf16),
            pltpu.VMEM((2, tokens2, width), bf16),
            pltpu.VMEM((2, tokens2, hidden), bf16),
            pltpu.VMEM((count, clip_rows, text), bf16),
            pltpu.VMEM((width, width), f32),
            pltpu.VMEM((count, lanes, LP), bf16),
            pltpu.VMEM((lanes, 128), f32),
            pltpu.SemaphoreType.DMA((4 + count,)),
        ],
    )

    whole_clips = n * 8
    text_block = (TEXT_CUTS, line, own_rows, cut_text)
    summed, text_sum, vsum, tile, grad_mod, grad_time2, grad_time1 = comm_call(
        functools.partial(scatter_kernel, n),
        6,
        (
            grad_own, grad_snd, text_part, vect.reshape(n, cols, 128), dmod, rdmod, loss_t,
            wm_own, temb, ww, hid, wt.reshape(whole_clips, width),
        ),
        [
            sds((9, cols, width), f32),
            sds((own_rows, wide_text), bf16),
            sds((cols, 128), f32),
            sds((8, width), f32),
            sds((cols, six), f32),
            sds((cols, width), f32),
            sds((cols, 256), f32),
        ],
        [(9,), (9 + TEXT_CUTS,), (9 + TEXT_CUTS,)]
        + [(TEXT_CUTS + 1, line)] * 2
        + [(8, line)] * 4
        + [(2, n), (2, n), (2,), (TEXT_CUTS,), (TEXT_CUTS,), (n,), (n,), (1,), (1,)],
        [VM] * 7,
        in_specs=[ANY] * 4 + [VM] * 8,
        scratch=[
            pltpu.VMEM(block, f32),
            pltpu.VMEM(block, bf16),
            pltpu.VMEM((8,) + block[1:], f32),
            pltpu.VMEM((8,) + block[1:], f32),
            pltpu.VMEM(block[1:], bf16),
            pltpu.VMEM(block[1:], bf16),
            pltpu.VMEM((TEXT_CUTS, line, 2, own_rows, cut_text), bf16),
        ]
        + [pltpu.VMEM(text_block, bf16)] * 3
        + [
            pltpu.VMEM((n, cols, 128), f32),
            pltpu.VMEM((n * 8 * count, width), f32),
            pltpu.VMEM((n, whole_clips, 128), f32),
            pltpu.VMEM((8 * count, width), f32),
            pltpu.VMEM((8 * count, width), f32),
        ],
    )

    att_m = jnp.swapaxes(attention_momentum, 1, 2)
    feed_m = jnp.swapaxes(feed_momentum, 1, 2)
    ua, uf, ga2, gf2, grad_mod, grad_time2, grad_time1, grad_v, stat = comm_call(
        functools.partial(settle_kernel, n),
        8,
        (
            vsum, tile, summed, att_m, feed_m.reshape(16, cols, width), grad_mod, grad_time2,
            grad_time1,
        ),
        [
            sds((n, cols, width), f32),
            sds((n, 4, cols, width), f32),
            sds((12, cols, width), f32),
            sds((16, cols, width), f32),
            sds((cols, six), f32),
            sds((cols, width), f32),
            sds((cols, 256), f32),
            sds((cols, 128), f32),
            sds((8, 128), f32),
        ],
        [(1,), (8,), (n,), (1,), (7, 3), (7, 3), (7,), (2, 4), (2, 4), (n,), (n,)],
        [ANY] * 7 + [VM] * 2,
        in_specs=[VM] * 3 + [ANY] * 5,
        scratch=[
            pltpu.VMEM((4, cols, 128), f32),
            pltpu.VMEM((4, 8, width), f32),
            pltpu.VMEM((8, 128), f32),
            pltpu.VMEM((n, 8, 128), f32),
            pltpu.VMEM((8, cols, width), f32),
            pltpu.VMEM((8, cols, width), f32),
        ],
    )
    xa, xf = local_call(
        muon_kernel,
        [sds((width, width), bf16), sds((hidden, width), bf16)],
        [SM] + [VM] * 2,
        (half_s, ua.reshape(width, width), uf.reshape(hidden, width)),
        [pltpu.VMEM((width, width), f32), pltpu.VMEM((width, width), f32)],
    )
    xa_all, xf_all, gy12, gy22 = comm_call(
        functools.partial(spread_kernel, n),
        10,
        (xa.reshape(n, cols, width), xf.reshape(n, feed_cols, width), text_sum, summed),
        [
            sds((12, cols, width), bf16),
            sds((4, feed_cols, width), bf16),
            sds((2, own_rows, wide_text), bf16),
            sds((cols, width), f32),
        ],
        [(n,), (8,), (23, 3), (23, 3), (8,), (3,)],
    )

    text_grad = gy12.reshape(2 * own_rows, wide_text)[:cols]
    side_m, side_v = side_first.T, side_second.T
    side_rows = side_t.shape[1]
    pieces = (
        ("embed", 0, 16),
        ("time", o_time, 256),
        ("time2", o_time + 256, width),
        ("text", o_text, text),
        ("text2", o_text2, width),
        ("head", o_head, 16),
        ("mod", o_mod, six),
    )
    rates = tuple(
        muon_rate * 0.2 * math.sqrt(columns) for columns in (n * cols, n * feed_cols)
    )
    grid = cols // 8 if cols % 8 == 0 else 1

    def by_rows(value):
        return value.reshape(-1, value.shape[-1])

    def rows_spec(value):
        return pl.BlockSpec((value.shape[0] // grid, value.shape[1]), lambda i: (i, 0))

    def whole_spec(value):
        return pl.BlockSpec(value.shape, lambda i: (0, 0))

    cutup = [by_rows(v) for v in (att_t, att_m, ga2, xa_all, feed_t, feed_m, gf2, xf_all)] + [
        side_t, side_m, side_v, grad_v, grad_time1, grad_time2, text_grad, gy22, grad_mod,
    ]
    fixed = [vector_weights, vector_first, vector_second, grad_v, text_grad]
    a_like, f_like, s_like = (sds(v.shape, f32) for v in (cutup[0], cutup[4], side_t))
    v_like = sds(vector_weights.shape, f32)

    def low_of(like):
        return sds(like.shape, bf16)

    row_outs = [
        a_like, a_like, low_of(a_like), f_like, f_like, low_of(f_like), s_like, s_like, s_like,
        low_of(s_like),
    ]
    whole_outs = [v_like, v_like, v_like, low_of(v_like), sds((1, 1), f32), sds((1, 1), f32)]
    (
        att_new, att_moment, att_low, feed_new, feed_moment, feed_low, side_new, side_first_new,
        side_second_new, side_low, vector_new, vector_first_new, vector_second_new, vector_low,
        loss_value, grad_norm,
    ) = pl.pallas_call(
        functools.partial(update_kernel, rates, pieces),
        grid=(grid,),
        out_shape=row_outs + whole_outs,
        in_specs=[SM, whole_spec(stat)] + [rows_spec(v) for v in cutup] + [whole_spec(v) for v in fixed],
        out_specs=[rows_spec(v) for v in row_outs] + [whole_spec(v) for v in whole_outs],
        scratch_shapes=[pltpu.SMEM((2,), f32)],
        compiler_params=pltpu.CompilerParams(vmem_limit_bytes=VMEM_LIMIT),
    )(step_count, stat, *cutup, *fixed)

    def att(value):
        return value.reshape(att_t.shape)

    def feed(value):
        return value.reshape(feed_t.shape)

    def back(value):
        return jnp.swapaxes(value, -1, -2)

    return (
        loss_value[0, 0],
        grad_norm[0, 0],
        back(att(att_new)),
        back(att(att_moment)),
        back(feed(feed_new)),
        back(feed(feed_moment)),
        back(side_new),
        back(side_first_new),
        back(side_second_new),
        vector_new,
        vector_first_new,
        vector_second_new,
        back(att(att_low)),
        back(feed(feed_low)),
        back(side_low),
        vector_low,
    )


def solution(mesh):
    column = P(None, "dp")
    matrix = P(None, None, "dp")
    return jax.shard_map(
        body,
        mesh=mesh,
        in_specs=(
            P("dp", None, None, None, None),
            P("dp", None, None, None, None),
            P("dp"),
            P("dp", None, None),
            P("dp"),
            matrix,
            matrix,
            column,
            column,
            matrix,
            matrix,
            column,
            column,
            column,
            column,
            P(),
        ),
        out_specs=(
            P(),
            P(),
            matrix,
            matrix,
            matrix,
            matrix,
            column,
            column,
            column,
            column,
            column,
            column,
            matrix,
            matrix,
            column,
            column,
        ),
        check_vma=False,
    )
```
